32 devices in a mesh: wide: 8 (over y, x, core), narrow: 4 (over z).
Axes of the slice: x: 2, y: 2, z: 4, core: 2. Of those that a mesh axis runs over, the one named last changes fastest.
Arguments:
- tokens: bfloat16 [2048, 2048], P('wide', 'narrow'), may hold values from -6 to 6
- gain_attn: bfloat16 [2048], P('narrow'), may hold values from 0.5 to 1.5
- w_query: bfloat16 [2048, 2048], P('wide', 'narrow'), may hold values from -0.1875 to 0.1875
- w_key: bfloat16 [2048, 2048], P('wide', 'narrow'), may hold values from -0.1875 to 0.1875
- w_value: bfloat16 [2048, 2048], P('wide', 'narrow'), may hold values from -0.125 to 0.125
- w_out: bfloat16 [2048, 2048], P('wide', 'narrow'), may hold values from -0.5 to 0.5
- gain_ffn: bfloat16 [2048], P('narrow'), may hold values from 0.5 to 1.5
- w_router: bfloat16 [2048, 4], P('wide'), may hold values from -0.09375 to 0.09375
- w_gate: bfloat16 [2048, 4, 5632], P('wide', None, 'narrow'), may hold values from -0.125 to 0.125
- w_up: bfloat16 [2048, 4, 5632], P('wide', None, 'narrow'), may hold values from -0.125 to 0.125
- w_down: bfloat16 [2048, 4, 5632], P('wide', None, 'narrow'), may hold values from -0.109375 to 0.109375
- segment: int32 [8, 256], P('wide'), may hold values from 0 to 12, never falling along the last dimension, each value on 1 to 102 neighbouring positions
- parents: int32 [8, 13], P('wide'), may hold values from 0 to 4, as said below
- expert_ids: int32 [2048, 2], P('wide'), may hold values from 0 to 3, all different within a row
- slot_order: int32 [8, 256], P('wide'), may hold values from 0 to 255, each once within a row
- cotangent: bfloat16 [2048, 2048], P('wide', 'narrow'), may hold values from -6 to 6
Outputs:
- output: bfloat16 [2048, 2048], P('wide', 'narrow')
- grad_tokens: float32 [2048, 2048], P('wide', 'narrow')
- grad_gain_attn: float32 [2048], P('narrow')
- grad_w_query: float32 [2048, 2048], P('wide', 'narrow')
- grad_w_key: float32 [2048, 2048], P('wide', 'narrow')
- grad_w_value: float32 [2048, 2048], P('wide', 'narrow')
- grad_w_out: float32 [2048, 2048], P('wide', 'narrow')
- grad_gain_ffn: float32 [2048], P('narrow')
- grad_w_router: float32 [2048, 4], P('wide')
- grad_w_gate: float32 [2048, 4, 5632], P('wide', None, 'narrow')
- grad_w_up: float32 [2048, 4, 5632], P('wide', None, 'narrow')
- grad_w_down: float32 [2048, 4, 5632], P('wide', None, 'narrow')
The draws below stay inside these ranges and needn't reach their ends.
Inputs may be any that keep to these rules, and one draw needn't show every extreme that they name: In every tree, segment 0 is the trunk and has entry 0; segments 1 to 4 have parent 0; segments 5 to 12 have parents among 1 to 4, two on each. `segment`: segment numbers never fall within a tree; all 13 segments are present. `expert_ids`: the two experts of a token differ. `slot_order`: each row is a permutation of the numbers below 256.
All inputs are finite; a program needn't handle non-finite values.
Results may differ from the reference program's by a relative error of at most 0.03.
Values may be sent and summed in bfloat16 or wider, within the bound.
A program may use at most 448 MiB of HBM per device.

```python
import math
import jax
import jax.numpy as jnp
import numpy as np
from jax import lax

D = 2048
HEADS = 16
HEAD_DIM = 128
FF = 5632
EXPERTS = 4
TOP = 2
SEGS = 13
TOK_DEV = 256
TREES = 8
TOKENS = 2048
CAP = 144


def draw_parents(key, part):
    tree_keys = jax.random.split(key, TREES)

    def one_tree(tree_key):
        order = jax.random.permutation(tree_key, 8).astype(jnp.int32)
        return jnp.concatenate([jnp.zeros((5,), jnp.int32), 1 + order // 2])
    return jax.vmap(one_tree)(tree_keys).astype(jnp.int32)


def block_scale(own_key, shape, cuts, least, top_value):
    loudness = 1.0
    for axis_at, parts in cuts:
        steps = jax.random.uniform(jax.random.fold_in(jax.random.fold_in(own_key, 6), axis_at), (parts,), jnp.float32, least / len(cuts), top_value / len(cuts))
        loudness = loudness * jnp.repeat(jnp.exp(steps), shape[axis_at] // parts).reshape((-1,) + (1,) * (len(shape) - 1 - axis_at))
    return loudness


def distinct(rng, rows, amount, top, lift):
    ranking = jax.random.permutation(jax.random.fold_in(rng, 1), amount)
    boost = ranking
    for power in range(3):
        boost = boost * boost // amount
    boost = boost * lift // amount
    tickets = jax.random.randint(jax.random.fold_in(rng, 2), (rows, amount), 0, 4096) + boost
    fixed_rows = jax.random.permutation(jax.random.fold_in(rng, 3), rows)[jnp.arange(amount) % rows]
    tickets = jnp.where(jnp.arange(rows)[:, None] == fixed_rows[None, :], 1 << 14, tickets)
    score = tickets * amount + jnp.arange(amount)
    return lax.top_k(score.astype(jnp.int32), top)[1].astype(jnp.int32)


def length_profile(count, total, bound, skew):
    portions = [(1 << 20) // math.isqrt(grade ** skew) + 1 for grade in range(2, count + 1)]
    surplus, given = total - bound - (count - 1), [1] * (count - 1)
    while surplus > 0:
        movable = [i for i in range(count - 1) if given[i] < bound]
        pool, budget = sum([portions[i] for i in movable]), surplus
        for i in movable:
            extra = min(bound - given[i], max(1, budget * portions[i] // pool), surplus)
            given[i] = given[i] + extra
            surplus = surplus - extra
    return np.array([bound] + given)


def uneven_parts(stream_key, number_of, total, most, slope):
    if number_of == 2:
        one = jax.random.randint(stream_key, (), max(1, total - most), min(most, total - 1) + 1)
        return jnp.stack([one, total - one])
    sizes = jnp.asarray(length_profile(number_of, total, most, slope), jnp.int32)
    twos = (number_of - 1) // 2
    giver, sink = sizes[1:1 + 2 * twos:2], sizes[2:2 + 2 * twos:2]
    margin = jnp.minimum(giver - 1, most - sink)
    passed = jax.random.randint(jax.random.fold_in(stream_key, 1), (twos,), 0, 1 << 20) % (margin + 1)
    sizes = sizes.at[1:1 + 2 * twos:2].set(giver - passed).at[2:2 + 2 * twos:2].set(sink + passed)
    return sizes[jax.random.permutation(jax.random.fold_in(stream_key, 2), number_of)]


def noise(rng, dims, deviation, most, shards=(), kind=jnp.bfloat16):
    loudness = block_scale(rng, dims, shards, -0.22, 0.18) if shards else 1.0
    values = jax.random.normal(rng, dims, jnp.float32) * deviation * loudness
    return jnp.minimum(jnp.maximum(values, -most), most).astype(kind)


def setup_inputs(seed: int = 0) -> dict:
    splits = jax.random.split(jax.random.key(seed), 17)
    tokens = noise(splits[0], (TOKENS, D), 1.0, 6.0, ((0, 8), (1, 4)))
    gain_attn = jnp.clip(1.0 + 0.1 * jax.random.normal(splits[1], (D,), jnp.float32), 0.5, 1.5).astype(jnp.bfloat16)
    w_query = noise(splits[2], (D, D), (D // 2) ** -0.5, 0.1875, ((0, 8), (1, 4)))
    w_key = noise(splits[3], (D, D), (D // 2) ** -0.5, 0.1875, ((0, 8), (1, 4)))
    w_value = noise(splits[4], (D, D), D ** -0.5, 0.125, ((0, 8), (1, 4)))
    w_out = noise(splits[5], (D, D), (D // 16) ** -0.5, 0.5, ((0, 8), (1, 4)))
    gain_ffn = jnp.clip(1.0 + 0.1 * jax.random.normal(splits[6], (D,), jnp.float32), 0.5, 1.5).astype(jnp.bfloat16)
    w_router = noise(splits[7], (D, EXPERTS), (2 * D) ** -0.5, 0.09375, ((0, 8),))
    w_gate = noise(splits[8], (D, EXPERTS, FF), D ** -0.5, 0.125, ((0, 8), (2, 4)))
    w_up = noise(splits[9], (D, EXPERTS, FF), D ** -0.5, 0.125, ((0, 8), (2, 4)))
    w_down = noise(splits[10], (D, EXPERTS, FF), (FF // 2) ** -0.5, 0.109375, ((0, 8), (2, 4)))
    segment = jax.vmap(lambda own: jnp.searchsorted(jnp.cumsum(uneven_parts(own, SEGS, TOK_DEV, 2 * TOK_DEV // 5, 1)), jnp.arange(TOK_DEV), side="right"))(jax.random.split(splits[11], TREES)).reshape((TREES, TOK_DEV)).astype(jnp.int32)
    parents = draw_parents(jax.random.fold_in(splits[16], 71), 0)
    expert_ids = distinct(splits[13], TOKENS, EXPERTS, TOP, 4096)
    slot_order = jax.vmap(lambda own: jax.random.permutation(own, TOK_DEV))(jax.random.split(splits[14], TREES)).reshape((TREES, TOK_DEV)).astype(jnp.int32)
    cotangent = noise(splits[15], (TOKENS, D), 1.0, 6.0, ((0, 8), (1, 4)))
    return dict(tokens=tokens, gain_attn=gain_attn, w_query=w_query, w_key=w_key, w_value=w_value, w_out=w_out, gain_ffn=gain_ffn, w_router=w_router, w_gate=w_gate, w_up=w_up, w_down=w_down, segment=segment, parents=parents, expert_ids=expert_ids, slot_order=slot_order, cotangent=cotangent)


HIGH_PREC = lax.Precision.HIGHEST
NORM_EPS = 1e-05
NEG_FILL = -1e+30
ROPE_BASE = 10000.0

@jax.custom_vjp
def low(v):
    return lax.optimization_barrier(v.astype(jnp.bfloat16)).astype(jnp.float32)

@jax.custom_vjp
def low_back(v):
    return v

def low_keep(v):
    return (low(v), None)

def low_pass(kept, grad):
    return (grad,)

def back_keep(v):
    return (v, None)

def back_low(kept, grad):
    return (low(grad),)
low.defvjp(low_keep, low_pass)
low_back.defvjp(back_keep, back_low)

def tree_layout(segment_row, parent_row):
    seg_ids = jnp.arange(SEGS, dtype=jnp.int32)
    member = (segment_row[:, None] == seg_ids[None, :]).astype(jnp.int32)
    parent_of = (parent_row[:, None] == seg_ids[None, :]) & (seg_ids[:, None] != 0)
    itself = seg_ids[:, None] == seg_ids[None, :]
    reach = itself
    for _ in range(3):
        reach = itself | jnp.any(parent_of[:, :, None] & reach[None, :, :], axis=1)
    lengths = lax.optimization_barrier(jnp.sum(member, 0))
    starts = lax.optimization_barrier(jnp.sum(jnp.where(seg_ids[None, :] < seg_ids[:, None], lengths[None, :], 0), 1))
    before = lax.optimization_barrier(jnp.sum(jnp.where(reach, lengths[None, :], 0), 1)) - lengths
    places = lax.optimization_barrier(jnp.sum(member * (before - starts)[None, :], 1)) + jnp.arange(segment_row.shape[0], dtype=jnp.int32)
    return (member.astype(jnp.float32), reach.astype(jnp.float32), places.astype(jnp.float32))

def visible(member, reach, first_row, block_rows):
    local_rows = lax.dynamic_slice_in_dim(member, first_row, block_rows, 0)
    lineage = jnp.dot(local_rows, reach, precision=HIGH_PREC)
    shared = jnp.dot(lineage, member.T, precision=HIGH_PREC) > 0.5
    row_at = first_row + jnp.arange(block_rows, dtype=jnp.int32)
    col_at = jnp.arange(member.shape[0], dtype=jnp.int32)
    return shared & (col_at[None, :] <= row_at[:, None])

def rotate(vectors, places, direction):
    half_dim = vectors.shape[-1] // 2
    freqs = ROPE_BASE ** (-2.0 * jnp.arange(half_dim, dtype=jnp.float32) / vectors.shape[-1])
    angles = places[:, None] * freqs[None, :]
    cosines = jnp.cos(angles)[:, None, :]
    sine_vals = direction * jnp.sin(angles)[:, None, :]
    first_half = vectors[..., :half_dim]
    second_half = vectors[..., half_dim:]
    return jnp.concatenate([first_half * cosines - second_half * sine_vals, second_half * cosines + first_half * sine_vals], -1)

def gate_pair(logits, hot_first, hot_second):
    chances = jax.nn.softmax(logits, axis=-1)
    first_share = lax.optimization_barrier(jnp.sum(chances * hot_first, 1))
    second_share = lax.optimization_barrier(jnp.sum(chances * hot_second, 1))
    pair_total = first_share + second_share
    return (first_share / pair_total, second_share / pair_total)

def route(expert_row, slot_rank):
    token_count = expert_row.shape[0]
    expert_range = jnp.arange(EXPERTS, dtype=jnp.int32)
    hot_first = (expert_row[:, 0:1] == expert_range[None, :]).astype(jnp.float32)
    hot_second = (expert_row[:, 1:2] == expert_range[None, :]).astype(jnp.float32)
    earlier = (slot_rank[None, :] < slot_rank[:, None]).astype(jnp.float32)
    count_first = lax.optimization_barrier(jnp.sum(earlier[:, :, None] * hot_first[None, :, :], 1))
    count_second = lax.optimization_barrier(jnp.sum(earlier[:, :, None] * hot_second[None, :, :], 1))
    ahead_first = lax.optimization_barrier(jnp.sum(count_first * hot_first, 1))
    ahead_second = lax.optimization_barrier(jnp.sum((count_second + lax.optimization_barrier(jnp.sum(hot_first, 0))[None, :]) * hot_second, 1))
    slot_index = jnp.stack([ahead_first, ahead_second], 1).astype(jnp.int32)
    kept_mask = slot_index < CAP
    flat_slot = jnp.where(kept_mask, expert_row * CAP + slot_index, EXPERTS * CAP).astype(jnp.int32)
    token_index = jnp.broadcast_to(jnp.arange(token_count, dtype=jnp.int32)[:, None], (token_count, 2))
    slot_table = jnp.full((EXPERTS * CAP + 1,), token_count, jnp.int32).at[flat_slot.reshape(-1)].set(token_index.reshape(-1))[:EXPERTS * CAP]
    return (hot_first, hot_second, kept_mask.astype(jnp.float32), flat_slot, slot_table)

def tree_forward(inputs, weight_list, member, reach, places, hot_first, hot_second, kept_mask, flat_slot, slot_table):
    gain_one, query_w, key_w, value_w, out_w, gain_two, router_w, gate_w, up_w, down_w = weight_list
    token_count = inputs.shape[0]
    block_rows = min(512, token_count)
    scale_factor = HEAD_DIM ** (-0.5)
    scale_one = lax.rsqrt(lax.optimization_barrier(jnp.mean(inputs * inputs, -1, keepdims=True)) + NORM_EPS)
    hidden_one = low(inputs * scale_one * gain_one)
    query_raw = low_back(jnp.dot(hidden_one, query_w, precision=HIGH_PREC))
    key_raw = low_back(jnp.dot(hidden_one, key_w, precision=HIGH_PREC))
    queries = low(rotate(query_raw.reshape(token_count, HEADS, HEAD_DIM), places, 1.0))
    keys_all = low(rotate(key_raw.reshape(token_count, HEADS, HEAD_DIM), places, 1.0))
    values_all = low_back(low(jnp.dot(hidden_one, value_w, precision=HIGH_PREC))).reshape(token_count, HEADS, HEAD_DIM)

    def one_block(block_id):
        first_row = block_id * block_rows
        query_block = lax.dynamic_slice_in_dim(queries, first_row, block_rows, 0)
        scores = low_back(scale_factor * jnp.einsum('bhd,thd->hbt', query_block, keys_all, precision=HIGH_PREC))
        scores = jnp.where(visible(member, reach, first_row, block_rows)[None], scores, NEG_FILL)
        weights_low = low(jax.nn.softmax(scores, axis=-1))
        return jnp.einsum('hbt,thd->bhd', weights_low, values_all, precision=HIGH_PREC)
    attended = lax.map(jax.checkpoint(one_block), jnp.arange(token_count // block_rows, dtype=jnp.int32))
    attended = low_back(low(attended.reshape(token_count, D)))
    branch = low_back(jnp.dot(attended, out_w.T, precision=HIGH_PREC))
    middle = inputs + branch
    scale_two = lax.rsqrt(lax.optimization_barrier(jnp.mean(middle * middle, -1, keepdims=True)) + NORM_EPS)
    hidden_two = low(middle * scale_two * gain_two)
    logits = low_back(jnp.dot(hidden_two, router_w, precision=HIGH_PREC))
    share_first, share_second = gate_pair(logits, hot_first, hot_second)
    padded_hidden = jnp.concatenate([hidden_two, jnp.zeros((1, D), jnp.float32)], 0)
    dispatched = jnp.take(padded_hidden, slot_table, axis=0).reshape(EXPERTS, CAP, D)
    gate_pre = low_back(jnp.einsum('ecd,def->ecf', dispatched, gate_w, precision=HIGH_PREC))
    up_pre = low_back(jnp.einsum('ecd,def->ecf', dispatched, up_w, precision=HIGH_PREC))
    activated = low(jax.nn.silu(gate_pre) * up_pre)
    expert_out = low_back(jnp.einsum('ecf,def->ecd', activated, down_w, precision=HIGH_PREC)).reshape(EXPERTS * CAP, D)
    padded_expert = jnp.concatenate([expert_out, jnp.zeros((1, D), jnp.float32)], 0)
    picked_first = jnp.take(padded_expert, flat_slot[:, 0], axis=0)
    picked_second = jnp.take(padded_expert, flat_slot[:, 1], axis=0)
    mixture = (kept_mask[:, 0] * share_first)[:, None] * picked_first + (kept_mask[:, 1] * share_second)[:, None] * picked_second
    return middle + mixture

def reference(tokens, gain_attn, w_query, w_key, w_value, w_out, gain_ffn, w_router, w_gate, w_up, w_down, segment, parents, expert_ids, slot_order, cotangent):
    weight_list = tuple((item.astype(jnp.float32) for item in (gain_attn, w_query, w_key, w_value, w_out, gain_ffn, w_router, w_gate, w_up, w_down)))
    tree_inputs = tokens.astype(jnp.float32).reshape(TREES, TOK_DEV, D)
    tree_grads = cotangent.astype(jnp.float32).reshape(TREES, TOK_DEV, D)
    tree_experts = expert_ids.reshape(TREES, TOK_DEV, TOP)

    def one_tree(totals, items):
        input_tree, grad_tree, segment_row, parent_row, expert_row, rank_row = items
        member, reach, places = tree_layout(segment_row, parent_row)
        hot_first, hot_second, kept_mask, flat_slot, slot_table = route(expert_row, rank_row)

        def forward(input_arg, *weight_args):
            return tree_forward(input_arg, weight_args, member, reach, places, hot_first, hot_second, kept_mask, flat_slot, slot_table)
        result, pull_back = jax.vjp(forward, input_tree, *weight_list)
        gradients = pull_back(grad_tree)
        totals = tuple((left_part + right_part for left_part, right_part in zip(totals, gradients[1:])))
        return (totals, (result.astype(jnp.bfloat16), gradients[0]))
    initial = tuple((jnp.zeros(item.shape, jnp.float32) for item in weight_list))
    totals, (results, input_grads) = lax.scan(one_tree, initial, (tree_inputs, tree_grads, segment, parents, tree_experts, slot_order))
    return (results.reshape(TOKENS, D), input_grads.reshape(TOKENS, D), totals[0], totals[1], totals[2], totals[3], totals[4], totals[5], totals[6], totals[7], totals[8], totals[9])
```

```python
import jax
import jax.numpy as jnp
from jax import lax
from jax.sharding import PartitionSpec as P

HEAD_DIM = 128
EXPERTS = 4
SEGS = 13
CAP = 144
SLOTS = EXPERTS * CAP
NORM_EPS = 1e-05
NEG_FILL = -1e30
ROPE_BASE = 10000.0
BF = jnp.bfloat16
F32 = jnp.float32


def mm(left, right, dims):
    return lax.dot_general(left, right, (dims, ((), ())), preferred_element_type=F32)


def rows_cols(left, right):
    return mm(left, right, ((1,), (0,)))


def rows_rows(left, right):
    return mm(left, right, ((1,), (1,)))


def cols_cols(left, right):
    return mm(left, right, ((0,), (0,)))


def tree_layout(segment_row, parent_row):
    seg_ids = jnp.arange(SEGS, dtype=jnp.int32)
    member = segment_row[:, None] == seg_ids[None, :]
    parent_of = (parent_row[:, None] == seg_ids[None, :]) & (seg_ids[:, None] != 0)
    itself = seg_ids[:, None] == seg_ids[None, :]
    reach = itself
    for _ in range(3):
        reach = itself | jnp.any(parent_of[:, :, None] & reach[None, :, :], axis=1)
    counts = member.astype(jnp.int32)
    lengths = jnp.sum(counts, 0)
    starts = jnp.sum(jnp.where(seg_ids[None, :] < seg_ids[:, None], lengths[None, :], 0), 1)
    before = jnp.sum(jnp.where(reach, lengths[None, :], 0), 1) - lengths
    row_at = jnp.arange(segment_row.shape[0], dtype=jnp.int32)
    places = jnp.sum(counts * (before - starts)[None, :], 1) + row_at
    member_low = member.astype(BF)
    lineage = rows_cols(member_low, reach.astype(BF)).astype(BF)
    shared = rows_rows(lineage, member_low) > 0.5
    seen = shared & (row_at[None, :] <= row_at[:, None])
    return seen, places.astype(F32)


def route(expert_row, slot_rank):
    expert_range = jnp.arange(EXPERTS, dtype=jnp.int32)
    hot_first = (expert_row[:, 0:1] == expert_range[None, :]).astype(F32)
    hot_second = (expert_row[:, 1:2] == expert_range[None, :]).astype(F32)
    earlier = (slot_rank[None, :] < slot_rank[:, None]).astype(BF)
    count_first = rows_cols(earlier, hot_first.astype(BF))
    count_second = rows_cols(earlier, hot_second.astype(BF))
    ahead_first = jnp.sum(count_first * hot_first, 1)
    ahead_second = jnp.sum((count_second + jnp.sum(hot_first, 0)[None, :]) * hot_second, 1)
    slot_index = jnp.stack([ahead_first, ahead_second], 1).astype(jnp.int32)
    kept = slot_index < CAP
    flat_slot = jnp.where(kept, expert_row * CAP + slot_index, SLOTS)
    slot_range = jnp.arange(SLOTS, dtype=jnp.int32)
    pick_first = flat_slot[:, 0:1] == slot_range[None, :]
    pick_second = flat_slot[:, 1:2] == slot_range[None, :]
    return hot_first, hot_second, kept.astype(F32), pick_first, pick_second


def rotate(vectors, cosines, sines):
    half_dim = HEAD_DIM // 2
    first_half = vectors[..., :half_dim]
    second_half = vectors[..., half_dim:]
    return jnp.concatenate(
        [
            first_half * cosines - second_half * sines,
            second_half * cosines + first_half * sines,
        ],
        -1,
    )


def gate_pair(logits, hot_first, hot_second):
    chances = jax.nn.softmax(logits, axis=-1)
    first_share = jnp.sum(chances * hot_first, 1)
    second_share = jnp.sum(chances * hot_second, 1)
    pair_total = first_share + second_share
    return (first_share / pair_total, second_share / pair_total)


def two_parts(column):
    high = column.astype(BF)
    return high, (column - high.astype(F32)).astype(BF)


def per_device(
    tokens, gain_attn, w_query, w_key, w_value, w_out, gain_ffn, w_router,
    w_gate, w_up, w_down, segment, parents, expert_ids, slot_order, cotangent,
):
    narrow_count = lax.axis_size("narrow")
    wide_count = lax.axis_size("wide")
    narrow_at = lax.axis_index("narrow")
    token_count, part_width = tokens.shape
    full_width = part_width * narrow_count
    hidden_width = w_gate.shape[2]
    rows_each = w_gate.shape[0]
    blocks = wide_count // 8
    quads = [
        [8 * block + 2 * chip + core for chip in range(4)]
        for block in range(blocks)
        for core in range(2)
    ]
    mates = [
        [8 * block + 2 * chip + core for block in range(blocks) for core in range(2)]
        for chip in range(4)
    ]

    def quad_swap(array):
        return lax.all_to_all(array, "wide", 0, 0, axis_index_groups=quads, tiled=True)

    def own_rows(weight):
        moved = quad_swap(jnp.transpose(weight, (1, 0, 2)))
        joined = lax.all_gather(moved, "wide", axis=0, axis_index_groups=mates, tiled=True)
        return joined.reshape(full_width, hidden_width)

    def mixed_features(rows):
        count = rows.shape[0]
        return rows.reshape(count, blocks, 4, 2, rows_each).transpose(0, 1, 3, 2, 4).reshape(
            count, full_width
        )

    def plain_features(rows):
        count = rows.shape[0]
        return rows.reshape(count, blocks, 2, 4, rows_each).transpose(0, 1, 3, 2, 4).reshape(
            count, full_width
        )

    def share_rows(grad):
        parts = grad.astype(BF).reshape(blocks * 2, 4, rows_each, hidden_width)
        summed = lax.psum_scatter(
            parts, "wide", scatter_dimension=0, axis_index_groups=mates, tiled=True
        )[0]
        return jnp.transpose(quad_swap(summed), (1, 0, 2)).astype(F32)

    gate_w, up_w, down_w = own_rows(w_gate), own_rows(w_up), own_rows(w_down)
    attn_w = lax.all_gather(
        jnp.stack([w_query, w_key, w_value, w_out], 1), "wide", axis=0, tiled=True
    )
    query_w, key_w, value_w, out_w = (attn_w[:, i] for i in range(4))
    router_w = lax.all_gather(w_router, "wide", axis=0, tiled=True)
    tokens_full = lax.all_gather(tokens, "narrow", axis=1, tiled=True)
    grad_full = lax.all_gather(cotangent, "narrow", axis=1, tiled=True)
    gains_full = lax.all_gather(jnp.stack([gain_attn, gain_ffn]), "narrow", axis=1, tiled=True)
    gain_first = gains_full[0].astype(F32)
    gain_second = gains_full[1].astype(F32)
    gain_first_loc = gain_attn.astype(F32)
    gain_second_loc = gain_ffn.astype(F32)

    seen, places = tree_layout(segment[0], parents[0])
    hot_first, hot_second, kept, pick_first, pick_second = route(expert_ids, slot_order[0])
    pick_first_low = pick_first.astype(BF)
    pick_second_low = pick_second.astype(BF)
    pick_both_low = (pick_first | pick_second).astype(BF)

    inputs_full = tokens_full.astype(F32)
    scale_first = lax.rsqrt(jnp.mean(inputs_full * inputs_full, -1, keepdims=True) + NORM_EPS)
    normed_first = inputs_full * scale_first
    hidden_first = (normed_first * gain_first).astype(BF)
    heads = part_width // HEAD_DIM
    half_dim = HEAD_DIM // 2
    freqs = ROPE_BASE ** (-2.0 * jnp.arange(half_dim, dtype=F32) / HEAD_DIM)
    angles = places[:, None] * freqs[None, :]
    cosines, sines = jnp.cos(angles), jnp.sin(angles)
    query_raw = rows_cols(hidden_first, query_w)
    key_raw = rows_cols(hidden_first, key_w)
    value_low = rows_cols(hidden_first, value_w).astype(BF)
    score_scale = HEAD_DIM ** (-0.5)

    def head_cols(array, head):
        return array[:, head * HEAD_DIM : (head + 1) * HEAD_DIM]

    saved = []
    outs = []
    for head in range(heads):
        query = rotate(head_cols(query_raw, head), cosines, sines).astype(BF)
        key = rotate(head_cols(key_raw, head), cosines, sines).astype(BF)
        value = head_cols(value_low, head)
        scores = jnp.where(seen, rows_rows(query, key) * score_scale, NEG_FILL)
        exps = jnp.exp(scores - jnp.max(scores, -1, keepdims=True))
        weights = exps / jnp.sum(exps, -1, keepdims=True)
        saved.append((query, key, value, weights))
        outs.append(rows_cols(weights.astype(BF), value).astype(BF))
    attended = jnp.concatenate(outs, 1)
    branch_part = rows_rows(attended, out_w).astype(BF)
    branch_loc = lax.psum_scatter(
        branch_part, "narrow", scatter_dimension=1, tiled=True
    ).astype(F32)
    middle = tokens.astype(F32) + branch_loc
    middle_full = lax.all_gather(middle.astype(BF), "narrow", axis=1, tiled=True).astype(F32)
    scale_second = lax.rsqrt(jnp.mean(middle_full * middle_full, -1, keepdims=True) + NORM_EPS)
    normed_second = middle_full * scale_second
    hidden_second = (normed_second * gain_second).astype(BF)
    logits = rows_cols(hidden_second, router_w)
    share_first, share_second = gate_pair(logits, hot_first, hot_second)
    weight_first = kept[:, 0] * share_first
    weight_second = kept[:, 1] * share_second

    slot_weight = jnp.sum(
        pick_first * weight_first[:, None] + pick_second * weight_second[:, None], 0
    )
    weight_high, weight_low = two_parts(slot_weight)
    pads = jnp.stack([weight_high, weight_low], 1)
    pads = jnp.pad(pads, ((0, 0), (0, 126)))
    sent_hidden = cols_cols(pick_both_low, hidden_second).astype(BF)
    sent_grad = cols_cols(pick_both_low, grad_full).astype(BF)
    sent = jnp.concatenate([sent_hidden, sent_grad, pads], 1)
    got = quad_swap(sent.reshape(EXPERTS, CAP, -1)).reshape(SLOTS, -1)
    slot_hidden = mixed_features(got[:, :full_width])
    slot_grad = mixed_features(got[:, full_width : 2 * full_width])
    slot_gate = got[:, 2 * full_width : 2 * full_width + 2].astype(F32)
    slot_gate = slot_gate[:, 0:1] + slot_gate[:, 1:2]

    gate_pre = rows_cols(slot_hidden, gate_w)
    up_pre = rows_cols(slot_hidden, up_w)
    sigmoid_gate = jax.nn.sigmoid(gate_pre)
    silu_gate = gate_pre * sigmoid_gate
    activated = (silu_gate * up_pre).astype(BF)
    expert_part = rows_rows(activated, down_w)
    act_raw = rows_cols(slot_grad, down_w)
    share_part = jnp.sum(act_raw * activated.astype(F32), 1, keepdims=True)
    grad_act = act_raw * slot_gate
    grad_gate_pre = (
        grad_act * up_pre * sigmoid_gate * (1.0 + gate_pre * (1.0 - sigmoid_gate))
    ).astype(BF)
    grad_up_pre = (grad_act * silu_gate).astype(BF)
    grad_slot = rows_rows(grad_gate_pre, gate_w) + rows_rows(grad_up_pre, up_w)
    stat_part = jnp.sum(slot_hidden.astype(F32) * grad_slot, 1, keepdims=True)
    extras = jnp.concatenate([*two_parts(share_part), *two_parts(stat_part)], 1)
    extras = jnp.pad(extras, ((0, 0), (0, 124)))
    back_parts = []
    expert_plain = plain_features(expert_part.astype(BF))
    slot_plain = plain_features(grad_slot.astype(BF))
    for part in range(narrow_count):
        cols = slice(part * part_width, (part + 1) * part_width)
        back_parts += [expert_plain[:, cols], slot_plain[:, cols], extras]
    back = lax.psum_scatter(
        jnp.concatenate(back_parts, 1), "narrow", scatter_dimension=1, tiled=True
    )
    back = quad_swap(back.reshape(EXPERTS, CAP, -1)).reshape(SLOTS, -1)
    picked_first = rows_cols(pick_first_low, back)
    picked_second = rows_cols(pick_second_low, back)
    output = (
        middle
        + weight_first[:, None] * picked_first[:, :part_width]
        + weight_second[:, None] * picked_second[:, :part_width]
    ).astype(BF)

    grad_weight = (slot_grad.astype(F32) * slot_gate).astype(BF)
    gate_out = share_rows(cols_cols(slot_hidden, grad_gate_pre))
    up_out = share_rows(cols_cols(slot_hidden, grad_up_pre))
    down_out = share_rows(cols_cols(grad_weight, activated))

    tail = 2 * part_width
    share_first_grad = picked_first[:, tail] + picked_first[:, tail + 1]
    share_second_grad = picked_second[:, tail] + picked_second[:, tail + 1]
    both = picked_first + picked_second
    stat_second = both[:, tail + 2] + both[:, tail + 3]
    grad_hidden_loc = both[:, part_width:tail]
    grad_local = cotangent.astype(F32)
    _, pull_gates = jax.vjp(lambda given: gate_pair(given, hot_first, hot_second), logits)
    (grad_logits,) = pull_gates((kept[:, 0] * share_first_grad, kept[:, 1] * share_second_grad))
    grad_logits_low = grad_logits.astype(BF)
    grad_router_rows = rows_rows(grad_logits_low, router_w)
    stat_total = stat_second + jnp.sum(normed_second * gain_second * grad_router_rows, 1)

    def take_cols(full_rows):
        return lax.dynamic_slice_in_dim(full_rows, narrow_at * part_width, part_width, 1)

    grad_hidden_loc = grad_hidden_loc + take_cols(grad_router_rows)
    normed_second_loc = take_cols(normed_second)
    grad_gain_second = jnp.sum(grad_hidden_loc * normed_second_loc, 0)
    grad_middle = grad_local + scale_second * (
        gain_second_loc * grad_hidden_loc - normed_second_loc * stat_total[:, None] / full_width
    )
    grad_router_w = cols_cols(hidden_second, grad_logits_low)
    grad_branch = lax.all_gather(grad_middle.astype(BF), "narrow", axis=1, tiled=True)
    grad_attended = rows_cols(grad_branch, out_w).astype(BF)
    grad_out_w = cols_cols(grad_branch, attended)
    grad_qs, grad_ks, grad_vs = [], [], []
    for head in range(heads):
        query, key, value, weights = saved[head]
        grad_out = head_cols(grad_attended, head)
        grad_weights = rows_rows(grad_out, value)
        inner = jnp.sum(weights * grad_weights, -1, keepdims=True)
        grad_scores = (weights * (grad_weights - inner)).astype(BF)
        grad_q = rows_cols(grad_scores, key) * score_scale
        grad_k = cols_cols(grad_scores, query) * score_scale
        grad_qs.append(rotate(grad_q, cosines, -sines).astype(BF))
        grad_ks.append(rotate(grad_k, cosines, -sines).astype(BF))
        grad_vs.append(cols_cols(weights.astype(BF), grad_out).astype(BF))
    grad_query_raw = jnp.concatenate(grad_qs, 1)
    grad_key_raw = jnp.concatenate(grad_ks, 1)
    grad_value_raw = jnp.concatenate(grad_vs, 1)
    grad_hidden_first = (
        rows_rows(grad_query_raw, query_w)
        + rows_rows(grad_key_raw, key_w)
        + rows_rows(grad_value_raw, value_w)
    )
    stat_first = jnp.sum(normed_first * gain_first * grad_hidden_first, 1, keepdims=True)
    extras = jnp.pad(jnp.concatenate(two_parts(stat_first), 1), ((0, 0), (0, 126)))
    grad_hidden_low = grad_hidden_first.astype(BF)
    first_parts = []
    for part in range(narrow_count):
        first_parts += [grad_hidden_low[:, part * part_width : (part + 1) * part_width], extras]
    first_back = lax.psum_scatter(
        jnp.concatenate(first_parts, 1), "narrow", scatter_dimension=1, tiled=True
    ).astype(F32)
    grad_first_loc = first_back[:, :part_width]
    stat_first = first_back[:, part_width : part_width + 1]
    stat_first = stat_first + first_back[:, part_width + 1 : part_width + 2]
    normed_first_loc = take_cols(normed_first)
    grad_gain_first = jnp.sum(grad_first_loc * normed_first_loc, 0)
    grad_tokens = grad_middle + scale_first * (
        gain_first_loc * grad_first_loc - normed_first_loc * stat_first / full_width
    )
    grad_attn_w = jnp.concatenate(
        [
            cols_cols(hidden_first, grad_query_raw).astype(BF),
            cols_cols(hidden_first, grad_key_raw).astype(BF),
            cols_cols(hidden_first, grad_value_raw).astype(BF),
            grad_out_w.astype(BF),
        ],
        1,
    )
    attn_summed = lax.psum_scatter(
        grad_attn_w, "wide", scatter_dimension=0, tiled=True
    ).astype(F32)
    router_summed = lax.psum_scatter(grad_router_w, "wide", scatter_dimension=0, tiled=True)
    gains_summed = lax.psum(jnp.stack([grad_gain_first, grad_gain_second]), "wide")
    return (
        output,
        grad_tokens,
        gains_summed[0],
        attn_summed[:, :part_width],
        attn_summed[:, part_width : 2 * part_width],
        attn_summed[:, 2 * part_width : 3 * part_width],
        attn_summed[:, 3 * part_width :],
        gains_summed[1],
        router_summed,
        gate_out,
        up_out,
        down_out,
    )


def solution(mesh):
    pair = P("wide", "narrow")
    part = P("narrow")
    rows = P("wide", None)
    cube = P("wide", None, "narrow")
    return jax.shard_map(
        per_device,
        mesh=mesh,
        in_specs=(
            pair, part, pair, pair, pair, pair, part, rows, cube, cube, cube,
            rows, rows, rows, rows, pair,
        ),
        out_specs=(
            pair, pair, part, pair, pair, pair, pair, part, rows, cube, cube, cube,
        ),
        check_vma=False,
    )
```

```python
import jax
import jax.numpy as jnp
from jax import lax
from jax.experimental import pallas as pl
from jax.experimental.pallas import tpu as pltpu
from jax.sharding import PartitionSpec as P

HEAD_DIM = 128
EXPERTS = 4
SEGS = 13
CAP = 144
SLOTS = EXPERTS * CAP
NORM_EPS = 1e-05
NEG_FILL = -1e30
ROPE_BASE = 10000.0
BF = jnp.bfloat16
F32 = jnp.float32


def mm(left, right, dims):
    return lax.dot_general(left, right, (dims, ((), ())), preferred_element_type=F32)


def rows_cols(left, right):
    return mm(left, right, ((1,), (0,)))


def rows_rows(left, right):
    return mm(left, right, ((1,), (1,)))


def cols_cols(left, right):
    return mm(left, right, ((0,), (0,)))


def tree_layout(segment_row, parent_row):
    seg_ids = jnp.arange(SEGS, dtype=jnp.int32)
    member = segment_row[:, None] == seg_ids[None, :]
    parent_of = (parent_row[:, None] == seg_ids[None, :]) & (seg_ids[:, None] != 0)
    itself = seg_ids[:, None] == seg_ids[None, :]
    reach = itself
    for _ in range(3):
        reach = itself | jnp.any(parent_of[:, :, None] & reach[None, :, :], axis=1)
    counts = member.astype(jnp.int32)
    lengths = jnp.sum(counts, 0)
    starts = jnp.sum(jnp.where(seg_ids[None, :] < seg_ids[:, None], lengths[None, :], 0), 1)
    before = jnp.sum(jnp.where(reach, lengths[None, :], 0), 1) - lengths
    row_at = jnp.arange(segment_row.shape[0], dtype=jnp.int32)
    places = jnp.sum(counts * (before - starts)[None, :], 1) + row_at
    member_low = member.astype(BF)
    lineage = rows_cols(member_low, reach.astype(BF)).astype(BF)
    shared = rows_rows(lineage, member_low) > 0.5
    seen = shared & (row_at[None, :] <= row_at[:, None])
    return seen, places.astype(F32)


def route(expert_row, slot_rank):
    expert_range = jnp.arange(EXPERTS, dtype=jnp.int32)
    hot_first = (expert_row[:, 0:1] == expert_range[None, :]).astype(F32)
    hot_second = (expert_row[:, 1:2] == expert_range[None, :]).astype(F32)
    earlier = (slot_rank[None, :] < slot_rank[:, None]).astype(BF)
    count_first = rows_cols(earlier, hot_first.astype(BF))
    count_second = rows_cols(earlier, hot_second.astype(BF))
    ahead_first = jnp.sum(count_first * hot_first, 1)
    ahead_second = jnp.sum((count_second + jnp.sum(hot_first, 0)[None, :]) * hot_second, 1)
    slot_index = jnp.stack([ahead_first, ahead_second], 1).astype(jnp.int32)
    kept = slot_index < CAP
    flat_slot = jnp.where(kept, expert_row * CAP + slot_index, SLOTS)
    slot_range = jnp.arange(SLOTS, dtype=jnp.int32)
    pick_first = flat_slot[:, 0:1] == slot_range[None, :]
    pick_second = flat_slot[:, 1:2] == slot_range[None, :]
    return hot_first, hot_second, kept.astype(F32), pick_first, pick_second


def rotate(vectors, cosines, sines):
    half_dim = HEAD_DIM // 2
    first_half = vectors[..., :half_dim]
    second_half = vectors[..., half_dim:]
    return jnp.concatenate(
        [
            first_half * cosines - second_half * sines,
            second_half * cosines + first_half * sines,
        ],
        -1,
    )


def gate_pair(logits, hot_first, hot_second):
    chances = jax.nn.softmax(logits, axis=-1)
    first_share = jnp.sum(chances * hot_first, 1)
    second_share = jnp.sum(chances * hot_second, 1)
    pair_total = first_share + second_share
    return (first_share / pair_total, second_share / pair_total)


def two_parts(column):
    high = column.astype(BF)
    return high, (column - high.astype(F32)).astype(BF)


MESH = pl.DeviceIdType.MESH
NEAR = 3


def low_dot(left, right):
    return jnp.dot(left, right, preferred_element_type=F32)


def places_of(n):
    return [lax.rem(n + step, 4) for step in (1, 2, 3)], [lax.rem(n + 4 - step, 4) for step in (1, 2, 3)]


def plane_of(chip):
    x, y = lax.rem(chip, 2), chip // 2
    return [2 * y + 1 - x, 2 * (1 - y) + x, 2 * (1 - y) + 1 - x]


def greet(narrow_peers, plane_peers, chip, core, mate):
    barrier = pltpu.get_barrier_semaphore()
    count = 0
    for peer in narrow_peers:
        pl.semaphore_signal(barrier, inc=1, device_id={"narrow": peer}, device_id_type=MESH)
        count += 1
    for peer in plane_peers:
        pl.semaphore_signal(
            barrier, inc=1, device_id={"wide": 2 * peer + core}, device_id_type=MESH
        )
        count += 1
    if mate:
        pl.semaphore_signal(
            barrier, inc=1, device_id={"wide": 2 * chip + 1 - core}, device_id_type=MESH
        )
        count += 1
    pl.semaphore_wait(barrier, count)


class Links:
    def __init__(self, sent, landed, local):
        self.sent, self.landed, self.local = sent, landed, local
        self.used, self.local_used = 0, 0
        self.waits = []

    def slot(self):
        self.used += 1
        return self.used - 1

    def send(self, source, target, device, slot, when=None):
        copy = pltpu.make_async_remote_copy(
            src_ref=source,
            dst_ref=target,
            send_sem=self.sent.at[slot],
            recv_sem=self.landed.at[slot],
            device_id=device,
            device_id_type=MESH,
        )
        if when is None:
            copy.start()
        else:
            pl.when(when)(copy.start)
        self.waits.append((copy, when))

    def land(self, target, device, slot, when=None):
        copy = pltpu.make_async_remote_copy(
            src_ref=target,
            dst_ref=target,
            send_sem=self.sent.at[slot],
            recv_sem=self.landed.at[slot],
            device_id=device,
            device_id_type=MESH,
        )
        if when is None:
            copy.wait_recv()
        else:
            pl.when(when)(copy.wait_recv)

    def move(self, source, target):
        copy = pltpu.make_async_copy(source, target, self.local.at[self.local_used])
        self.local_used += 1
        copy.start()
        self.waits.append((copy, "local"))
        return copy

    def finish(self):
        for copy, when in self.waits:
            if when == "local":
                copy.wait()
            elif when is None:
                copy.wait_send()
            else:
                pl.when(when)(copy.wait_send)


class Chain:
    def __init__(self, links, n, block):
        self.links, self.n, self.block = links, n, block
        self.slots = [(links.slot(), links.slot()) for _ in range(3)]

    def start(self, step):
        n, links = self.n, self.links
        right, left = self.slots[step]
        block = self.block(lax.rem(n + 4 - step, 4))
        links.send(
            block, block, {"narrow": lax.rem(n + 1, 4)}, right,
            (n < 3) & (n >= step),
        )
        block = self.block(lax.rem(n + step, 4))
        links.send(
            block, block, {"narrow": lax.rem(n + 3, 4)}, left,
            (n > 0) & (n + step <= 3),
        )

    def land(self, step):
        n, links = self.n, self.links
        right, left = self.slots[step]
        links.land(
            self.block(lax.rem(n + 7 - step, 4)), {"narrow": lax.rem(n + 3, 4)}, right,
            n >= step + 1,
        )
        links.land(
            self.block(lax.rem(n + 1 + step, 4)), {"narrow": lax.rem(n + 1, 4)}, left,
            n + 1 + step <= 3,
        )


FRONT_SLOTS = 72


def front_body(
    tok_ref, cot_ref, gains_ref, wq_ref, wk_ref, wv_ref, wo_ref, router_ref, moved_ref,
    rows_ref, cols_ref, freq_ref,
    qkvw_out, outw_out, expert_out, x_out, dy_out, gate_out, middle_out, hidden_out,
    tokens_out, qkv_out, prob_out, att_out, stat_out, rope_out, pick_out,
    pack, tok_pack, qkvw, outw, cot_send, y_send, br_send, br_recv, stat_send, stat_recv,
    gate_send, sent, landed, local,
):
    n = lax.axis_index("narrow")
    w = lax.axis_index("wide")
    chip, core = w // 2, lax.rem(w, 2)
    to_z, from_z = places_of(n)
    plane = plane_of(chip)
    links = Links(sent, landed, local)
    mate = {"wide": 2 * chip + 1 - core}

    def at_plane(peer):
        return {"wide": 2 * peer + core}

    token_count, part_width = tok_ref.shape
    greet(to_z, plane, chip, core, True)

    tok_pack[0:token_count, :] = tok_ref[...]
    tok_pack[token_count : token_count + 2, :] = gains_ref[...]
    tok_slots = [links.slot() for _ in range(NEAR)]
    for step in range(NEAR):
        links.send(tok_pack, tokens_out.at[n], {"narrow": to_z[step]}, tok_slots[step])
    pack[:, 0:512] = wq_ref[...]
    pack[:, 512:1024] = wk_ref[...]
    pack[:, 1024:1536] = wv_ref[...]
    pack[:, 1536:1664] = router_ref[...]
    in_slots = [links.slot() for _ in range(NEAR)]
    for step in range(NEAR):
        links.send(pack, qkvw.at[w], at_plane(plane[step]), in_slots[step])
    in_mate = [links.slot() for _ in range(4)]
    links.send(pack, qkvw.at[w], mate, in_mate[3])
    out_slots = [links.slot() for _ in range(NEAR)]
    for step in range(NEAR):
        links.send(wo_ref, outw.at[w], at_plane(plane[step]), out_slots[step])
    out_mate = [links.slot() for _ in range(4)]
    links.send(wo_ref, outw.at[w], mate, out_mate[3])
    tokens_out[n] = tok_pack[...]
    qkvw[w] = pack[...]
    outw[w] = wo_ref[...]

    wide_shape = (token_count, token_count)
    row_at = lax.broadcasted_iota(jnp.int32, wide_shape, 0)
    col_at = lax.broadcasted_iota(jnp.int32, wide_shape, 1)
    seg_row, rank_row = rows_ref[0:1, :], rows_ref[2:3, :]
    seg_col, par_col, rank_col = cols_ref[:, 0:1], cols_ref[:, 1:2], cols_ref[:, 2:3]
    seen = ((seg_row == seg_col) | (seg_row == par_col) | (seg_row == 0)) & (col_at <= row_at)
    spots = jnp.sum(jnp.where(seen, 1.0, 0.0), 1, keepdims=True) - 1.0
    angles = spots * freq_ref[...]
    cosines = jnp.cos(angles)
    lane_at = lax.broadcasted_iota(jnp.int32, angles.shape, 1)
    sines = jnp.sin(angles) * jnp.where(lane_at < HEAD_DIM // 2, -1.0, 1.0)
    rope_out[0] = cosines
    rope_out[1] = sines
    kind = lax.broadcasted_iota(jnp.int32, (8, token_count), 0)
    first_row, second_row = rows_ref[3:4, :], rows_ref[4:5, :]
    hot_first = jnp.where(kind == first_row, 1.0, 0.0)
    hot_second = jnp.where(kind == second_row, 1.0, 0.0)
    earlier = jnp.where(rank_col < rank_row, 1.0, 0.0).astype(BF)
    count_first = low_dot(hot_first.astype(BF), earlier)
    count_second = low_dot(hot_second.astype(BF), earlier)
    count_second = count_second + jnp.sum(hot_first, 1, keepdims=True)
    slot_first = jnp.sum(count_first * hot_first, 0, keepdims=True)
    slot_second = jnp.sum(count_second * hot_second, 0, keepdims=True)
    kept_first = jnp.where(slot_first < CAP, 1.0, 0.0)
    kept_second = jnp.where(slot_second < CAP, 1.0, 0.0)
    flat_first = jnp.where(slot_first < CAP, first_row * CAP + slot_first.astype(jnp.int32), SLOTS)
    flat_second = jnp.where(
        slot_second < CAP, second_row * CAP + slot_second.astype(jnp.int32), SLOTS
    )
    slot_at = lax.broadcasted_iota(jnp.int32, (SLOTS, token_count), 0)
    pick_first = jnp.where(slot_at == flat_first, 1.0, 0.0)
    pick_second = jnp.where(slot_at == flat_second, 1.0, 0.0)
    pick_out[0] = pick_first.astype(BF)
    pick_out[1] = pick_second.astype(BF)
    pick_both = (pick_first + pick_second).astype(BF)

    def column_block(array):
        return lambda m: array.at[:, pl.ds(pl.multiple_of(m * part_width, part_width), part_width)]

    def slot_block(array, owner):
        return array.at[
            pl.ds(pl.multiple_of(owner * CAP, 16), CAP),
            pl.ds(pl.multiple_of(n * part_width, part_width), part_width),
        ]

    def dispatch(rows, buffer, array):
        slots = [links.slot() for _ in range(NEAR)]
        buffer[...] = low_dot(pick_both, rows).astype(BF)
        for step in range(NEAR):
            links.send(
                buffer.at[pl.ds(pl.multiple_of(plane[step] * CAP, 16), CAP), :],
                slot_block(array, chip), at_plane(plane[step]), slots[step],
            )
        own = links.move(
            buffer.at[pl.ds(pl.multiple_of(chip * CAP, 16), CAP), :], slot_block(array, chip)
        )
        return slots, own

    def arrive(array, state):
        slots, own = state
        for step in range(NEAR):
            links.land(slot_block(array, plane[step]), at_plane(plane[step]), slots[step])
        own.wait()
        links.waits = [item for item in links.waits if item[0] is not own]

    dy_state = dispatch(cot_ref[...], cot_send, dy_out)
    dy_chain = Chain(links, n, column_block(dy_out))

    for step in range(NEAR):
        links.land(tokens_out.at[from_z[step]], {"narrow": from_z[step]}, tok_slots[step])
    total = jnp.zeros((token_count, 1), F32)
    for m in range(4):
        part = tokens_out[m, 0:token_count, :].astype(F32)
        total = total + jnp.sum(part * part, 1, keepdims=True)
    scale_first = lax.rsqrt(total * (1.0 / (4 * part_width)) + NORM_EPS)
    for m in range(4):
        part = tokens_out[m, 0:token_count, :].astype(F32)
        gain = tokens_out[m, token_count : token_count + 1, :].astype(F32)
        hidden_out[:, m * part_width : (m + 1) * part_width] = (part * scale_first * gain).astype(BF)

    arrive(dy_out, dy_state)
    dy_chain.start(0)

    for step in range(NEAR):
        owner = 2 * plane[step] + core
        links.land(qkvw.at[owner], at_plane(plane[step]), in_slots[step])
        links.send(qkvw.at[owner], qkvw.at[owner], mate, in_mate[step])
    for step in range(NEAR):
        links.land(qkvw.at[2 * plane[step] + 1 - core], mate, in_mate[step])
    links.land(qkvw.at[2 * chip + 1 - core], mate, in_mate[3])
    saved_in = links.move(qkvw, qkvw_out)

    expert_slots = [[links.slot() for _ in range(NEAR)] for _ in range(3)]
    expert_mate = [[links.slot() for _ in range(4)] for _ in range(3)]
    for kind_at in range(3):
        for step in range(NEAR):
            links.send(
                moved_ref.at[kind_at, plane[step]], expert_out.at[kind_at, chip, core],
                at_plane(plane[step]), expert_slots[kind_at][step],
            )
        links.send(
            moved_ref.at[kind_at, chip], expert_out.at[kind_at, chip, core], mate,
            expert_mate[kind_at][3],
        )
        links.move(moved_ref.at[kind_at, chip], expert_out.at[kind_at, chip, core])

    def pass_on(kind_at):
        for step in range(NEAR):
            block = expert_out.at[kind_at, plane[step], core]
            links.land(block, at_plane(plane[step]), expert_slots[kind_at][step])
            links.send(block, block, mate, expert_mate[kind_at][step])

    def all_there(kind_at):
        for step in range(NEAR):
            links.land(
                expert_out.at[kind_at, plane[step], 1 - core], mate, expert_mate[kind_at][step]
            )
        links.land(expert_out.at[kind_at, chip, 1 - core], mate, expert_mate[kind_at][3])

    dy_chain.land(0)
    dy_chain.start(1)

    hidden = hidden_out[...]
    score_scale = HEAD_DIM ** (-0.5)
    raws = []
    for part in range(3):
        weight = qkvw[:, :, part * 512 : (part + 1) * 512].reshape(4 * part_width, part_width)
        raws.append(low_dot(hidden, weight))
    for head in range(part_width // HEAD_DIM):
        cols = slice(head * HEAD_DIM, (head + 1) * HEAD_DIM)
        turned = []
        for part in range(2):
            raw = raws[part][:, cols]
            turned.append(
                (raw * cosines + pltpu.roll(raw, HEAD_DIM // 2, 1) * sines).astype(BF)
            )
            qkv_out[part, :, cols] = turned[part]
        value = raws[2][:, cols].astype(BF)
        qkv_out[2, :, cols] = value
        scores = rows_rows(turned[0], turned[1]) * score_scale
        scores = jnp.where(seen, scores, NEG_FILL)
        exps = jnp.exp(scores - jnp.max(scores, 1, keepdims=True))
        weights = exps / jnp.sum(exps, 1, keepdims=True)
        prob_out[head] = weights
        att_out[:, cols] = low_dot(weights.astype(BF), value).astype(BF)

    dy_chain.land(1)
    dy_chain.start(2)

    for step in range(NEAR):
        owner = 2 * plane[step] + core
        links.land(outw.at[owner], at_plane(plane[step]), out_slots[step])
        links.send(outw.at[owner], outw.at[owner], mate, out_mate[step])
    for step in range(NEAR):
        links.land(outw.at[2 * plane[step] + 1 - core], mate, out_mate[step])
    links.land(outw.at[2 * chip + 1 - core], mate, out_mate[3])
    links.move(outw, outw_out)

    attended = att_out[...]

    def branch(m):
        weight = outw[pl.ds(2 * m, 2)].reshape(part_width, part_width)
        return rows_rows(attended, weight)

    br_slots = [links.slot() for _ in range(NEAR)]
    for step in range(NEAR):
        br_send[step] = branch(to_z[step]).astype(BF)
        links.send(br_send.at[step], br_recv.at[step], {"narrow": to_z[step]}, br_slots[step])
    middle = tok_ref[...].astype(F32) + branch(n)
    for step in range(NEAR):
        links.land(br_recv.at[step], {"narrow": from_z[step]}, br_slots[step])
        middle = middle + br_recv[step].astype(F32)
    middle_out[...] = middle
    x_state = dispatch(middle.astype(BF), y_send, x_out)
    x_chain = Chain(links, n, column_block(x_out))

    gain_second = gains_ref[1:2, :].astype(F32)
    router = qkvw[pl.ds(2 * n, 2), :, 1536:1664].reshape(part_width, 128)
    logit_part = mm(router, (middle * gain_second).astype(BF), ((0,), (1,)))[0:8, :]
    square = middle * middle
    square_high = square.astype(BF)
    square_low = (square - square_high.astype(F32)).astype(BF)
    ones = jnp.ones((8, part_width), BF)
    square_sum = rows_rows(ones, square_high) + rows_rows(ones, square_low)
    stat = jnp.where(kind == 4, square_sum, logit_part)
    stat_send[...] = stat
    stat_slots = [links.slot() for _ in range(NEAR)]
    for step in range(NEAR):
        links.send(stat_send, stat_recv.at[step], {"narrow": to_z[step]}, stat_slots[step])

    arrive(x_out, x_state)
    x_chain.start(0)
    for step in range(NEAR):
        links.land(stat_recv.at[step], {"narrow": from_z[step]}, stat_slots[step])
        stat = stat + stat_recv[step]
    stat_out[...] = stat
    scale_row = lax.rsqrt(stat[4:5, :] * (1.0 / (4 * part_width)) + NORM_EPS)
    logits = jnp.where(kind < EXPERTS, stat * scale_row, NEG_FILL)
    chances = jnp.exp(logits - jnp.max(logits, 0, keepdims=True))
    chances = chances / jnp.sum(chances, 0, keepdims=True)
    share_first = jnp.sum(chances * hot_first, 0, keepdims=True)
    share_second = jnp.sum(chances * hot_second, 0, keepdims=True)
    both = share_first + share_second
    weighted = pick_first * (share_first / both) + pick_second * (share_second / both)
    slot_gate = jnp.sum(weighted, 1, keepdims=True)
    gate_send[...] = jnp.broadcast_to(slot_gate, (SLOTS, 128))

    def gate_rows(array, owner):
        return array.at[pl.ds(pl.multiple_of(owner * CAP, 16), CAP), :]

    gate_slots = [links.slot() for _ in range(NEAR)]
    for step in range(NEAR):
        links.send(
            gate_rows(gate_send, plane[step]), gate_rows(gate_out, chip),
            at_plane(plane[step]), gate_slots[step],
        )
    links.move(gate_rows(gate_send, chip), gate_rows(gate_out, chip))

    pass_on(0)
    x_chain.land(0)
    x_chain.start(1)
    x_chain.land(1)
    x_chain.start(2)
    pass_on(1)
    x_chain.land(2)
    dy_chain.land(2)
    for step in range(NEAR):
        links.land(gate_rows(gate_out, plane[step]), at_plane(plane[step]), gate_slots[step])
    pass_on(2)
    for kind_at in range(3):
        all_there(kind_at)
    links.finish()


def front_call(tokens, cotangent, gains, weights, router, moved, rows, cols, freqs):
    token_count, part_width = tokens.shape
    full = 4 * part_width
    hidden_width = moved.shape[3]
    rows_each = moved.shape[2]
    heads = part_width // HEAD_DIM
    vmem = pl.BlockSpec(memory_space=pltpu.VMEM)
    hbm = pl.BlockSpec(memory_space=pl.ANY)

    def arr(shape, dtype):
        return jax.ShapeDtypeStruct(shape, dtype)

    return pl.pallas_call(
        front_body,
        out_shape=(
            arr((8, rows_each, 1664), BF),
            arr((8, rows_each, part_width), BF),
            arr((3, 4, 2, rows_each, hidden_width), BF),
            arr((SLOTS, full), BF),
            arr((SLOTS, full), BF),
            arr((SLOTS, 128), F32),
            arr((token_count, part_width), F32),
            arr((token_count, full), BF),
            arr((4, token_count + 16, part_width), BF),
            arr((3, token_count, part_width), BF),
            arr((heads, token_count, token_count), F32),
            arr((token_count, part_width), BF),
            arr((8, token_count), F32),
            arr((2, token_count, HEAD_DIM), F32),
            arr((2, SLOTS, token_count), BF),
        ),
        in_specs=[vmem] * 8 + [hbm] + [vmem] * 3,
        out_specs=(hbm, hbm, hbm) + (vmem,) * 12,
        scratch_shapes=[
            pltpu.VMEM((rows_each, 1664), BF),
            pltpu.VMEM((token_count + 16, part_width), BF),
            pltpu.VMEM((8, rows_each, 1664), BF),
            pltpu.VMEM((8, rows_each, part_width), BF),
            pltpu.VMEM((SLOTS, part_width), BF),
            pltpu.VMEM((SLOTS, part_width), BF),
            pltpu.VMEM((NEAR, token_count, part_width), BF),
            pltpu.VMEM((NEAR, token_count, part_width), BF),
            pltpu.VMEM((8, token_count), F32),
            pltpu.VMEM((NEAR, 8, token_count), F32),
            pltpu.VMEM((SLOTS, 128), F32),
            pltpu.SemaphoreType.DMA((FRONT_SLOTS,)),
            pltpu.SemaphoreType.DMA((FRONT_SLOTS,)),
            pltpu.SemaphoreType.DMA((16,)),
        ],
        compiler_params=pltpu.CompilerParams(
            collective_id=0, has_side_effects=True, vmem_limit_bytes=60 * 1024 * 1024
        ),
        cost_estimate=pl.CostEstimate(
            flops=6_000_000_000, bytes_accessed=60_000_000, transcendentals=400_000
        ),
        name="front",
    )(tokens, cotangent, gains, *weights, router, moved, rows, cols, freqs)


def per_device(
    tokens, gain_attn, w_query, w_key, w_value, w_out, gain_ffn, w_router,
    w_gate, w_up, w_down, segment, parents, expert_ids, slot_order, cotangent,
):
    narrow_count = lax.axis_size("narrow")
    wide_count = lax.axis_size("wide")
    narrow_at = lax.axis_index("narrow")
    token_count, part_width = tokens.shape
    full_width = part_width * narrow_count
    hidden_width = w_gate.shape[2]
    rows_each = w_gate.shape[0]
    blocks = wide_count // 8
    quads = [
        [8 * block + 2 * chip + core for chip in range(4)]
        for block in range(blocks)
        for core in range(2)
    ]
    mates = [
        [8 * block + 2 * chip + core for block in range(blocks) for core in range(2)]
        for chip in range(4)
    ]

    def quad_swap(array):
        return lax.all_to_all(array, "wide", 0, 0, axis_index_groups=quads, tiled=True)

    def own_rows(weight):
        moved = quad_swap(jnp.transpose(weight, (1, 0, 2)))
        joined = lax.all_gather(moved, "wide", axis=0, axis_index_groups=mates, tiled=True)
        joined = joined.reshape(blocks, 2, 4, rows_each, hidden_width).transpose(0, 2, 1, 3, 4)
        return joined.reshape(full_width, hidden_width)

    def share_rows(grad):
        parts = grad.astype(BF).reshape(blocks, 4, 2, rows_each, hidden_width)
        parts = parts.transpose(0, 2, 1, 3, 4).reshape(blocks * 2, 4, rows_each, hidden_width)
        summed = lax.psum_scatter(
            parts, "wide", scatter_dimension=0, axis_index_groups=mates, tiled=True
        )[0]
        return jnp.transpose(quad_swap(summed), (1, 0, 2)).astype(F32)

    def head_cols(array, head):
        return array[:, head * HEAD_DIM : (head + 1) * HEAD_DIM]

    heads = part_width // HEAD_DIM
    half_dim = HEAD_DIM // 2
    freqs = ROPE_BASE ** (-2.0 * jnp.arange(half_dim, dtype=F32) / HEAD_DIM)
    score_scale = HEAD_DIM ** (-0.5)
    gains = jnp.stack([gain_attn, gain_ffn])
    gain_first_loc = gain_attn.astype(F32)
    gain_second_loc = gain_ffn.astype(F32)
    hot_first, hot_second, kept, pick_first, pick_second = route(expert_ids, slot_order[0])

    if wide_count == 8 and narrow_count == 4:
        seg = segment[0]
        seg_ids = jnp.arange(SEGS, dtype=jnp.int32)
        above = jnp.sum(jnp.where(seg[:, None] == seg_ids[None, :], parents[0][None, :], 0), 1)
        table = jnp.stack([seg, above, slot_order[0], expert_ids[:, 0], expert_ids[:, 1]] + [seg] * 3)
        moved = jnp.stack([jnp.transpose(item, (1, 0, 2)) for item in (w_gate, w_up, w_down)])
        (
            in_w, out_w8, expert_w, slot_mid, slot_grad, slot_gate, middle, hidden_first,
            token_parts, qkv, probs, attended, stat, rope, picks,
        ) = front_call(
            tokens, cotangent, gains, (w_query, w_key, w_value, w_out),
            jnp.pad(w_router, ((0, 0), (0, 124))), moved, table, table.T,
            jnp.tile(freqs, 2)[None, :],
        )
        in_w = in_w.reshape(full_width, 1664)
        query_w, key_w, value_w = (in_w[:, i * 512 : (i + 1) * 512] for i in range(3))
        router_w = in_w[:, 1536 : 1536 + EXPERTS]
        out_w = out_w8.reshape(full_width, part_width)
        gate_w, up_w, down_w = (expert_w[i].reshape(full_width, hidden_width) for i in range(3))
        slot_gate = slot_gate[:, 0:1]
        token_rows = token_parts[:, :token_count]
        tokens_full = jnp.concatenate([token_rows[i] for i in range(4)], 1)
        gains_full = jnp.concatenate([token_parts[i, token_count : token_count + 2] for i in range(4)], 1)
        cosines, sines = rope[0][:, :half_dim], rope[1][:, half_dim:]
        inputs_full = tokens_full.astype(F32)
        scale_first = lax.rsqrt(jnp.mean(inputs_full * inputs_full, -1, keepdims=True) + NORM_EPS)
        normed_first = inputs_full * scale_first
        gain_first = gains_full[0].astype(F32)
        gain_second = gains_full[1].astype(F32)
        saved = [
            tuple(qkv[i, :, h * HEAD_DIM : (h + 1) * HEAD_DIM] for i in range(3)) + (probs[h],)
            for h in range(heads)
        ]
        scale_second = lax.rsqrt(stat[4] / full_width + NORM_EPS)[:, None]
        logits = stat[:EXPERTS].T * scale_second
        slot_mid = slot_mid.astype(F32)
        slot_scale = lax.rsqrt(jnp.mean(slot_mid * slot_mid, -1, keepdims=True) + NORM_EPS)
        slot_hidden = (slot_mid * slot_scale * gain_second).astype(BF)
        pick_first_low, pick_second_low = picks[0].T, picks[1].T
        pick_both_low = pick_first_low + pick_second_low
        share_first, share_second = gate_pair(logits, hot_first, hot_second)
        weight_first = kept[:, 0] * share_first
        weight_second = kept[:, 1] * share_second
        middle_full = lax.all_gather(middle.astype(BF), "narrow", axis=1, tiled=True).astype(F32)
        normed_second = middle_full * scale_second
        hidden_second = (normed_second * gain_second).astype(BF)
    else:
        gate_w, up_w, down_w = own_rows(w_gate), own_rows(w_up), own_rows(w_down)
        attn_w = lax.all_gather(
            jnp.stack([w_query, w_key, w_value, w_out], 1), "wide", axis=0, tiled=True
        )
        query_w, key_w, value_w, out_w = (attn_w[:, i] for i in range(4))
        router_w = lax.all_gather(w_router, "wide", axis=0, tiled=True)
        tokens_full = lax.all_gather(tokens, "narrow", axis=1, tiled=True)
        grad_full = lax.all_gather(cotangent, "narrow", axis=1, tiled=True)
        gains_full = lax.all_gather(gains, "narrow", axis=1, tiled=True)
        gain_first = gains_full[0].astype(F32)
        gain_second = gains_full[1].astype(F32)

        seen, places = tree_layout(segment[0], parents[0])
        pick_first_low = pick_first.astype(BF)
        pick_second_low = pick_second.astype(BF)
        pick_both_low = (pick_first | pick_second).astype(BF)

        inputs_full = tokens_full.astype(F32)
        scale_first = lax.rsqrt(jnp.mean(inputs_full * inputs_full, -1, keepdims=True) + NORM_EPS)
        normed_first = inputs_full * scale_first
        hidden_first = (normed_first * gain_first).astype(BF)
        angles = places[:, None] * freqs[None, :]
        cosines, sines = jnp.cos(angles), jnp.sin(angles)
        query_raw = rows_cols(hidden_first, query_w)
        key_raw = rows_cols(hidden_first, key_w)
        value_low = rows_cols(hidden_first, value_w).astype(BF)

        saved = []
        outs = []
        for head in range(heads):
            query = rotate(head_cols(query_raw, head), cosines, sines).astype(BF)
            key = rotate(head_cols(key_raw, head), cosines, sines).astype(BF)
            value = head_cols(value_low, head)
            scores = jnp.where(seen, rows_rows(query, key) * score_scale, NEG_FILL)
            exps = jnp.exp(scores - jnp.max(scores, -1, keepdims=True))
            weights = exps / jnp.sum(exps, -1, keepdims=True)
            saved.append((query, key, value, weights))
            outs.append(rows_cols(weights.astype(BF), value).astype(BF))
        attended = jnp.concatenate(outs, 1)
        branch_part = rows_rows(attended, out_w).astype(BF)
        branch_loc = lax.psum_scatter(
            branch_part, "narrow", scatter_dimension=1, tiled=True
        ).astype(F32)
        middle = tokens.astype(F32) + branch_loc
        middle_full = lax.all_gather(middle.astype(BF), "narrow", axis=1, tiled=True).astype(F32)
        scale_second = lax.rsqrt(jnp.mean(middle_full * middle_full, -1, keepdims=True) + NORM_EPS)
        normed_second = middle_full * scale_second
        hidden_second = (normed_second * gain_second).astype(BF)
        logits = rows_cols(hidden_second, router_w)
        share_first, share_second = gate_pair(logits, hot_first, hot_second)
        weight_first = kept[:, 0] * share_first
        weight_second = kept[:, 1] * share_second

        slot_weight = jnp.sum(
            pick_first * weight_first[:, None] + pick_second * weight_second[:, None], 0
        )
        weight_high, weight_low = two_parts(slot_weight)
        pads = jnp.stack([weight_high, weight_low], 1)
        pads = jnp.pad(pads, ((0, 0), (0, 126)))
        sent_hidden = cols_cols(pick_both_low, hidden_second).astype(BF)
        sent_grad = cols_cols(pick_both_low, grad_full).astype(BF)
        sent = jnp.concatenate([sent_hidden, sent_grad, pads], 1)
        got = quad_swap(sent.reshape(EXPERTS, CAP, -1)).reshape(SLOTS, -1)
        slot_hidden = got[:, :full_width]
        slot_grad = got[:, full_width : 2 * full_width]
        slot_gate = got[:, 2 * full_width : 2 * full_width + 2].astype(F32)
        slot_gate = slot_gate[:, 0:1] + slot_gate[:, 1:2]

    gate_pre = rows_cols(slot_hidden, gate_w)
    up_pre = rows_cols(slot_hidden, up_w)
    sigmoid_gate = jax.nn.sigmoid(gate_pre)
    silu_gate = gate_pre * sigmoid_gate
    activated = (silu_gate * up_pre).astype(BF)
    expert_part = rows_rows(activated, down_w)
    act_raw = rows_cols(slot_grad, down_w)
    share_part = jnp.sum(act_raw * activated.astype(F32), 1, keepdims=True)
    grad_act = act_raw * slot_gate
    grad_gate_pre = (
        grad_act * up_pre * sigmoid_gate * (1.0 + gate_pre * (1.0 - sigmoid_gate))
    ).astype(BF)
    grad_up_pre = (grad_act * silu_gate).astype(BF)
    grad_slot = rows_rows(grad_gate_pre, gate_w) + rows_rows(grad_up_pre, up_w)
    stat_part = jnp.sum(slot_hidden.astype(F32) * grad_slot, 1, keepdims=True)
    extras = jnp.concatenate([*two_parts(share_part), *two_parts(stat_part)], 1)
    extras = jnp.pad(extras, ((0, 0), (0, 124)))
    back_parts = []
    expert_plain = expert_part.astype(BF)
    slot_plain = grad_slot.astype(BF)
    for part in range(narrow_count):
        cols = slice(part * part_width, (part + 1) * part_width)
        back_parts += [expert_plain[:, cols], slot_plain[:, cols], extras]
    back = lax.psum_scatter(
        jnp.concatenate(back_parts, 1), "narrow", scatter_dimension=1, tiled=True
    )
    back = quad_swap(back.reshape(EXPERTS, CAP, -1)).reshape(SLOTS, -1)
    picked_first = rows_cols(pick_first_low, back)
    picked_second = rows_cols(pick_second_low, back)
    output = (
        middle
        + weight_first[:, None] * picked_first[:, :part_width]
        + weight_second[:, None] * picked_second[:, :part_width]
    ).astype(BF)

    grad_weight = (slot_grad.astype(F32) * slot_gate).astype(BF)
    gate_out = share_rows(cols_cols(slot_hidden, grad_gate_pre))
    up_out = share_rows(cols_cols(slot_hidden, grad_up_pre))
    down_out = share_rows(cols_cols(grad_weight, activated))

    tail = 2 * part_width
    share_first_grad = picked_first[:, tail] + picked_first[:, tail + 1]
    share_second_grad = picked_second[:, tail] + picked_second[:, tail + 1]
    both = picked_first + picked_second
    stat_second = both[:, tail + 2] + both[:, tail + 3]
    grad_hidden_loc = both[:, part_width:tail]
    grad_local = cotangent.astype(F32)
    _, pull_gates = jax.vjp(lambda given: gate_pair(given, hot_first, hot_second), logits)
    (grad_logits,) = pull_gates((kept[:, 0] * share_first_grad, kept[:, 1] * share_second_grad))
    grad_logits_low = grad_logits.astype(BF)
    grad_router_rows = rows_rows(grad_logits_low, router_w)
    stat_total = stat_second + jnp.sum(normed_second * gain_second * grad_router_rows, 1)

    def take_cols(full_rows):
        return lax.dynamic_slice_in_dim(full_rows, narrow_at * part_width, part_width, 1)

    grad_hidden_loc = grad_hidden_loc + take_cols(grad_router_rows)
    normed_second_loc = take_cols(normed_second)
    grad_gain_second = jnp.sum(grad_hidden_loc * normed_second_loc, 0)
    grad_middle = grad_local + scale_second * (
        gain_second_loc * grad_hidden_loc - normed_second_loc * stat_total[:, None] / full_width
    )
    grad_router_w = cols_cols(hidden_second, grad_logits_low)
    grad_branch = lax.all_gather(grad_middle.astype(BF), "narrow", axis=1, tiled=True)
    grad_attended = rows_cols(grad_branch, out_w).astype(BF)
    grad_out_w = cols_cols(grad_branch, attended)
    grad_qs, grad_ks, grad_vs = [], [], []
    for head in range(heads):
        query, key, value, weights = saved[head]
        grad_out = head_cols(grad_attended, head)
        grad_weights = rows_rows(grad_out, value)
        inner = jnp.sum(weights * grad_weights, -1, keepdims=True)
        grad_scores = (weights * (grad_weights - inner)).astype(BF)
        grad_q = rows_cols(grad_scores, key) * score_scale
        grad_k = cols_cols(grad_scores, query) * score_scale
        grad_qs.append(rotate(grad_q, cosines, -sines).astype(BF))
        grad_ks.append(rotate(grad_k, cosines, -sines).astype(BF))
        grad_vs.append(cols_cols(weights.astype(BF), grad_out).astype(BF))
    grad_query_raw = jnp.concatenate(grad_qs, 1)
    grad_key_raw = jnp.concatenate(grad_ks, 1)
    grad_value_raw = jnp.concatenate(grad_vs, 1)
    grad_hidden_first = (
        rows_rows(grad_query_raw, query_w)
        + rows_rows(grad_key_raw, key_w)
        + rows_rows(grad_value_raw, value_w)
    )
    stat_first = jnp.sum(normed_first * gain_first * grad_hidden_first, 1, keepdims=True)
    extras = jnp.pad(jnp.concatenate(two_parts(stat_first), 1), ((0, 0), (0, 126)))
    grad_hidden_low = grad_hidden_first.astype(BF)
    first_parts = []
    for part in range(narrow_count):
        first_parts += [grad_hidden_low[:, part * part_width : (part + 1) * part_width], extras]
    first_back = lax.psum_scatter(
        jnp.concatenate(first_parts, 1), "narrow", scatter_dimension=1, tiled=True
    ).astype(F32)
    grad_first_loc = first_back[:, :part_width]
    stat_first = first_back[:, part_width : part_width + 1]
    stat_first = stat_first + first_back[:, part_width + 1 : part_width + 2]
    normed_first_loc = take_cols(normed_first)
    grad_gain_first = jnp.sum(grad_first_loc * normed_first_loc, 0)
    grad_tokens = grad_middle + scale_first * (
        gain_first_loc * grad_first_loc - normed_first_loc * stat_first / full_width
    )
    grad_attn_w = jnp.concatenate(
        [
            cols_cols(hidden_first, grad_query_raw).astype(BF),
            cols_cols(hidden_first, grad_key_raw).astype(BF),
            cols_cols(hidden_first, grad_value_raw).astype(BF),
            grad_out_w.astype(BF),
        ],
        1,
    )
    attn_summed = lax.psum_scatter(
        grad_attn_w, "wide", scatter_dimension=0, tiled=True
    ).astype(F32)
    router_summed = lax.psum_scatter(grad_router_w, "wide", scatter_dimension=0, tiled=True)
    gains_summed = lax.psum(jnp.stack([grad_gain_first, grad_gain_second]), "wide")
    return (
        output,
        grad_tokens,
        gains_summed[0],
        attn_summed[:, :part_width],
        attn_summed[:, part_width : 2 * part_width],
        attn_summed[:, 2 * part_width : 3 * part_width],
        attn_summed[:, 3 * part_width :],
        gains_summed[1],
        router_summed,
        gate_out,
        up_out,
        down_out,
    )


def solution(mesh):
    pair = P("wide", "narrow")
    part = P("narrow")
    rows = P("wide", None)
    cube = P("wide", None, "narrow")
    return jax.shard_map(
        per_device,
        mesh=mesh,
        in_specs=(
            pair, part, pair, pair, pair, pair, part, rows, cube, cube, cube,
            rows, rows, rows, rows, pair,
        ),
        out_specs=(
            pair, pair, part, pair, pair, pair, pair, part, rows, cube, cube, cube,
        ),
        check_vma=False,
    )
```

```python
import jax
import jax.numpy as jnp
from jax import lax
from jax.experimental import pallas as pl
from jax.experimental.pallas import tpu as pltpu
from jax.sharding import PartitionSpec as P

HEAD_DIM = 128
EXPERTS = 4
SEGS = 13
CAP = 144
SLOTS = EXPERTS * CAP
NORM_EPS = 1e-05
NEG_FILL = -1e30
ROPE_BASE = 10000.0
BF = jnp.bfloat16
F32 = jnp.float32


def mm(left, right, dims):
    return lax.dot_general(left, right, (dims, ((), ())), preferred_element_type=F32)


def rows_cols(left, right):
    return mm(left, right, ((1,), (0,)))


def rows_rows(left, right):
    return mm(left, right, ((1,), (1,)))


def cols_cols(left, right):
    return mm(left, right, ((0,), (0,)))


def tree_layout(segment_row, parent_row):
    seg_ids = jnp.arange(SEGS, dtype=jnp.int32)
    member = segment_row[:, None] == seg_ids[None, :]
    parent_of = (parent_row[:, None] == seg_ids[None, :]) & (seg_ids[:, None] != 0)
    itself = seg_ids[:, None] == seg_ids[None, :]
    reach = itself
    for _ in range(3):
        reach = itself | jnp.any(parent_of[:, :, None] & reach[None, :, :], axis=1)
    counts = member.astype(jnp.int32)
    lengths = jnp.sum(counts, 0)
    starts = jnp.sum(jnp.where(seg_ids[None, :] < seg_ids[:, None], lengths[None, :], 0), 1)
    before = jnp.sum(jnp.where(reach, lengths[None, :], 0), 1) - lengths
    row_at = jnp.arange(segment_row.shape[0], dtype=jnp.int32)
    places = jnp.sum(counts * (before - starts)[None, :], 1) + row_at
    member_low = member.astype(BF)
    lineage = rows_cols(member_low, reach.astype(BF)).astype(BF)
    shared = rows_rows(lineage, member_low) > 0.5
    seen = shared & (row_at[None, :] <= row_at[:, None])
    return seen, places.astype(F32)


def route(expert_row, slot_rank):
    expert_range = jnp.arange(EXPERTS, dtype=jnp.int32)
    hot_first = (expert_row[:, 0:1] == expert_range[None, :]).astype(F32)
    hot_second = (expert_row[:, 1:2] == expert_range[None, :]).astype(F32)
    earlier = (slot_rank[None, :] < slot_rank[:, None]).astype(BF)
    count_first = rows_cols(earlier, hot_first.astype(BF))
    count_second = rows_cols(earlier, hot_second.astype(BF))
    ahead_first = jnp.sum(count_first * hot_first, 1)
    ahead_second = jnp.sum((count_second + jnp.sum(hot_first, 0)[None, :]) * hot_second, 1)
    slot_index = jnp.stack([ahead_first, ahead_second], 1).astype(jnp.int32)
    kept = slot_index < CAP
    flat_slot = jnp.where(kept, expert_row * CAP + slot_index, SLOTS)
    slot_range = jnp.arange(SLOTS, dtype=jnp.int32)
    pick_first = flat_slot[:, 0:1] == slot_range[None, :]
    pick_second = flat_slot[:, 1:2] == slot_range[None, :]
    return hot_first, hot_second, kept.astype(F32), pick_first, pick_second


def rotate(vectors, cosines, sines):
    half_dim = HEAD_DIM // 2
    first_half = vectors[..., :half_dim]
    second_half = vectors[..., half_dim:]
    return jnp.concatenate(
        [
            first_half * cosines - second_half * sines,
            second_half * cosines + first_half * sines,
        ],
        -1,
    )


def gate_pair(logits, hot_first, hot_second):
    chances = jax.nn.softmax(logits, axis=-1)
    first_share = jnp.sum(chances * hot_first, 1)
    second_share = jnp.sum(chances * hot_second, 1)
    pair_total = first_share + second_share
    return (first_share / pair_total, second_share / pair_total)


def two_parts(column):
    high = column.astype(BF)
    return high, (column - high.astype(F32)).astype(BF)


MESH = pl.DeviceIdType.MESH
NEAR = 3


def low_dot(left, right):
    return jnp.dot(left, right, preferred_element_type=F32)


def places_of(n):
    return [lax.rem(n + step, 4) for step in (1, 2, 3)], [lax.rem(n + 4 - step, 4) for step in (1, 2, 3)]


def plane_of(chip):
    x, y = lax.rem(chip, 2), chip // 2
    return [2 * y + 1 - x, 2 * (1 - y) + x, 2 * (1 - y) + 1 - x]


def greet(narrow_peers, plane_peers, chip, core, mate):
    barrier = pltpu.get_barrier_semaphore()
    count = 0
    for peer in narrow_peers:
        pl.semaphore_signal(barrier, inc=1, device_id={"narrow": peer}, device_id_type=MESH)
        count += 1
    for peer in plane_peers:
        pl.semaphore_signal(
            barrier, inc=1, device_id={"wide": 2 * peer + core}, device_id_type=MESH
        )
        count += 1
    if mate:
        pl.semaphore_signal(
            barrier, inc=1, device_id={"wide": 2 * chip + 1 - core}, device_id_type=MESH
        )
        count += 1
    pl.semaphore_wait(barrier, count)


class Links:
    def __init__(self, sent, landed, local):
        self.sent, self.landed, self.local = sent, landed, local
        self.used, self.local_used = 0, 0
        self.waits = []

    def slot(self):
        self.used += 1
        return self.used - 1

    def send(self, source, target, device, slot, when=None):
        copy = pltpu.make_async_remote_copy(
            src_ref=source,
            dst_ref=target,
            send_sem=self.sent.at[slot],
            recv_sem=self.landed.at[slot],
            device_id=device,
            device_id_type=MESH,
        )
        if when is None:
            copy.start()
        else:
            pl.when(when)(copy.start)
        self.waits.append((copy, when))

    def land(self, target, device, slot, when=None):
        copy = pltpu.make_async_remote_copy(
            src_ref=target,
            dst_ref=target,
            send_sem=self.sent.at[slot],
            recv_sem=self.landed.at[slot],
            device_id=device,
            device_id_type=MESH,
        )
        if when is None:
            copy.wait_recv()
        else:
            pl.when(when)(copy.wait_recv)

    def move(self, source, target):
        copy = pltpu.make_async_copy(source, target, self.local.at[self.local_used])
        self.local_used += 1
        copy.start()
        self.waits.append((copy, "local"))
        return copy

    def finish(self):
        for copy, when in self.waits:
            if when == "local":
                copy.wait()
            elif when is None:
                copy.wait_send()
            else:
                pl.when(when)(copy.wait_send)


class Chain:
    def __init__(self, links, n, block):
        self.links, self.n, self.block = links, n, block
        self.slots = [(links.slot(), links.slot()) for _ in range(3)]

    def start(self, step):
        n, links = self.n, self.links
        right, left = self.slots[step]
        block = self.block(lax.rem(n + 4 - step, 4))
        links.send(
            block, block, {"narrow": lax.rem(n + 1, 4)}, right,
            (n < 3) & (n >= step),
        )
        block = self.block(lax.rem(n + step, 4))
        links.send(
            block, block, {"narrow": lax.rem(n + 3, 4)}, left,
            (n > 0) & (n + step <= 3),
        )

    def land(self, step):
        n, links = self.n, self.links
        right, left = self.slots[step]
        links.land(
            self.block(lax.rem(n + 7 - step, 4)), {"narrow": lax.rem(n + 3, 4)}, right,
            n >= step + 1,
        )
        links.land(
            self.block(lax.rem(n + 1 + step, 4)), {"narrow": lax.rem(n + 1, 4)}, left,
            n + 1 + step <= 3,
        )


FRONT_SLOTS = 72


def front_body(
    tok_ref, cot_ref, gains_ref, wq_ref, wk_ref, wv_ref, wo_ref, router_ref, moved_ref,
    rows_ref, cols_ref, freq_ref,
    qkvw_out, outw_out, expert_out, x_out, dy_out, gate_out, middle_out, hidden_out,
    tokens_out, qkv_out, prob_out, att_out, stat_out, rope_out, pick_out,
    pack, tok_pack, qkvw, outw, cot_send, y_send, br_send, br_recv, stat_send, stat_recv,
    gate_send, sent, landed, local,
):
    n = lax.axis_index("narrow")
    w = lax.axis_index("wide")
    chip, core = w // 2, lax.rem(w, 2)
    to_z, from_z = places_of(n)
    plane = plane_of(chip)
    links = Links(sent, landed, local)
    mate = {"wide": 2 * chip + 1 - core}

    def at_plane(peer):
        return {"wide": 2 * peer + core}

    token_count, part_width = tok_ref.shape
    greet(to_z, plane, chip, core, True)

    tok_pack[0:token_count, :] = tok_ref[...]
    tok_pack[token_count : token_count + 2, :] = gains_ref[...]
    tok_slots = [links.slot() for _ in range(NEAR)]
    for step in range(NEAR):
        links.send(tok_pack, tokens_out.at[n], {"narrow": to_z[step]}, tok_slots[step])
    pack[:, 0:512] = wq_ref[...]
    pack[:, 512:1024] = wk_ref[...]
    pack[:, 1024:1536] = wv_ref[...]
    pack[:, 1536:1664] = router_ref[...]
    in_slots = [links.slot() for _ in range(NEAR)]
    for step in range(NEAR):
        links.send(pack, qkvw.at[w], at_plane(plane[step]), in_slots[step])
    in_mate = [links.slot() for _ in range(4)]
    links.send(pack, qkvw.at[w], mate, in_mate[3])
    out_slots = [links.slot() for _ in range(NEAR)]
    for step in range(NEAR):
        links.send(wo_ref, outw.at[w], at_plane(plane[step]), out_slots[step])
    out_mate = [links.slot() for _ in range(4)]
    links.send(wo_ref, outw.at[w], mate, out_mate[3])
    tokens_out[n] = tok_pack[...]
    qkvw[w] = pack[...]
    outw[w] = wo_ref[...]

    wide_shape = (token_count, token_count)
    row_at = lax.broadcasted_iota(jnp.int32, wide_shape, 0)
    col_at = lax.broadcasted_iota(jnp.int32, wide_shape, 1)
    seg_row, rank_row = rows_ref[0:1, :], rows_ref[2:3, :]
    seg_col, par_col, rank_col = cols_ref[:, 0:1], cols_ref[:, 1:2], cols_ref[:, 2:3]
    seen = ((seg_row == seg_col) | (seg_row == par_col) | (seg_row == 0)) & (col_at <= row_at)
    spots = jnp.sum(jnp.where(seen, 1.0, 0.0), 1, keepdims=True) - 1.0
    angles = spots * freq_ref[...]
    cosines = jnp.cos(angles)
    lane_at = lax.broadcasted_iota(jnp.int32, angles.shape, 1)
    sines = jnp.sin(angles) * jnp.where(lane_at < HEAD_DIM // 2, -1.0, 1.0)
    rope_out[0] = cosines
    rope_out[1] = sines
    kind = lax.broadcasted_iota(jnp.int32, (8, token_count), 0)
    first_row, second_row = rows_ref[3:4, :], rows_ref[4:5, :]
    hot_first = jnp.where(kind == first_row, 1.0, 0.0)
    hot_second = jnp.where(kind == second_row, 1.0, 0.0)
    earlier = jnp.where(rank_col < rank_row, 1.0, 0.0).astype(BF)
    count_first = low_dot(hot_first.astype(BF), earlier)
    count_second = low_dot(hot_second.astype(BF), earlier)
    count_second = count_second + jnp.sum(hot_first, 1, keepdims=True)
    slot_first = jnp.sum(count_first * hot_first, 0, keepdims=True)
    slot_second = jnp.sum(count_second * hot_second, 0, keepdims=True)
    kept_first = jnp.where(slot_first < CAP, 1.0, 0.0)
    kept_second = jnp.where(slot_second < CAP, 1.0, 0.0)
    flat_first = jnp.where(slot_first < CAP, first_row * CAP + slot_first.astype(jnp.int32), SLOTS)
    flat_second = jnp.where(
        slot_second < CAP, second_row * CAP + slot_second.astype(jnp.int32), SLOTS
    )
    slot_at = lax.broadcasted_iota(jnp.int32, (SLOTS, token_count), 0)
    pick_first = jnp.where(slot_at == flat_first, 1.0, 0.0)
    pick_second = jnp.where(slot_at == flat_second, 1.0, 0.0)
    pick_out[0] = pick_first.astype(BF)
    pick_out[1] = pick_second.astype(BF)
    pick_both = (pick_first + pick_second).astype(BF)

    def column_block(array):
        return lambda m: array.at[:, pl.ds(pl.multiple_of(m * part_width, part_width), part_width)]

    def slot_block(array, owner):
        return array.at[
            pl.ds(pl.multiple_of(owner * CAP, 16), CAP),
            pl.ds(pl.multiple_of(n * part_width, part_width), part_width),
        ]

    def dispatch(rows, buffer, array):
        slots = [links.slot() for _ in range(NEAR)]
        buffer[...] = low_dot(pick_both, rows).astype(BF)
        for step in range(NEAR):
            links.send(
                buffer.at[pl.ds(pl.multiple_of(plane[step] * CAP, 16), CAP), :],
                slot_block(array, chip), at_plane(plane[step]), slots[step],
            )
        own = links.move(
            buffer.at[pl.ds(pl.multiple_of(chip * CAP, 16), CAP), :], slot_block(array, chip)
        )
        return slots, own

    def arrive(array, state):
        slots, own = state
        for step in range(NEAR):
            links.land(slot_block(array, plane[step]), at_plane(plane[step]), slots[step])
        own.wait()
        links.waits = [item for item in links.waits if item[0] is not own]

    dy_state = dispatch(cot_ref[...], cot_send, dy_out)
    dy_chain = Chain(links, n, column_block(dy_out))

    for step in range(NEAR):
        links.land(tokens_out.at[from_z[step]], {"narrow": from_z[step]}, tok_slots[step])
    total = jnp.zeros((token_count, 1), F32)
    for m in range(4):
        part = tokens_out[m, 0:token_count, :].astype(F32)
        total = total + jnp.sum(part * part, 1, keepdims=True)
    scale_first = lax.rsqrt(total * (1.0 / (4 * part_width)) + NORM_EPS)
    for m in range(4):
        part = tokens_out[m, 0:token_count, :].astype(F32)
        gain = tokens_out[m, token_count : token_count + 1, :].astype(F32)
        hidden_out[:, m * part_width : (m + 1) * part_width] = (part * scale_first * gain).astype(BF)

    arrive(dy_out, dy_state)
    dy_chain.start(0)

    for step in range(NEAR):
        owner = 2 * plane[step] + core
        links.land(qkvw.at[owner], at_plane(plane[step]), in_slots[step])
        links.send(qkvw.at[owner], qkvw.at[owner], mate, in_mate[step])
    for step in range(NEAR):
        links.land(qkvw.at[2 * plane[step] + 1 - core], mate, in_mate[step])
    links.land(qkvw.at[2 * chip + 1 - core], mate, in_mate[3])
    saved_in = links.move(qkvw, qkvw_out)

    expert_slots = [[links.slot() for _ in range(NEAR)] for _ in range(3)]
    expert_mate = [[links.slot() for _ in range(4)] for _ in range(3)]
    for kind_at in range(3):
        for step in range(NEAR):
            links.send(
                moved_ref.at[kind_at, plane[step]], expert_out.at[kind_at, chip, core],
                at_plane(plane[step]), expert_slots[kind_at][step],
            )
        links.send(
            moved_ref.at[kind_at, chip], expert_out.at[kind_at, chip, core], mate,
            expert_mate[kind_at][3],
        )
        links.move(moved_ref.at[kind_at, chip], expert_out.at[kind_at, chip, core])

    def pass_on(kind_at):
        for step in range(NEAR):
            block = expert_out.at[kind_at, plane[step], core]
            links.land(block, at_plane(plane[step]), expert_slots[kind_at][step])
            links.send(block, block, mate, expert_mate[kind_at][step])

    def all_there(kind_at):
        for step in range(NEAR):
            links.land(
                expert_out.at[kind_at, plane[step], 1 - core], mate, expert_mate[kind_at][step]
            )
        links.land(expert_out.at[kind_at, chip, 1 - core], mate, expert_mate[kind_at][3])

    dy_chain.land(0)
    dy_chain.start(1)

    hidden = hidden_out[...]
    score_scale = HEAD_DIM ** (-0.5)
    raws = []
    for part in range(3):
        weight = qkvw[:, :, part * 512 : (part + 1) * 512].reshape(4 * part_width, part_width)
        raws.append(low_dot(hidden, weight))
    for head in range(part_width // HEAD_DIM):
        cols = slice(head * HEAD_DIM, (head + 1) * HEAD_DIM)
        turned = []
        for part in range(2):
            raw = raws[part][:, cols]
            turned.append(
                (raw * cosines + pltpu.roll(raw, HEAD_DIM // 2, 1) * sines).astype(BF)
            )
            qkv_out[part, :, cols] = turned[part]
        value = raws[2][:, cols].astype(BF)
        qkv_out[2, :, cols] = value
        scores = rows_rows(turned[0], turned[1]) * score_scale
        scores = jnp.where(seen, scores, NEG_FILL)
        exps = jnp.exp(scores - jnp.max(scores, 1, keepdims=True))
        weights = exps / jnp.sum(exps, 1, keepdims=True)
        prob_out[head] = weights
        att_out[:, cols] = low_dot(weights.astype(BF), value).astype(BF)

    dy_chain.land(1)
    dy_chain.start(2)

    for step in range(NEAR):
        owner = 2 * plane[step] + core
        links.land(outw.at[owner], at_plane(plane[step]), out_slots[step])
        links.send(outw.at[owner], outw.at[owner], mate, out_mate[step])
    for step in range(NEAR):
        links.land(outw.at[2 * plane[step] + 1 - core], mate, out_mate[step])
    links.land(outw.at[2 * chip + 1 - core], mate, out_mate[3])
    links.move(outw, outw_out)

    attended = att_out[...]

    def branch(m):
        weight = outw[pl.ds(2 * m, 2)].reshape(part_width, part_width)
        return rows_rows(attended, weight)

    br_slots = [links.slot() for _ in range(NEAR)]
    for step in range(NEAR):
        br_send[step] = branch(to_z[step]).astype(BF)
        links.send(br_send.at[step], br_recv.at[step], {"narrow": to_z[step]}, br_slots[step])
    middle = tok_ref[...].astype(F32) + branch(n)
    for step in range(NEAR):
        links.land(br_recv.at[step], {"narrow": from_z[step]}, br_slots[step])
        middle = middle + br_recv[step].astype(F32)
    middle_out[...] = middle
    x_state = dispatch(middle.astype(BF), y_send, x_out)
    x_chain = Chain(links, n, column_block(x_out))

    gain_second = gains_ref[1:2, :].astype(F32)
    router = qkvw[pl.ds(2 * n, 2), :, 1536:1664].reshape(part_width, 128)
    logit_part = mm(router, (middle * gain_second).astype(BF), ((0,), (1,)))[0:8, :]
    square = middle * middle
    square_high = square.astype(BF)
    square_low = (square - square_high.astype(F32)).astype(BF)
    ones = jnp.ones((8, part_width), BF)
    square_sum = rows_rows(ones, square_high) + rows_rows(ones, square_low)
    stat = jnp.where(kind == 4, square_sum, logit_part)
    stat_send[...] = stat
    stat_slots = [links.slot() for _ in range(NEAR)]
    for step in range(NEAR):
        links.send(stat_send, stat_recv.at[step], {"narrow": to_z[step]}, stat_slots[step])

    arrive(x_out, x_state)
    x_chain.start(0)
    for step in range(NEAR):
        links.land(stat_recv.at[step], {"narrow": from_z[step]}, stat_slots[step])
        stat = stat + stat_recv[step]
    stat_out[...] = stat
    scale_row = lax.rsqrt(stat[4:5, :] * (1.0 / (4 * part_width)) + NORM_EPS)
    logits = jnp.where(kind < EXPERTS, stat * scale_row, NEG_FILL)
    chances = jnp.exp(logits - jnp.max(logits, 0, keepdims=True))
    chances = chances / jnp.sum(chances, 0, keepdims=True)
    share_first = jnp.sum(chances * hot_first, 0, keepdims=True)
    share_second = jnp.sum(chances * hot_second, 0, keepdims=True)
    both = share_first + share_second
    weighted = pick_first * (share_first / both) + pick_second * (share_second / both)
    slot_gate = jnp.sum(weighted, 1, keepdims=True)
    gate_send[...] = jnp.broadcast_to(slot_gate, (SLOTS, 128))

    def gate_rows(array, owner):
        return array.at[pl.ds(pl.multiple_of(owner * CAP, 16), CAP), :]

    gate_slots = [links.slot() for _ in range(NEAR)]
    for step in range(NEAR):
        links.send(
            gate_rows(gate_send, plane[step]), gate_rows(gate_out, chip),
            at_plane(plane[step]), gate_slots[step],
        )
    links.move(gate_rows(gate_send, chip), gate_rows(gate_out, chip))

    pass_on(0)
    x_chain.land(0)
    x_chain.start(1)
    x_chain.land(1)
    x_chain.start(2)
    pass_on(1)
    x_chain.land(2)
    dy_chain.land(2)
    for step in range(NEAR):
        links.land(gate_rows(gate_out, plane[step]), at_plane(plane[step]), gate_slots[step])
    pass_on(2)
    for kind_at in range(3):
        all_there(kind_at)
    links.finish()


def front_call(tokens, cotangent, gains, weights, router, moved, rows, cols, freqs):
    token_count, part_width = tokens.shape
    full = 4 * part_width
    hidden_width = moved.shape[3]
    rows_each = moved.shape[2]
    heads = part_width // HEAD_DIM
    vmem = pl.BlockSpec(memory_space=pltpu.VMEM)
    hbm = pl.BlockSpec(memory_space=pl.ANY)

    def arr(shape, dtype):
        return jax.ShapeDtypeStruct(shape, dtype)

    return pl.pallas_call(
        front_body,
        out_shape=(
            arr((8, rows_each, 1664), BF),
            arr((8, rows_each, part_width), BF),
            arr((3, 4, 2, rows_each, hidden_width), BF),
            arr((SLOTS, full), BF),
            arr((SLOTS, full), BF),
            arr((SLOTS, 128), F32),
            arr((token_count, part_width), F32),
            arr((token_count, full), BF),
            arr((4, token_count + 16, part_width), BF),
            arr((3, token_count, part_width), BF),
            arr((heads, token_count, token_count), F32),
            arr((token_count, part_width), BF),
            arr((8, token_count), F32),
            arr((2, token_count, HEAD_DIM), F32),
            arr((2, SLOTS, token_count), BF),
        ),
        in_specs=[vmem] * 8 + [hbm] + [vmem] * 3,
        out_specs=(hbm, hbm, hbm) + (vmem,) * 12,
        scratch_shapes=[
            pltpu.VMEM((rows_each, 1664), BF),
            pltpu.VMEM((token_count + 16, part_width), BF),
            pltpu.VMEM((8, rows_each, 1664), BF),
            pltpu.VMEM((8, rows_each, part_width), BF),
            pltpu.VMEM((SLOTS, part_width), BF),
            pltpu.VMEM((SLOTS, part_width), BF),
            pltpu.VMEM((NEAR, token_count, part_width), BF),
            pltpu.VMEM((NEAR, token_count, part_width), BF),
            pltpu.VMEM((8, token_count), F32),
            pltpu.VMEM((NEAR, 8, token_count), F32),
            pltpu.VMEM((SLOTS, 128), F32),
            pltpu.SemaphoreType.DMA((FRONT_SLOTS,)),
            pltpu.SemaphoreType.DMA((FRONT_SLOTS,)),
            pltpu.SemaphoreType.DMA((16,)),
        ],
        compiler_params=pltpu.CompilerParams(
            collective_id=0, has_side_effects=True, vmem_limit_bytes=60 * 1024 * 1024
        ),
        cost_estimate=pl.CostEstimate(
            flops=6_000_000_000, bytes_accessed=60_000_000, transcendentals=400_000
        ),
        name="front",
    )(tokens, cotangent, gains, *weights, router, moved, rows, cols, freqs)


MID_SLOTS = 48


def column_tiles(width):
    tiles, start = [], 0
    while start < width:
        size = min(256, width - start)
        tiles.append((start, size))
        start += size
    return tiles


def mid_body(
    x_ref, dy_ref, gate_ref, tokens_ref, w_ref,
    back_mid_out, back_exp_out, extra_out, grads_out,
    weights, hidden, graded, hidden_cat, graded_cat, act_cat, gate_cat, up_cat,
    rs_send, rs_recv, ext_send, ext_recv, sent, landed, local,
):
    n = lax.axis_index("narrow")
    w = lax.axis_index("wide")
    chip, core = w // 2, lax.rem(w, 2)
    to_z, from_z = places_of(n)
    links = Links(sent, landed, local)
    mate = {"wide": 2 * chip + 1 - core}
    slots, full = x_ref.shape
    part_width = full // 4
    rows_each = full // 8
    hidden_width = weights.shape[2]
    tiles = column_tiles(hidden_width)

    loads = [
        [
            links.move(w_ref.at[kind, c, k], weights.at[kind, pl.ds((2 * c + k) * rows_each, rows_each), :])
            for c in range(4)
            for k in range(2)
        ]
        for kind in range(3)
    ]
    links.waits = []
    greet(to_z, [], chip, core, True)

    total = jnp.zeros((slots, 1), F32)
    for m in range(4):
        part = x_ref[:, m * part_width : (m + 1) * part_width].astype(F32)
        total = total + jnp.sum(part * part, 1, keepdims=True)
    scale = lax.rsqrt(total * (1.0 / full) + NORM_EPS)
    slot_gate = gate_ref[:, 0:1]
    for m in range(4):
        cols = slice(m * part_width, (m + 1) * part_width)
        gain = tokens_ref[m, 257:258, :].astype(F32)
        hidden[:, cols] = (x_ref[:, cols].astype(F32) * scale * gain).astype(BF)
        graded[:, cols] = (dy_ref[:, cols].astype(F32) * slot_gate).astype(BF)

    def to_mate(source, target):
        slot = links.slot()
        links.send(source, target.at[core], mate, slot)
        return lambda: links.land(target.at[1 - core], mate, slot)

    def parity_exchange(source, target):
        lands = []
        for c in range(4):
            cols = pl.ds(c * rows_each, rows_each)
            theirs = pl.ds(pl.multiple_of((2 * c + 1 - core) * rows_each, rows_each), rows_each)
            ours = pl.ds(pl.multiple_of((2 * c + core) * rows_each, rows_each), rows_each)
            slot = links.slot()
            links.send(source.at[:, theirs], target.at[core, :, cols], mate, slot)
            target[core, :, c * rows_each : (c + 1) * rows_each] = source[:, ours]
            lands.append((target.at[1 - core, :, cols], slot))
        return lambda: [links.land(block, mate, slot) for block, slot in lands]

    hidden_there = parity_exchange(hidden, hidden_cat)
    graded_there = parity_exchange(graded, graded_cat)

    for kind in range(3):
        for load in loads[kind]:
            load.wait()
    share = jnp.zeros((slots, 1), F32)
    for start, size in tiles:
        cols = slice(start, start + size)
        gate_pre = low_dot(hidden[...], weights[0, :, cols])
        up_pre = low_dot(hidden[...], weights[1, :, cols])
        act_raw = low_dot(dy_ref[...], weights[2, :, cols])
        sigmoid = 1.0 / (1.0 + jnp.exp(-gate_pre))
        silu = gate_pre * sigmoid
        activated = (silu * up_pre).astype(BF)
        share = share + jnp.sum(act_raw * activated.astype(F32), 1, keepdims=True)
        grad_act = act_raw * slot_gate
        act_cat[core, :, cols] = activated
        gate_cat[core, :, cols] = (
            grad_act * up_pre * (sigmoid * (1.0 + gate_pre * (1.0 - sigmoid)))
        ).astype(BF)
        up_cat[core, :, cols] = (grad_act * silu).astype(BF)

    grad_gate, grad_up = gate_cat[core], up_cat[core]
    stat = jnp.zeros((slots, 1), F32)
    mid_slots = [links.slot() for _ in range(NEAR)]
    for step in range(NEAR + 1):
        owner = to_z[step] if step < NEAR else n
        rows = pl.ds(pl.multiple_of(owner * part_width, part_width), part_width)
        block = rows_rows(grad_gate, weights[0, rows, :]) + rows_rows(grad_up, weights[1, rows, :])
        cols = pl.ds(pl.multiple_of(owner * part_width, part_width), part_width)
        stat = stat + jnp.sum(hidden[:, cols].astype(F32) * block, 1, keepdims=True)
        if step < NEAR:
            rs_send[0, step] = block.astype(BF)
            links.send(
                rs_send.at[0, step], rs_recv.at[0, step], {"narrow": owner}, mid_slots[step]
            )
        else:
            own_mid = block
    lane_at = lax.broadcasted_iota(jnp.int32, (slots, 128), 1)
    columns = jnp.where(lane_at == 0, share, jnp.where(lane_at == 1, stat, 0.0))
    high = columns.astype(BF)
    rest = (columns - high.astype(F32)).astype(BF)
    pick = jnp.where(
        lax.broadcasted_iota(jnp.int32, (8, 128), 0) == lax.broadcasted_iota(jnp.int32, (8, 128), 1),
        1.0, 0.0,
    ).astype(BF)
    extra = rows_rows(pick, high) + rows_rows(pick, rest)
    ext_send[...] = extra
    ext_slots = [links.slot() for _ in range(NEAR)]
    for step in range(NEAR):
        links.send(ext_send, ext_recv.at[step], {"narrow": to_z[step]}, ext_slots[step])
    acts_there = [to_mate(item.at[core], item) for item in (act_cat, gate_cat, up_cat)]

    activated = act_cat[core]
    exp_slots = [links.slot() for _ in range(NEAR)]
    for step in range(NEAR + 1):
        owner = to_z[step] if step < NEAR else n
        rows = pl.ds(pl.multiple_of(owner * part_width, part_width), part_width)
        block = rows_rows(activated, weights[2, rows, :])
        if step < NEAR:
            rs_send[1, step] = block.astype(BF)
            links.send(
                rs_send.at[1, step], rs_recv.at[1, step], {"narrow": owner}, exp_slots[step]
            )
        else:
            own_exp = block

    hidden_there()
    graded_there()
    for there in acts_there:
        there()
    pairs = ((hidden_cat, gate_cat), (hidden_cat, up_cat), (graded_cat, act_cat))
    for kind, (left, right) in enumerate(pairs):
        left_rows = left[...].reshape(2 * slots, full // 2)
        for start, size in tiles:
            cols = slice(start, start + size)
            right_rows = right[:, :, cols].reshape(2 * slots, size)
            weights[kind, 0 : full // 2, cols] = cols_cols(left_rows, right_rows).astype(BF)
        links.move(weights.at[kind, pl.ds(0, full // 2), :], grads_out.at[kind])

    for step in range(NEAR):
        links.land(ext_recv.at[step], {"narrow": from_z[step]}, ext_slots[step])
        extra = extra + ext_recv[step]
    high = extra.astype(BF)
    rest = (extra - high.astype(F32)).astype(BF)
    place = lax.broadcasted_iota(jnp.int32, (8, 128), 0) * 2
    lanes = lax.broadcasted_iota(jnp.int32, (8, 128), 1)
    spread_high = jnp.where(place == lanes, 1.0, 0.0).astype(BF)
    spread_low = jnp.where(place + 1 == lanes, 1.0, 0.0).astype(BF)
    columns = mm(high, spread_high, ((0,), (0,))) + mm(rest, spread_low, ((0,), (0,)))
    extra_out[...] = jnp.where(lane_at == 4, 1.0, columns).astype(BF)
    for which, target in ((0, back_mid_out), (1, back_exp_out)):
        block = own_mid if which == 0 else own_exp
        for step in range(NEAR):
            links.land(
                rs_recv.at[which, step], {"narrow": from_z[step]},
                (mid_slots, exp_slots)[which][step],
            )
            block = block + rs_recv[which, step].astype(F32)
        target[...] = block.astype(BF)
    links.finish()


def mid_call(slot_mid, slot_grad, slot_gate, token_parts, expert_w):
    slots, full = slot_mid.shape
    part_width = full // 4
    rows_each, hidden_width = expert_w.shape[3:]
    vmem = pl.BlockSpec(memory_space=pltpu.VMEM)
    hbm = pl.BlockSpec(memory_space=pl.ANY)

    def arr(shape, dtype):
        return jax.ShapeDtypeStruct(shape, dtype)

    return pl.pallas_call(
        mid_body,
        out_shape=(
            arr((slots, part_width), BF),
            arr((slots, part_width), BF),
            arr((slots, 128), BF),
            arr((3, full // 2, hidden_width), BF),
        ),
        in_specs=[vmem] * 4 + [hbm],
        out_specs=(vmem, vmem, vmem, hbm),
        scratch_shapes=[
            pltpu.VMEM((3, full, hidden_width), BF),
            pltpu.VMEM((slots, full), BF),
            pltpu.VMEM((slots, full), BF),
            pltpu.VMEM((2, slots, full // 2), BF),
            pltpu.VMEM((2, slots, full // 2), BF),
            pltpu.VMEM((2, slots, hidden_width), BF),
            pltpu.VMEM((2, slots, hidden_width), BF),
            pltpu.VMEM((2, slots, hidden_width), BF),
            pltpu.VMEM((2, NEAR, slots, part_width), BF),
            pltpu.VMEM((2, NEAR, slots, part_width), BF),
            pltpu.VMEM((8, slots), F32),
            pltpu.VMEM((NEAR, 8, slots), F32),
            pltpu.SemaphoreType.DMA((MID_SLOTS,)),
            pltpu.SemaphoreType.DMA((MID_SLOTS,)),
            pltpu.SemaphoreType.DMA((32,)),
        ],
        compiler_params=pltpu.CompilerParams(
            collective_id=1, has_side_effects=True, vmem_limit_bytes=62 * 1024 * 1024
        ),
        cost_estimate=pl.CostEstimate(
            flops=30_000_000_000, bytes_accessed=40_000_000, transcendentals=800_000
        ),
        name="mid",
    )(slot_mid, slot_grad, slot_gate, token_parts, expert_w)


TAIL_SLOTS = 72


def tail_body(
    mid_ref, exp_ref, ext_ref, moved_ref, picks_ref, stat_ref, cols_ref, middle_ref, cot_ref,
    tok_ref, tokens_ref, qkv_ref, prob_ref, att_ref, rope_ref, hidden_ref, qkvw_ref, outw_ref,
    output_out, grad_tokens_out, grad_q_out, grad_k_out, grad_v_out, grad_o_out, small_out,
    router_out, expert_out,
    qkvw, outw, ret_mid, ret_exp, ret_ext, branch, hidden_cat, branch_cat, att_cat, proj_cat,
    proj_send, proj_recv, first_send, first_recv, col_send, col_recv, small_mate, small_sum,
    small_recv, last_mate, last_sum, last_recv, sent, landed, local,
):
    n = lax.axis_index("narrow")
    w = lax.axis_index("wide")
    chip, core = w // 2, lax.rem(w, 2)
    to_z, from_z = places_of(n)
    plane = plane_of(chip)
    links = Links(sent, landed, local)
    mate = {"wide": 2 * chip + 1 - core}
    token_count, part_width = tok_ref.shape
    full = 4 * part_width
    rows_each = full // 8
    heads = part_width // HEAD_DIM
    half = full // 2

    def at_plane(peer):
        return {"wide": 2 * peer + core}

    def cap_rows(array, owner):
        return array.at[pl.ds(pl.multiple_of(owner * CAP, 16), CAP), :]

    loads = [links.move(qkvw_ref, qkvw), links.move(outw_ref, outw)]
    links.waits = []
    greet(to_z, plane, chip, core, True)

    back_slots = []
    for source, target in ((mid_ref, ret_mid), (ext_ref, ret_ext), (exp_ref, ret_exp)):
        slots = [links.slot() for _ in range(NEAR)]
        for step in range(NEAR):
            links.send(
                cap_rows(source, plane[step]), cap_rows(target, chip), at_plane(plane[step]),
                slots[step],
            )
        own = links.move(cap_rows(source, chip), cap_rows(target, chip))
        links.waits.pop()
        back_slots.append((target, slots, own))

    def returned(which):
        target, slots, own = back_slots[which]
        for step in range(NEAR):
            links.land(cap_rows(target, plane[step]), at_plane(plane[step]), slots[step])
        own.wait()
        return target[...]

    expert_slots = {}
    for kind in (2, 0, 1):
        expert_slots[kind] = [links.slot() for _ in range(NEAR)]
        for step in range(NEAR):
            block = pl.ds(pl.multiple_of(plane[step] * rows_each, rows_each), rows_each)
            links.send(
                moved_ref.at[kind, block, :], expert_out.at[kind, chip], at_plane(plane[step]),
                expert_slots[kind][step],
            )
        block = pl.ds(pl.multiple_of(chip * rows_each, rows_each), rows_each)
        links.move(moved_ref.at[kind, block, :], expert_out.at[kind, chip])

    def to_mate(source, target):
        slot = links.slot()
        links.send(source, target.at[core], mate, slot)
        return lambda: links.land(target.at[1 - core], mate, slot)

    def parity_exchange(source, target):
        lands = []
        for c in range(4):
            cols = pl.ds(c * rows_each, rows_each)
            theirs = pl.ds(pl.multiple_of((2 * c + 1 - core) * rows_each, rows_each), rows_each)
            ours = pl.ds(pl.multiple_of((2 * c + core) * rows_each, rows_each), rows_each)
            slot = links.slot()
            links.send(source.at[:, theirs], target.at[core, :, cols], mate, slot)
            target[core, :, c * rows_each : (c + 1) * rows_each] = source[:, ours]
            lands.append((target.at[1 - core, :, cols], slot))
        return lambda: [links.land(block, mate, slot) for block, slot in lands]

    hidden_there = parity_exchange(hidden_ref, hidden_cat)
    att_cat[core] = att_ref[...]
    att_there = to_mate(att_ref, att_cat)

    stat = jnp.concatenate([stat_ref[...], jnp.zeros((120, token_count), F32)], 0).T
    lane_at = lax.broadcasted_iota(jnp.int32, (token_count, 128), 1)
    scale_second = lax.rsqrt(stat[:, 4:5] * (1.0 / full) + NORM_EPS)
    logits = stat * scale_second
    hot_first = lane_at == cols_ref[:, 3:4]
    hot_second = lane_at == cols_ref[:, 4:5]
    logit_first = jnp.sum(jnp.where(hot_first, logits, 0.0), 1, keepdims=True)
    logit_second = jnp.sum(jnp.where(hot_second, logits, 0.0), 1, keepdims=True)
    apart = logit_first - logit_second
    share_first = 1.0 / (1.0 + jnp.exp(-apart))
    share_second = 1.0 / (1.0 + jnp.exp(apart))
    normed = middle_ref[...] * scale_second
    gain_second = tokens_ref[n, token_count + 1 : token_count + 2, :].astype(F32)
    hidden_second = (normed * gain_second).astype(BF)
    for load in loads:
        load.wait()
    router = qkvw[pl.ds(2 * n, 2), :, 1536:1664].reshape(part_width, 128)

    rows_mid = returned(0)
    rows_ext = returned(1)
    ext_first = cols_cols(picks_ref[0], rows_ext)
    ext_second = cols_cols(picks_ref[1], rows_ext)
    ext_both = ext_first + ext_second
    grad_share = ext_first[:, 0:1] + ext_first[:, 1:2] - ext_second[:, 0:1] - ext_second[:, 1:2]
    delta = (grad_share * share_first * share_second).astype(BF).astype(F32)
    grad_logits = jnp.where(hot_first, delta, jnp.where(hot_second, -delta, 0.0)).astype(BF)
    stat_total = ext_both[:, 2:3] + ext_both[:, 3:4] + delta * apart
    grad_hidden = cols_cols(picks_ref[0] + picks_ref[1], rows_mid) + rows_rows(grad_logits, router)
    grad_middle = cot_ref[...].astype(F32) + scale_second * (
        gain_second * grad_hidden - normed * (stat_total * (1.0 / full))
    )
    own_cols = pl.ds(pl.multiple_of(n * part_width, part_width), part_width)
    branch[:, own_cols] = grad_middle.astype(BF)
    branch_slots = [links.slot() for _ in range(NEAR)]
    for step in range(NEAR):
        links.send(
            branch.at[:, own_cols], branch.at[:, own_cols], {"narrow": to_z[step]},
            branch_slots[step],
        )

    router_part = cols_cols(grad_logits, hidden_second)[0:8, :]
    gain_part = jnp.sum(grad_hidden * normed, 0, keepdims=True)
    kind_at = lax.broadcasted_iota(jnp.int32, (8, part_width), 0)
    small = jnp.where(kind_at == 4, gain_part, router_part)
    small_mate[core] = small
    small_there = to_mate(small_mate.at[core], small_mate)

    rows_exp = returned(2)
    output_out[...] = (
        middle_ref[...]
        + share_first * cols_cols(picks_ref[0], rows_exp)
        + share_second * cols_cols(picks_ref[1], rows_exp)
    ).astype(BF)

    small_there()
    small = small_mate[0] + small_mate[1]
    small_sum[...] = small
    small_slots = [links.slot() for _ in range(NEAR)]
    for step in range(NEAR):
        links.send(small_sum, small_recv.at[step], at_plane(plane[step]), small_slots[step])

    for step in range(NEAR):
        cols = pl.ds(pl.multiple_of(from_z[step] * part_width, part_width), part_width)
        links.land(branch.at[:, cols], {"narrow": from_z[step]}, branch_slots[step])
    branch_there = parity_exchange(branch, branch_cat)
    grad_att = low_dot(branch[...], outw[...].reshape(full, part_width)).astype(BF)
    cosines, sines = rope_ref[0], rope_ref[1]
    score_scale = HEAD_DIM ** (-0.5)
    stat_first = jnp.zeros((token_count, 1), F32)
    for head in range(heads):
        cols = slice(head * HEAD_DIM, (head + 1) * HEAD_DIM)
        query, key, value = (qkv_ref[i, :, cols] for i in range(3))
        grad_out = grad_att[:, cols]
        weights = prob_ref[head]
        grad_weights = rows_rows(grad_out, value)
        inner = jnp.sum(weights * grad_weights, 1, keepdims=True)
        grad_scores = (weights * (grad_weights - inner)).astype(BF)
        grad_query = low_dot(grad_scores, key) * score_scale
        grad_key = cols_cols(grad_scores, query) * score_scale
        grad_value = cols_cols(weights.astype(BF), grad_out)
        products = (
            grad_query * query.astype(F32)
            + grad_key * key.astype(F32)
            + grad_value * value.astype(F32)
        )
        stat_first = stat_first + jnp.sum(products, 1, keepdims=True)
        for part, grad in ((0, grad_query), (1, grad_key)):
            turned = grad * cosines - pltpu.roll(grad, HEAD_DIM // 2, 1) * sines
            proj_cat[core, :, part * 512 + head * 128 : part * 512 + (head + 1) * 128] = (
                turned.astype(BF)
            )
        proj_cat[core, :, 1024 + head * 128 : 1024 + (head + 1) * 128] = grad_value.astype(BF)
    proj_there = to_mate(proj_cat.at[core], proj_cat)
    high = stat_first.astype(BF)
    rest = (stat_first - high.astype(F32)).astype(BF)
    col_send[...] = jnp.where(
        lane_at == 0, high.astype(F32), jnp.where(lane_at == 1, rest.astype(F32), 0.0)
    ).astype(BF)
    col_slots = [links.slot() for _ in range(NEAR)]
    for step in range(NEAR):
        links.send(col_send, col_recv.at[step], {"narrow": to_z[step]}, col_slots[step])
    grads = proj_cat[core]

    def first_block(m):
        weight = qkvw[pl.ds(2 * m, 2), :, 0:1536].reshape(part_width, 1536)
        return rows_rows(grads, weight)

    first_slots = [links.slot() for _ in range(NEAR)]
    for step in range(NEAR):
        first_send[step] = first_block(to_z[step]).astype(BF)
        links.send(
            first_send.at[step], first_recv.at[step], {"narrow": to_z[step]}, first_slots[step]
        )

    branch_there()
    att_there()
    proj_send[:, 1536:2048] = cols_cols(
        branch_cat[...].reshape(2 * token_count, half), att_cat[...].reshape(2 * token_count, part_width)
    ).astype(BF)
    hidden_there()
    proj_there()
    hidden_rows = hidden_cat[...].reshape(2 * token_count, half)
    for part in range(3):
        cols = slice(part * 512, (part + 1) * 512)
        proj_send[:, cols] = cols_cols(
            hidden_rows, proj_cat[:, :, cols].reshape(2 * token_count, part_width)
        ).astype(BF)

    def proj_rows(owner):
        return pl.ds(pl.multiple_of(owner * rows_each, rows_each), rows_each)

    proj_slots = [links.slot() for _ in range(NEAR)]
    for step in range(NEAR):
        links.send(
            proj_send.at[proj_rows(plane[step]), :], proj_recv.at[step], at_plane(plane[step]),
            proj_slots[step],
        )

    grad_first = first_block(n)
    stat_first = high.astype(F32) + rest.astype(F32)
    total = jnp.zeros((token_count, 1), F32)
    for m in range(4):
        part = tokens_ref[m, 0:token_count, :].astype(F32)
        total = total + jnp.sum(part * part, 1, keepdims=True)
    scale_first = lax.rsqrt(total * (1.0 / full) + NORM_EPS)
    normed_first = tok_ref[...].astype(F32) * scale_first
    gain_first = tokens_ref[n, token_count : token_count + 1, :].astype(F32)
    for step in range(NEAR):
        links.land(col_recv.at[step], {"narrow": from_z[step]}, col_slots[step])
        stat_first = stat_first + (
            col_recv[step, :, 0:1].astype(F32) + col_recv[step, :, 1:2].astype(F32)
        )
    for step in range(NEAR):
        links.land(first_recv.at[step], {"narrow": from_z[step]}, first_slots[step])
        grad_first = grad_first + first_recv[step].astype(F32)
    grad_tokens_out[...] = grad_middle + scale_first * (
        gain_first * grad_first - normed_first * (stat_first * (1.0 / full))
    )
    gain_part = jnp.sum(grad_first * normed_first, 0, keepdims=True)
    last_mate[core] = jnp.broadcast_to(gain_part, (8, part_width))
    last_there = to_mate(last_mate.at[core], last_mate)

    for step in range(NEAR):
        links.land(small_recv.at[step], at_plane(plane[step]), small_slots[step])
        small = small + small_recv[step]
    last_there()
    last = last_mate[0] + last_mate[1]
    last_sum[...] = last
    last_slots = [links.slot() for _ in range(NEAR)]
    for step in range(NEAR):
        links.send(last_sum, last_recv.at[step], at_plane(plane[step]), last_slots[step])
    router_out[:, own_cols] = small
    router_slots = [links.slot() for _ in range(NEAR)]
    for step in range(NEAR):
        links.send(
            router_out.at[:, own_cols], router_out.at[:, own_cols], {"narrow": to_z[step]},
            router_slots[step],
        )
    for step in range(NEAR):
        links.land(last_recv.at[step], at_plane(plane[step]), last_slots[step])
        last = last + last_recv[step]
    small_out[...] = jnp.where(kind_at == 5, last, small)
    for step in range(NEAR):
        cols = pl.ds(pl.multiple_of(from_z[step] * part_width, part_width), part_width)
        links.land(router_out.at[:, cols], {"narrow": from_z[step]}, router_slots[step])

    summed = proj_send[proj_rows(chip), :].astype(F32)
    for step in range(NEAR):
        links.land(proj_recv.at[step], at_plane(plane[step]), proj_slots[step])
        summed = summed + proj_recv[step].astype(F32)
    for part, target in enumerate((grad_q_out, grad_k_out, grad_v_out, grad_o_out)):
        target[...] = summed[:, part * 512 : (part + 1) * 512]
    for kind in (2, 0, 1):
        for step in range(NEAR):
            links.land(
                expert_out.at[kind, plane[step]], at_plane(plane[step]), expert_slots[kind][step]
            )
    links.finish()


def tail_call(*args):
    slots, part_width = args[0].shape
    half, hidden_width = args[3].shape[1:]
    token_count = args[9].shape[0]
    full, rows_each = 2 * half, half // 4
    vmem = pl.BlockSpec(memory_space=pltpu.VMEM)
    hbm = pl.BlockSpec(memory_space=pl.ANY)

    def arr(shape, dtype):
        return jax.ShapeDtypeStruct(shape, dtype)

    own = (token_count, part_width)
    return pl.pallas_call(
        tail_body,
        out_shape=(
            arr(own, BF),
            arr(own, F32),
            arr((rows_each, part_width), F32),
            arr((rows_each, part_width), F32),
            arr((rows_each, part_width), F32),
            arr((rows_each, part_width), F32),
            arr((8, part_width), F32),
            arr((8, full), F32),
            arr((3, 4, rows_each, hidden_width), BF),
        ),
        in_specs=[vmem] * 3 + [hbm] + [vmem] * 12 + [hbm] * 2,
        out_specs=(vmem,) * 8 + (hbm,),
        scratch_shapes=[
            pltpu.VMEM((8, rows_each, 1664), BF),
            pltpu.VMEM((8, rows_each, part_width), BF),
            pltpu.VMEM((slots, part_width), BF),
            pltpu.VMEM((slots, part_width), BF),
            pltpu.VMEM((slots, 128), BF),
            pltpu.VMEM((token_count, full), BF),
            pltpu.VMEM((2, token_count, half), BF),
            pltpu.VMEM((2, token_count, half), BF),
            pltpu.VMEM((2, token_count, part_width), BF),
            pltpu.VMEM((2, token_count, 1536), BF),
            pltpu.VMEM((half, full), BF),
            pltpu.VMEM((NEAR, rows_each, full), BF),
            pltpu.VMEM((NEAR,) + own, BF),
            pltpu.VMEM((NEAR,) + own, BF),
            pltpu.VMEM((token_count, 128), BF),
            pltpu.VMEM((NEAR, token_count, 128), BF),
            pltpu.VMEM((2, 8, part_width), F32),
            pltpu.VMEM((8, part_width), F32),
            pltpu.VMEM((NEAR, 8, part_width), F32),
            pltpu.VMEM((2, 8, part_width), F32),
            pltpu.VMEM((8, part_width), F32),
            pltpu.VMEM((NEAR, 8, part_width), F32),
            pltpu.SemaphoreType.DMA((TAIL_SLOTS,)),
            pltpu.SemaphoreType.DMA((TAIL_SLOTS,)),
            pltpu.SemaphoreType.DMA((16,)),
        ],
        compiler_params=pltpu.CompilerParams(
            collective_id=2, has_side_effects=True, vmem_limit_bytes=60 * 1024 * 1024
        ),
        cost_estimate=pl.CostEstimate(
            flops=6_000_000_000, bytes_accessed=60_000_000, transcendentals=1_000
        ),
        name="tail",
    )(*args)


def plain_device(
    tokens, gain_attn, w_query, w_key, w_value, w_out, gain_ffn, w_router,
    w_gate, w_up, w_down, segment, parents, expert_ids, slot_order, cotangent,
):
    narrow_count = lax.axis_size("narrow")
    wide_count = lax.axis_size("wide")
    narrow_at = lax.axis_index("narrow")
    token_count, part_width = tokens.shape
    full_width = part_width * narrow_count
    hidden_width = w_gate.shape[2]
    rows_each = w_gate.shape[0]
    blocks = wide_count // 8
    quads = [
        [8 * block + 2 * chip + core for chip in range(4)]
        for block in range(blocks)
        for core in range(2)
    ]
    mates = [
        [8 * block + 2 * chip + core for block in range(blocks) for core in range(2)]
        for chip in range(4)
    ]

    def quad_swap(array):
        return lax.all_to_all(array, "wide", 0, 0, axis_index_groups=quads, tiled=True)

    def own_rows(weight):
        moved = quad_swap(jnp.transpose(weight, (1, 0, 2)))
        joined = lax.all_gather(moved, "wide", axis=0, axis_index_groups=mates, tiled=True)
        joined = joined.reshape(blocks, 2, 4, rows_each, hidden_width).transpose(0, 2, 1, 3, 4)
        return joined.reshape(full_width, hidden_width)

    def share_rows(grad):
        parts = grad.astype(BF).reshape(blocks, 4, 2, rows_each, hidden_width)
        parts = parts.transpose(0, 2, 1, 3, 4).reshape(blocks * 2, 4, rows_each, hidden_width)
        summed = lax.psum_scatter(
            parts, "wide", scatter_dimension=0, axis_index_groups=mates, tiled=True
        )[0]
        return jnp.transpose(quad_swap(summed), (1, 0, 2)).astype(F32)

    def head_cols(array, head):
        return array[:, head * HEAD_DIM : (head + 1) * HEAD_DIM]

    heads = part_width // HEAD_DIM
    half_dim = HEAD_DIM // 2
    freqs = ROPE_BASE ** (-2.0 * jnp.arange(half_dim, dtype=F32) / HEAD_DIM)
    score_scale = HEAD_DIM ** (-0.5)
    gains = jnp.stack([gain_attn, gain_ffn])
    gain_first_loc = gain_attn.astype(F32)
    gain_second_loc = gain_ffn.astype(F32)
    hot_first, hot_second, kept, pick_first, pick_second = route(expert_ids, slot_order[0])

    gate_w, up_w, down_w = own_rows(w_gate), own_rows(w_up), own_rows(w_down)
    attn_w = lax.all_gather(
        jnp.stack([w_query, w_key, w_value, w_out], 1), "wide", axis=0, tiled=True
    )
    query_w, key_w, value_w, out_w = (attn_w[:, i] for i in range(4))
    router_w = lax.all_gather(w_router, "wide", axis=0, tiled=True)
    tokens_full = lax.all_gather(tokens, "narrow", axis=1, tiled=True)
    grad_full = lax.all_gather(cotangent, "narrow", axis=1, tiled=True)
    gains_full = lax.all_gather(gains, "narrow", axis=1, tiled=True)
    gain_first = gains_full[0].astype(F32)
    gain_second = gains_full[1].astype(F32)

    seen, places = tree_layout(segment[0], parents[0])
    pick_first_low = pick_first.astype(BF)
    pick_second_low = pick_second.astype(BF)
    pick_both_low = (pick_first | pick_second).astype(BF)

    inputs_full = tokens_full.astype(F32)
    scale_first = lax.rsqrt(jnp.mean(inputs_full * inputs_full, -1, keepdims=True) + NORM_EPS)
    normed_first = inputs_full * scale_first
    hidden_first = (normed_first * gain_first).astype(BF)
    angles = places[:, None] * freqs[None, :]
    cosines, sines = jnp.cos(angles), jnp.sin(angles)
    query_raw = rows_cols(hidden_first, query_w)
    key_raw = rows_cols(hidden_first, key_w)
    value_low = rows_cols(hidden_first, value_w).astype(BF)

    saved = []
    outs = []
    for head in range(heads):
        query = rotate(head_cols(query_raw, head), cosines, sines).astype(BF)
        key = rotate(head_cols(key_raw, head), cosines, sines).astype(BF)
        value = head_cols(value_low, head)
        scores = jnp.where(seen, rows_rows(query, key) * score_scale, NEG_FILL)
        exps = jnp.exp(scores - jnp.max(scores, -1, keepdims=True))
        weights = exps / jnp.sum(exps, -1, keepdims=True)
        saved.append((query, key, value, weights))
        outs.append(rows_cols(weights.astype(BF), value).astype(BF))
    attended = jnp.concatenate(outs, 1)
    branch_part = rows_rows(attended, out_w).astype(BF)
    branch_loc = lax.psum_scatter(
        branch_part, "narrow", scatter_dimension=1, tiled=True
    ).astype(F32)
    middle = tokens.astype(F32) + branch_loc
    middle_full = lax.all_gather(middle.astype(BF), "narrow", axis=1, tiled=True).astype(F32)
    scale_second = lax.rsqrt(jnp.mean(middle_full * middle_full, -1, keepdims=True) + NORM_EPS)
    normed_second = middle_full * scale_second
    hidden_second = (normed_second * gain_second).astype(BF)
    logits = rows_cols(hidden_second, router_w)
    share_first, share_second = gate_pair(logits, hot_first, hot_second)
    weight_first = kept[:, 0] * share_first
    weight_second = kept[:, 1] * share_second

    slot_weight = jnp.sum(
        pick_first * weight_first[:, None] + pick_second * weight_second[:, None], 0
    )
    weight_high, weight_low = two_parts(slot_weight)
    pads = jnp.stack([weight_high, weight_low], 1)
    pads = jnp.pad(pads, ((0, 0), (0, 126)))
    sent_hidden = cols_cols(pick_both_low, hidden_second).astype(BF)
    sent_grad = cols_cols(pick_both_low, grad_full).astype(BF)
    sent = jnp.concatenate([sent_hidden, sent_grad, pads], 1)
    got = quad_swap(sent.reshape(EXPERTS, CAP, -1)).reshape(SLOTS, -1)
    slot_hidden = got[:, :full_width]
    slot_grad = got[:, full_width : 2 * full_width]
    slot_gate = got[:, 2 * full_width : 2 * full_width + 2].astype(F32)
    slot_gate = slot_gate[:, 0:1] + slot_gate[:, 1:2]

    gate_pre = rows_cols(slot_hidden, gate_w)
    up_pre = rows_cols(slot_hidden, up_w)
    sigmoid_gate = jax.nn.sigmoid(gate_pre)
    silu_gate = gate_pre * sigmoid_gate
    activated = (silu_gate * up_pre).astype(BF)
    expert_part = rows_rows(activated, down_w)
    act_raw = rows_cols(slot_grad, down_w)
    share_part = jnp.sum(act_raw * activated.astype(F32), 1, keepdims=True)
    grad_act = act_raw * slot_gate
    grad_gate_pre = (
        grad_act * up_pre * sigmoid_gate * (1.0 + gate_pre * (1.0 - sigmoid_gate))
    ).astype(BF)
    grad_up_pre = (grad_act * silu_gate).astype(BF)
    grad_slot = rows_rows(grad_gate_pre, gate_w) + rows_rows(grad_up_pre, up_w)
    stat_part = jnp.sum(slot_hidden.astype(F32) * grad_slot, 1, keepdims=True)
    extras = jnp.concatenate([*two_parts(share_part), *two_parts(stat_part)], 1)
    extras = jnp.pad(extras, ((0, 0), (0, 124)))
    back_parts = []
    expert_plain = expert_part.astype(BF)
    slot_plain = grad_slot.astype(BF)
    for part in range(narrow_count):
        cols = slice(part * part_width, (part + 1) * part_width)
        back_parts += [expert_plain[:, cols], slot_plain[:, cols], extras]
    back = lax.psum_scatter(
        jnp.concatenate(back_parts, 1), "narrow", scatter_dimension=1, tiled=True
    )
    back = quad_swap(back.reshape(EXPERTS, CAP, -1)).reshape(SLOTS, -1)
    picked_first = rows_cols(pick_first_low, back)
    picked_second = rows_cols(pick_second_low, back)
    output = (
        middle
        + weight_first[:, None] * picked_first[:, :part_width]
        + weight_second[:, None] * picked_second[:, :part_width]
    ).astype(BF)

    grad_weight = (slot_grad.astype(F32) * slot_gate).astype(BF)
    gate_out = share_rows(cols_cols(slot_hidden, grad_gate_pre))
    up_out = share_rows(cols_cols(slot_hidden, grad_up_pre))
    down_out = share_rows(cols_cols(grad_weight, activated))

    tail = 2 * part_width
    share_first_grad = picked_first[:, tail] + picked_first[:, tail + 1]
    share_second_grad = picked_second[:, tail] + picked_second[:, tail + 1]
    both = picked_first + picked_second
    stat_second = both[:, tail + 2] + both[:, tail + 3]
    grad_hidden_loc = both[:, part_width:tail]
    grad_local = cotangent.astype(F32)
    _, pull_gates = jax.vjp(lambda given: gate_pair(given, hot_first, hot_second), logits)
    (grad_logits,) = pull_gates((kept[:, 0] * share_first_grad, kept[:, 1] * share_second_grad))
    grad_logits_low = grad_logits.astype(BF)
    grad_router_rows = rows_rows(grad_logits_low, router_w)
    stat_total = stat_second + jnp.sum(normed_second * gain_second * grad_router_rows, 1)

    def take_cols(full_rows):
        return lax.dynamic_slice_in_dim(full_rows, narrow_at * part_width, part_width, 1)

    grad_hidden_loc = grad_hidden_loc + take_cols(grad_router_rows)
    normed_second_loc = take_cols(normed_second)
    grad_gain_second = jnp.sum(grad_hidden_loc * normed_second_loc, 0)
    grad_middle = grad_local + scale_second * (
        gain_second_loc * grad_hidden_loc - normed_second_loc * stat_total[:, None] / full_width
    )
    grad_router_w = cols_cols(hidden_second, grad_logits_low)
    grad_branch = lax.all_gather(grad_middle.astype(BF), "narrow", axis=1, tiled=True)
    grad_attended = rows_cols(grad_branch, out_w).astype(BF)
    grad_out_w = cols_cols(grad_branch, attended)
    grad_qs, grad_ks, grad_vs = [], [], []
    for head in range(heads):
        query, key, value, weights = saved[head]
        grad_out = head_cols(grad_attended, head)
        grad_weights = rows_rows(grad_out, value)
        inner = jnp.sum(weights * grad_weights, -1, keepdims=True)
        grad_scores = (weights * (grad_weights - inner)).astype(BF)
        grad_q = rows_cols(grad_scores, key) * score_scale
        grad_k = cols_cols(grad_scores, query) * score_scale
        grad_qs.append(rotate(grad_q, cosines, -sines).astype(BF))
        grad_ks.append(rotate(grad_k, cosines, -sines).astype(BF))
        grad_vs.append(cols_cols(weights.astype(BF), grad_out).astype(BF))
    grad_query_raw = jnp.concatenate(grad_qs, 1)
    grad_key_raw = jnp.concatenate(grad_ks, 1)
    grad_value_raw = jnp.concatenate(grad_vs, 1)
    grad_hidden_first = (
        rows_rows(grad_query_raw, query_w)
        + rows_rows(grad_key_raw, key_w)
        + rows_rows(grad_value_raw, value_w)
    )
    stat_first = jnp.sum(normed_first * gain_first * grad_hidden_first, 1, keepdims=True)
    extras = jnp.pad(jnp.concatenate(two_parts(stat_first), 1), ((0, 0), (0, 126)))
    grad_hidden_low = grad_hidden_first.astype(BF)
    first_parts = []
    for part in range(narrow_count):
        first_parts += [grad_hidden_low[:, part * part_width : (part + 1) * part_width], extras]
    first_back = lax.psum_scatter(
        jnp.concatenate(first_parts, 1), "narrow", scatter_dimension=1, tiled=True
    ).astype(F32)
    grad_first_loc = first_back[:, :part_width]
    stat_first = first_back[:, part_width : part_width + 1]
    stat_first = stat_first + first_back[:, part_width + 1 : part_width + 2]
    normed_first_loc = take_cols(normed_first)
    grad_gain_first = jnp.sum(grad_first_loc * normed_first_loc, 0)
    grad_tokens = grad_middle + scale_first * (
        gain_first_loc * grad_first_loc - normed_first_loc * stat_first / full_width
    )
    grad_attn_w = jnp.concatenate(
        [
            cols_cols(hidden_first, grad_query_raw).astype(BF),
            cols_cols(hidden_first, grad_key_raw).astype(BF),
            cols_cols(hidden_first, grad_value_raw).astype(BF),
            grad_out_w.astype(BF),
        ],
        1,
    )
    attn_summed = lax.psum_scatter(
        grad_attn_w, "wide", scatter_dimension=0, tiled=True
    ).astype(F32)
    router_summed = lax.psum_scatter(grad_router_w, "wide", scatter_dimension=0, tiled=True)
    gains_summed = lax.psum(jnp.stack([grad_gain_first, grad_gain_second]), "wide")
    return (
        output,
        grad_tokens,
        gains_summed[0],
        attn_summed[:, :part_width],
        attn_summed[:, part_width : 2 * part_width],
        attn_summed[:, 2 * part_width : 3 * part_width],
        attn_summed[:, 3 * part_width :],
        gains_summed[1],
        router_summed,
        gate_out,
        up_out,
        down_out,
    )


def per_device(
    tokens, gain_attn, w_query, w_key, w_value, w_out, gain_ffn, w_router,
    w_gate, w_up, w_down, segment, parents, expert_ids, slot_order, cotangent,
):
    if lax.axis_size("wide") != 8 or lax.axis_size("narrow") != 4:
        return plain_device(
            tokens, gain_attn, w_query, w_key, w_value, w_out, gain_ffn, w_router,
            w_gate, w_up, w_down, segment, parents, expert_ids, slot_order, cotangent,
        )
    rows_each = w_router.shape[0]
    freqs = ROPE_BASE ** (-2.0 * jnp.arange(HEAD_DIM // 2, dtype=F32) / HEAD_DIM)
    seg = segment[0]
    seg_ids = jnp.arange(SEGS, dtype=jnp.int32)
    above = jnp.sum(jnp.where(seg[:, None] == seg_ids[None, :], parents[0][None, :], 0), 1)
    table = jnp.stack(
        [seg, above, slot_order[0], expert_ids[:, 0], expert_ids[:, 1], seg, seg, seg]
    )
    moved = jnp.stack([jnp.transpose(item, (1, 0, 2)) for item in (w_gate, w_up, w_down)])
    (
        in_w, out_w, expert_w, slot_mid, slot_grad, slot_gate, middle, hidden_first,
        token_parts, qkv, probs, attended, stat, rope, picks,
    ) = front_call(
        tokens, cotangent, jnp.stack([gain_attn, gain_ffn]), (w_query, w_key, w_value, w_out),
        jnp.pad(w_router, ((0, 0), (0, 128 - EXPERTS))), moved, table, table.T,
        jnp.tile(freqs, 2)[None, :],
    )
    back_mid, back_exp, back_ext, grads = mid_call(
        slot_mid, slot_grad, slot_gate, token_parts, expert_w
    )
    (
        output, grad_tokens, grad_q, grad_k, grad_v, grad_o, small, router, experts,
    ) = tail_call(
        back_mid, back_exp, back_ext, grads, picks, stat, table.T, middle, cotangent, tokens,
        token_parts, qkv, probs, attended, rope, hidden_first, in_w, out_w,
    )
    gate_out, up_out, down_out = (
        jnp.transpose(experts[kind], (1, 0, 2)).astype(F32) for kind in range(3)
    )
    router = lax.dynamic_slice_in_dim(
        router[:EXPERTS], lax.axis_index("wide") * rows_each, rows_each, 1
    ).T
    return (
        output, grad_tokens, small[5], grad_q, grad_k, grad_v, grad_o, small[4], router,
        gate_out, up_out, down_out,
    )


def solution(mesh):
    pair = P("wide", "narrow")
    part = P("narrow")
    rows = P("wide", None)
    cube = P("wide", None, "narrow")
    return jax.shard_map(
        per_device,
        mesh=mesh,
        in_specs=(
            pair, part, pair, pair, pair, pair, part, rows, cube, cube, cube,
            rows, rows, rows, rows, pair,
        ),
        out_specs=(
            pair, pair, part, pair, pair, pair, pair, part, rows, cube, cube, cube,
        ),
        check_vma=False,
    )
```

```python
import jax
import jax.numpy as jnp
from jax import lax
from jax.experimental import pallas as pl
from jax.experimental.pallas import tpu as pltpu
from jax.sharding import PartitionSpec as P

HEAD_DIM = 128
EXPERTS = 4
SEGS = 13
CAP = 144
SLOTS = EXPERTS * CAP
NORM_EPS = 1e-05
NEG_FILL = -1e30
ROPE_BASE = 10000.0
BF = jnp.bfloat16
F32 = jnp.float32


def mm(left, right, dims):
    return lax.dot_general(left, right, (dims, ((), ())), preferred_element_type=F32)


def rows_cols(left, right):
    return mm(left, right, ((1,), (0,)))


def rows_rows(left, right):
    return mm(left, right, ((1,), (1,)))


def cols_cols(left, right):
    return mm(left, right, ((0,), (0,)))


def tree_layout(segment_row, parent_row):
    seg_ids = jnp.arange(SEGS, dtype=jnp.int32)
    member = segment_row[:, None] == seg_ids[None, :]
    parent_of = (parent_row[:, None] == seg_ids[None, :]) & (seg_ids[:, None] != 0)
    itself = seg_ids[:, None] == seg_ids[None, :]
    reach = itself
    for _ in range(3):
        reach = itself | jnp.any(parent_of[:, :, None] & reach[None, :, :], axis=1)
    counts = member.astype(jnp.int32)
    lengths = jnp.sum(counts, 0)
    starts = jnp.sum(jnp.where(seg_ids[None, :] < seg_ids[:, None], lengths[None, :], 0), 1)
    before = jnp.sum(jnp.where(reach, lengths[None, :], 0), 1) - lengths
    row_at = jnp.arange(segment_row.shape[0], dtype=jnp.int32)
    places = jnp.sum(counts * (before - starts)[None, :], 1) + row_at
    member_low = member.astype(BF)
    lineage = rows_cols(member_low, reach.astype(BF)).astype(BF)
    shared = rows_rows(lineage, member_low) > 0.5
    seen = shared & (row_at[None, :] <= row_at[:, None])
    return seen, places.astype(F32)


def route(expert_row, slot_rank):
    expert_range = jnp.arange(EXPERTS, dtype=jnp.int32)
    hot_first = (expert_row[:, 0:1] == expert_range[None, :]).astype(F32)
    hot_second = (expert_row[:, 1:2] == expert_range[None, :]).astype(F32)
    earlier = (slot_rank[None, :] < slot_rank[:, None]).astype(BF)
    count_first = rows_cols(earlier, hot_first.astype(BF))
    count_second = rows_cols(earlier, hot_second.astype(BF))
    ahead_first = jnp.sum(count_first * hot_first, 1)
    ahead_second = jnp.sum((count_second + jnp.sum(hot_first, 0)[None, :]) * hot_second, 1)
    slot_index = jnp.stack([ahead_first, ahead_second], 1).astype(jnp.int32)
    kept = slot_index < CAP
    flat_slot = jnp.where(kept, expert_row * CAP + slot_index, SLOTS)
    slot_range = jnp.arange(SLOTS, dtype=jnp.int32)
    pick_first = flat_slot[:, 0:1] == slot_range[None, :]
    pick_second = flat_slot[:, 1:2] == slot_range[None, :]
    return hot_first, hot_second, kept.astype(F32), pick_first, pick_second


def rotate(vectors, cosines, sines):
    half_dim = HEAD_DIM // 2
    first_half = vectors[..., :half_dim]
    second_half = vectors[..., half_dim:]
    return jnp.concatenate(
        [
            first_half * cosines - second_half * sines,
            second_half * cosines + first_half * sines,
        ],
        -1,
    )


def gate_pair(logits, hot_first, hot_second):
    chances = jax.nn.softmax(logits, axis=-1)
    first_share = jnp.sum(chances * hot_first, 1)
    second_share = jnp.sum(chances * hot_second, 1)
    pair_total = first_share + second_share
    return (first_share / pair_total, second_share / pair_total)


def two_parts(column):
    high = column.astype(BF)
    return high, (column - high.astype(F32)).astype(BF)


MESH = pl.DeviceIdType.MESH
NEAR = 3


def low_dot(left, right):
    return jnp.dot(left, right, preferred_element_type=F32)


def places_of(n):
    return [lax.rem(n + step, 4) for step in (1, 2, 3)], [lax.rem(n + 4 - step, 4) for step in (1, 2, 3)]


def plane_of(chip):
    x, y = lax.rem(chip, 2), chip // 2
    return [2 * y + 1 - x, 2 * (1 - y) + x, 2 * (1 - y) + 1 - x]


def greet(narrow_peers, plane_peers, chip, core, mate):
    barrier = pltpu.get_barrier_semaphore()
    count = 0
    for peer in narrow_peers:
        pl.semaphore_signal(barrier, inc=1, device_id={"narrow": peer}, device_id_type=MESH)
        count += 1
    for peer in plane_peers:
        pl.semaphore_signal(
            barrier, inc=1, device_id={"wide": 2 * peer + core}, device_id_type=MESH
        )
        count += 1
    if mate:
        pl.semaphore_signal(
            barrier, inc=1, device_id={"wide": 2 * chip + 1 - core}, device_id_type=MESH
        )
        count += 1
    pl.semaphore_wait(barrier, count)


class Links:
    def __init__(self, sent, landed, local):
        self.sent, self.landed, self.local = sent, landed, local
        self.used, self.local_used = 0, 0
        self.waits = []

    def slot(self):
        self.used += 1
        return self.used - 1

    def send(self, source, target, device, slot, when=None):
        copy = pltpu.make_async_remote_copy(
            src_ref=source,
            dst_ref=target,
            send_sem=self.sent.at[slot],
            recv_sem=self.landed.at[slot],
            device_id=device,
            device_id_type=MESH,
        )
        if when is None:
            copy.start()
        else:
            pl.when(when)(copy.start)
        self.waits.append((copy, when))

    def land(self, target, device, slot, when=None):
        copy = pltpu.make_async_remote_copy(
            src_ref=target,
            dst_ref=target,
            send_sem=self.sent.at[slot],
            recv_sem=self.landed.at[slot],
            device_id=device,
            device_id_type=MESH,
        )
        if when is None:
            copy.wait_recv()
        else:
            pl.when(when)(copy.wait_recv)

    def move(self, source, target):
        copy = pltpu.make_async_copy(source, target, self.local.at[self.local_used])
        self.local_used += 1
        copy.start()
        self.waits.append((copy, "local"))
        return copy

    def finish(self):
        for copy, when in self.waits:
            if when == "local":
                copy.wait()
            elif when is None:
                copy.wait_send()
            else:
                pl.when(when)(copy.wait_send)


class Chain:
    def __init__(self, links, n, block):
        self.links, self.n, self.block = links, n, block
        self.slots = [(links.slot(), links.slot()) for _ in range(3)]

    def start(self, step):
        n, links = self.n, self.links
        right, left = self.slots[step]
        block = self.block(lax.rem(n + 4 - step, 4))
        links.send(
            block, block, {"narrow": lax.rem(n + 1, 4)}, right,
            (n < 3) & (n >= step),
        )
        block = self.block(lax.rem(n + step, 4))
        links.send(
            block, block, {"narrow": lax.rem(n + 3, 4)}, left,
            (n > 0) & (n + step <= 3),
        )

    def land(self, step):
        n, links = self.n, self.links
        right, left = self.slots[step]
        links.land(
            self.block(lax.rem(n + 7 - step, 4)), {"narrow": lax.rem(n + 3, 4)}, right,
            n >= step + 1,
        )
        links.land(
            self.block(lax.rem(n + 1 + step, 4)), {"narrow": lax.rem(n + 1, 4)}, left,
            n + 1 + step <= 3,
        )


FRONT_SLOTS = 72


def front_body(
    tok_ref, cot_ref, gains_ref, wq_ref, wk_ref, wv_ref, wo_ref, router_ref, moved_ref,
    rows_ref, cols_ref, freq_ref,
    qkvw_out, outw_out, expert_out, x_out, dy_out, gate_out, middle_out, hidden_out,
    tokens_out, qkv_out, prob_out, att_out, stat_out, rope_out, pick_out,
    pack, tok_pack, qkvw, outw, cot_send, y_send, br_send, br_recv, stat_send, stat_recv,
    gate_send, sent, landed, local,
):
    n = lax.axis_index("narrow")
    w = lax.axis_index("wide")
    chip, core = w // 2, lax.rem(w, 2)
    to_z, from_z = places_of(n)
    plane = plane_of(chip)
    links = Links(sent, landed, local)
    mate = {"wide": 2 * chip + 1 - core}

    def at_plane(peer):
        return {"wide": 2 * peer + core}

    token_count, part_width = tok_ref.shape
    greet(to_z, plane, chip, core, True)

    tok_pack[0:token_count, :] = tok_ref[...]
    tok_pack[token_count : token_count + 2, :] = gains_ref[...]
    tok_slots = [links.slot() for _ in range(NEAR)]
    for step in range(NEAR):
        links.send(tok_pack, tokens_out.at[n], {"narrow": to_z[step]}, tok_slots[step])
    wide_shape = (token_count, token_count)
    row_at = lax.broadcasted_iota(jnp.int32, wide_shape, 0)
    col_at = lax.broadcasted_iota(jnp.int32, wide_shape, 1)
    seg_row, rank_row = rows_ref[0:1, :], rows_ref[2:3, :]
    seg_col, par_col, rank_col = cols_ref[:, 0:1], cols_ref[:, 1:2], cols_ref[:, 2:3]
    seen = ((seg_row == seg_col) | (seg_row == par_col) | (seg_row == 0)) & (col_at <= row_at)
    spots = jnp.sum(jnp.where(seen, 1.0, 0.0), 1, keepdims=True) - 1.0
    angles = spots * freq_ref[...]
    cosines = jnp.cos(angles)
    lane_at = lax.broadcasted_iota(jnp.int32, angles.shape, 1)
    sines = jnp.sin(angles) * jnp.where(lane_at < HEAD_DIM // 2, -1.0, 1.0)
    rope_out[0] = cosines
    rope_out[1] = sines
    kind = lax.broadcasted_iota(jnp.int32, (8, token_count), 0)
    first_row, second_row = rows_ref[3:4, :], rows_ref[4:5, :]
    hot_first = jnp.where(kind == first_row, 1.0, 0.0)
    hot_second = jnp.where(kind == second_row, 1.0, 0.0)
    earlier = jnp.where(rank_col < rank_row, 1.0, 0.0).astype(BF)
    count_first = low_dot(hot_first.astype(BF), earlier)
    count_second = low_dot(hot_second.astype(BF), earlier)
    count_second = count_second + jnp.sum(hot_first, 1, keepdims=True)
    slot_first = jnp.sum(count_first * hot_first, 0, keepdims=True)
    slot_second = jnp.sum(count_second * hot_second, 0, keepdims=True)
    kept_first = jnp.where(slot_first < CAP, 1.0, 0.0)
    kept_second = jnp.where(slot_second < CAP, 1.0, 0.0)
    flat_first = jnp.where(slot_first < CAP, first_row * CAP + slot_first.astype(jnp.int32), SLOTS)
    flat_second = jnp.where(
        slot_second < CAP, second_row * CAP + slot_second.astype(jnp.int32), SLOTS
    )
    slot_at = lax.broadcasted_iota(jnp.int32, (SLOTS, token_count), 0)
    pick_first = jnp.where(slot_at == flat_first, 1.0, 0.0)
    pick_second = jnp.where(slot_at == flat_second, 1.0, 0.0)
    pick_out[0] = pick_first.astype(BF)
    pick_out[1] = pick_second.astype(BF)
    pick_both = (pick_first + pick_second).astype(BF)

    def column_block(array):
        return lambda m: array.at[:, pl.ds(pl.multiple_of(m * part_width, part_width), part_width)]

    def slot_block(array, owner):
        return array.at[
            pl.ds(pl.multiple_of(owner * CAP, 16), CAP),
            pl.ds(pl.multiple_of(n * part_width, part_width), part_width),
        ]

    def dispatch(rows, buffer, array):
        slots = [links.slot() for _ in range(NEAR)]
        buffer[...] = low_dot(pick_both, rows).astype(BF)
        for step in range(NEAR):
            links.send(
                buffer.at[pl.ds(pl.multiple_of(plane[step] * CAP, 16), CAP), :],
                slot_block(array, chip), at_plane(plane[step]), slots[step],
            )
        own = links.move(
            buffer.at[pl.ds(pl.multiple_of(chip * CAP, 16), CAP), :], slot_block(array, chip)
        )
        return slots, own

    def arrive(array, state):
        slots, own = state
        for step in range(NEAR):
            links.land(slot_block(array, plane[step]), at_plane(plane[step]), slots[step])
        own.wait()
        links.waits = [item for item in links.waits if item[0] is not own]

    dy_state = dispatch(cot_ref[...], cot_send, dy_out)
    dy_chain = Chain(links, n, column_block(dy_out))

    pack[:, 0:512] = wq_ref[...]
    pack[:, 512:1024] = wk_ref[...]
    pack[:, 1024:1536] = wv_ref[...]
    pack[:, 1536:1664] = router_ref[...]
    in_slots = [links.slot() for _ in range(NEAR)]
    for step in range(NEAR):
        links.send(pack, qkvw.at[w], at_plane(plane[step]), in_slots[step])
    in_mate = [links.slot() for _ in range(4)]
    links.send(pack, qkvw.at[w], mate, in_mate[3])
    out_slots = [links.slot() for _ in range(NEAR)]
    for step in range(NEAR):
        links.send(wo_ref, outw.at[w], at_plane(plane[step]), out_slots[step])
    out_mate = [links.slot() for _ in range(4)]
    links.send(wo_ref, outw.at[w], mate, out_mate[3])
    tokens_out[n] = tok_pack[...]
    qkvw[w] = pack[...]
    outw[w] = wo_ref[...]

    for step in range(NEAR):
        links.land(tokens_out.at[from_z[step]], {"narrow": from_z[step]}, tok_slots[step])
    total = jnp.zeros((token_count, 1), F32)
    for m in range(4):
        part = tokens_out[m, 0:token_count, :].astype(F32)
        total = total + jnp.sum(part * part, 1, keepdims=True)
    scale_first = lax.rsqrt(total * (1.0 / (4 * part_width)) + NORM_EPS)
    for m in range(4):
        part = tokens_out[m, 0:token_count, :].astype(F32)
        gain = tokens_out[m, token_count : token_count + 1, :].astype(F32)
        hidden_out[:, m * part_width : (m + 1) * part_width] = (part * scale_first * gain).astype(BF)

    arrive(dy_out, dy_state)
    dy_chain.start(0)

    for step in range(NEAR):
        owner = 2 * plane[step] + core
        links.land(qkvw.at[owner], at_plane(plane[step]), in_slots[step])
        links.send(qkvw.at[owner], qkvw.at[owner], mate, in_mate[step])
    for step in range(NEAR):
        links.land(qkvw.at[2 * plane[step] + 1 - core], mate, in_mate[step])
    links.land(qkvw.at[2 * chip + 1 - core], mate, in_mate[3])
    saved_in = links.move(qkvw, qkvw_out)

    expert_slots = [[links.slot() for _ in range(NEAR)] for _ in range(3)]
    expert_mate = [[links.slot() for _ in range(4)] for _ in range(3)]
    for kind_at in range(3):
        for step in range(NEAR):
            links.send(
                moved_ref.at[kind_at, plane[step]], expert_out.at[kind_at, chip, core],
                at_plane(plane[step]), expert_slots[kind_at][step],
            )
        links.send(
            moved_ref.at[kind_at, chip], expert_out.at[kind_at, chip, core], mate,
            expert_mate[kind_at][3],
        )
        links.move(moved_ref.at[kind_at, chip], expert_out.at[kind_at, chip, core])

    def pass_on(kind_at):
        for step in range(NEAR):
            block = expert_out.at[kind_at, plane[step], core]
            links.land(block, at_plane(plane[step]), expert_slots[kind_at][step])
            links.send(block, block, mate, expert_mate[kind_at][step])

    def all_there(kind_at):
        for step in range(NEAR):
            links.land(
                expert_out.at[kind_at, plane[step], 1 - core], mate, expert_mate[kind_at][step]
            )
        links.land(expert_out.at[kind_at, chip, 1 - core], mate, expert_mate[kind_at][3])

    dy_chain.land(0)
    dy_chain.start(1)

    hidden = hidden_out[...]
    score_scale = HEAD_DIM ** (-0.5)
    raws = []
    for part in range(3):
        weight = qkvw[:, :, part * 512 : (part + 1) * 512].reshape(4 * part_width, part_width)
        raws.append(low_dot(hidden, weight))
    for head in range(part_width // HEAD_DIM):
        cols = slice(head * HEAD_DIM, (head + 1) * HEAD_DIM)
        turned = []
        for part in range(2):
            raw = raws[part][:, cols]
            turned.append(
                (raw * cosines + pltpu.roll(raw, HEAD_DIM // 2, 1) * sines).astype(BF)
            )
            qkv_out[part, :, cols] = turned[part]
        value = raws[2][:, cols].astype(BF)
        qkv_out[2, :, cols] = value
        scores = rows_rows(turned[0], turned[1]) * score_scale
        scores = jnp.where(seen, scores, NEG_FILL)
        exps = jnp.exp(scores - jnp.max(scores, 1, keepdims=True))
        weights = exps / jnp.sum(exps, 1, keepdims=True)
        prob_out[head] = weights
        att_out[:, cols] = low_dot(weights.astype(BF), value).astype(BF)

    dy_chain.land(1)
    dy_chain.start(2)

    for step in range(NEAR):
        owner = 2 * plane[step] + core
        links.land(outw.at[owner], at_plane(plane[step]), out_slots[step])
        links.send(outw.at[owner], outw.at[owner], mate, out_mate[step])
    for step in range(NEAR):
        links.land(outw.at[2 * plane[step] + 1 - core], mate, out_mate[step])
    links.land(outw.at[2 * chip + 1 - core], mate, out_mate[3])
    links.move(outw, outw_out)

    attended = att_out[...]

    def branch(m):
        weight = outw[pl.ds(2 * m, 2)].reshape(part_width, part_width)
        return rows_rows(attended, weight)

    br_slots = [links.slot() for _ in range(NEAR)]
    for step in range(NEAR):
        br_send[step] = branch(to_z[step]).astype(BF)
        links.send(br_send.at[step], br_recv.at[step], {"narrow": to_z[step]}, br_slots[step])
    middle = tok_ref[...].astype(F32) + branch(n)
    for step in range(NEAR):
        links.land(br_recv.at[step], {"narrow": from_z[step]}, br_slots[step])
        middle = middle + br_recv[step].astype(F32)
    middle_out[...] = middle
    x_state = dispatch(middle.astype(BF), y_send, x_out)
    x_chain = Chain(links, n, column_block(x_out))

    gain_second = gains_ref[1:2, :].astype(F32)
    router = qkvw[pl.ds(2 * n, 2), :, 1536:1664].reshape(part_width, 128)
    logit_part = mm(router, (middle * gain_second).astype(BF), ((0,), (1,)))[0:8, :]
    square = middle * middle
    square_high = square.astype(BF)
    square_low = (square - square_high.astype(F32)).astype(BF)
    ones = jnp.ones((8, part_width), BF)
    square_sum = rows_rows(ones, square_high) + rows_rows(ones, square_low)
    stat = jnp.where(kind == 4, square_sum, logit_part)
    stat_send[...] = stat
    stat_slots = [links.slot() for _ in range(NEAR)]
    for step in range(NEAR):
        links.send(stat_send, stat_recv.at[step], {"narrow": to_z[step]}, stat_slots[step])

    arrive(x_out, x_state)
    x_chain.start(0)
    for step in range(NEAR):
        links.land(stat_recv.at[step], {"narrow": from_z[step]}, stat_slots[step])
        stat = stat + stat_recv[step]
    stat_out[...] = stat
    scale_row = lax.rsqrt(stat[4:5, :] * (1.0 / (4 * part_width)) + NORM_EPS)
    logits = jnp.where(kind < EXPERTS, stat * scale_row, NEG_FILL)
    chances = jnp.exp(logits - jnp.max(logits, 0, keepdims=True))
    chances = chances / jnp.sum(chances, 0, keepdims=True)
    share_first = jnp.sum(chances * hot_first, 0, keepdims=True)
    share_second = jnp.sum(chances * hot_second, 0, keepdims=True)
    both = share_first + share_second
    weighted = pick_first * (share_first / both) + pick_second * (share_second / both)
    slot_gate = jnp.sum(weighted, 1, keepdims=True)
    gate_send[...] = jnp.broadcast_to(slot_gate, (SLOTS, 128))

    def gate_rows(array, owner):
        return array.at[pl.ds(pl.multiple_of(owner * CAP, 16), CAP), :]

    gate_slots = [links.slot() for _ in range(NEAR)]
    for step in range(NEAR):
        links.send(
            gate_rows(gate_send, plane[step]), gate_rows(gate_out, chip),
            at_plane(plane[step]), gate_slots[step],
        )
    links.move(gate_rows(gate_send, chip), gate_rows(gate_out, chip))

    pass_on(0)
    x_chain.land(0)
    x_chain.start(1)
    x_chain.land(1)
    x_chain.start(2)
    pass_on(1)
    x_chain.land(2)
    dy_chain.land(2)
    for step in range(NEAR):
        links.land(gate_rows(gate_out, plane[step]), at_plane(plane[step]), gate_slots[step])
    pass_on(2)
    for kind_at in range(3):
        all_there(kind_at)
    links.finish()


def front_call(tokens, cotangent, gains, weights, router, moved, rows, cols, freqs):
    token_count, part_width = tokens.shape
    full = 4 * part_width
    hidden_width = moved.shape[3]
    rows_each = moved.shape[2]
    heads = part_width // HEAD_DIM
    vmem = pl.BlockSpec(memory_space=pltpu.VMEM)
    hbm = pl.BlockSpec(memory_space=pl.ANY)

    def arr(shape, dtype):
        return jax.ShapeDtypeStruct(shape, dtype)

    return pl.pallas_call(
        front_body,
        out_shape=(
            arr((8, rows_each, 1664), BF),
            arr((8, rows_each, part_width), BF),
            arr((3, 4, 2, rows_each, hidden_width), BF),
            arr((SLOTS, full), BF),
            arr((SLOTS, full), BF),
            arr((SLOTS, 128), F32),
            arr((token_count, part_width), F32),
            arr((token_count, full), BF),
            arr((4, token_count + 16, part_width), BF),
            arr((3, token_count, part_width), BF),
            arr((heads, token_count, token_count), F32),
            arr((token_count, part_width), BF),
            arr((8, token_count), F32),
            arr((2, token_count, HEAD_DIM), F32),
            arr((2, SLOTS, token_count), BF),
        ),
        in_specs=[vmem] * 8 + [hbm] + [vmem] * 3,
        out_specs=(hbm, hbm, hbm) + (vmem,) * 12,
        scratch_shapes=[
            pltpu.VMEM((rows_each, 1664), BF),
            pltpu.VMEM((token_count + 16, part_width), BF),
            pltpu.VMEM((8, rows_each, 1664), BF),
            pltpu.VMEM((8, rows_each, part_width), BF),
            pltpu.VMEM((SLOTS, part_width), BF),
            pltpu.VMEM((SLOTS, part_width), BF),
            pltpu.VMEM((NEAR, token_count, part_width), BF),
            pltpu.VMEM((NEAR, token_count, part_width), BF),
            pltpu.VMEM((8, token_count), F32),
            pltpu.VMEM((NEAR, 8, token_count), F32),
            pltpu.VMEM((SLOTS, 128), F32),
            pltpu.SemaphoreType.DMA((FRONT_SLOTS,)),
            pltpu.SemaphoreType.DMA((FRONT_SLOTS,)),
            pltpu.SemaphoreType.DMA((16,)),
        ],
        compiler_params=pltpu.CompilerParams(
            collective_id=0, has_side_effects=True, vmem_limit_bytes=60 * 1024 * 1024
        ),
        cost_estimate=pl.CostEstimate(
            flops=6_000_000_000, bytes_accessed=60_000_000, transcendentals=400_000
        ),
        name="front",
    )(tokens, cotangent, gains, *weights, router, moved, rows, cols, freqs)


MID_SLOTS = 48


def column_tiles(width):
    tiles, start = [], 0
    while start < width:
        size = min(256, width - start)
        tiles.append((start, size))
        start += size
    return tiles


def mid_body(
    x_ref, dy_ref, gate_ref, tokens_ref, w_ref,
    back_mid_out, back_exp_out, extra_out, grads_out, expert_out,
    weights, hidden, graded, hidden_cat, graded_cat, act_cat, gate_cat, up_cat,
    rs_send, rs_recv, ext_send, ext_recv, sent, landed, local,
):
    n = lax.axis_index("narrow")
    w = lax.axis_index("wide")
    chip, core = w // 2, lax.rem(w, 2)
    to_z, from_z = places_of(n)
    plane = plane_of(chip)
    links = Links(sent, landed, local)
    mate = {"wide": 2 * chip + 1 - core}
    slots, full = x_ref.shape
    part_width = full // 4
    rows_each = full // 8
    hidden_width = weights.shape[2]
    tiles = column_tiles(hidden_width)

    loads = [
        [
            links.move(w_ref.at[kind, c, k], weights.at[kind, pl.ds((2 * c + k) * rows_each, rows_each), :])
            for c in range(4)
            for k in range(2)
        ]
        for kind in range(3)
    ]
    links.waits = []
    greet(to_z, plane, chip, core, True)

    total = jnp.zeros((slots, 1), F32)
    for m in range(4):
        part = x_ref[:, m * part_width : (m + 1) * part_width].astype(F32)
        total = total + jnp.sum(part * part, 1, keepdims=True)
    scale = lax.rsqrt(total * (1.0 / full) + NORM_EPS)
    slot_gate = gate_ref[:, 0:1]
    for m in range(4):
        cols = slice(m * part_width, (m + 1) * part_width)
        gain = tokens_ref[m, 257:258, :].astype(F32)
        hidden[:, cols] = (x_ref[:, cols].astype(F32) * scale * gain).astype(BF)
        graded[:, cols] = (dy_ref[:, cols].astype(F32) * slot_gate).astype(BF)

    def to_mate(source, target):
        slot = links.slot()
        links.send(source, target.at[core], mate, slot)
        return lambda: links.land(target.at[1 - core], mate, slot)

    def parity_exchange(source, target):
        lands = []
        for c in range(4):
            cols = pl.ds(c * rows_each, rows_each)
            theirs = pl.ds(pl.multiple_of((2 * c + 1 - core) * rows_each, rows_each), rows_each)
            ours = pl.ds(pl.multiple_of((2 * c + core) * rows_each, rows_each), rows_each)
            slot = links.slot()
            links.send(source.at[:, theirs], target.at[core, :, cols], mate, slot)
            target[core, :, c * rows_each : (c + 1) * rows_each] = source[:, ours]
            lands.append((target.at[1 - core, :, cols], slot))
        return lambda: [links.land(block, mate, slot) for block, slot in lands]

    hidden_there = parity_exchange(hidden, hidden_cat)
    graded_there = parity_exchange(graded, graded_cat)

    for kind in range(3):
        for load in loads[kind]:
            load.wait()
    share = jnp.zeros((slots, 1), F32)
    for start, size in tiles:
        cols = slice(start, start + size)
        gate_pre = low_dot(hidden[...], weights[0, :, cols])
        up_pre = low_dot(hidden[...], weights[1, :, cols])
        act_raw = low_dot(dy_ref[...], weights[2, :, cols])
        sigmoid = 1.0 / (1.0 + jnp.exp(-gate_pre))
        silu = gate_pre * sigmoid
        activated = (silu * up_pre).astype(BF)
        share = share + jnp.sum(act_raw * activated.astype(F32), 1, keepdims=True)
        grad_act = act_raw * slot_gate
        act_cat[core, :, cols] = activated
        gate_cat[core, :, cols] = (
            grad_act * up_pre * (sigmoid * (1.0 + gate_pre * (1.0 - sigmoid)))
        ).astype(BF)
        up_cat[core, :, cols] = (grad_act * silu).astype(BF)

    grad_gate, grad_up = gate_cat[core], up_cat[core]
    stat = jnp.zeros((slots, 1), F32)
    mid_slots = [links.slot() for _ in range(NEAR)]
    for step in range(NEAR + 1):
        owner = to_z[step] if step < NEAR else n
        rows = pl.ds(pl.multiple_of(owner * part_width, part_width), part_width)
        block = rows_rows(grad_gate, weights[0, rows, :]) + rows_rows(grad_up, weights[1, rows, :])
        cols = pl.ds(pl.multiple_of(owner * part_width, part_width), part_width)
        stat = stat + jnp.sum(hidden[:, cols].astype(F32) * block, 1, keepdims=True)
        if step < NEAR:
            rs_send[0, step] = block.astype(BF)
            links.send(
                rs_send.at[0, step], rs_recv.at[0, step], {"narrow": owner}, mid_slots[step]
            )
        else:
            own_mid = block
    lane_at = lax.broadcasted_iota(jnp.int32, (slots, 128), 1)
    columns = jnp.where(lane_at == 0, share, jnp.where(lane_at == 1, stat, 0.0))
    high = columns.astype(BF)
    rest = (columns - high.astype(F32)).astype(BF)
    pick = jnp.where(
        lax.broadcasted_iota(jnp.int32, (8, 128), 0) == lax.broadcasted_iota(jnp.int32, (8, 128), 1),
        1.0, 0.0,
    ).astype(BF)
    extra = rows_rows(pick, high) + rows_rows(pick, rest)
    ext_send[...] = extra
    ext_slots = [links.slot() for _ in range(NEAR)]
    for step in range(NEAR):
        links.send(ext_send, ext_recv.at[step], {"narrow": to_z[step]}, ext_slots[step])
    acts_there = [to_mate(item.at[core], item) for item in (act_cat, gate_cat, up_cat)]

    half = full // 2
    expert_slots = {}

    def weight_grad(left, right, kind, start_row):
        left_rows = left[...].reshape(2 * slots, half)
        for start, size in tiles:
            cols = slice(start, start + size)
            right_rows = right[:, :, cols].reshape(2 * slots, size)
            weights[kind, start_row : start_row + half, cols] = cols_cols(
                left_rows, right_rows
            ).astype(BF)

    def share_out(index, kind, start_row):
        expert_slots[index] = [links.slot() for _ in range(NEAR)]

        def block(owner):
            first = pl.multiple_of(start_row + owner * rows_each, rows_each)
            return weights.at[kind, pl.ds(first, rows_each), :]

        for step in range(NEAR):
            links.send(
                block(plane[step]), expert_out.at[index, chip],
                {"wide": 2 * plane[step] + core}, expert_slots[index][step],
            )
        links.move(block(chip), expert_out.at[index, chip])

    graded_there()
    for there in acts_there[:1]:
        there()
    weight_grad(graded_cat, act_cat, 0, 0)
    share_out(0, 0, 0)
    hidden_there()
    for there in acts_there[1:]:
        there()
    weight_grad(hidden_cat, gate_cat, 0, half)
    share_out(1, 0, half)

    activated = act_cat[core]
    exp_slots = [links.slot() for _ in range(NEAR)]
    for step in range(NEAR + 1):
        owner = to_z[step] if step < NEAR else n
        rows = pl.ds(pl.multiple_of(owner * part_width, part_width), part_width)
        block = rows_rows(activated, weights[2, rows, :])
        if step < NEAR:
            rs_send[1, step] = block.astype(BF)
            links.send(
                rs_send.at[1, step], rs_recv.at[1, step], {"narrow": owner}, exp_slots[step]
            )
        else:
            own_exp = block

    weight_grad(hidden_cat, up_cat, 1, 0)
    links.move(weights.at[1, pl.ds(0, half), :], grads_out)

    for step in range(NEAR):
        links.land(ext_recv.at[step], {"narrow": from_z[step]}, ext_slots[step])
        extra = extra + ext_recv[step]
    high = extra.astype(BF)
    rest = (extra - high.astype(F32)).astype(BF)
    place = lax.broadcasted_iota(jnp.int32, (8, 128), 0) * 2
    lanes = lax.broadcasted_iota(jnp.int32, (8, 128), 1)
    spread_high = jnp.where(place == lanes, 1.0, 0.0).astype(BF)
    spread_low = jnp.where(place + 1 == lanes, 1.0, 0.0).astype(BF)
    columns = mm(high, spread_high, ((0,), (0,))) + mm(rest, spread_low, ((0,), (0,)))
    extra_out[...] = jnp.where(lane_at == 4, 1.0, columns).astype(BF)
    for which, target in ((0, back_mid_out), (1, back_exp_out)):
        block = own_mid if which == 0 else own_exp
        for step in range(NEAR):
            links.land(
                rs_recv.at[which, step], {"narrow": from_z[step]},
                (mid_slots, exp_slots)[which][step],
            )
            block = block + rs_recv[which, step].astype(F32)
        target[...] = block.astype(BF)
    for index in range(2):
        for step in range(NEAR):
            links.land(
                expert_out.at[index, plane[step]], {"wide": 2 * plane[step] + core},
                expert_slots[index][step],
            )
    links.finish()


def mid_call(slot_mid, slot_grad, slot_gate, token_parts, expert_w):
    slots, full = slot_mid.shape
    part_width = full // 4
    rows_each, hidden_width = expert_w.shape[3:]
    vmem = pl.BlockSpec(memory_space=pltpu.VMEM)
    hbm = pl.BlockSpec(memory_space=pl.ANY)

    def arr(shape, dtype):
        return jax.ShapeDtypeStruct(shape, dtype)

    return pl.pallas_call(
        mid_body,
        out_shape=(
            arr((slots, part_width), BF),
            arr((slots, part_width), BF),
            arr((slots, 128), BF),
            arr((full // 2, hidden_width), BF),
            arr((2, 4, rows_each, hidden_width), BF),
        ),
        in_specs=[vmem] * 4 + [hbm],
        out_specs=(vmem, vmem, vmem, hbm, hbm),
        scratch_shapes=[
            pltpu.VMEM((3, full, hidden_width), BF),
            pltpu.VMEM((slots, full), BF),
            pltpu.VMEM((slots, full), BF),
            pltpu.VMEM((2, slots, full // 2), BF),
            pltpu.VMEM((2, slots, full // 2), BF),
            pltpu.VMEM((2, slots, hidden_width), BF),
            pltpu.VMEM((2, slots, hidden_width), BF),
            pltpu.VMEM((2, slots, hidden_width), BF),
            pltpu.VMEM((2, NEAR, slots, part_width), BF),
            pltpu.VMEM((2, NEAR, slots, part_width), BF),
            pltpu.VMEM((8, slots), F32),
            pltpu.VMEM((NEAR, 8, slots), F32),
            pltpu.SemaphoreType.DMA((MID_SLOTS,)),
            pltpu.SemaphoreType.DMA((MID_SLOTS,)),
            pltpu.SemaphoreType.DMA((32,)),
        ],
        compiler_params=pltpu.CompilerParams(
            collective_id=1, has_side_effects=True, vmem_limit_bytes=62 * 1024 * 1024
        ),
        cost_estimate=pl.CostEstimate(
            flops=30_000_000_000, bytes_accessed=40_000_000, transcendentals=800_000
        ),
        name="mid",
    )(slot_mid, slot_grad, slot_gate, token_parts, expert_w)


TAIL_SLOTS = 72


def tail_body(
    mid_ref, exp_ref, ext_ref, moved_ref, picks_ref, stat_ref, cols_ref, middle_ref, cot_ref,
    tok_ref, tokens_ref, qkv_ref, prob_ref, att_ref, rope_ref, hidden_ref, qkvw_ref, outw_ref,
    output_out, grad_tokens_out, grad_q_out, grad_k_out, grad_v_out, grad_o_out, small_out,
    router_out, expert_out,
    qkvw, outw, ret_mid, ret_exp, ret_ext, branch, hidden_cat, branch_cat, att_cat, proj_cat,
    proj_send, proj_recv, first_send, first_recv, col_send, col_recv, small_mate, small_sum,
    small_recv, last_mate, last_sum, last_recv, sent, landed, local,
):
    n = lax.axis_index("narrow")
    w = lax.axis_index("wide")
    chip, core = w // 2, lax.rem(w, 2)
    to_z, from_z = places_of(n)
    plane = plane_of(chip)
    links = Links(sent, landed, local)
    mate = {"wide": 2 * chip + 1 - core}
    token_count, part_width = tok_ref.shape
    full = 4 * part_width
    rows_each = full // 8
    heads = part_width // HEAD_DIM
    half = full // 2

    def at_plane(peer):
        return {"wide": 2 * peer + core}

    def cap_rows(array, owner):
        return array.at[pl.ds(pl.multiple_of(owner * CAP, 16), CAP), :]

    loads = [links.move(qkvw_ref, qkvw), links.move(outw_ref, outw)]
    links.waits = []
    greet(to_z, plane, chip, core, True)

    back_slots = []
    for source, target in ((mid_ref, ret_mid), (ext_ref, ret_ext), (exp_ref, ret_exp)):
        slots = [links.slot() for _ in range(NEAR)]
        for step in range(NEAR):
            links.send(
                cap_rows(source, plane[step]), cap_rows(target, chip), at_plane(plane[step]),
                slots[step],
            )
        own = links.move(cap_rows(source, chip), cap_rows(target, chip))
        links.waits.pop()
        back_slots.append((target, slots, own))

    def returned(which):
        target, slots, own = back_slots[which]
        for step in range(NEAR):
            links.land(cap_rows(target, plane[step]), at_plane(plane[step]), slots[step])
        own.wait()
        return target[...]

    expert_slots = [links.slot() for _ in range(NEAR)]
    for step in range(NEAR):
        block = pl.ds(pl.multiple_of(plane[step] * rows_each, rows_each), rows_each)
        links.send(
            moved_ref.at[block, :], expert_out.at[chip], at_plane(plane[step]), expert_slots[step]
        )
    block = pl.ds(pl.multiple_of(chip * rows_each, rows_each), rows_each)
    links.move(moved_ref.at[block, :], expert_out.at[chip])

    def to_mate(source, target):
        slot = links.slot()
        links.send(source, target.at[core], mate, slot)
        return lambda: links.land(target.at[1 - core], mate, slot)

    def parity_exchange(source, target):
        lands = []
        for c in range(4):
            cols = pl.ds(c * rows_each, rows_each)
            theirs = pl.ds(pl.multiple_of((2 * c + 1 - core) * rows_each, rows_each), rows_each)
            ours = pl.ds(pl.multiple_of((2 * c + core) * rows_each, rows_each), rows_each)
            slot = links.slot()
            links.send(source.at[:, theirs], target.at[core, :, cols], mate, slot)
            target[core, :, c * rows_each : (c + 1) * rows_each] = source[:, ours]
            lands.append((target.at[1 - core, :, cols], slot))
        return lambda: [links.land(block, mate, slot) for block, slot in lands]

    hidden_there = parity_exchange(hidden_ref, hidden_cat)
    att_cat[core] = att_ref[...]
    att_there = to_mate(att_ref, att_cat)

    stat = jnp.concatenate([stat_ref[...], jnp.zeros((120, token_count), F32)], 0).T
    lane_at = lax.broadcasted_iota(jnp.int32, (token_count, 128), 1)
    scale_second = lax.rsqrt(stat[:, 4:5] * (1.0 / full) + NORM_EPS)
    logits = stat * scale_second
    hot_first = lane_at == cols_ref[:, 3:4]
    hot_second = lane_at == cols_ref[:, 4:5]
    logit_first = jnp.sum(jnp.where(hot_first, logits, 0.0), 1, keepdims=True)
    logit_second = jnp.sum(jnp.where(hot_second, logits, 0.0), 1, keepdims=True)
    apart = logit_first - logit_second
    share_first = 1.0 / (1.0 + jnp.exp(-apart))
    share_second = 1.0 / (1.0 + jnp.exp(apart))
    normed = middle_ref[...] * scale_second
    gain_second = tokens_ref[n, token_count + 1 : token_count + 2, :].astype(F32)
    hidden_second = (normed * gain_second).astype(BF)
    for load in loads:
        load.wait()
    router = qkvw[pl.ds(2 * n, 2), :, 1536:1664].reshape(part_width, 128)

    rows_mid = returned(0)
    rows_ext = returned(1)
    ext_first = cols_cols(picks_ref[0], rows_ext)
    ext_second = cols_cols(picks_ref[1], rows_ext)
    ext_both = ext_first + ext_second
    grad_share = ext_first[:, 0:1] + ext_first[:, 1:2] - ext_second[:, 0:1] - ext_second[:, 1:2]
    delta = (grad_share * share_first * share_second).astype(BF).astype(F32)
    grad_logits = jnp.where(hot_first, delta, jnp.where(hot_second, -delta, 0.0)).astype(BF)
    stat_total = ext_both[:, 2:3] + ext_both[:, 3:4] + delta * apart
    grad_hidden = cols_cols(picks_ref[0] + picks_ref[1], rows_mid) + rows_rows(grad_logits, router)
    grad_middle = cot_ref[...].astype(F32) + scale_second * (
        gain_second * grad_hidden - normed * (stat_total * (1.0 / full))
    )
    own_cols = pl.ds(pl.multiple_of(n * part_width, part_width), part_width)
    branch[:, own_cols] = grad_middle.astype(BF)
    branch_slots = [links.slot() for _ in range(NEAR)]
    for step in range(NEAR):
        links.send(
            branch.at[:, own_cols], branch.at[:, own_cols], {"narrow": to_z[step]},
            branch_slots[step],
        )

    router_part = cols_cols(grad_logits, hidden_second)[0:8, :]
    gain_part = jnp.sum(grad_hidden * normed, 0, keepdims=True)
    kind_at = lax.broadcasted_iota(jnp.int32, (8, part_width), 0)
    small = jnp.where(kind_at == 4, gain_part, router_part)
    small_mate[core] = small
    small_there = to_mate(small_mate.at[core], small_mate)

    rows_exp = returned(2)
    output_out[...] = (
        middle_ref[...]
        + share_first * cols_cols(picks_ref[0], rows_exp)
        + share_second * cols_cols(picks_ref[1], rows_exp)
    ).astype(BF)

    small_there()
    small = small_mate[0] + small_mate[1]
    small_sum[...] = small
    small_slots = [links.slot() for _ in range(NEAR)]
    for step in range(NEAR):
        links.send(small_sum, small_recv.at[step], at_plane(plane[step]), small_slots[step])

    for step in range(NEAR):
        cols = pl.ds(pl.multiple_of(from_z[step] * part_width, part_width), part_width)
        links.land(branch.at[:, cols], {"narrow": from_z[step]}, branch_slots[step])
    branch_there = parity_exchange(branch, branch_cat)
    grad_att = low_dot(branch[...], outw[...].reshape(full, part_width)).astype(BF)
    cosines, sines = rope_ref[0], rope_ref[1]
    score_scale = HEAD_DIM ** (-0.5)
    stat_first = jnp.zeros((token_count, 1), F32)
    for head in range(heads):
        cols = slice(head * HEAD_DIM, (head + 1) * HEAD_DIM)
        query, key, value = (qkv_ref[i, :, cols] for i in range(3))
        grad_out = grad_att[:, cols]
        weights = prob_ref[head]
        grad_weights = rows_rows(grad_out, value)
        inner = jnp.sum(weights * grad_weights, 1, keepdims=True)
        grad_scores = (weights * (grad_weights - inner)).astype(BF)
        grad_query = low_dot(grad_scores, key) * score_scale
        grad_key = cols_cols(grad_scores, query) * score_scale
        grad_value = cols_cols(weights.astype(BF), grad_out)
        products = (
            grad_query * query.astype(F32)
            + grad_key * key.astype(F32)
            + grad_value * value.astype(F32)
        )
        stat_first = stat_first + jnp.sum(products, 1, keepdims=True)
        for part, grad in ((0, grad_query), (1, grad_key)):
            turned = grad * cosines - pltpu.roll(grad, HEAD_DIM // 2, 1) * sines
            proj_cat[core, :, part * 512 + head * 128 : part * 512 + (head + 1) * 128] = (
                turned.astype(BF)
            )
        proj_cat[core, :, 1024 + head * 128 : 1024 + (head + 1) * 128] = grad_value.astype(BF)
    proj_there = to_mate(proj_cat.at[core], proj_cat)
    high = stat_first.astype(BF)
    rest = (stat_first - high.astype(F32)).astype(BF)
    col_send[...] = jnp.where(
        lane_at == 0, high.astype(F32), jnp.where(lane_at == 1, rest.astype(F32), 0.0)
    ).astype(BF)
    col_slots = [links.slot() for _ in range(NEAR)]
    for step in range(NEAR):
        links.send(col_send, col_recv.at[step], {"narrow": to_z[step]}, col_slots[step])
    grads = proj_cat[core]

    def first_block(m):
        weight = qkvw[pl.ds(2 * m, 2), :, 0:1536].reshape(part_width, 1536)
        return rows_rows(grads, weight)

    first_slots = [links.slot() for _ in range(NEAR)]
    for step in range(NEAR):
        first_send[step] = first_block(to_z[step]).astype(BF)
        links.send(
            first_send.at[step], first_recv.at[step], {"narrow": to_z[step]}, first_slots[step]
        )

    branch_there()
    att_there()
    proj_send[:, 1536:2048] = cols_cols(
        branch_cat[...].reshape(2 * token_count, half), att_cat[...].reshape(2 * token_count, part_width)
    ).astype(BF)
    hidden_there()
    proj_there()
    hidden_rows = hidden_cat[...].reshape(2 * token_count, half)
    for part in range(3):
        cols = slice(part * 512, (part + 1) * 512)
        proj_send[:, cols] = cols_cols(
            hidden_rows, proj_cat[:, :, cols].reshape(2 * token_count, part_width)
        ).astype(BF)

    def proj_rows(owner):
        return pl.ds(pl.multiple_of(owner * rows_each, rows_each), rows_each)

    proj_slots = [links.slot() for _ in range(NEAR)]
    for step in range(NEAR):
        links.send(
            proj_send.at[proj_rows(plane[step]), :], proj_recv.at[step], at_plane(plane[step]),
            proj_slots[step],
        )

    grad_first = first_block(n)
    stat_first = high.astype(F32) + rest.astype(F32)
    total = jnp.zeros((token_count, 1), F32)
    for m in range(4):
        part = tokens_ref[m, 0:token_count, :].astype(F32)
        total = total + jnp.sum(part * part, 1, keepdims=True)
    scale_first = lax.rsqrt(total * (1.0 / full) + NORM_EPS)
    normed_first = tok_ref[...].astype(F32) * scale_first
    gain_first = tokens_ref[n, token_count : token_count + 1, :].astype(F32)
    for step in range(NEAR):
        links.land(col_recv.at[step], {"narrow": from_z[step]}, col_slots[step])
        stat_first = stat_first + (
            col_recv[step, :, 0:1].astype(F32) + col_recv[step, :, 1:2].astype(F32)
        )
    for step in range(NEAR):
        links.land(first_recv.at[step], {"narrow": from_z[step]}, first_slots[step])
        grad_first = grad_first + first_recv[step].astype(F32)
    grad_tokens_out[...] = grad_middle + scale_first * (
        gain_first * grad_first - normed_first * (stat_first * (1.0 / full))
    )
    gain_part = jnp.sum(grad_first * normed_first, 0, keepdims=True)
    last_mate[core] = jnp.broadcast_to(gain_part, (8, part_width))
    last_there = to_mate(last_mate.at[core], last_mate)

    for step in range(NEAR):
        links.land(small_recv.at[step], at_plane(plane[step]), small_slots[step])
        small = small + small_recv[step]
    last_there()
    last = last_mate[0] + last_mate[1]
    last_sum[...] = last
    last_slots = [links.slot() for _ in range(NEAR)]
    for step in range(NEAR):
        links.send(last_sum, last_recv.at[step], at_plane(plane[step]), last_slots[step])
    router_out[:, own_cols] = small
    router_slots = [links.slot() for _ in range(NEAR)]
    for step in range(NEAR):
        links.send(
            router_out.at[:, own_cols], router_out.at[:, own_cols], {"narrow": to_z[step]},
            router_slots[step],
        )
    for step in range(NEAR):
        links.land(last_recv.at[step], at_plane(plane[step]), last_slots[step])
        last = last + last_recv[step]
    small_out[...] = jnp.where(kind_at == 5, last, small)
    for step in range(NEAR):
        cols = pl.ds(pl.multiple_of(from_z[step] * part_width, part_width), part_width)
        links.land(router_out.at[:, cols], {"narrow": from_z[step]}, router_slots[step])

    summed = proj_send[proj_rows(chip), :].astype(F32)
    for step in range(NEAR):
        links.land(proj_recv.at[step], at_plane(plane[step]), proj_slots[step])
        summed = summed + proj_recv[step].astype(F32)
    for part, target in enumerate((grad_q_out, grad_k_out, grad_v_out, grad_o_out)):
        target[...] = summed[:, part * 512 : (part + 1) * 512]
    for step in range(NEAR):
        links.land(expert_out.at[plane[step]], at_plane(plane[step]), expert_slots[step])
    links.finish()


def tail_call(*args):
    slots, part_width = args[0].shape
    half, hidden_width = args[3].shape
    token_count = args[9].shape[0]
    full, rows_each = 2 * half, half // 4
    vmem = pl.BlockSpec(memory_space=pltpu.VMEM)
    hbm = pl.BlockSpec(memory_space=pl.ANY)

    def arr(shape, dtype):
        return jax.ShapeDtypeStruct(shape, dtype)

    own = (token_count, part_width)
    return pl.pallas_call(
        tail_body,
        out_shape=(
            arr(own, BF),
            arr(own, F32),
            arr((rows_each, part_width), F32),
            arr((rows_each, part_width), F32),
            arr((rows_each, part_width), F32),
            arr((rows_each, part_width), F32),
            arr((8, part_width), F32),
            arr((8, full), F32),
            arr((4, rows_each, hidden_width), BF),
        ),
        in_specs=[vmem] * 3 + [hbm] + [vmem] * 12 + [hbm] * 2,
        out_specs=(vmem,) * 8 + (hbm,),
        scratch_shapes=[
            pltpu.VMEM((8, rows_each, 1664), BF),
            pltpu.VMEM((8, rows_each, part_width), BF),
            pltpu.VMEM((slots, part_width), BF),
            pltpu.VMEM((slots, part_width), BF),
            pltpu.VMEM((slots, 128), BF),
            pltpu.VMEM((token_count, full), BF),
            pltpu.VMEM((2, token_count, half), BF),
            pltpu.VMEM((2, token_count, half), BF),
            pltpu.VMEM((2, token_count, part_width), BF),
            pltpu.VMEM((2, token_count, 1536), BF),
            pltpu.VMEM((half, full), BF),
            pltpu.VMEM((NEAR, rows_each, full), BF),
            pltpu.VMEM((NEAR,) + own, BF),
            pltpu.VMEM((NEAR,) + own, BF),
            pltpu.VMEM((token_count, 128), BF),
            pltpu.VMEM((NEAR, token_count, 128), BF),
            pltpu.VMEM((2, 8, part_width), F32),
            pltpu.VMEM((8, part_width), F32),
            pltpu.VMEM((NEAR, 8, part_width), F32),
            pltpu.VMEM((2, 8, part_width), F32),
            pltpu.VMEM((8, part_width), F32),
            pltpu.VMEM((NEAR, 8, part_width), F32),
            pltpu.SemaphoreType.DMA((TAIL_SLOTS,)),
            pltpu.SemaphoreType.DMA((TAIL_SLOTS,)),
            pltpu.SemaphoreType.DMA((16,)),
        ],
        compiler_params=pltpu.CompilerParams(
            collective_id=2, has_side_effects=True, vmem_limit_bytes=60 * 1024 * 1024
        ),
        cost_estimate=pl.CostEstimate(
            flops=6_000_000_000, bytes_accessed=60_000_000, transcendentals=1_000
        ),
        name="tail",
    )(*args)


def plain_device(
    tokens, gain_attn, w_query, w_key, w_value, w_out, gain_ffn, w_router,
    w_gate, w_up, w_down, segment, parents, expert_ids, slot_order, cotangent,
):
    narrow_count = lax.axis_size("narrow")
    wide_count = lax.axis_size("wide")
    narrow_at = lax.axis_index("narrow")
    token_count, part_width = tokens.shape
    full_width = part_width * narrow_count
    hidden_width = w_gate.shape[2]
    rows_each = w_gate.shape[0]
    blocks = wide_count // 8
    quads = [
        [8 * block + 2 * chip + core for chip in range(4)]
        for block in range(blocks)
        for core in range(2)
    ]
    mates = [
        [8 * block + 2 * chip + core for block in range(blocks) for core in range(2)]
        for chip in range(4)
    ]

    def quad_swap(array):
        return lax.all_to_all(array, "wide", 0, 0, axis_index_groups=quads, tiled=True)

    def own_rows(weight):
        moved = quad_swap(jnp.transpose(weight, (1, 0, 2)))
        joined = lax.all_gather(moved, "wide", axis=0, axis_index_groups=mates, tiled=True)
        joined = joined.reshape(blocks, 2, 4, rows_each, hidden_width).transpose(0, 2, 1, 3, 4)
        return joined.reshape(full_width, hidden_width)

    def share_rows(grad):
        parts = grad.astype(BF).reshape(blocks, 4, 2, rows_each, hidden_width)
        parts = parts.transpose(0, 2, 1, 3, 4).reshape(blocks * 2, 4, rows_each, hidden_width)
        summed = lax.psum_scatter(
            parts, "wide", scatter_dimension=0, axis_index_groups=mates, tiled=True
        )[0]
        return jnp.transpose(quad_swap(summed), (1, 0, 2)).astype(F32)

    def head_cols(array, head):
        return array[:, head * HEAD_DIM : (head + 1) * HEAD_DIM]

    heads = part_width // HEAD_DIM
    half_dim = HEAD_DIM // 2
    freqs = ROPE_BASE ** (-2.0 * jnp.arange(half_dim, dtype=F32) / HEAD_DIM)
    score_scale = HEAD_DIM ** (-0.5)
    gains = jnp.stack([gain_attn, gain_ffn])
    gain_first_loc = gain_attn.astype(F32)
    gain_second_loc = gain_ffn.astype(F32)
    hot_first, hot_second, kept, pick_first, pick_second = route(expert_ids, slot_order[0])

    gate_w, up_w, down_w = own_rows(w_gate), own_rows(w_up), own_rows(w_down)
    attn_w = lax.all_gather(
        jnp.stack([w_query, w_key, w_value, w_out], 1), "wide", axis=0, tiled=True
    )
    query_w, key_w, value_w, out_w = (attn_w[:, i] for i in range(4))
    router_w = lax.all_gather(w_router, "wide", axis=0, tiled=True)
    tokens_full = lax.all_gather(tokens, "narrow", axis=1, tiled=True)
    grad_full = lax.all_gather(cotangent, "narrow", axis=1, tiled=True)
    gains_full = lax.all_gather(gains, "narrow", axis=1, tiled=True)
    gain_first = gains_full[0].astype(F32)
    gain_second = gains_full[1].astype(F32)

    seen, places = tree_layout(segment[0], parents[0])
    pick_first_low = pick_first.astype(BF)
    pick_second_low = pick_second.astype(BF)
    pick_both_low = (pick_first | pick_second).astype(BF)

    inputs_full = tokens_full.astype(F32)
    scale_first = lax.rsqrt(jnp.mean(inputs_full * inputs_full, -1, keepdims=True) + NORM_EPS)
    normed_first = inputs_full * scale_first
    hidden_first = (normed_first * gain_first).astype(BF)
    angles = places[:, None] * freqs[None, :]
    cosines, sines = jnp.cos(angles), jnp.sin(angles)
    query_raw = rows_cols(hidden_first, query_w)
    key_raw = rows_cols(hidden_first, key_w)
    value_low = rows_cols(hidden_first, value_w).astype(BF)

    saved = []
    outs = []
    for head in range(heads):
        query = rotate(head_cols(query_raw, head), cosines, sines).astype(BF)
        key = rotate(head_cols(key_raw, head), cosines, sines).astype(BF)
        value = head_cols(value_low, head)
        scores = jnp.where(seen, rows_rows(query, key) * score_scale, NEG_FILL)
        exps = jnp.exp(scores - jnp.max(scores, -1, keepdims=True))
        weights = exps / jnp.sum(exps, -1, keepdims=True)
        saved.append((query, key, value, weights))
        outs.append(rows_cols(weights.astype(BF), value).astype(BF))
    attended = jnp.concatenate(outs, 1)
    branch_part = rows_rows(attended, out_w).astype(BF)
    branch_loc = lax.psum_scatter(
        branch_part, "narrow", scatter_dimension=1, tiled=True
    ).astype(F32)
    middle = tokens.astype(F32) + branch_loc
    middle_full = lax.all_gather(middle.astype(BF), "narrow", axis=1, tiled=True).astype(F32)
    scale_second = lax.rsqrt(jnp.mean(middle_full * middle_full, -1, keepdims=True) + NORM_EPS)
    normed_second = middle_full * scale_second
    hidden_second = (normed_second * gain_second).astype(BF)
    logits = rows_cols(hidden_second, router_w)
    share_first, share_second = gate_pair(logits, hot_first, hot_second)
    weight_first = kept[:, 0] * share_first
    weight_second = kept[:, 1] * share_second

    slot_weight = jnp.sum(
        pick_first * weight_first[:, None] + pick_second * weight_second[:, None], 0
    )
    weight_high, weight_low = two_parts(slot_weight)
    pads = jnp.stack([weight_high, weight_low], 1)
    pads = jnp.pad(pads, ((0, 0), (0, 126)))
    sent_hidden = cols_cols(pick_both_low, hidden_second).astype(BF)
    sent_grad = cols_cols(pick_both_low, grad_full).astype(BF)
    sent = jnp.concatenate([sent_hidden, sent_grad, pads], 1)
    got = quad_swap(sent.reshape(EXPERTS, CAP, -1)).reshape(SLOTS, -1)
    slot_hidden = got[:, :full_width]
    slot_grad = got[:, full_width : 2 * full_width]
    slot_gate = got[:, 2 * full_width : 2 * full_width + 2].astype(F32)
    slot_gate = slot_gate[:, 0:1] + slot_gate[:, 1:2]

    gate_pre = rows_cols(slot_hidden, gate_w)
    up_pre = rows_cols(slot_hidden, up_w)
    sigmoid_gate = jax.nn.sigmoid(gate_pre)
    silu_gate = gate_pre * sigmoid_gate
    activated = (silu_gate * up_pre).astype(BF)
    expert_part = rows_rows(activated, down_w)
    act_raw = rows_cols(slot_grad, down_w)
    share_part = jnp.sum(act_raw * activated.astype(F32), 1, keepdims=True)
    grad_act = act_raw * slot_gate
    grad_gate_pre = (
        grad_act * up_pre * sigmoid_gate * (1.0 + gate_pre * (1.0 - sigmoid_gate))
    ).astype(BF)
    grad_up_pre = (grad_act * silu_gate).astype(BF)
    grad_slot = rows_rows(grad_gate_pre, gate_w) + rows_rows(grad_up_pre, up_w)
    stat_part = jnp.sum(slot_hidden.astype(F32) * grad_slot, 1, keepdims=True)
    extras = jnp.concatenate([*two_parts(share_part), *two_parts(stat_part)], 1)
    extras = jnp.pad(extras, ((0, 0), (0, 124)))
    back_parts = []
    expert_plain = expert_part.astype(BF)
    slot_plain = grad_slot.astype(BF)
    for part in range(narrow_count):
        cols = slice(part * part_width, (part + 1) * part_width)
        back_parts += [expert_plain[:, cols], slot_plain[:, cols], extras]
    back = lax.psum_scatter(
        jnp.concatenate(back_parts, 1), "narrow", scatter_dimension=1, tiled=True
    )
    back = quad_swap(back.reshape(EXPERTS, CAP, -1)).reshape(SLOTS, -1)
    picked_first = rows_cols(pick_first_low, back)
    picked_second = rows_cols(pick_second_low, back)
    output = (
        middle
        + weight_first[:, None] * picked_first[:, :part_width]
        + weight_second[:, None] * picked_second[:, :part_width]
    ).astype(BF)

    grad_weight = (slot_grad.astype(F32) * slot_gate).astype(BF)
    gate_out = share_rows(cols_cols(slot_hidden, grad_gate_pre))
    up_out = share_rows(cols_cols(slot_hidden, grad_up_pre))
    down_out = share_rows(cols_cols(grad_weight, activated))

    tail = 2 * part_width
    share_first_grad = picked_first[:, tail] + picked_first[:, tail + 1]
    share_second_grad = picked_second[:, tail] + picked_second[:, tail + 1]
    both = picked_first + picked_second
    stat_second = both[:, tail + 2] + both[:, tail + 3]
    grad_hidden_loc = both[:, part_width:tail]
    grad_local = cotangent.astype(F32)
    _, pull_gates = jax.vjp(lambda given: gate_pair(given, hot_first, hot_second), logits)
    (grad_logits,) = pull_gates((kept[:, 0] * share_first_grad, kept[:, 1] * share_second_grad))
    grad_logits_low = grad_logits.astype(BF)
    grad_router_rows = rows_rows(grad_logits_low, router_w)
    stat_total = stat_second + jnp.sum(normed_second * gain_second * grad_router_rows, 1)

    def take_cols(full_rows):
        return lax.dynamic_slice_in_dim(full_rows, narrow_at * part_width, part_width, 1)

    grad_hidden_loc = grad_hidden_loc + take_cols(grad_router_rows)
    normed_second_loc = take_cols(normed_second)
    grad_gain_second = jnp.sum(grad_hidden_loc * normed_second_loc, 0)
    grad_middle = grad_local + scale_second * (
        gain_second_loc * grad_hidden_loc - normed_second_loc * stat_total[:, None] / full_width
    )
    grad_router_w = cols_cols(hidden_second, grad_logits_low)
    grad_branch = lax.all_gather(grad_middle.astype(BF), "narrow", axis=1, tiled=True)
    grad_attended = rows_cols(grad_branch, out_w).astype(BF)
    grad_out_w = cols_cols(grad_branch, attended)
    grad_qs, grad_ks, grad_vs = [], [], []
    for head in range(heads):
        query, key, value, weights = saved[head]
        grad_out = head_cols(grad_attended, head)
        grad_weights = rows_rows(grad_out, value)
        inner = jnp.sum(weights * grad_weights, -1, keepdims=True)
        grad_scores = (weights * (grad_weights - inner)).astype(BF)
        grad_q = rows_cols(grad_scores, key) * score_scale
        grad_k = cols_cols(grad_scores, query) * score_scale
        grad_qs.append(rotate(grad_q, cosines, -sines).astype(BF))
        grad_ks.append(rotate(grad_k, cosines, -sines).astype(BF))
        grad_vs.append(cols_cols(weights.astype(BF), grad_out).astype(BF))
    grad_query_raw = jnp.concatenate(grad_qs, 1)
    grad_key_raw = jnp.concatenate(grad_ks, 1)
    grad_value_raw = jnp.concatenate(grad_vs, 1)
    grad_hidden_first = (
        rows_rows(grad_query_raw, query_w)
        + rows_rows(grad_key_raw, key_w)
        + rows_rows(grad_value_raw, value_w)
    )
    stat_first = jnp.sum(normed_first * gain_first * grad_hidden_first, 1, keepdims=True)
    extras = jnp.pad(jnp.concatenate(two_parts(stat_first), 1), ((0, 0), (0, 126)))
    grad_hidden_low = grad_hidden_first.astype(BF)
    first_parts = []
    for part in range(narrow_count):
        first_parts += [grad_hidden_low[:, part * part_width : (part + 1) * part_width], extras]
    first_back = lax.psum_scatter(
        jnp.concatenate(first_parts, 1), "narrow", scatter_dimension=1, tiled=True
    ).astype(F32)
    grad_first_loc = first_back[:, :part_width]
    stat_first = first_back[:, part_width : part_width + 1]
    stat_first = stat_first + first_back[:, part_width + 1 : part_width + 2]
    normed_first_loc = take_cols(normed_first)
    grad_gain_first = jnp.sum(grad_first_loc * normed_first_loc, 0)
    grad_tokens = grad_middle + scale_first * (
        gain_first_loc * grad_first_loc - normed_first_loc * stat_first / full_width
    )
    grad_attn_w = jnp.concatenate(
        [
            cols_cols(hidden_first, grad_query_raw).astype(BF),
            cols_cols(hidden_first, grad_key_raw).astype(BF),
            cols_cols(hidden_first, grad_value_raw).astype(BF),
            grad_out_w.astype(BF),
        ],
        1,
    )
    attn_summed = lax.psum_scatter(
        grad_attn_w, "wide", scatter_dimension=0, tiled=True
    ).astype(F32)
    router_summed = lax.psum_scatter(grad_router_w, "wide", scatter_dimension=0, tiled=True)
    gains_summed = lax.psum(jnp.stack([grad_gain_first, grad_gain_second]), "wide")
    return (
        output,
        grad_tokens,
        gains_summed[0],
        attn_summed[:, :part_width],
        attn_summed[:, part_width : 2 * part_width],
        attn_summed[:, 2 * part_width : 3 * part_width],
        attn_summed[:, 3 * part_width :],
        gains_summed[1],
        router_summed,
        gate_out,
        up_out,
        down_out,
    )


def per_device(
    tokens, gain_attn, w_query, w_key, w_value, w_out, gain_ffn, w_router,
    w_gate, w_up, w_down, segment, parents, expert_ids, slot_order, cotangent,
):
    if lax.axis_size("wide") != 8 or lax.axis_size("narrow") != 4:
        return plain_device(
            tokens, gain_attn, w_query, w_key, w_value, w_out, gain_ffn, w_router,
            w_gate, w_up, w_down, segment, parents, expert_ids, slot_order, cotangent,
        )
    rows_each = w_router.shape[0]
    freqs = ROPE_BASE ** (-2.0 * jnp.arange(HEAD_DIM // 2, dtype=F32) / HEAD_DIM)
    seg = segment[0]
    seg_ids = jnp.arange(SEGS, dtype=jnp.int32)
    above = jnp.sum(jnp.where(seg[:, None] == seg_ids[None, :], parents[0][None, :], 0), 1)
    table = jnp.stack(
        [seg, above, slot_order[0], expert_ids[:, 0], expert_ids[:, 1], seg, seg, seg]
    )
    moved = jnp.stack([jnp.transpose(item, (1, 0, 2)) for item in (w_gate, w_up, w_down)])
    (
        in_w, out_w, expert_w, slot_mid, slot_grad, slot_gate, middle, hidden_first,
        token_parts, qkv, probs, attended, stat, rope, picks,
    ) = front_call(
        tokens, cotangent, jnp.stack([gain_attn, gain_ffn]), (w_query, w_key, w_value, w_out),
        jnp.pad(w_router, ((0, 0), (0, 128 - EXPERTS))), moved, table, table.T,
        jnp.tile(freqs, 2)[None, :],
    )
    back_mid, back_exp, back_ext, grads, early_experts = mid_call(
        slot_mid, slot_grad, slot_gate, token_parts, expert_w
    )
    (
        output, grad_tokens, grad_q, grad_k, grad_v, grad_o, small, router, experts,
    ) = tail_call(
        back_mid, back_exp, back_ext, grads, picks, stat, table.T, middle, cotangent, tokens,
        token_parts, qkv, probs, attended, rope, hidden_first, in_w, out_w,
    )
    gate_out, up_out, down_out = (
        jnp.transpose(item, (1, 0, 2)).astype(F32)
        for item in (early_experts[1], experts, early_experts[0])
    )
    router = lax.dynamic_slice_in_dim(
        router[:EXPERTS], lax.axis_index("wide") * rows_each, rows_each, 1
    ).T
    return (
        output, grad_tokens, small[5], grad_q, grad_k, grad_v, grad_o, small[4], router,
        gate_out, up_out, down_out,
    )


def solution(mesh):
    pair = P("wide", "narrow")
    part = P("narrow")
    rows = P("wide", None)
    cube = P("wide", None, "narrow")
    return jax.shard_map(
        per_device,
        mesh=mesh,
        in_specs=(
            pair, part, pair, pair, pair, pair, part, rows, cube, cube, cube,
            rows, rows, rows, rows, pair,
        ),
        out_specs=(
            pair, pair, part, pair, pair, pair, pair, part, rows, cube, cube, cube,
        ),
        check_vma=False,
    )
```

```python
import math

import jax
import jax.numpy as jnp
from jax import lax
from jax.experimental import pallas as pl
from jax.experimental.pallas import tpu as pltpu
from jax.sharding import PartitionSpec as P

HEAD_DIM = 128
EXPERTS = 4
SEGS = 13
CAP = 144
SLOTS = EXPERTS * CAP
NORM_EPS = 1e-05
NEG_FILL = -1e30
ROPE_BASE = 10000.0
BF = jnp.bfloat16
F32 = jnp.float32


def mm(left, right, dims):
    return lax.dot_general(left, right, (dims, ((), ())), preferred_element_type=F32)


def rows_cols(left, right):
    return mm(left, right, ((1,), (0,)))


def rows_rows(left, right):
    return mm(left, right, ((1,), (1,)))


def cols_cols(left, right):
    return mm(left, right, ((0,), (0,)))


def tree_layout(segment_row, parent_row):
    seg_ids = jnp.arange(SEGS, dtype=jnp.int32)
    member = segment_row[:, None] == seg_ids[None, :]
    parent_of = (parent_row[:, None] == seg_ids[None, :]) & (seg_ids[:, None] != 0)
    itself = seg_ids[:, None] == seg_ids[None, :]
    reach = itself
    for _ in range(3):
        reach = itself | jnp.any(parent_of[:, :, None] & reach[None, :, :], axis=1)
    counts = member.astype(jnp.int32)
    lengths = jnp.sum(counts, 0)
    starts = jnp.sum(jnp.where(seg_ids[None, :] < seg_ids[:, None], lengths[None, :], 0), 1)
    before = jnp.sum(jnp.where(reach, lengths[None, :], 0), 1) - lengths
    row_at = jnp.arange(segment_row.shape[0], dtype=jnp.int32)
    places = jnp.sum(counts * (before - starts)[None, :], 1) + row_at
    member_low = member.astype(BF)
    lineage = rows_cols(member_low, reach.astype(BF)).astype(BF)
    shared = rows_rows(lineage, member_low) > 0.5
    seen = shared & (row_at[None, :] <= row_at[:, None])
    return seen, places.astype(F32)


def route(expert_row, slot_rank):
    expert_range = jnp.arange(EXPERTS, dtype=jnp.int32)
    hot_first = (expert_row[:, 0:1] == expert_range[None, :]).astype(F32)
    hot_second = (expert_row[:, 1:2] == expert_range[None, :]).astype(F32)
    earlier = (slot_rank[None, :] < slot_rank[:, None]).astype(BF)
    count_first = rows_cols(earlier, hot_first.astype(BF))
    count_second = rows_cols(earlier, hot_second.astype(BF))
    ahead_first = jnp.sum(count_first * hot_first, 1)
    ahead_second = jnp.sum((count_second + jnp.sum(hot_first, 0)[None, :]) * hot_second, 1)
    slot_index = jnp.stack([ahead_first, ahead_second], 1).astype(jnp.int32)
    kept = slot_index < CAP
    flat_slot = jnp.where(kept, expert_row * CAP + slot_index, SLOTS)
    slot_range = jnp.arange(SLOTS, dtype=jnp.int32)
    pick_first = flat_slot[:, 0:1] == slot_range[None, :]
    pick_second = flat_slot[:, 1:2] == slot_range[None, :]
    return hot_first, hot_second, kept.astype(F32), pick_first, pick_second


def rotate(vectors, cosines, sines):
    half_dim = HEAD_DIM // 2
    first_half = vectors[..., :half_dim]
    second_half = vectors[..., half_dim:]
    return jnp.concatenate(
        [
            first_half * cosines - second_half * sines,
            second_half * cosines + first_half * sines,
        ],
        -1,
    )


def gate_pair(logits, hot_first, hot_second):
    chances = jax.nn.softmax(logits, axis=-1)
    first_share = jnp.sum(chances * hot_first, 1)
    second_share = jnp.sum(chances * hot_second, 1)
    pair_total = first_share + second_share
    return (first_share / pair_total, second_share / pair_total)


def two_parts(column):
    high = column.astype(BF)
    return high, (column - high.astype(F32)).astype(BF)


MESH = pl.DeviceIdType.MESH
NEAR = 3


def low_dot(left, right):
    return jnp.dot(left, right, preferred_element_type=F32)


def places_of(n):
    return [lax.rem(n + step, 4) for step in (1, 2, 3)], [lax.rem(n + 4 - step, 4) for step in (1, 2, 3)]


def plane_of(chip):
    x, y = lax.rem(chip, 2), chip // 2
    return [2 * y + 1 - x, 2 * (1 - y) + x, 2 * (1 - y) + 1 - x]


def greet(narrow_peers, plane_peers, chip, core, mate):
    barrier = pltpu.get_barrier_semaphore()
    count = 0
    for peer in narrow_peers:
        pl.semaphore_signal(barrier, inc=1, device_id={"narrow": peer}, device_id_type=MESH)
        count += 1
    for peer in plane_peers:
        pl.semaphore_signal(
            barrier, inc=1, device_id={"wide": 2 * peer + core}, device_id_type=MESH
        )
        count += 1
    if mate:
        pl.semaphore_signal(
            barrier, inc=1, device_id={"wide": 2 * chip + 1 - core}, device_id_type=MESH
        )
        count += 1
    pl.semaphore_wait(barrier, count)


class Links:
    def __init__(self, sent, landed, local):
        self.sent, self.landed, self.local = sent, landed, local
        self.used, self.local_used = 0, 0
        self.waits = []

    def slot(self):
        self.used += 1
        return self.used - 1

    def send(self, source, target, device, slot, when=None):
        copy = pltpu.make_async_remote_copy(
            src_ref=source,
            dst_ref=target,
            send_sem=self.sent.at[slot],
            recv_sem=self.landed.at[slot],
            device_id=device,
            device_id_type=MESH,
        )
        if when is None:
            copy.start()
        else:
            pl.when(when)(copy.start)
        self.waits.append((copy, when))

    def land(self, target, device, slot, when=None):
        copy = pltpu.make_async_remote_copy(
            src_ref=target,
            dst_ref=target,
            send_sem=self.sent.at[slot],
            recv_sem=self.landed.at[slot],
            device_id=device,
            device_id_type=MESH,
        )
        if when is None:
            copy.wait_recv()
        else:
            pl.when(when)(copy.wait_recv)

    def move(self, source, target):
        copy = pltpu.make_async_copy(source, target, self.local.at[self.local_used])
        self.local_used += 1
        copy.start()
        self.waits.append((copy, "local"))
        return copy

    def finish(self):
        for copy, when in self.waits:
            if when == "local":
                copy.wait()
            elif when is None:
                copy.wait_send()
            else:
                pl.when(when)(copy.wait_send)


class Chain:
    def __init__(self, links, n, block):
        self.links, self.n, self.block = links, n, block
        self.slots = [(links.slot(), links.slot()) for _ in range(3)]

    def start(self, step):
        n, links = self.n, self.links
        right, left = self.slots[step]
        block = self.block(lax.rem(n + 4 - step, 4))
        links.send(
            block, block, {"narrow": lax.rem(n + 1, 4)}, right,
            (n < 3) & (n >= step),
        )
        block = self.block(lax.rem(n + step, 4))
        links.send(
            block, block, {"narrow": lax.rem(n + 3, 4)}, left,
            (n > 0) & (n + step <= 3),
        )

    def land(self, step):
        n, links = self.n, self.links
        right, left = self.slots[step]
        links.land(
            self.block(lax.rem(n + 7 - step, 4)), {"narrow": lax.rem(n + 3, 4)}, right,
            n >= step + 1,
        )
        links.land(
            self.block(lax.rem(n + 1 + step, 4)), {"narrow": lax.rem(n + 1, 4)}, left,
            n + 1 + step <= 3,
        )


class LineSum:
    def __init__(self, links, n, outbox, inbox):
        self.links, self.n, self.outbox, self.inbox = links, n, outbox, inbox
        self.inner = (n == 1) | (n == 2)
        self.outer = (n == 0) | (n == 3)
        self.targets = [3 - n, lax.rem(3 * n + 2, 5), lax.rem(2 * n + 1, 5)]
        self.next = 1 + lax.rem(n, 2)
        self.slots = [links.slot() for _ in range(6)]

    def put(self, step, part):
        links, outbox, inbox = self.links, self.outbox, self.inbox
        outbox[step] = part.astype(BF)
        goal = {"narrow": self.next if step == 0 else self.targets[step]}
        far, near = self.slots[2 * step], self.slots[2 * step + 1]
        if step == 0:
            links.send(outbox.at[0], inbox.at[3], goal, far, self.outer)
            links.send(outbox.at[0], inbox.at[0], goal, near, self.inner)
        elif step == 1:
            links.send(outbox.at[1], inbox.at[1], goal, far, self.outer)
            links.send(outbox.at[1], inbox.at[0], goal, near, self.inner)
        else:
            links.send(outbox.at[2], inbox.at[2], goal, far, self.outer)

    def relay(self):
        links, outbox, inbox = self.links, self.outbox, self.inbox
        home = {"narrow": 3 * (self.n // 2)}
        links.land(inbox.at[3], home, self.slots[0], self.inner)

        @pl.when(self.inner)
        def _():
            outbox[2] = (outbox[2].astype(F32) + inbox[3].astype(F32)).astype(BF)

        goal = {"narrow": self.targets[2]}
        links.send(outbox.at[2], inbox.at[1], goal, self.slots[5], self.inner)

    def total(self, own):
        links, inbox = self.links, self.inbox
        outer, inner = self.outer, self.inner
        other = {"narrow": lax.rem(self.n + 1, 4)}
        links.land(inbox.at[0], other, self.slots[1], inner)
        links.land(inbox.at[0], other, self.slots[3], outer)
        links.land(inbox.at[1], other, self.slots[2], inner)
        links.land(inbox.at[1], other, self.slots[5], outer)
        links.land(inbox.at[2], other, self.slots[4], inner)

        @pl.when(outer)
        def _():
            inbox[2] = jnp.zeros(inbox.shape[1:], BF)

        for index in range(3):
            own = own + inbox[index].astype(F32)
        return own


FRONT_SLOTS = 72


def front_body(
    tok_ref, cot_ref, gains_ref, wq_ref, wk_ref, wv_ref, wo_ref, router_ref, gate_ref, up_ref,
    down_ref, segment_ref, parents_ref, ids_ref, rank_ref,
    qkvw_out, outw_out, expert_out, x_out, dy_out, gate_out, middle_out, hidden_out,
    tokens_out, qkv_out, prob_out, att_out, stat_out, rope_out, pick_out, cols_out,
    raw, moved_ref, pack, tok_pack, qkvw, outw, cot_send, y_send, br_send, br_recv, stat_send, stat_recv,
    gate_send, sent, landed, local,
):
    n = lax.axis_index("narrow")
    w = lax.axis_index("wide")
    chip, core = w // 2, lax.rem(w, 2)
    to_z, from_z = places_of(n)
    plane = plane_of(chip)
    links = Links(sent, landed, local)
    mate = {"wide": 2 * chip + 1 - core}

    def at_plane(peer):
        return {"wide": 2 * peer + core}

    token_count, part_width = tok_ref.shape
    rows_each = raw.shape[1]
    raw_loads = [
        links.move(source, raw.at[kind_at]) for kind_at, source in enumerate((gate_ref, up_ref, down_ref))
    ]
    links.waits = []
    greet(to_z, plane, chip, core, True)

    def by_expert(kind_at):
        raw_loads[kind_at].wait()
        for expert in range(EXPERTS):
            for start in range(0, rows_each, 64):
                moved_ref[kind_at, expert, start : start + 64, :] = raw[
                    kind_at, start : start + 64, expert, :
                ]

    tok_pack[0:token_count, :] = tok_ref[...]
    tok_pack[token_count : token_count + 2, :] = gains_ref[...]
    tok_slots = [links.slot() for _ in range(NEAR)]
    for step in range(NEAR):
        links.send(tok_pack, tokens_out.at[n], {"narrow": to_z[step]}, tok_slots[step])
    wide_shape = (token_count, token_count)
    row_at = lax.broadcasted_iota(jnp.int32, wide_shape, 0)
    col_at = lax.broadcasted_iota(jnp.int32, wide_shape, 1)
    seg_row, rank_row = segment_ref[...], rank_ref[...]
    first_row, second_row = ids_ref[0:1, :], ids_ref[1:2, :]
    stacked = [item.astype(F32) for item in (seg_row, rank_row, first_row, second_row)]
    columns = jnp.concatenate(stacked + [jnp.zeros((124, token_count), F32)], 0).T
    cols_out[...] = columns
    columns = columns.astype(jnp.int32)
    seg_col, rank_col = columns[:, 0:1], columns[:, 1:2]
    segs = parents_ref.shape[1]
    of_seg = lax.broadcasted_iota(jnp.int32, (token_count, segs), 1) == seg_col
    par_col = jnp.sum(
        jnp.where(of_seg, parents_ref[...].astype(F32), 0.0), 1, keepdims=True
    ).astype(jnp.int32)
    seen = ((seg_row == seg_col) | (seg_row == par_col) | (seg_row == 0)) & (col_at <= row_at)
    spots = jnp.sum(jnp.where(seen, 1.0, 0.0), 1, keepdims=True) - 1.0
    lane_at = lax.broadcasted_iota(jnp.int32, (token_count, HEAD_DIM), 1)
    turn = lax.rem(lane_at, HEAD_DIM // 2).astype(F32) * (-2.0 / HEAD_DIM * math.log(ROPE_BASE))
    angles = spots * jnp.exp(turn)
    cosines = jnp.cos(angles)
    sines = jnp.sin(angles) * jnp.where(lane_at < HEAD_DIM // 2, -1.0, 1.0)
    rope_out[0] = cosines
    rope_out[1] = sines
    kind = lax.broadcasted_iota(jnp.int32, (8, token_count), 0)
    hot_first = jnp.where(kind == first_row, 1.0, 0.0)
    hot_second = jnp.where(kind == second_row, 1.0, 0.0)
    earlier = jnp.where(rank_col < rank_row, 1.0, 0.0).astype(BF)
    count_first = low_dot(hot_first.astype(BF), earlier)
    count_second = low_dot(hot_second.astype(BF), earlier)
    count_second = count_second + jnp.sum(hot_first, 1, keepdims=True)
    slot_first = jnp.sum(count_first * hot_first, 0, keepdims=True)
    slot_second = jnp.sum(count_second * hot_second, 0, keepdims=True)
    kept_first = jnp.where(slot_first < CAP, 1.0, 0.0)
    kept_second = jnp.where(slot_second < CAP, 1.0, 0.0)
    flat_first = jnp.where(slot_first < CAP, first_row * CAP + slot_first.astype(jnp.int32), SLOTS)
    flat_second = jnp.where(
        slot_second < CAP, second_row * CAP + slot_second.astype(jnp.int32), SLOTS
    )
    slot_at = lax.broadcasted_iota(jnp.int32, (SLOTS, token_count), 0)
    pick_first = jnp.where(slot_at == flat_first, 1.0, 0.0)
    pick_second = jnp.where(slot_at == flat_second, 1.0, 0.0)
    pick_out[0] = pick_first.astype(BF)
    pick_out[1] = pick_second.astype(BF)
    pick_both = (pick_first + pick_second).astype(BF)

    def column_block(array):
        return lambda m: array.at[:, pl.ds(pl.multiple_of(m * part_width, part_width), part_width)]

    def slot_block(array, owner):
        return array.at[
            pl.ds(pl.multiple_of(owner * CAP, 16), CAP),
            pl.ds(pl.multiple_of(n * part_width, part_width), part_width),
        ]

    def dispatch(rows, buffer, array):
        slots = [links.slot() for _ in range(NEAR)]
        buffer[...] = low_dot(pick_both, rows).astype(BF)
        for step in range(NEAR):
            links.send(
                buffer.at[pl.ds(pl.multiple_of(plane[step] * CAP, 16), CAP), :],
                slot_block(array, chip), at_plane(plane[step]), slots[step],
            )
        own = links.move(
            buffer.at[pl.ds(pl.multiple_of(chip * CAP, 16), CAP), :], slot_block(array, chip)
        )
        return slots, own

    def arrive(array, state):
        slots, own = state
        for step in range(NEAR):
            links.land(slot_block(array, plane[step]), at_plane(plane[step]), slots[step])
        own.wait()
        links.waits = [item for item in links.waits if item[0] is not own]

    dy_state = dispatch(cot_ref[...], cot_send, dy_out)
    dy_chain = Chain(links, n, column_block(dy_out))

    pack[:, 0:512] = wq_ref[...]
    pack[:, 512:1024] = wk_ref[...]
    pack[:, 1024:1536] = wv_ref[...]
    router_rows = jnp.concatenate(
        [router_ref[...].astype(F32), jnp.zeros((128 - EXPERTS, rows_each), F32)], 0
    )
    pack[:, 1536:1664] = router_rows.T.astype(BF)
    in_slots = [links.slot() for _ in range(NEAR)]
    for step in range(NEAR):
        links.send(pack, qkvw.at[w], at_plane(plane[step]), in_slots[step])
    in_mate = [links.slot() for _ in range(4)]
    links.send(pack, qkvw.at[w], mate, in_mate[3])
    out_slots = [links.slot() for _ in range(NEAR)]
    for step in range(NEAR):
        links.send(wo_ref, outw.at[w], at_plane(plane[step]), out_slots[step])
    out_mate = [links.slot() for _ in range(4)]
    links.send(wo_ref, outw.at[w], mate, out_mate[3])
    tokens_out[n] = tok_pack[...]
    qkvw[w] = pack[...]
    outw[w] = wo_ref[...]

    by_expert(0)
    for step in range(NEAR):
        links.land(tokens_out.at[from_z[step]], {"narrow": from_z[step]}, tok_slots[step])
    total = jnp.zeros((token_count, 1), F32)
    for m in range(4):
        part = tokens_out[m, 0:token_count, :].astype(F32)
        total = total + jnp.sum(part * part, 1, keepdims=True)
    scale_first = lax.rsqrt(total * (1.0 / (4 * part_width)) + NORM_EPS)
    for m in range(4):
        part = tokens_out[m, 0:token_count, :].astype(F32)
        gain = tokens_out[m, token_count : token_count + 1, :].astype(F32)
        hidden_out[:, m * part_width : (m + 1) * part_width] = (part * scale_first * gain).astype(BF)

    arrive(dy_out, dy_state)
    dy_chain.start(0)
    by_expert(1)

    for step in range(NEAR):
        owner = 2 * plane[step] + core
        links.land(qkvw.at[owner], at_plane(plane[step]), in_slots[step])
        links.send(qkvw.at[owner], qkvw.at[owner], mate, in_mate[step])
    for step in range(NEAR):
        links.land(qkvw.at[2 * plane[step] + 1 - core], mate, in_mate[step])
    links.land(qkvw.at[2 * chip + 1 - core], mate, in_mate[3])
    saved_in = links.move(qkvw, qkvw_out)

    expert_slots = [[links.slot() for _ in range(NEAR)] for _ in range(3)]
    expert_mate = [[links.slot() for _ in range(4)] for _ in range(3)]
    def set_out(kind_at):
        for step in range(NEAR):
            links.send(
                moved_ref.at[kind_at, plane[step]], expert_out.at[kind_at, chip, core],
                at_plane(plane[step]), expert_slots[kind_at][step],
            )
        links.send(
            moved_ref.at[kind_at, chip], expert_out.at[kind_at, chip, core], mate,
            expert_mate[kind_at][3],
        )
        links.move(moved_ref.at[kind_at, chip], expert_out.at[kind_at, chip, core])

    set_out(0)
    set_out(1)

    def pass_on(kind_at):
        for step in range(NEAR):
            block = expert_out.at[kind_at, plane[step], core]
            links.land(block, at_plane(plane[step]), expert_slots[kind_at][step])
            links.send(block, block, mate, expert_mate[kind_at][step])

    def all_there(kind_at):
        for step in range(NEAR):
            links.land(
                expert_out.at[kind_at, plane[step], 1 - core], mate, expert_mate[kind_at][step]
            )
        links.land(expert_out.at[kind_at, chip, 1 - core], mate, expert_mate[kind_at][3])

    dy_chain.land(0)
    dy_chain.start(1)
    by_expert(2)

    hidden = hidden_out[...]
    score_scale = HEAD_DIM ** (-0.5)
    raws = []
    for part in range(3):
        weight = qkvw[:, :, part * 512 : (part + 1) * 512].reshape(4 * part_width, part_width)
        raws.append(low_dot(hidden, weight))
    for head in range(part_width // HEAD_DIM):
        cols = slice(head * HEAD_DIM, (head + 1) * HEAD_DIM)
        turned = []
        for part in range(2):
            raw = raws[part][:, cols]
            turned.append(
                (raw * cosines + pltpu.roll(raw, HEAD_DIM // 2, 1) * sines).astype(BF)
            )
            qkv_out[part, :, cols] = turned[part]
        value = raws[2][:, cols].astype(BF)
        qkv_out[2, :, cols] = value
        scores = rows_rows(turned[0], turned[1]) * score_scale
        scores = jnp.where(seen, scores, NEG_FILL)
        exps = jnp.exp(scores - jnp.max(scores, 1, keepdims=True))
        weights = exps / jnp.sum(exps, 1, keepdims=True)
        prob_out[head] = weights
        att_out[:, cols] = low_dot(weights.astype(BF), value).astype(BF)

    dy_chain.land(1)
    dy_chain.start(2)

    for step in range(NEAR):
        owner = 2 * plane[step] + core
        links.land(outw.at[owner], at_plane(plane[step]), out_slots[step])
        links.send(outw.at[owner], outw.at[owner], mate, out_mate[step])
    for step in range(NEAR):
        links.land(outw.at[2 * plane[step] + 1 - core], mate, out_mate[step])
    links.land(outw.at[2 * chip + 1 - core], mate, out_mate[3])
    links.move(outw, outw_out)

    attended = att_out[...]

    def branch(m):
        weight = outw[pl.ds(2 * m, 2)].reshape(part_width, part_width)
        return rows_rows(attended, weight)

    br_slots = [links.slot() for _ in range(NEAR)]
    for step in range(NEAR):
        br_send[step] = branch(to_z[step]).astype(BF)
        links.send(br_send.at[step], br_recv.at[step], {"narrow": to_z[step]}, br_slots[step])
    middle = tok_ref[...].astype(F32) + branch(n)
    for step in range(NEAR):
        links.land(br_recv.at[step], {"narrow": from_z[step]}, br_slots[step])
        middle = middle + br_recv[step].astype(F32)
    middle_out[...] = middle
    x_state = dispatch(middle.astype(BF), y_send, x_out)
    x_chain = Chain(links, n, column_block(x_out))

    set_out(2)

    gain_second = gains_ref[1:2, :].astype(F32)
    router = qkvw[pl.ds(2 * n, 2), :, 1536:1664].reshape(part_width, 128)
    logit_part = mm(router, (middle * gain_second).astype(BF), ((0,), (1,)))[0:8, :]
    square = middle * middle
    square_high = square.astype(BF)
    square_low = (square - square_high.astype(F32)).astype(BF)
    ones = jnp.ones((8, part_width), BF)
    square_sum = rows_rows(ones, square_high) + rows_rows(ones, square_low)
    stat = jnp.where(kind == 4, square_sum, logit_part)
    stat_send[...] = stat
    stat_slots = [links.slot() for _ in range(NEAR)]
    for step in range(NEAR):
        links.send(stat_send, stat_recv.at[step], {"narrow": to_z[step]}, stat_slots[step])

    arrive(x_out, x_state)
    x_chain.start(0)
    for step in range(NEAR):
        links.land(stat_recv.at[step], {"narrow": from_z[step]}, stat_slots[step])
        stat = stat + stat_recv[step]
    stat_out[...] = stat
    scale_row = lax.rsqrt(stat[4:5, :] * (1.0 / (4 * part_width)) + NORM_EPS)
    logits = jnp.where(kind < EXPERTS, stat * scale_row, NEG_FILL)
    chances = jnp.exp(logits - jnp.max(logits, 0, keepdims=True))
    chances = chances / jnp.sum(chances, 0, keepdims=True)
    share_first = jnp.sum(chances * hot_first, 0, keepdims=True)
    share_second = jnp.sum(chances * hot_second, 0, keepdims=True)
    both = share_first + share_second
    weighted = pick_first * (share_first / both) + pick_second * (share_second / both)
    slot_gate = jnp.sum(weighted, 1, keepdims=True)
    gate_send[...] = jnp.broadcast_to(slot_gate, (SLOTS, 128))

    def gate_rows(array, owner):
        return array.at[pl.ds(pl.multiple_of(owner * CAP, 16), CAP), :]

    gate_slots = [links.slot() for _ in range(NEAR)]
    for step in range(NEAR):
        links.send(
            gate_rows(gate_send, plane[step]), gate_rows(gate_out, chip),
            at_plane(plane[step]), gate_slots[step],
        )
    links.move(gate_rows(gate_send, chip), gate_rows(gate_out, chip))

    pass_on(0)
    x_chain.land(0)
    x_chain.start(1)
    x_chain.land(1)
    x_chain.start(2)
    pass_on(1)
    x_chain.land(2)
    dy_chain.land(2)
    for step in range(NEAR):
        links.land(gate_rows(gate_out, plane[step]), at_plane(plane[step]), gate_slots[step])
    pass_on(2)
    for kind_at in range(3):
        all_there(kind_at)
    links.finish()


def front_call(tokens, cotangent, gains, weights, router, experts, segment, parents, ids, rank):
    token_count, part_width = tokens.shape
    full = 4 * part_width
    rows_each, _, hidden_width = experts[0].shape
    heads = part_width // HEAD_DIM
    vmem = pl.BlockSpec(memory_space=pltpu.VMEM)
    hbm = pl.BlockSpec(memory_space=pl.ANY)

    def arr(shape, dtype):
        return jax.ShapeDtypeStruct(shape, dtype)

    return pl.pallas_call(
        front_body,
        out_shape=(
            arr((8, rows_each, 1664), BF),
            arr((8, rows_each, part_width), BF),
            arr((3, 4, 2, rows_each, hidden_width), BF),
            arr((SLOTS, full), BF),
            arr((SLOTS, full), BF),
            arr((SLOTS, 128), F32),
            arr((token_count, part_width), F32),
            arr((token_count, full), BF),
            arr((4, token_count + 16, part_width), BF),
            arr((3, token_count, part_width), BF),
            arr((heads, token_count, token_count), F32),
            arr((token_count, part_width), BF),
            arr((8, token_count), F32),
            arr((2, token_count, HEAD_DIM), F32),
            arr((2, SLOTS, token_count), BF),
            arr((token_count, 128), F32),
        ),
        in_specs=[vmem] * 8 + [hbm] * 3 + [vmem] * 4,
        out_specs=(hbm, hbm, hbm) + (vmem,) * 13,
        scratch_shapes=[
            pltpu.VMEM((3, rows_each, EXPERTS, hidden_width), BF),
            pltpu.VMEM((3, EXPERTS, rows_each, hidden_width), BF),
            pltpu.VMEM((rows_each, 1664), BF),
            pltpu.VMEM((token_count + 16, part_width), BF),
            pltpu.VMEM((8, rows_each, 1664), BF),
            pltpu.VMEM((8, rows_each, part_width), BF),
            pltpu.VMEM((SLOTS, part_width), BF),
            pltpu.VMEM((SLOTS, part_width), BF),
            pltpu.VMEM((NEAR, token_count, part_width), BF),
            pltpu.VMEM((NEAR, token_count, part_width), BF),
            pltpu.VMEM((8, token_count), F32),
            pltpu.VMEM((NEAR, 8, token_count), F32),
            pltpu.VMEM((SLOTS, 128), F32),
            pltpu.SemaphoreType.DMA((FRONT_SLOTS,)),
            pltpu.SemaphoreType.DMA((FRONT_SLOTS,)),
            pltpu.SemaphoreType.DMA((16,)),
        ],
        compiler_params=pltpu.CompilerParams(
            collective_id=0, has_side_effects=True, vmem_limit_bytes=60 * 1024 * 1024
        ),
        cost_estimate=pl.CostEstimate(
            flops=6_000_000_000, bytes_accessed=60_000_000, transcendentals=400_000
        ),
        name="front",
    )(tokens, cotangent, gains, *weights, router, *experts, segment, parents, ids, rank)


MID_SLOTS = 48


def column_tiles(width):
    tiles, start = [], 0
    while start < width:
        size = min(256, width - start)
        tiles.append((start, size))
        start += size
    return tiles


def mid_body(
    x_ref, dy_ref, gate_ref, tokens_ref, w_ref,
    back_mid_out, back_exp_out, extra_out, grads_out, expert_out,
    weights, hidden, graded, hidden_cat, graded_cat, act_cat, gate_cat, up_cat,
    rs_send, rs_recv, ext_send, ext_recv, sent, landed, local,
):
    n = lax.axis_index("narrow")
    w = lax.axis_index("wide")
    chip, core = w // 2, lax.rem(w, 2)
    to_z, from_z = places_of(n)
    plane = plane_of(chip)
    links = Links(sent, landed, local)
    mate = {"wide": 2 * chip + 1 - core}
    slots, full = x_ref.shape
    part_width = full // 4
    rows_each = full // 8
    hidden_width = weights.shape[2]
    tiles = column_tiles(hidden_width)

    loads = [
        [
            links.move(w_ref.at[kind, c, k], weights.at[kind, pl.ds((2 * c + k) * rows_each, rows_each), :])
            for c in range(4)
            for k in range(2)
        ]
        for kind in range(3)
    ]
    links.waits = []
    greet(to_z, plane, chip, core, True)

    total = jnp.zeros((slots, 1), F32)
    for m in range(4):
        part = x_ref[:, m * part_width : (m + 1) * part_width].astype(F32)
        total = total + jnp.sum(part * part, 1, keepdims=True)
    scale = lax.rsqrt(total * (1.0 / full) + NORM_EPS)
    slot_gate = gate_ref[:, 0:1]
    for m in range(4):
        cols = slice(m * part_width, (m + 1) * part_width)
        gain = tokens_ref[m, 257:258, :].astype(F32)
        hidden[:, cols] = (x_ref[:, cols].astype(F32) * scale * gain).astype(BF)
        graded[:, cols] = (dy_ref[:, cols].astype(F32) * slot_gate).astype(BF)

    def to_mate(source, target):
        slot = links.slot()
        links.send(source, target.at[core], mate, slot)
        return lambda: links.land(target.at[1 - core], mate, slot)

    def parity_exchange(source, target):
        lands = []
        for c in range(4):
            cols = pl.ds(c * rows_each, rows_each)
            theirs = pl.ds(pl.multiple_of((2 * c + 1 - core) * rows_each, rows_each), rows_each)
            ours = pl.ds(pl.multiple_of((2 * c + core) * rows_each, rows_each), rows_each)
            slot = links.slot()
            links.send(source.at[:, theirs], target.at[core, :, cols], mate, slot)
            target[core, :, c * rows_each : (c + 1) * rows_each] = source[:, ours]
            lands.append((target.at[1 - core, :, cols], slot))
        return lambda: [links.land(block, mate, slot) for block, slot in lands]

    hidden_there = parity_exchange(hidden, hidden_cat)
    graded_there = parity_exchange(graded, graded_cat)

    for kind in range(3):
        for load in loads[kind]:
            load.wait()
    share = jnp.zeros((slots, 1), F32)
    for start, size in tiles:
        cols = slice(start, start + size)
        gate_pre = low_dot(hidden[...], weights[0, :, cols])
        up_pre = low_dot(hidden[...], weights[1, :, cols])
        act_raw = low_dot(dy_ref[...], weights[2, :, cols])
        sigmoid = 1.0 / (1.0 + jnp.exp(-gate_pre))
        silu = gate_pre * sigmoid
        activated = (silu * up_pre).astype(BF)
        share = share + jnp.sum(act_raw * activated.astype(F32), 1, keepdims=True)
        grad_act = act_raw * slot_gate
        act_cat[core, :, cols] = activated
        gate_cat[core, :, cols] = (
            grad_act * up_pre * (sigmoid * (1.0 + gate_pre * (1.0 - sigmoid)))
        ).astype(BF)
        up_cat[core, :, cols] = (grad_act * silu).astype(BF)

    grad_gate, grad_up = gate_cat[core], up_cat[core]
    stat = jnp.zeros((slots, 1), F32)
    mid_sum = LineSum(links, n, rs_send.at[0], rs_recv.at[0])
    for step in range(NEAR + 1):
        owner = mid_sum.targets[step] if step < NEAR else n
        rows = pl.ds(pl.multiple_of(owner * part_width, part_width), part_width)
        block = rows_rows(grad_gate, weights[0, rows, :]) + rows_rows(grad_up, weights[1, rows, :])
        cols = pl.ds(pl.multiple_of(owner * part_width, part_width), part_width)
        stat = stat + jnp.sum(hidden[:, cols].astype(F32) * block, 1, keepdims=True)
        if step < NEAR:
            mid_sum.put(step, block)
        else:
            own_mid = block
    lane_at = lax.broadcasted_iota(jnp.int32, (slots, 128), 1)
    columns = jnp.where(lane_at == 0, share, jnp.where(lane_at == 1, stat, 0.0))
    high = columns.astype(BF)
    rest = (columns - high.astype(F32)).astype(BF)
    pick = jnp.where(
        lax.broadcasted_iota(jnp.int32, (8, 128), 0) == lax.broadcasted_iota(jnp.int32, (8, 128), 1),
        1.0, 0.0,
    ).astype(BF)
    extra = rows_rows(pick, high) + rows_rows(pick, rest)
    ext_send[...] = extra
    ext_slots = [links.slot() for _ in range(NEAR)]
    for step in range(NEAR):
        links.send(ext_send, ext_recv.at[step], {"narrow": to_z[step]}, ext_slots[step])
    acts_there = [to_mate(item.at[core], item) for item in (act_cat, gate_cat, up_cat)]

    half = full // 2
    expert_slots = {}

    def weight_grad(left, right, kind, start_row):
        left_rows = left[...].reshape(2 * slots, half)
        for start, size in tiles:
            cols = slice(start, start + size)
            right_rows = right[:, :, cols].reshape(2 * slots, size)
            weights[kind, start_row : start_row + half, cols] = cols_cols(
                left_rows, right_rows
            ).astype(BF)

    def share_out(index, kind, start_row):
        expert_slots[index] = [links.slot() for _ in range(NEAR)]

        def block(owner):
            first = pl.multiple_of(start_row + owner * rows_each, rows_each)
            return weights.at[kind, pl.ds(first, rows_each), :]

        for step in range(NEAR):
            links.send(
                block(plane[step]), expert_out.at[index, chip],
                {"wide": 2 * plane[step] + core}, expert_slots[index][step],
            )
        links.move(block(chip), expert_out.at[index, chip])

    graded_there()
    for there in acts_there[:1]:
        there()
    weight_grad(graded_cat, act_cat, 0, 0)
    share_out(0, 0, 0)
    mid_sum.relay()
    activated = act_cat[core]
    exp_sum = LineSum(links, n, rs_send.at[1], rs_recv.at[1])
    for step in range(NEAR + 1):
        owner = exp_sum.targets[step] if step < NEAR else n
        rows = pl.ds(pl.multiple_of(owner * part_width, part_width), part_width)
        block = rows_rows(activated, weights[2, rows, :])
        if step < NEAR:
            exp_sum.put(step, block)
        else:
            own_exp = block

    hidden_there()
    for there in acts_there[1:]:
        there()
    weight_grad(hidden_cat, gate_cat, 0, half)
    share_out(1, 0, half)
    exp_sum.relay()
    weight_grad(hidden_cat, up_cat, 1, 0)
    links.move(weights.at[1, pl.ds(0, half), :], grads_out)

    for step in range(NEAR):
        links.land(ext_recv.at[step], {"narrow": from_z[step]}, ext_slots[step])
        extra = extra + ext_recv[step]
    high = extra.astype(BF)
    rest = (extra - high.astype(F32)).astype(BF)
    place = lax.broadcasted_iota(jnp.int32, (8, 128), 0) * 2
    lanes = lax.broadcasted_iota(jnp.int32, (8, 128), 1)
    spread_high = jnp.where(place == lanes, 1.0, 0.0).astype(BF)
    spread_low = jnp.where(place + 1 == lanes, 1.0, 0.0).astype(BF)
    columns = mm(high, spread_high, ((0,), (0,))) + mm(rest, spread_low, ((0,), (0,)))
    extra_out[...] = jnp.where(lane_at == 4, 1.0, columns).astype(BF)
    back_mid_out[...] = mid_sum.total(own_mid).astype(BF)
    back_exp_out[...] = exp_sum.total(own_exp).astype(BF)
    for index in range(2):
        for step in range(NEAR):
            links.land(
                expert_out.at[index, plane[step]], {"wide": 2 * plane[step] + core},
                expert_slots[index][step],
            )
    links.finish()


def mid_call(slot_mid, slot_grad, slot_gate, token_parts, expert_w):
    slots, full = slot_mid.shape
    part_width = full // 4
    rows_each, hidden_width = expert_w.shape[3:]
    vmem = pl.BlockSpec(memory_space=pltpu.VMEM)
    hbm = pl.BlockSpec(memory_space=pl.ANY)

    def arr(shape, dtype):
        return jax.ShapeDtypeStruct(shape, dtype)

    return pl.pallas_call(
        mid_body,
        out_shape=(
            arr((slots, part_width), BF),
            arr((slots, part_width), BF),
            arr((slots, 128), BF),
            arr((full // 2, hidden_width), BF),
            arr((2, 4, rows_each, hidden_width), BF),
        ),
        in_specs=[vmem] * 4 + [hbm],
        out_specs=(vmem, vmem, vmem, hbm, hbm),
        scratch_shapes=[
            pltpu.VMEM((3, full, hidden_width), BF),
            pltpu.VMEM((slots, full), BF),
            pltpu.VMEM((slots, full), BF),
            pltpu.VMEM((2, slots, full // 2), BF),
            pltpu.VMEM((2, slots, full // 2), BF),
            pltpu.VMEM((2, slots, hidden_width), BF),
            pltpu.VMEM((2, slots, hidden_width), BF),
            pltpu.VMEM((2, slots, hidden_width), BF),
            pltpu.VMEM((2, NEAR, slots, part_width), BF),
            pltpu.VMEM((2, NEAR + 1, slots, part_width), BF),
            pltpu.VMEM((8, slots), F32),
            pltpu.VMEM((NEAR, 8, slots), F32),
            pltpu.SemaphoreType.DMA((MID_SLOTS,)),
            pltpu.SemaphoreType.DMA((MID_SLOTS,)),
            pltpu.SemaphoreType.DMA((32,)),
        ],
        compiler_params=pltpu.CompilerParams(
            collective_id=1, has_side_effects=True, vmem_limit_bytes=62 * 1024 * 1024
        ),
        cost_estimate=pl.CostEstimate(
            flops=30_000_000_000, bytes_accessed=40_000_000, transcendentals=800_000
        ),
        name="mid",
    )(slot_mid, slot_grad, slot_gate, token_parts, expert_w)


TAIL_SLOTS = 72


def tail_body(
    mid_ref, exp_ref, ext_ref, moved_ref, picks_ref, stat_ref, cols_ref, middle_ref, cot_ref,
    tok_ref, tokens_ref, qkv_ref, prob_ref, att_ref, rope_ref, hidden_ref, qkvw_ref, outw_ref,
    output_out, grad_tokens_out, summed_out, small_out,
    router_out, expert_out,
    router_all, qkvw, outw, ret_mid, ret_exp, ret_ext, branch, hidden_cat, branch_cat, att_cat, proj_cat,
    proj_send, proj_recv, first_send, first_recv, col_send, col_recv, small_mate, small_sum,
    small_recv, last_mate, last_sum, last_recv, sent, landed, local,
):
    n = lax.axis_index("narrow")
    w = lax.axis_index("wide")
    chip, core = w // 2, lax.rem(w, 2)
    to_z, from_z = places_of(n)
    plane = plane_of(chip)
    links = Links(sent, landed, local)
    mate = {"wide": 2 * chip + 1 - core}
    token_count, part_width = tok_ref.shape
    full = 4 * part_width
    rows_each = full // 8
    heads = part_width // HEAD_DIM
    half = full // 2

    def at_plane(peer):
        return {"wide": 2 * peer + core}

    def cap_rows(array, owner):
        return array.at[pl.ds(pl.multiple_of(owner * CAP, 16), CAP), :]

    loads = [links.move(qkvw_ref, qkvw), links.move(outw_ref, outw)]
    links.waits = []
    greet(to_z, plane, chip, core, True)

    back_slots = []
    for source, target in ((mid_ref, ret_mid), (ext_ref, ret_ext), (exp_ref, ret_exp)):
        slots = [links.slot() for _ in range(NEAR)]
        for step in range(NEAR):
            links.send(
                cap_rows(source, plane[step]), cap_rows(target, chip), at_plane(plane[step]),
                slots[step],
            )
        own = links.move(cap_rows(source, chip), cap_rows(target, chip))
        links.waits.pop()
        back_slots.append((target, slots, own))

    def returned(which):
        target, slots, own = back_slots[which]
        for step in range(NEAR):
            links.land(cap_rows(target, plane[step]), at_plane(plane[step]), slots[step])
        own.wait()
        return target[...]

    expert_slots = [links.slot() for _ in range(NEAR)]
    for step in range(NEAR):
        block = pl.ds(pl.multiple_of(plane[step] * rows_each, rows_each), rows_each)
        links.send(
            moved_ref.at[block, :], expert_out.at[chip], at_plane(plane[step]), expert_slots[step]
        )
    block = pl.ds(pl.multiple_of(chip * rows_each, rows_each), rows_each)
    links.move(moved_ref.at[block, :], expert_out.at[chip])

    def to_mate(source, target):
        slot = links.slot()
        links.send(source, target.at[core], mate, slot)
        return lambda: links.land(target.at[1 - core], mate, slot)

    def parity_exchange(source, target):
        lands = []
        for c in range(4):
            cols = pl.ds(c * rows_each, rows_each)
            theirs = pl.ds(pl.multiple_of((2 * c + 1 - core) * rows_each, rows_each), rows_each)
            ours = pl.ds(pl.multiple_of((2 * c + core) * rows_each, rows_each), rows_each)
            slot = links.slot()
            links.send(source.at[:, theirs], target.at[core, :, cols], mate, slot)
            target[core, :, c * rows_each : (c + 1) * rows_each] = source[:, ours]
            lands.append((target.at[1 - core, :, cols], slot))
        return lambda: [links.land(block, mate, slot) for block, slot in lands]

    hidden_there = parity_exchange(hidden_ref, hidden_cat)
    att_cat[core] = att_ref[...]
    att_there = to_mate(att_ref, att_cat)

    stat = jnp.concatenate([stat_ref[...], jnp.zeros((120, token_count), F32)], 0).T
    lane_at = lax.broadcasted_iota(jnp.int32, (token_count, 128), 1)
    scale_second = lax.rsqrt(stat[:, 4:5] * (1.0 / full) + NORM_EPS)
    logits = stat * scale_second
    hot_first = lane_at == cols_ref[:, 2:3].astype(jnp.int32)
    hot_second = lane_at == cols_ref[:, 3:4].astype(jnp.int32)
    logit_first = jnp.sum(jnp.where(hot_first, logits, 0.0), 1, keepdims=True)
    logit_second = jnp.sum(jnp.where(hot_second, logits, 0.0), 1, keepdims=True)
    apart = logit_first - logit_second
    share_first = 1.0 / (1.0 + jnp.exp(-apart))
    share_second = 1.0 / (1.0 + jnp.exp(apart))
    normed = middle_ref[...] * scale_second
    gain_second = tokens_ref[n, token_count + 1 : token_count + 2, :].astype(F32)
    hidden_second = (normed * gain_second).astype(BF)
    for load in loads:
        load.wait()
    router = qkvw[pl.ds(2 * n, 2), :, 1536:1664].reshape(part_width, 128)

    rows_mid = returned(0)
    rows_ext = returned(1)
    ext_first = cols_cols(picks_ref[0], rows_ext)
    ext_second = cols_cols(picks_ref[1], rows_ext)
    ext_both = ext_first + ext_second
    grad_share = ext_first[:, 0:1] + ext_first[:, 1:2] - ext_second[:, 0:1] - ext_second[:, 1:2]
    delta = (grad_share * share_first * share_second).astype(BF).astype(F32)
    grad_logits = jnp.where(hot_first, delta, jnp.where(hot_second, -delta, 0.0)).astype(BF)
    stat_total = ext_both[:, 2:3] + ext_both[:, 3:4] + delta * apart
    grad_hidden = cols_cols(picks_ref[0] + picks_ref[1], rows_mid) + rows_rows(grad_logits, router)
    grad_middle = cot_ref[...].astype(F32) + scale_second * (
        gain_second * grad_hidden - normed * (stat_total * (1.0 / full))
    )
    own_cols = pl.ds(pl.multiple_of(n * part_width, part_width), part_width)
    branch[:, own_cols] = grad_middle.astype(BF)
    branch_slots = [links.slot() for _ in range(NEAR)]
    for step in range(NEAR):
        links.send(
            branch.at[:, own_cols], branch.at[:, own_cols], {"narrow": to_z[step]},
            branch_slots[step],
        )

    router_part = cols_cols(grad_logits, hidden_second)[0:8, :]
    gain_part = jnp.sum(grad_hidden * normed, 0, keepdims=True)
    kind_at = lax.broadcasted_iota(jnp.int32, (8, part_width), 0)
    small = jnp.where(kind_at == 4, gain_part, router_part)
    small_mate[core] = small
    small_there = to_mate(small_mate.at[core], small_mate)

    small_there()
    small = small_mate[0] + small_mate[1]
    small_sum[...] = small
    small_slots = [links.slot() for _ in range(NEAR)]
    for step in range(NEAR):
        links.send(small_sum, small_recv.at[step], at_plane(plane[step]), small_slots[step])

    for step in range(NEAR):
        cols = pl.ds(pl.multiple_of(from_z[step] * part_width, part_width), part_width)
        links.land(branch.at[:, cols], {"narrow": from_z[step]}, branch_slots[step])
    branch_there = parity_exchange(branch, branch_cat)
    grad_att = low_dot(branch[...], outw[...].reshape(full, part_width)).astype(BF)

    def proj_rows(owner):
        return pl.ds(pl.multiple_of(owner * rows_each, rows_each), rows_each)

    proj_slots = {}

    def proj_set_out(name, cols):
        proj_slots[name] = [links.slot() for _ in range(NEAR)]
        for step in range(NEAR):
            links.send(
                proj_send.at[proj_rows(plane[step]), cols], proj_recv.at[step, :, cols],
                at_plane(plane[step]), proj_slots[name][step],
            )

    branch_there()
    att_there()
    proj_send[:, 1536:2048] = cols_cols(
        branch_cat[...].reshape(2 * token_count, half), att_cat[...].reshape(2 * token_count, part_width)
    ).astype(BF)
    proj_set_out(3, pl.ds(1536, 512))
    cosines, sines = rope_ref[0], rope_ref[1]
    score_scale = HEAD_DIM ** (-0.5)
    stat_first = jnp.zeros((token_count, 1), F32)
    for head in range(heads):
        cols = slice(head * HEAD_DIM, (head + 1) * HEAD_DIM)
        query, key, value = (qkv_ref[i, :, cols] for i in range(3))
        grad_out = grad_att[:, cols]
        weights = prob_ref[head]
        grad_weights = rows_rows(grad_out, value)
        inner = jnp.sum(weights * grad_weights, 1, keepdims=True)
        grad_scores = (weights * (grad_weights - inner)).astype(BF)
        grad_query = low_dot(grad_scores, key) * score_scale
        grad_key = cols_cols(grad_scores, query) * score_scale
        grad_value = cols_cols(weights.astype(BF), grad_out)
        products = (
            grad_query * query.astype(F32)
            + grad_key * key.astype(F32)
            + grad_value * value.astype(F32)
        )
        stat_first = stat_first + jnp.sum(products, 1, keepdims=True)
        for part, grad in ((0, grad_query), (1, grad_key)):
            turned = grad * cosines - pltpu.roll(grad, HEAD_DIM // 2, 1) * sines
            proj_cat[core, :, part * 512 + head * 128 : part * 512 + (head + 1) * 128] = (
                turned.astype(BF)
            )
        proj_cat[core, :, 1024 + head * 128 : 1024 + (head + 1) * 128] = grad_value.astype(BF)
    proj_there = to_mate(proj_cat.at[core], proj_cat)
    high = stat_first.astype(BF)
    rest = (stat_first - high.astype(F32)).astype(BF)
    col_send[...] = jnp.where(
        lane_at == 0, high.astype(F32), jnp.where(lane_at == 1, rest.astype(F32), 0.0)
    ).astype(BF)
    col_slots = [links.slot() for _ in range(NEAR)]
    for step in range(NEAR):
        links.send(col_send, col_recv.at[step], {"narrow": to_z[step]}, col_slots[step])
    grads = proj_cat[core]

    def first_block(m):
        weight = qkvw[pl.ds(2 * m, 2), :, 0:1536].reshape(part_width, 1536)
        return rows_rows(grads, weight)

    first_slots = [links.slot() for _ in range(NEAR)]
    for step in range(NEAR):
        first_send[step] = first_block(to_z[step]).astype(BF)
        links.send(
            first_send.at[step], first_recv.at[step], {"narrow": to_z[step]}, first_slots[step]
        )

    hidden_there()
    proj_there()
    hidden_rows = hidden_cat[...].reshape(2 * token_count, half)
    for part in range(3):
        cols = slice(part * 512, (part + 1) * 512)
        proj_send[:, cols] = cols_cols(
            hidden_rows, proj_cat[:, :, cols].reshape(2 * token_count, part_width)
        ).astype(BF)
        proj_set_out(part, pl.ds(part * 512, 512))

    rows_exp = returned(2)
    output_out[...] = (
        middle_ref[...]
        + share_first * cols_cols(picks_ref[0], rows_exp)
        + share_second * cols_cols(picks_ref[1], rows_exp)
    ).astype(BF)

    grad_first = first_block(n)
    stat_first = high.astype(F32) + rest.astype(F32)
    total = jnp.zeros((token_count, 1), F32)
    for m in range(4):
        part = tokens_ref[m, 0:token_count, :].astype(F32)
        total = total + jnp.sum(part * part, 1, keepdims=True)
    scale_first = lax.rsqrt(total * (1.0 / full) + NORM_EPS)
    normed_first = tok_ref[...].astype(F32) * scale_first
    gain_first = tokens_ref[n, token_count : token_count + 1, :].astype(F32)
    for step in range(NEAR):
        links.land(col_recv.at[step], {"narrow": from_z[step]}, col_slots[step])
        stat_first = stat_first + (
            col_recv[step, :, 0:1].astype(F32) + col_recv[step, :, 1:2].astype(F32)
        )
    for step in range(NEAR):
        links.land(first_recv.at[step], {"narrow": from_z[step]}, first_slots[step])
        grad_first = grad_first + first_recv[step].astype(F32)
    grad_tokens_out[...] = grad_middle + scale_first * (
        gain_first * grad_first - normed_first * (stat_first * (1.0 / full))
    )
    gain_part = jnp.sum(grad_first * normed_first, 0, keepdims=True)
    last_mate[core] = jnp.broadcast_to(gain_part, (8, part_width))
    last_there = to_mate(last_mate.at[core], last_mate)

    for step in range(NEAR):
        links.land(small_recv.at[step], at_plane(plane[step]), small_slots[step])
        small = small + small_recv[step]
    last_there()
    last = last_mate[0] + last_mate[1]
    last_sum[...] = last
    last_slots = [links.slot() for _ in range(NEAR)]
    for step in range(NEAR):
        links.send(last_sum, last_recv.at[step], at_plane(plane[step]), last_slots[step])
    router_all[:, own_cols] = small
    router_slots = [links.slot() for _ in range(NEAR)]
    for step in range(NEAR):
        links.send(
            router_all.at[:, own_cols], router_all.at[:, own_cols], {"narrow": to_z[step]},
            router_slots[step],
        )
    for step in range(NEAR):
        links.land(last_recv.at[step], at_plane(plane[step]), last_slots[step])
        last = last + last_recv[step]
    small_out[...] = jnp.where(kind_at == 5, last, small)
    for step in range(NEAR):
        cols = pl.ds(pl.multiple_of(from_z[step] * part_width, part_width), part_width)
        links.land(router_all.at[:, cols], {"narrow": from_z[step]}, router_slots[step])

    router_out[...] = router_all[:, pl.ds(pl.multiple_of(w * rows_each, rows_each), rows_each)]
    summed = proj_send[proj_rows(chip), :].astype(F32)
    for step in range(NEAR):
        for name, slots in proj_slots.items():
            cols = pl.ds(name * 512, 512)
            links.land(proj_recv.at[step, :, cols], at_plane(plane[step]), slots[step])
        summed = summed + proj_recv[step].astype(F32)
    summed_out[...] = summed
    for step in range(NEAR):
        links.land(expert_out.at[plane[step]], at_plane(plane[step]), expert_slots[step])
    links.finish()


def tail_call(*args):
    slots, part_width = args[0].shape
    half, hidden_width = args[3].shape
    token_count = args[9].shape[0]
    full, rows_each = 2 * half, half // 4
    vmem = pl.BlockSpec(memory_space=pltpu.VMEM)
    hbm = pl.BlockSpec(memory_space=pl.ANY)

    def arr(shape, dtype):
        return jax.ShapeDtypeStruct(shape, dtype)

    own = (token_count, part_width)
    return pl.pallas_call(
        tail_body,
        out_shape=(
            arr(own, BF),
            arr(own, F32),
            arr((rows_each, full), F32),
            arr((8, part_width), F32),
            arr((8, rows_each), F32),
            arr((4, rows_each, hidden_width), BF),
        ),
        in_specs=[vmem] * 3 + [hbm] + [vmem] * 12 + [hbm] * 2,
        out_specs=(vmem,) * 5 + (hbm,),
        scratch_shapes=[
            pltpu.VMEM((8, full), F32),
            pltpu.VMEM((8, rows_each, 1664), BF),
            pltpu.VMEM((8, rows_each, part_width), BF),
            pltpu.VMEM((slots, part_width), BF),
            pltpu.VMEM((slots, part_width), BF),
            pltpu.VMEM((slots, 128), BF),
            pltpu.VMEM((token_count, full), BF),
            pltpu.VMEM((2, token_count, half), BF),
            pltpu.VMEM((2, token_count, half), BF),
            pltpu.VMEM((2, token_count, part_width), BF),
            pltpu.VMEM((2, token_count, 1536), BF),
            pltpu.VMEM((half, full), BF),
            pltpu.VMEM((NEAR, rows_each, full), BF),
            pltpu.VMEM((NEAR,) + own, BF),
            pltpu.VMEM((NEAR,) + own, BF),
            pltpu.VMEM((token_count, 128), BF),
            pltpu.VMEM((NEAR, token_count, 128), BF),
            pltpu.VMEM((2, 8, part_width), F32),
            pltpu.VMEM((8, part_width), F32),
            pltpu.VMEM((NEAR, 8, part_width), F32),
            pltpu.VMEM((2, 8, part_width), F32),
            pltpu.VMEM((8, part_width), F32),
            pltpu.VMEM((NEAR, 8, part_width), F32),
            pltpu.SemaphoreType.DMA((TAIL_SLOTS,)),
            pltpu.SemaphoreType.DMA((TAIL_SLOTS,)),
            pltpu.SemaphoreType.DMA((16,)),
        ],
        compiler_params=pltpu.CompilerParams(
            collective_id=2, has_side_effects=True, vmem_limit_bytes=60 * 1024 * 1024
        ),
        cost_estimate=pl.CostEstimate(
            flops=6_000_000_000, bytes_accessed=60_000_000, transcendentals=1_000
        ),
        name="tail",
    )(*args)


def finish_body(
    down_ref, gate_ref, up_ref, output_ref, tokens_ref, summed_ref,
    gate_out, up_out, down_out, output_out, tokens_out, *proj_outs,
):
    for source, target in ((gate_ref, gate_out), (up_ref, up_out), (down_ref, down_out)):
        for expert in range(EXPERTS):
            target[:, expert, :] = source[expert].astype(F32)
    output_out[...] = output_ref[...]
    tokens_out[...] = tokens_ref[...]
    width = tokens_ref.shape[1]
    for part, target in enumerate(proj_outs):
        target[...] = summed_ref[:, part * width : (part + 1) * width].astype(F32)


def finish_call(early, late, output, grad_tokens, summed):
    _, rows_each, hidden_width = late.shape
    token_count, part_width = output.shape
    step = 32

    def flat(width):
        return pl.BlockSpec((step, width), lambda i: (i, 0))

    def cube(which):
        return pl.BlockSpec((None, EXPERTS, step, hidden_width), lambda i: (which, 0, i, 0))

    spread = pl.BlockSpec((step, EXPERTS, hidden_width), lambda i: (i, 0, 0))

    def arr(shape, dtype):
        return jax.ShapeDtypeStruct(shape, dtype)

    return pl.pallas_call(
        finish_body,
        grid=(rows_each // step,),
        out_shape=(arr((rows_each, EXPERTS, hidden_width), F32),) * 3
        + (arr(output.shape, BF), arr(output.shape, F32))
        + (arr((rows_each, part_width), F32),) * 4,
        in_specs=[
            cube(0), cube(1),
            pl.BlockSpec((EXPERTS, step, hidden_width), lambda i: (0, i, 0)),
            flat(part_width), flat(part_width), flat(4 * part_width),
        ],
        out_specs=(spread,) * 3 + (flat(part_width),) * 6,
        name="finish",
    )(early, early, late, output, grad_tokens, summed)


def plain_device(
    tokens, gain_attn, w_query, w_key, w_value, w_out, gain_ffn, w_router,
    w_gate, w_up, w_down, segment, parents, expert_ids, slot_order, cotangent,
):
    narrow_count = lax.axis_size("narrow")
    wide_count = lax.axis_size("wide")
    narrow_at = lax.axis_index("narrow")
    token_count, part_width = tokens.shape
    full_width = part_width * narrow_count
    hidden_width = w_gate.shape[2]
    rows_each = w_gate.shape[0]
    blocks = wide_count // 8
    quads = [
        [8 * block + 2 * chip + core for chip in range(4)]
        for block in range(blocks)
        for core in range(2)
    ]
    mates = [
        [8 * block + 2 * chip + core for block in range(blocks) for core in range(2)]
        for chip in range(4)
    ]

    def quad_swap(array):
        return lax.all_to_all(array, "wide", 0, 0, axis_index_groups=quads, tiled=True)

    def own_rows(weight):
        moved = quad_swap(jnp.transpose(weight, (1, 0, 2)))
        joined = lax.all_gather(moved, "wide", axis=0, axis_index_groups=mates, tiled=True)
        joined = joined.reshape(blocks, 2, 4, rows_each, hidden_width).transpose(0, 2, 1, 3, 4)
        return joined.reshape(full_width, hidden_width)

    def share_rows(grad):
        parts = grad.astype(BF).reshape(blocks, 4, 2, rows_each, hidden_width)
        parts = parts.transpose(0, 2, 1, 3, 4).reshape(blocks * 2, 4, rows_each, hidden_width)
        summed = lax.psum_scatter(
            parts, "wide", scatter_dimension=0, axis_index_groups=mates, tiled=True
        )[0]
        return jnp.transpose(quad_swap(summed), (1, 0, 2)).astype(F32)

    def head_cols(array, head):
        return array[:, head * HEAD_DIM : (head + 1) * HEAD_DIM]

    heads = part_width // HEAD_DIM
    half_dim = HEAD_DIM // 2
    freqs = ROPE_BASE ** (-2.0 * jnp.arange(half_dim, dtype=F32) / HEAD_DIM)
    score_scale = HEAD_DIM ** (-0.5)
    gains = jnp.stack([gain_attn, gain_ffn])
    gain_first_loc = gain_attn.astype(F32)
    gain_second_loc = gain_ffn.astype(F32)
    hot_first, hot_second, kept, pick_first, pick_second = route(expert_ids, slot_order[0])

    gate_w, up_w, down_w = own_rows(w_gate), own_rows(w_up), own_rows(w_down)
    attn_w = lax.all_gather(
        jnp.stack([w_query, w_key, w_value, w_out], 1), "wide", axis=0, tiled=True
    )
    query_w, key_w, value_w, out_w = (attn_w[:, i] for i in range(4))
    router_w = lax.all_gather(w_router, "wide", axis=0, tiled=True)
    tokens_full = lax.all_gather(tokens, "narrow", axis=1, tiled=True)
    grad_full = lax.all_gather(cotangent, "narrow", axis=1, tiled=True)
    gains_full = lax.all_gather(gains, "narrow", axis=1, tiled=True)
    gain_first = gains_full[0].astype(F32)
    gain_second = gains_full[1].astype(F32)

    seen, places = tree_layout(segment[0], parents[0])
    pick_first_low = pick_first.astype(BF)
    pick_second_low = pick_second.astype(BF)
    pick_both_low = (pick_first | pick_second).astype(BF)

    inputs_full = tokens_full.astype(F32)
    scale_first = lax.rsqrt(jnp.mean(inputs_full * inputs_full, -1, keepdims=True) + NORM_EPS)
    normed_first = inputs_full * scale_first
    hidden_first = (normed_first * gain_first).astype(BF)
    angles = places[:, None] * freqs[None, :]
    cosines, sines = jnp.cos(angles), jnp.sin(angles)
    query_raw = rows_cols(hidden_first, query_w)
    key_raw = rows_cols(hidden_first, key_w)
    value_low = rows_cols(hidden_first, value_w).astype(BF)

    saved = []
    outs = []
    for head in range(heads):
        query = rotate(head_cols(query_raw, head), cosines, sines).astype(BF)
        key = rotate(head_cols(key_raw, head), cosines, sines).astype(BF)
        value = head_cols(value_low, head)
        scores = jnp.where(seen, rows_rows(query, key) * score_scale, NEG_FILL)
        exps = jnp.exp(scores - jnp.max(scores, -1, keepdims=True))
        weights = exps / jnp.sum(exps, -1, keepdims=True)
        saved.append((query, key, value, weights))
        outs.append(rows_cols(weights.astype(BF), value).astype(BF))
    attended = jnp.concatenate(outs, 1)
    branch_part = rows_rows(attended, out_w).astype(BF)
    branch_loc = lax.psum_scatter(
        branch_part, "narrow", scatter_dimension=1, tiled=True
    ).astype(F32)
    middle = tokens.astype(F32) + branch_loc
    middle_full = lax.all_gather(middle.astype(BF), "narrow", axis=1, tiled=True).astype(F32)
    scale_second = lax.rsqrt(jnp.mean(middle_full * middle_full, -1, keepdims=True) + NORM_EPS)
    normed_second = middle_full * scale_second
    hidden_second = (normed_second * gain_second).astype(BF)
    logits = rows_cols(hidden_second, router_w)
    share_first, share_second = gate_pair(logits, hot_first, hot_second)
    weight_first = kept[:, 0] * share_first
    weight_second = kept[:, 1] * share_second

    slot_weight = jnp.sum(
        pick_first * weight_first[:, None] + pick_second * weight_second[:, None], 0
    )
    weight_high, weight_low = two_parts(slot_weight)
    pads = jnp.stack([weight_high, weight_low], 1)
    pads = jnp.pad(pads, ((0, 0), (0, 126)))
    sent_hidden = cols_cols(pick_both_low, hidden_second).astype(BF)
    sent_grad = cols_cols(pick_both_low, grad_full).astype(BF)
    sent = jnp.concatenate([sent_hidden, sent_grad, pads], 1)
    got = quad_swap(sent.reshape(EXPERTS, CAP, -1)).reshape(SLOTS, -1)
    slot_hidden = got[:, :full_width]
    slot_grad = got[:, full_width : 2 * full_width]
    slot_gate = got[:, 2 * full_width : 2 * full_width + 2].astype(F32)
    slot_gate = slot_gate[:, 0:1] + slot_gate[:, 1:2]

    gate_pre = rows_cols(slot_hidden, gate_w)
    up_pre = rows_cols(slot_hidden, up_w)
    sigmoid_gate = jax.nn.sigmoid(gate_pre)
    silu_gate = gate_pre * sigmoid_gate
    activated = (silu_gate * up_pre).astype(BF)
    expert_part = rows_rows(activated, down_w)
    act_raw = rows_cols(slot_grad, down_w)
    share_part = jnp.sum(act_raw * activated.astype(F32), 1, keepdims=True)
    grad_act = act_raw * slot_gate
    grad_gate_pre = (
        grad_act * up_pre * sigmoid_gate * (1.0 + gate_pre * (1.0 - sigmoid_gate))
    ).astype(BF)
    grad_up_pre = (grad_act * silu_gate).astype(BF)
    grad_slot = rows_rows(grad_gate_pre, gate_w) + rows_rows(grad_up_pre, up_w)
    stat_part = jnp.sum(slot_hidden.astype(F32) * grad_slot, 1, keepdims=True)
    extras = jnp.concatenate([*two_parts(share_part), *two_parts(stat_part)], 1)
    extras = jnp.pad(extras, ((0, 0), (0, 124)))
    back_parts = []
    expert_plain = expert_part.astype(BF)
    slot_plain = grad_slot.astype(BF)
    for part in range(narrow_count):
        cols = slice(part * part_width, (part + 1) * part_width)
        back_parts += [expert_plain[:, cols], slot_plain[:, cols], extras]
    back = lax.psum_scatter(
        jnp.concatenate(back_parts, 1), "narrow", scatter_dimension=1, tiled=True
    )
    back = quad_swap(back.reshape(EXPERTS, CAP, -1)).reshape(SLOTS, -1)
    picked_first = rows_cols(pick_first_low, back)
    picked_second = rows_cols(pick_second_low, back)
    output = (
        middle
        + weight_first[:, None] * picked_first[:, :part_width]
        + weight_second[:, None] * picked_second[:, :part_width]
    ).astype(BF)

    grad_weight = (slot_grad.astype(F32) * slot_gate).astype(BF)
    gate_out = share_rows(cols_cols(slot_hidden, grad_gate_pre))
    up_out = share_rows(cols_cols(slot_hidden, grad_up_pre))
    down_out = share_rows(cols_cols(grad_weight, activated))

    tail = 2 * part_width
    share_first_grad = picked_first[:, tail] + picked_first[:, tail + 1]
    share_second_grad = picked_second[:, tail] + picked_second[:, tail + 1]
    both = picked_first + picked_second
    stat_second = both[:, tail + 2] + both[:, tail + 3]
    grad_hidden_loc = both[:, part_width:tail]
    grad_local = cotangent.astype(F32)
    _, pull_gates = jax.vjp(lambda given: gate_pair(given, hot_first, hot_second), logits)
    (grad_logits,) = pull_gates((kept[:, 0] * share_first_grad, kept[:, 1] * share_second_grad))
    grad_logits_low = grad_logits.astype(BF)
    grad_router_rows = rows_rows(grad_logits_low, router_w)
    stat_total = stat_second + jnp.sum(normed_second * gain_second * grad_router_rows, 1)

    def take_cols(full_rows):
        return lax.dynamic_slice_in_dim(full_rows, narrow_at * part_width, part_width, 1)

    grad_hidden_loc = grad_hidden_loc + take_cols(grad_router_rows)
    normed_second_loc = take_cols(normed_second)
    grad_gain_second = jnp.sum(grad_hidden_loc * normed_second_loc, 0)
    grad_middle = grad_local + scale_second * (
        gain_second_loc * grad_hidden_loc - normed_second_loc * stat_total[:, None] / full_width
    )
    grad_router_w = cols_cols(hidden_second, grad_logits_low)
    grad_branch = lax.all_gather(grad_middle.astype(BF), "narrow", axis=1, tiled=True)
    grad_attended = rows_cols(grad_branch, out_w).astype(BF)
    grad_out_w = cols_cols(grad_branch, attended)
    grad_qs, grad_ks, grad_vs = [], [], []
    for head in range(heads):
        query, key, value, weights = saved[head]
        grad_out = head_cols(grad_attended, head)
        grad_weights = rows_rows(grad_out, value)
        inner = jnp.sum(weights * grad_weights, -1, keepdims=True)
        grad_scores = (weights * (grad_weights - inner)).astype(BF)
        grad_q = rows_cols(grad_scores, key) * score_scale
        grad_k = cols_cols(grad_scores, query) * score_scale
        grad_qs.append(rotate(grad_q, cosines, -sines).astype(BF))
        grad_ks.append(rotate(grad_k, cosines, -sines).astype(BF))
        grad_vs.append(cols_cols(weights.astype(BF), grad_out).astype(BF))
    grad_query_raw = jnp.concatenate(grad_qs, 1)
    grad_key_raw = jnp.concatenate(grad_ks, 1)
    grad_value_raw = jnp.concatenate(grad_vs, 1)
    grad_hidden_first = (
        rows_rows(grad_query_raw, query_w)
        + rows_rows(grad_key_raw, key_w)
        + rows_rows(grad_value_raw, value_w)
    )
    stat_first = jnp.sum(normed_first * gain_first * grad_hidden_first, 1, keepdims=True)
    extras = jnp.pad(jnp.concatenate(two_parts(stat_first), 1), ((0, 0), (0, 126)))
    grad_hidden_low = grad_hidden_first.astype(BF)
    first_parts = []
    for part in range(narrow_count):
        first_parts += [grad_hidden_low[:, part * part_width : (part + 1) * part_width], extras]
    first_back = lax.psum_scatter(
        jnp.concatenate(first_parts, 1), "narrow", scatter_dimension=1, tiled=True
    ).astype(F32)
    grad_first_loc = first_back[:, :part_width]
    stat_first = first_back[:, part_width : part_width + 1]
    stat_first = stat_first + first_back[:, part_width + 1 : part_width + 2]
    normed_first_loc = take_cols(normed_first)
    grad_gain_first = jnp.sum(grad_first_loc * normed_first_loc, 0)
    grad_tokens = grad_middle + scale_first * (
        gain_first_loc * grad_first_loc - normed_first_loc * stat_first / full_width
    )
    grad_attn_w = jnp.concatenate(
        [
            cols_cols(hidden_first, grad_query_raw).astype(BF),
            cols_cols(hidden_first, grad_key_raw).astype(BF),
            cols_cols(hidden_first, grad_value_raw).astype(BF),
            grad_out_w.astype(BF),
        ],
        1,
    )
    attn_summed = lax.psum_scatter(
        grad_attn_w, "wide", scatter_dimension=0, tiled=True
    ).astype(F32)
    router_summed = lax.psum_scatter(grad_router_w, "wide", scatter_dimension=0, tiled=True)
    gains_summed = lax.psum(jnp.stack([grad_gain_first, grad_gain_second]), "wide")
    return (
        output,
        grad_tokens,
        gains_summed[0],
        attn_summed[:, :part_width],
        attn_summed[:, part_width : 2 * part_width],
        attn_summed[:, 2 * part_width : 3 * part_width],
        attn_summed[:, 3 * part_width :],
        gains_summed[1],
        router_summed,
        gate_out,
        up_out,
        down_out,
    )


def per_device(
    tokens, gain_attn, w_query, w_key, w_value, w_out, gain_ffn, w_router,
    w_gate, w_up, w_down, segment, parents, expert_ids, slot_order, cotangent,
):
    if lax.axis_size("wide") != 8 or lax.axis_size("narrow") != 4:
        return plain_device(
            tokens, gain_attn, w_query, w_key, w_value, w_out, gain_ffn, w_router,
            w_gate, w_up, w_down, segment, parents, expert_ids, slot_order, cotangent,
        )
    (
        in_w, out_w, expert_w, slot_mid, slot_grad, slot_gate, middle, hidden_first,
        token_parts, qkv, probs, attended, stat, rope, picks, columns,
    ) = front_call(
        tokens, cotangent, jnp.stack([gain_attn, gain_ffn]), (w_query, w_key, w_value, w_out),
        w_router.T, (w_gate, w_up, w_down), segment, parents, expert_ids.T, slot_order,
    )
    back_mid, back_exp, back_ext, grads, early_experts = mid_call(
        slot_mid, slot_grad, slot_gate, token_parts, expert_w
    )
    (
        output, grad_tokens, summed, small, router, experts,
    ) = tail_call(
        back_mid, back_exp, back_ext, grads, picks, stat, columns, middle, cotangent, tokens,
        token_parts, qkv, probs, attended, rope, hidden_first, in_w, out_w,
    )
    gate_out, up_out, down_out, output, grad_tokens, grad_q, grad_k, grad_v, grad_o = finish_call(
        early_experts, experts, output, grad_tokens, summed
    )
    return (
        output, grad_tokens, small[5], grad_q, grad_k, grad_v, grad_o, small[4],
        router[:EXPERTS].T, gate_out, up_out, down_out,
    )


def solution(mesh):
    pair = P("wide", "narrow")
    part = P("narrow")
    rows = P("wide", None)
    cube = P("wide", None, "narrow")
    return jax.shard_map(
        per_device,
        mesh=mesh,
        in_specs=(
            pair, part, pair, pair, pair, pair, part, rows, cube, cube, cube,
            rows, rows, rows, rows, pair,
        ),
        out_specs=(
            pair, pair, part, pair, pair, pair, pair, part, rows, cube, cube, cube,
        ),
        check_vma=False,
    )
```

```python
import math

import jax
import jax.numpy as jnp
from jax import lax
from jax.experimental import pallas as pl
from jax.experimental.pallas import tpu as pltpu
from jax.sharding import PartitionSpec as P

HEAD_DIM = 128
EXPERTS = 4
SEGS = 13
CAP = 144
SLOTS = EXPERTS * CAP
NORM_EPS = 1e-05
NEG_FILL = -1e30
ROPE_BASE = 10000.0
BF = jnp.bfloat16
F32 = jnp.float32


def mm(left, right, dims):
    return lax.dot_general(left, right, (dims, ((), ())), preferred_element_type=F32)


def rows_cols(left, right):
    return mm(left, right, ((1,), (0,)))


def rows_rows(left, right):
    return mm(left, right, ((1,), (1,)))


def cols_cols(left, right):
    return mm(left, right, ((0,), (0,)))


def tree_layout(segment_row, parent_row):
    seg_ids = jnp.arange(SEGS, dtype=jnp.int32)
    member = segment_row[:, None] == seg_ids[None, :]
    parent_of = (parent_row[:, None] == seg_ids[None, :]) & (seg_ids[:, None] != 0)
    itself = seg_ids[:, None] == seg_ids[None, :]
    reach = itself
    for _ in range(3):
        reach = itself | jnp.any(parent_of[:, :, None] & reach[None, :, :], axis=1)
    counts = member.astype(jnp.int32)
    lengths = jnp.sum(counts, 0)
    starts = jnp.sum(jnp.where(seg_ids[None, :] < seg_ids[:, None], lengths[None, :], 0), 1)
    before = jnp.sum(jnp.where(reach, lengths[None, :], 0), 1) - lengths
    row_at = jnp.arange(segment_row.shape[0], dtype=jnp.int32)
    places = jnp.sum(counts * (before - starts)[None, :], 1) + row_at
    member_low = member.astype(BF)
    lineage = rows_cols(member_low, reach.astype(BF)).astype(BF)
    shared = rows_rows(lineage, member_low) > 0.5
    seen = shared & (row_at[None, :] <= row_at[:, None])
    return seen, places.astype(F32)


def route(expert_row, slot_rank):
    expert_range = jnp.arange(EXPERTS, dtype=jnp.int32)
    hot_first = (expert_row[:, 0:1] == expert_range[None, :]).astype(F32)
    hot_second = (expert_row[:, 1:2] == expert_range[None, :]).astype(F32)
    earlier = (slot_rank[None, :] < slot_rank[:, None]).astype(BF)
    count_first = rows_cols(earlier, hot_first.astype(BF))
    count_second = rows_cols(earlier, hot_second.astype(BF))
    ahead_first = jnp.sum(count_first * hot_first, 1)
    ahead_second = jnp.sum((count_second + jnp.sum(hot_first, 0)[None, :]) * hot_second, 1)
    slot_index = jnp.stack([ahead_first, ahead_second], 1).astype(jnp.int32)
    kept = slot_index < CAP
    flat_slot = jnp.where(kept, expert_row * CAP + slot_index, SLOTS)
    slot_range = jnp.arange(SLOTS, dtype=jnp.int32)
    pick_first = flat_slot[:, 0:1] == slot_range[None, :]
    pick_second = flat_slot[:, 1:2] == slot_range[None, :]
    return hot_first, hot_second, kept.astype(F32), pick_first, pick_second


def rotate(vectors, cosines, sines):
    half_dim = HEAD_DIM // 2
    first_half = vectors[..., :half_dim]
    second_half = vectors[..., half_dim:]
    return jnp.concatenate(
        [
            first_half * cosines - second_half * sines,
            second_half * cosines + first_half * sines,
        ],
        -1,
    )


def gate_pair(logits, hot_first, hot_second):
    chances = jax.nn.softmax(logits, axis=-1)
    first_share = jnp.sum(chances * hot_first, 1)
    second_share = jnp.sum(chances * hot_second, 1)
    pair_total = first_share + second_share
    return (first_share / pair_total, second_share / pair_total)


def two_parts(column):
    high = column.astype(BF)
    return high, (column - high.astype(F32)).astype(BF)


MESH = pl.DeviceIdType.MESH
NEAR = 3


def low_dot(left, right):
    return jnp.dot(left, right, preferred_element_type=F32)


def places_of(n):
    return [lax.rem(n + step, 4) for step in (1, 2, 3)], [lax.rem(n + 4 - step, 4) for step in (1, 2, 3)]


def plane_of(chip):
    x, y = lax.rem(chip, 2), chip // 2
    return [2 * y + 1 - x, 2 * (1 - y) + x, 2 * (1 - y) + 1 - x]


def greet(narrow_peers, plane_peers, chip, core, mate):
    barrier = pltpu.get_barrier_semaphore()
    count = 0
    for peer in narrow_peers:
        pl.semaphore_signal(barrier, inc=1, device_id={"narrow": peer}, device_id_type=MESH)
        count += 1
    for peer in plane_peers:
        pl.semaphore_signal(
            barrier, inc=1, device_id={"wide": 2 * peer + core}, device_id_type=MESH
        )
        count += 1
    if mate:
        pl.semaphore_signal(
            barrier, inc=1, device_id={"wide": 2 * chip + 1 - core}, device_id_type=MESH
        )
        count += 1
    pl.semaphore_wait(barrier, count)


class Links:
    def __init__(self, sent, landed, local):
        self.sent, self.landed, self.local = sent, landed, local
        self.used, self.local_used = 0, 0
        self.waits = []

    def slot(self):
        self.used += 1
        return self.used - 1

    def send(self, source, target, device, slot, when=None):
        copy = pltpu.make_async_remote_copy(
            src_ref=source,
            dst_ref=target,
            send_sem=self.sent.at[slot],
            recv_sem=self.landed.at[slot],
            device_id=device,
            device_id_type=MESH,
        )
        if when is None:
            copy.start()
        else:
            pl.when(when)(copy.start)
        self.waits.append((copy, when))

    def land(self, target, device, slot, when=None):
        copy = pltpu.make_async_remote_copy(
            src_ref=target,
            dst_ref=target,
            send_sem=self.sent.at[slot],
            recv_sem=self.landed.at[slot],
            device_id=device,
            device_id_type=MESH,
        )
        if when is None:
            copy.wait_recv()
        else:
            pl.when(when)(copy.wait_recv)

    def move(self, source, target):
        copy = pltpu.make_async_copy(source, target, self.local.at[self.local_used])
        self.local_used += 1
        copy.start()
        self.waits.append((copy, "local"))
        return copy

    def finish(self):
        for copy, when in self.waits:
            if when == "local":
                copy.wait()
            elif when is None:
                copy.wait_send()
            else:
                pl.when(when)(copy.wait_send)


class Chain:
    def __init__(self, links, n, block):
        self.links, self.n, self.block = links, n, block
        self.slots = [(links.slot(), links.slot()) for _ in range(3)]

    def start(self, step):
        n, links = self.n, self.links
        right, left = self.slots[step]
        block = self.block(lax.rem(n + 4 - step, 4))
        links.send(
            block, block, {"narrow": lax.rem(n + 1, 4)}, right,
            (n < 3) & (n >= step),
        )
        block = self.block(lax.rem(n + step, 4))
        links.send(
            block, block, {"narrow": lax.rem(n + 3, 4)}, left,
            (n > 0) & (n + step <= 3),
        )

    def land(self, step):
        n, links = self.n, self.links
        right, left = self.slots[step]
        links.land(
            self.block(lax.rem(n + 7 - step, 4)), {"narrow": lax.rem(n + 3, 4)}, right,
            n >= step + 1,
        )
        links.land(
            self.block(lax.rem(n + 1 + step, 4)), {"narrow": lax.rem(n + 1, 4)}, left,
            n + 1 + step <= 3,
        )


class LineSum:
    def __init__(self, links, n, outbox, inbox):
        self.links, self.n, self.outbox, self.inbox = links, n, outbox, inbox
        self.inner = (n == 1) | (n == 2)
        self.outer = (n == 0) | (n == 3)
        self.targets = [3 - n, lax.rem(3 * n + 2, 5), lax.rem(2 * n + 1, 5)]
        self.next = 1 + lax.rem(n, 2)
        self.slots = [links.slot() for _ in range(6)]

    def put(self, step, part):
        links, outbox, inbox = self.links, self.outbox, self.inbox
        outbox[step] = part.astype(BF)
        goal = {"narrow": self.next if step == 0 else self.targets[step]}
        far, near = self.slots[2 * step], self.slots[2 * step + 1]
        if step == 0:
            links.send(outbox.at[0], inbox.at[3], goal, far, self.outer)
            links.send(outbox.at[0], inbox.at[0], goal, near, self.inner)
        elif step == 1:
            links.send(outbox.at[1], inbox.at[1], goal, far, self.outer)
            links.send(outbox.at[1], inbox.at[0], goal, near, self.inner)
        else:
            links.send(outbox.at[2], inbox.at[2], goal, far, self.outer)

    def join(self):
        links, outbox, inbox = self.links, self.outbox, self.inbox
        home = {"narrow": 3 * (self.n // 2)}
        links.land(inbox.at[3], home, self.slots[0], self.inner)

        @pl.when(self.inner)
        def _():
            outbox[2] = (outbox[2].astype(F32) + inbox[3].astype(F32)).astype(BF)

    def relay(self):
        self.join()
        goal = {"narrow": self.targets[2]}
        self.links.send(
            self.outbox.at[2], self.inbox.at[1], goal, self.slots[5], self.inner
        )

    def early(self, own):
        links, inbox = self.links, self.inbox
        other = {"narrow": lax.rem(self.n + 1, 4)}
        links.land(inbox.at[0], other, self.slots[1], self.inner)
        links.land(inbox.at[0], other, self.slots[3], self.outer)
        links.land(inbox.at[1], other, self.slots[2], self.inner)

        @pl.when(self.outer)
        def _():
            inbox[1] = jnp.zeros(inbox.shape[1:], BF)

        return own + inbox[0].astype(F32) + inbox[1].astype(F32)

    def total(self, own):
        links, inbox = self.links, self.inbox
        outer, inner = self.outer, self.inner
        other = {"narrow": lax.rem(self.n + 1, 4)}
        links.land(inbox.at[0], other, self.slots[1], inner)
        links.land(inbox.at[0], other, self.slots[3], outer)
        links.land(inbox.at[1], other, self.slots[2], inner)
        links.land(inbox.at[1], other, self.slots[5], outer)
        links.land(inbox.at[2], other, self.slots[4], inner)

        @pl.when(outer)
        def _():
            inbox[2] = jnp.zeros(inbox.shape[1:], BF)

        for index in range(3):
            own = own + inbox[index].astype(F32)
        return own


class PlaneGather:
    def __init__(self, links, chip, core, plane, mate, source, blocks):
        self.links, self.chip, self.core, self.plane, self.mate = links, chip, core, plane, mate
        self.blocks = blocks
        self.slots = [links.slot() for _ in range(4)]
        self.mate_slots = [links.slot() for _ in range(4)]
        own = 2 * chip + core
        for side in range(2):
            links.send(source, blocks.at[own], self.at_plane(plane[side]), self.slots[side])
        links.send(source, blocks.at[own], mate, self.mate_slots[3])

    def at_plane(self, peer):
        return {"wide": 2 * peer + self.core}

    def half(self, peer, side):
        rows = self.blocks.shape[1] // 2
        return self.blocks.at[2 * peer + self.core, pl.ds(side * rows, rows), :]

    def pass_on(self):
        links, plane = self.links, self.plane
        for side in range(2):
            block = self.blocks.at[2 * plane[side] + self.core]
            links.land(block, self.at_plane(plane[side]), self.slots[side])
            part = self.half(plane[side], side)
            links.send(part, part, self.at_plane(plane[1 - side]), self.slots[2 + side])
            links.send(block, block, self.mate, self.mate_slots[side])

    def far(self):
        links, plane = self.links, self.plane
        for side in range(2):
            links.land(
                self.half(plane[2], side), self.at_plane(plane[1 - side]), self.slots[2 + side]
            )
        block = self.blocks.at[2 * plane[2] + self.core]
        links.send(block, block, self.mate, self.mate_slots[2])

    def finish(self):
        links, plane = self.links, self.plane
        for step in range(NEAR):
            block = self.blocks.at[2 * plane[step] + 1 - self.core]
            links.land(block, self.mate, self.mate_slots[step])
        links.land(self.blocks.at[2 * self.chip + 1 - self.core], self.mate, self.mate_slots[3])


FRONT_SLOTS = 104


def front_body(
    tok_ref, cot_ref, gains_ref, wq_ref, wk_ref, wv_ref, wo_ref, router_ref, gate_ref, up_ref,
    down_ref, segment_ref, parents_ref, ids_ref, rank_ref,
    qkvw_out, outw_out, expert_out, x_out, dy_out, gate_out, middle_out, hidden_out,
    tokens_out, qkv_out, prob_out, att_out, stat_out, rope_out, pick_out, cols_out,
    raw, moved_ref, pack, tok_pack, qkvw, outw, cot_send, y_send, br_send, br_recv, stat_send, stat_recv,
    gate_send, sent, landed, local,
):
    n = lax.axis_index("narrow")
    w = lax.axis_index("wide")
    chip, core = w // 2, lax.rem(w, 2)
    to_z, from_z = places_of(n)
    plane = plane_of(chip)
    links = Links(sent, landed, local)
    mate = {"wide": 2 * chip + 1 - core}

    def at_plane(peer):
        return {"wide": 2 * peer + core}

    token_count, part_width = tok_ref.shape
    rows_each = raw.shape[1]
    raw_loads = [
        links.move(source, raw.at[kind_at]) for kind_at, source in enumerate((gate_ref, up_ref, down_ref))
    ]
    links.waits = []
    greet(to_z, plane, chip, core, True)

    def by_expert(kind_at):
        raw_loads[kind_at].wait()
        for expert in range(EXPERTS):
            for start in range(0, rows_each, 64):
                moved_ref[kind_at, expert, start : start + 64, :] = raw[
                    kind_at, start : start + 64, expert, :
                ]

    tok_pack[0:token_count, :] = tok_ref[...]
    tok_pack[token_count : token_count + 2, :] = gains_ref[...]
    tokens_out[n] = tok_pack[...]
    tok_chain = Chain(links, n, lambda m: tokens_out.at[m])
    tok_chain.start(0)
    wide_shape = (token_count, token_count)
    row_at = lax.broadcasted_iota(jnp.int32, wide_shape, 0)
    col_at = lax.broadcasted_iota(jnp.int32, wide_shape, 1)
    seg_row, rank_row = segment_ref[...], rank_ref[...]
    first_row, second_row = ids_ref[0:1, :], ids_ref[1:2, :]
    stacked = [item.astype(F32) for item in (seg_row, rank_row, first_row, second_row)]
    columns = jnp.concatenate(stacked + [jnp.zeros((124, token_count), F32)], 0).T
    cols_out[...] = columns
    columns = columns.astype(jnp.int32)
    seg_col, rank_col = columns[:, 0:1], columns[:, 1:2]
    segs = parents_ref.shape[1]
    of_seg = lax.broadcasted_iota(jnp.int32, (token_count, segs), 1) == seg_col
    par_col = jnp.sum(
        jnp.where(of_seg, parents_ref[...].astype(F32), 0.0), 1, keepdims=True
    ).astype(jnp.int32)
    seen = ((seg_row == seg_col) | (seg_row == par_col) | (seg_row == 0)) & (col_at <= row_at)
    spots = jnp.sum(jnp.where(seen, 1.0, 0.0), 1, keepdims=True) - 1.0
    lane_at = lax.broadcasted_iota(jnp.int32, (token_count, HEAD_DIM), 1)
    turn = lax.rem(lane_at, HEAD_DIM // 2).astype(F32) * (-2.0 / HEAD_DIM * math.log(ROPE_BASE))
    angles = spots * jnp.exp(turn)
    cosines = jnp.cos(angles)
    sines = jnp.sin(angles) * jnp.where(lane_at < HEAD_DIM // 2, -1.0, 1.0)
    rope_out[0] = cosines
    rope_out[1] = sines
    kind = lax.broadcasted_iota(jnp.int32, (8, token_count), 0)
    hot_first = jnp.where(kind == first_row, 1.0, 0.0)
    hot_second = jnp.where(kind == second_row, 1.0, 0.0)
    earlier = jnp.where(rank_col < rank_row, 1.0, 0.0).astype(BF)
    count_first = low_dot(hot_first.astype(BF), earlier)
    count_second = low_dot(hot_second.astype(BF), earlier)
    count_second = count_second + jnp.sum(hot_first, 1, keepdims=True)
    slot_first = jnp.sum(count_first * hot_first, 0, keepdims=True)
    slot_second = jnp.sum(count_second * hot_second, 0, keepdims=True)
    kept_first = jnp.where(slot_first < CAP, 1.0, 0.0)
    kept_second = jnp.where(slot_second < CAP, 1.0, 0.0)
    flat_first = jnp.where(slot_first < CAP, first_row * CAP + slot_first.astype(jnp.int32), SLOTS)
    flat_second = jnp.where(
        slot_second < CAP, second_row * CAP + slot_second.astype(jnp.int32), SLOTS
    )
    slot_at = lax.broadcasted_iota(jnp.int32, (SLOTS, token_count), 0)
    pick_first = jnp.where(slot_at == flat_first, 1.0, 0.0)
    pick_second = jnp.where(slot_at == flat_second, 1.0, 0.0)
    pick_out[0] = pick_first.astype(BF)
    pick_out[1] = pick_second.astype(BF)
    pick_both = (pick_first + pick_second).astype(BF)

    def column_block(array):
        return lambda m: array.at[:, pl.ds(pl.multiple_of(m * part_width, part_width), part_width)]

    def slot_block(array, owner):
        return array.at[
            pl.ds(pl.multiple_of(owner * CAP, 16), CAP),
            pl.ds(pl.multiple_of(n * part_width, part_width), part_width),
        ]

    def dispatch(rows, buffer, array):
        slots = [links.slot() for _ in range(NEAR)]
        buffer[...] = low_dot(pick_both, rows).astype(BF)
        for step in range(NEAR):
            links.send(
                buffer.at[pl.ds(pl.multiple_of(plane[step] * CAP, 16), CAP), :],
                slot_block(array, chip), at_plane(plane[step]), slots[step],
            )
        own = links.move(
            buffer.at[pl.ds(pl.multiple_of(chip * CAP, 16), CAP), :], slot_block(array, chip)
        )
        return slots, own

    def arrive(array, state):
        slots, own = state
        for step in range(NEAR):
            links.land(slot_block(array, plane[step]), at_plane(plane[step]), slots[step])
        own.wait()
        links.waits = [item for item in links.waits if item[0] is not own]

    dy_state = dispatch(cot_ref[...], cot_send, dy_out)
    dy_chain = Chain(links, n, column_block(dy_out))

    pack[:, 0:512] = wq_ref[...]
    pack[:, 512:1024] = wk_ref[...]
    pack[:, 1024:1536] = wv_ref[...]
    router_rows = jnp.concatenate(
        [router_ref[...].astype(F32), jnp.zeros((128 - EXPERTS, rows_each), F32)], 0
    )
    pack[:, 1536:1664] = router_rows.T.astype(BF)
    in_gather = PlaneGather(links, chip, core, plane, mate, pack, qkvw)
    qkvw[w] = pack[...]
    outw[w] = wo_ref[...]

    tok_chain.land(0)
    tok_chain.start(1)
    by_expert(0)
    tok_chain.land(1)
    tok_chain.start(2)
    arrive(dy_out, dy_state)
    dy_chain.start(0)
    tok_chain.land(2)
    in_gather.pass_on()
    out_gather = PlaneGather(links, chip, core, plane, mate, wo_ref, outw)
    total = jnp.zeros((token_count, 1), F32)
    for m in range(4):
        part = tokens_out[m, 0:token_count, :].astype(F32)
        total = total + jnp.sum(part * part, 1, keepdims=True)
    scale_first = lax.rsqrt(total * (1.0 / (4 * part_width)) + NORM_EPS)
    for m in range(4):
        part = tokens_out[m, 0:token_count, :].astype(F32)
        gain = tokens_out[m, token_count : token_count + 1, :].astype(F32)
        hidden_out[:, m * part_width : (m + 1) * part_width] = (part * scale_first * gain).astype(BF)

    by_expert(1)

    in_gather.far()
    out_gather.pass_on()
    in_gather.finish()
    saved_in = links.move(qkvw, qkvw_out)

    expert_slots = [[links.slot() for _ in range(NEAR)] for _ in range(3)]
    expert_mate = [[links.slot() for _ in range(4)] for _ in range(3)]
    def set_out(kind_at):
        for step in range(NEAR):
            links.send(
                moved_ref.at[kind_at, plane[step]], expert_out.at[kind_at, chip, core],
                at_plane(plane[step]), expert_slots[kind_at][step],
            )
        links.send(
            moved_ref.at[kind_at, chip], expert_out.at[kind_at, chip, core], mate,
            expert_mate[kind_at][3],
        )
        links.move(moved_ref.at[kind_at, chip], expert_out.at[kind_at, chip, core])

    set_out(0)
    set_out(1)

    def pass_on(kind_at):
        for step in range(NEAR):
            block = expert_out.at[kind_at, plane[step], core]
            links.land(block, at_plane(plane[step]), expert_slots[kind_at][step])
            links.send(block, block, mate, expert_mate[kind_at][step])

    def all_there(kind_at):
        for step in range(NEAR):
            links.land(
                expert_out.at[kind_at, plane[step], 1 - core], mate, expert_mate[kind_at][step]
            )
        links.land(expert_out.at[kind_at, chip, 1 - core], mate, expert_mate[kind_at][3])

    dy_chain.land(0)
    dy_chain.start(1)
    by_expert(2)

    hidden = hidden_out[...]
    score_scale = HEAD_DIM ** (-0.5)
    raws = []
    for part in range(3):
        weight = qkvw[:, :, part * 512 : (part + 1) * 512].reshape(4 * part_width, part_width)
        raws.append(low_dot(hidden, weight))
    for head in range(part_width // HEAD_DIM):
        cols = slice(head * HEAD_DIM, (head + 1) * HEAD_DIM)
        turned = []
        for part in range(2):
            raw = raws[part][:, cols]
            turned.append(
                (raw * cosines + pltpu.roll(raw, HEAD_DIM // 2, 1) * sines).astype(BF)
            )
            qkv_out[part, :, cols] = turned[part]
        value = raws[2][:, cols].astype(BF)
        qkv_out[2, :, cols] = value
        scores = rows_rows(turned[0], turned[1]) * score_scale
        scores = jnp.where(seen, scores, NEG_FILL)
        exps = jnp.exp(scores - jnp.max(scores, 1, keepdims=True))
        weights = exps / jnp.sum(exps, 1, keepdims=True)
        prob_out[head] = weights
        att_out[:, cols] = low_dot(weights.astype(BF), value).astype(BF)

    dy_chain.land(1)
    dy_chain.start(2)
    out_gather.far()

    out_gather.finish()
    links.move(outw, outw_out)

    attended = att_out[...]

    def branch(m):
        weight = outw[pl.ds(2 * m, 2)].reshape(part_width, part_width)
        return rows_rows(attended, weight)

    branch_sum = LineSum(links, n, br_send, br_recv)
    for step in range(NEAR):
        branch_sum.put(step, branch(branch_sum.targets[step]))
    middle = tok_ref[...].astype(F32) + branch(n)
    branch_sum.relay()
    middle = branch_sum.total(middle)
    middle_out[...] = middle
    x_state = dispatch(middle.astype(BF), y_send, x_out)

    def cap_block(owner):
        return lambda m: x_out.at[
            pl.ds(pl.multiple_of(owner * CAP, 16), CAP),
            pl.ds(pl.multiple_of(m * part_width, part_width), part_width),
        ]

    x_chains = [Chain(links, n, cap_block(owner)) for owner in (chip, *plane)]
    x_slots, x_own = x_state
    x_own.wait()
    links.waits = [item for item in links.waits if item[0] is not x_own]
    x_chains[0].start(0)

    set_out(2)

    gain_second = gains_ref[1:2, :].astype(F32)
    router = qkvw[pl.ds(2 * n, 2), :, 1536:1664].reshape(part_width, 128)
    logit_part = mm(router, (middle * gain_second).astype(BF), ((0,), (1,)))[0:8, :]
    square = middle * middle
    square_high = square.astype(BF)
    square_low = (square - square_high.astype(F32)).astype(BF)
    ones = jnp.ones((8, part_width), BF)
    square_sum = rows_rows(ones, square_high) + rows_rows(ones, square_low)
    stat = jnp.where(kind == 4, square_sum, logit_part)
    stat_send[...] = stat
    stat_slots = [links.slot() for _ in range(NEAR)]
    for step in range(NEAR):
        links.send(stat_send, stat_recv.at[step], {"narrow": to_z[step]}, stat_slots[step])

    for step in range(NEAR):
        links.land(slot_block(x_out, plane[step]), at_plane(plane[step]), x_slots[step])
        x_chains[1 + step].start(0)
    for step in range(NEAR):
        links.land(stat_recv.at[step], {"narrow": from_z[step]}, stat_slots[step])
        stat = stat + stat_recv[step]
    stat_out[...] = stat
    scale_row = lax.rsqrt(stat[4:5, :] * (1.0 / (4 * part_width)) + NORM_EPS)
    logits = jnp.where(kind < EXPERTS, stat * scale_row, NEG_FILL)
    chances = jnp.exp(logits - jnp.max(logits, 0, keepdims=True))
    chances = chances / jnp.sum(chances, 0, keepdims=True)
    share_first = jnp.sum(chances * hot_first, 0, keepdims=True)
    share_second = jnp.sum(chances * hot_second, 0, keepdims=True)
    both = share_first + share_second
    weighted = pick_first * (share_first / both) + pick_second * (share_second / both)
    slot_gate = jnp.sum(weighted, 1, keepdims=True)
    gate_send[...] = jnp.broadcast_to(slot_gate, (SLOTS, 128))

    def gate_rows(array, owner):
        return array.at[pl.ds(pl.multiple_of(owner * CAP, 16), CAP), :]

    gate_slots = [links.slot() for _ in range(NEAR)]
    for step in range(NEAR):
        links.send(
            gate_rows(gate_send, plane[step]), gate_rows(gate_out, chip),
            at_plane(plane[step]), gate_slots[step],
        )
    links.move(gate_rows(gate_send, chip), gate_rows(gate_out, chip))

    for step in range(2):
        for chain in x_chains:
            chain.land(step)
            chain.start(step + 1)
        pass_on(step)
    for chain in x_chains:
        chain.land(2)
    dy_chain.land(2)
    for step in range(NEAR):
        links.land(gate_rows(gate_out, plane[step]), at_plane(plane[step]), gate_slots[step])
    pass_on(2)
    for kind_at in range(3):
        all_there(kind_at)
    links.finish()


def front_call(tokens, cotangent, gains, weights, router, experts, segment, parents, ids, rank):
    token_count, part_width = tokens.shape
    full = 4 * part_width
    rows_each, _, hidden_width = experts[0].shape
    heads = part_width // HEAD_DIM
    vmem = pl.BlockSpec(memory_space=pltpu.VMEM)
    hbm = pl.BlockSpec(memory_space=pl.ANY)

    def arr(shape, dtype):
        return jax.ShapeDtypeStruct(shape, dtype)

    return pl.pallas_call(
        front_body,
        out_shape=(
            arr((8, rows_each, 1664), BF),
            arr((8, rows_each, part_width), BF),
            arr((3, 4, 2, rows_each, hidden_width), BF),
            arr((SLOTS, full), BF),
            arr((SLOTS, full), BF),
            arr((SLOTS, 128), F32),
            arr((token_count, part_width), F32),
            arr((token_count, full), BF),
            arr((4, token_count + 16, part_width), BF),
            arr((3, token_count, part_width), BF),
            arr((heads, token_count, token_count), F32),
            arr((token_count, part_width), BF),
            arr((8, token_count), F32),
            arr((2, token_count, HEAD_DIM), F32),
            arr((2, SLOTS, token_count), BF),
            arr((token_count, 128), F32),
        ),
        in_specs=[vmem] * 8 + [hbm] * 3 + [vmem] * 4,
        out_specs=(hbm, hbm, hbm) + (vmem,) * 13,
        scratch_shapes=[
            pltpu.VMEM((3, rows_each, EXPERTS, hidden_width), BF),
            pltpu.VMEM((3, EXPERTS, rows_each, hidden_width), BF),
            pltpu.VMEM((rows_each, 1664), BF),
            pltpu.VMEM((token_count + 16, part_width), BF),
            pltpu.VMEM((8, rows_each, 1664), BF),
            pltpu.VMEM((8, rows_each, part_width), BF),
            pltpu.VMEM((SLOTS, part_width), BF),
            pltpu.VMEM((SLOTS, part_width), BF),
            pltpu.VMEM((NEAR, token_count, part_width), BF),
            pltpu.VMEM((NEAR + 1, token_count, part_width), BF),
            pltpu.VMEM((8, token_count), F32),
            pltpu.VMEM((NEAR, 8, token_count), F32),
            pltpu.VMEM((SLOTS, 128), F32),
            pltpu.SemaphoreType.DMA((FRONT_SLOTS,)),
            pltpu.SemaphoreType.DMA((FRONT_SLOTS,)),
            pltpu.SemaphoreType.DMA((16,)),
        ],
        compiler_params=pltpu.CompilerParams(
            collective_id=0, has_side_effects=True, vmem_limit_bytes=60 * 1024 * 1024
        ),
        cost_estimate=pl.CostEstimate(
            flops=6_000_000_000, bytes_accessed=60_000_000, transcendentals=400_000
        ),
        name="front",
    )(tokens, cotangent, gains, *weights, router, *experts, segment, parents, ids, rank)


MID_SLOTS = 48


TILE = 512


def mid_body(
    x_ref, dy_ref, gate_ref, tokens_ref, w_ref,
    back_mid_out, back_exp_out, last_exp_out, extra_out, grads_out, expert_out,
    weights, hidden, graded_send, hidden_cat, graded_cat, act_cat, gate_cat, up_cat,
    turned, rs_send, rs_recv, ext_send, ext_recv, sent, landed, local,
):
    n = lax.axis_index("narrow")
    w = lax.axis_index("wide")
    chip, core = w // 2, lax.rem(w, 2)
    to_z, from_z = places_of(n)
    plane = plane_of(chip)
    links = Links(sent, landed, local)
    mate = {"wide": 2 * chip + 1 - core}
    slots, full = hidden.shape
    part_width = full // 4
    rows_each = full // 8
    half = full // 2
    hidden_width = weights.shape[2]

    x_load = links.move(x_ref, hidden)
    loads = [
        links.move(
            w_ref.at[kind, c, k],
            weights.at[kind, pl.ds((2 * c + k) * rows_each, rows_each), :],
        )
        for kind in range(3)
        for c in range(4)
        for k in range(2)
    ]
    links.waits = []
    greet(to_z, plane, chip, core, True)

    slot_gate = gate_ref[:, 0:1]
    for c in range(4):
        theirs = pl.ds(pl.multiple_of((2 * c + 1 - core) * rows_each, rows_each), rows_each)
        ours = pl.ds(pl.multiple_of((2 * c + core) * rows_each, rows_each), rows_each)
        cols = slice(c * rows_each, (c + 1) * rows_each)
        graded_cat[core, :, cols] = (dy_ref[:, ours].astype(F32) * slot_gate).astype(BF)
        graded_send[:, cols] = (dy_ref[:, theirs].astype(F32) * slot_gate).astype(BF)

    def to_mate(source, target):
        slot = links.slot()
        links.send(source, target.at[core], mate, slot)
        return lambda: links.land(target.at[1 - core], mate, slot)

    graded_there = to_mate(graded_send, graded_cat)
    x_load.wait()
    total = jnp.zeros((slots, 1), F32)
    for m in range(4):
        part = hidden[:, m * part_width : (m + 1) * part_width].astype(F32)
        total = total + jnp.sum(part * part, 1, keepdims=True)
    scale = lax.rsqrt(total * (1.0 / full) + NORM_EPS)
    gain_row = tokens_ref.shape[1] - 15
    for m in range(4):
        cols = slice(m * part_width, (m + 1) * part_width)
        gain = tokens_ref[m, gain_row : gain_row + 1, :].astype(F32)
        hidden[:, cols] = (hidden[:, cols].astype(F32) * scale * gain).astype(BF)
    hidden_slots = [links.slot() for _ in range(4)]
    for c in range(4):
        cols = pl.ds(c * rows_each, rows_each)
        theirs = pl.ds(pl.multiple_of((2 * c + 1 - core) * rows_each, rows_each), rows_each)
        ours = pl.ds(pl.multiple_of((2 * c + core) * rows_each, rows_each), rows_each)
        links.send(hidden.at[:, theirs], hidden_cat.at[core, :, cols], mate, hidden_slots[c])
        hidden_cat[core, :, c * rows_each : (c + 1) * rows_each] = hidden[:, ours]
    for load in loads:
        load.wait()

    def one_tile(cols, rows):
        gate_pre = low_dot(hidden[rows, :], weights[0, :, cols])
        up_pre = low_dot(hidden[rows, :], weights[1, :, cols])
        act_raw = low_dot(dy_ref[rows, :], weights[2, :, cols])
        sigmoid = 1.0 / (1.0 + jnp.exp(-gate_pre))
        silu = gate_pre * sigmoid
        activated = (silu * up_pre).astype(BF)
        grad_act = act_raw * gate_ref[rows, 0:1]
        act_cat[core, rows, cols] = activated
        gate_cat[core, rows, cols] = (
            grad_act * up_pre * (sigmoid * (1.0 + gate_pre * (1.0 - sigmoid)))
        ).astype(BF)
        up_cat[core, rows, cols] = (grad_act * silu).astype(BF)
        return jnp.sum(act_raw * activated.astype(F32), 1, keepdims=True)

    def over_tiles(tile, body, carry):
        whole = hidden_width // tile
        carry = lax.fori_loop(
            0, whole, lambda t, value: body(pl.ds(pl.multiple_of(t * tile, tile), tile), value), carry
        )
        if hidden_width % tile:
            carry = body(pl.ds(whole * tile, hidden_width % tile), carry)
        return carry

    share = over_tiles(
        TILE,
        lambda cols, value: tuple(
            value[index] + one_tile(cols, pl.ds(index * (slots // 2), slots // 2))
            for index in range(2)
        ),
        (jnp.zeros((slots // 2, 1), F32),) * 2,
    )
    share = jnp.concatenate(share, 0)
    acts_there = [to_mate(item.at[core], item) for item in (act_cat, gate_cat, up_cat)]

    grad_gate, grad_up = gate_cat.at[core], up_cat.at[core]
    mid_sum = LineSum(links, n, rs_send.at[0], rs_recv.at[0])

    def mid_part(owner):
        rows = pl.ds(pl.multiple_of(owner * part_width, part_width), part_width)
        block = rows_rows(grad_gate[...], weights[0, rows, :])
        block = block + rows_rows(grad_up[...], weights[1, rows, :])
        return block, jnp.sum(hidden[:, rows].astype(F32) * block, 1, keepdims=True)

    stat = jnp.zeros((slots, 1), F32)
    for step in range(NEAR):
        block, part = mid_part(mid_sum.targets[step])
        mid_sum.put(step, block)
        stat = stat + part
    block, part = mid_part(n)
    back_mid_out[...] = block.astype(BF)
    stat = stat + part
    lane_at = lax.broadcasted_iota(jnp.int32, (slots, 128), 1)
    columns = jnp.where(lane_at == 0, share, jnp.where(lane_at == 1, stat, 0.0))
    high = columns.astype(BF)
    rest = (columns - high.astype(F32)).astype(BF)
    pick = jnp.where(
        lax.broadcasted_iota(jnp.int32, (8, 128), 0) == lax.broadcasted_iota(jnp.int32, (8, 128), 1),
        1.0, 0.0,
    ).astype(BF)
    extra = rows_rows(pick, high) + rows_rows(pick, rest)
    ext_send[...] = extra
    ext_slots = [links.slot() for _ in range(NEAR)]
    for step in range(NEAR):
        links.send(ext_send, ext_recv.at[step], {"narrow": to_z[step]}, ext_slots[step])

    expert_slots = {}

    def weight_grad(right, kind, start_row):
        def body(cols, value):
            right_rows = right[:, :, cols].reshape(2 * slots, cols.size)
            weights[kind, start_row : start_row + half, cols] = low_dot(
                turned[...], right_rows
            ).astype(BF)
            return value

        over_tiles(TILE, body, 0)

    def share_out(index, kind, start_row):
        expert_slots[index] = [links.slot() for _ in range(NEAR)]

        def block(owner):
            first = pl.multiple_of(start_row + owner * rows_each, rows_each)
            return weights.at[kind, pl.ds(first, rows_each), :]

        for step in range(NEAR):
            links.send(
                block(plane[step]), expert_out.at[index, chip],
                {"wide": 2 * plane[step] + core}, expert_slots[index][step],
            )
        links.move(block(chip), expert_out.at[index, chip])

    graded_there()
    acts_there[0]()
    turned[...] = graded_cat[...].reshape(2 * slots, half).T
    weight_grad(act_cat, 0, 0)
    share_out(0, 0, 0)
    mid_sum.relay()

    activated = act_cat.at[core]
    exp_sum = LineSum(links, n, rs_send.at[1], rs_recv.at[1])

    def exp_part(owner):
        rows = pl.ds(pl.multiple_of(owner * part_width, part_width), part_width)
        return rows_rows(activated[...], weights[2, rows, :])

    for step in range(NEAR):
        if step < 2:
            exp_sum.put(step, exp_part(exp_sum.targets[step]))
        else:
            rs_send[1, 2] = exp_part(exp_sum.targets[2]).astype(BF)
    back_exp_out[...] = exp_part(n).astype(BF)
    for slot in hidden_slots:
        index = hidden_slots.index(slot)
        links.land(
            hidden_cat.at[1 - core, :, pl.ds(index * rows_each, rows_each)], mate, slot
        )
    for there in acts_there[1:]:
        there()
    turned[...] = hidden_cat[...].reshape(2 * slots, half).T
    weight_grad(gate_cat, 0, half)
    share_out(1, 0, half)
    weight_grad(up_cat, 1, 0)
    links.move(weights.at[1, pl.ds(0, half), :], grads_out)

    for step in range(NEAR):
        links.land(ext_recv.at[step], {"narrow": from_z[step]}, ext_slots[step])
        extra = extra + ext_recv[step]
    high = extra.astype(BF)
    rest = (extra - high.astype(F32)).astype(BF)
    place = lax.broadcasted_iota(jnp.int32, (8, 128), 0) * 2
    lanes = lax.broadcasted_iota(jnp.int32, (8, 128), 1)
    spread_high = jnp.where(place == lanes, 1.0, 0.0).astype(BF)
    spread_low = jnp.where(place + 1 == lanes, 1.0, 0.0).astype(BF)
    columns = mm(high, spread_high, ((0,), (0,))) + mm(rest, spread_low, ((0,), (0,)))
    extra_out[...] = jnp.where(lane_at == 4, 1.0, columns).astype(BF)
    back_mid_out[...] = mid_sum.total(back_mid_out[...].astype(F32)).astype(BF)
    exp_sum.join()
    last_exp_out[...] = rs_send[1, 2]
    back_exp_out[...] = exp_sum.early(back_exp_out[...].astype(F32)).astype(BF)
    for index in range(2):
        for step in range(NEAR):
            links.land(
                expert_out.at[index, plane[step]], {"wide": 2 * plane[step] + core},
                expert_slots[index][step],
            )
    links.finish()


def mid_call(slot_mid, slot_grad, slot_gate, token_parts, expert_w):
    slots, full = slot_mid.shape
    part_width = full // 4
    rows_each, hidden_width = expert_w.shape[3:]
    vmem = pl.BlockSpec(memory_space=pltpu.VMEM)
    hbm = pl.BlockSpec(memory_space=pl.ANY)

    def arr(shape, dtype):
        return jax.ShapeDtypeStruct(shape, dtype)

    return pl.pallas_call(
        mid_body,
        out_shape=(
            arr((slots, part_width), BF),
            arr((slots, part_width), BF),
            arr((slots, part_width), BF),
            arr((slots, 128), BF),
            arr((full // 2, hidden_width), BF),
            arr((2, 4, rows_each, hidden_width), BF),
        ),
        in_specs=[hbm] + [vmem] * 3 + [hbm],
        out_specs=(vmem,) * 4 + (hbm, hbm),
        scratch_shapes=[
            pltpu.VMEM((3, full, hidden_width), BF),
            pltpu.VMEM((slots, full), BF),
            pltpu.VMEM((slots, full // 2), BF),
            pltpu.VMEM((2, slots, full // 2), BF),
            pltpu.VMEM((2, slots, full // 2), BF),
            pltpu.VMEM((2, slots, hidden_width), BF),
            pltpu.VMEM((2, slots, hidden_width), BF),
            pltpu.VMEM((2, slots, hidden_width), BF),
            pltpu.VMEM((full // 2, 2 * slots), BF),
            pltpu.VMEM((2, NEAR, slots, part_width), BF),
            pltpu.VMEM((2, NEAR + 1, slots, part_width), BF),
            pltpu.VMEM((8, slots), F32),
            pltpu.VMEM((NEAR, 8, slots), F32),
            pltpu.SemaphoreType.DMA((MID_SLOTS,)),
            pltpu.SemaphoreType.DMA((MID_SLOTS,)),
            pltpu.SemaphoreType.DMA((32,)),
        ],
        compiler_params=pltpu.CompilerParams(
            collective_id=1, has_side_effects=True, vmem_limit_bytes=62 * 1024 * 1024
        ),
        cost_estimate=pl.CostEstimate(
            flops=30_000_000_000, bytes_accessed=40_000_000, transcendentals=800_000
        ),
        name="mid",
    )(slot_mid, slot_grad, slot_gate, token_parts, expert_w)


class PlaneSum:
    def __init__(self, links, core, chip, plane, first, send, inbox):
        self.links, self.core, self.chip = links, core, chip
        self.near, self.next, self.far = plane[first], plane[1 - first], plane[2]
        self.send, self.inbox = send, inbox
        self.slots = [links.slot() for _ in range(3)]

    def at(self, peer):
        return {"wide": 2 * peer + self.core}

    def block(self, owner):
        rows = self.inbox.shape[1]
        return self.send.at[pl.ds(pl.multiple_of(owner * rows, rows), rows), :]

    def start(self):
        links = self.links
        links.send(self.block(self.far), self.inbox.at[1], self.at(self.near), self.slots[1])
        links.send(self.block(self.near), self.inbox.at[0], self.at(self.near), self.slots[0])

    def turn(self):
        links = self.links
        links.land(self.inbox.at[1], self.at(self.near), self.slots[1])
        block = self.block(self.next)
        block[...] = (block[...].astype(F32) + self.inbox[1].astype(F32)).astype(BF)
        links.send(block, self.inbox.at[2], self.at(self.next), self.slots[2])

    def total(self):
        links = self.links
        links.land(self.inbox.at[0], self.at(self.near), self.slots[0])
        links.land(self.inbox.at[2], self.at(self.next), self.slots[2])
        own = self.block(self.chip)[...].astype(F32)
        return own + self.inbox[0].astype(F32) + self.inbox[2].astype(F32)


TAIL_SLOTS = 72


def tail_body(
    mid_ref, exp_ref, last_ref, ext_ref, moved_ref, picks_ref, stat_ref, cols_ref, middle_ref, cot_ref,
    tok_ref, tokens_ref, qkv_ref, prob_ref, att_ref, rope_ref, hidden_ref, qkvw_ref, outw_ref,
    output_out, grad_tokens_out, summed_out, small_out,
    router_out, expert_out,
    exp_in, exp_sum, router_all, qkvw, outw, ret_mid, ret_exp, ret_ext, branch, hidden_cat, branch_cat, att_cat, proj_cat,
    proj_send, proj_recv, first_send, first_recv, col_send, col_recv, small_mate, small_sum,
    small_recv, last_mate, last_sum, last_recv, sent, landed, local,
):
    n = lax.axis_index("narrow")
    w = lax.axis_index("wide")
    chip, core = w // 2, lax.rem(w, 2)
    to_z, from_z = places_of(n)
    plane = plane_of(chip)
    links = Links(sent, landed, local)
    mate = {"wide": 2 * chip + 1 - core}
    token_count, part_width = tok_ref.shape
    full = 4 * part_width
    rows_each = full // 8
    heads = part_width // HEAD_DIM
    half = full // 2

    def at_plane(peer):
        return {"wide": 2 * peer + core}

    def cap_rows(array, owner):
        return array.at[pl.ds(pl.multiple_of(owner * CAP, 16), CAP), :]

    loads = [links.move(qkvw_ref, qkvw), links.move(outw_ref, outw)]
    links.waits = []
    greet(to_z, plane, chip, core, True)

    last_slot = links.slot()
    links.send(last_ref, exp_in, {"narrow": lax.rem(2 * n + 1, 5)}, last_slot)

    back_slots = []

    def give_back(source, target):
        slots = [links.slot() for _ in range(NEAR)]
        for step in range(NEAR):
            links.send(
                cap_rows(source, plane[step]), cap_rows(target, chip), at_plane(plane[step]),
                slots[step],
            )
        own = links.move(cap_rows(source, chip), cap_rows(target, chip))
        links.waits.pop()
        back_slots.append((target, slots, own))

    give_back(mid_ref, ret_mid)
    give_back(ext_ref, ret_ext)

    def returned(which):
        target, slots, own = back_slots[which]
        for step in range(NEAR):
            links.land(cap_rows(target, plane[step]), at_plane(plane[step]), slots[step])
        own.wait()
        return target[...]

    expert_slots = [links.slot() for _ in range(NEAR)]
    for step in range(NEAR):
        block = pl.ds(pl.multiple_of(plane[step] * rows_each, rows_each), rows_each)
        links.send(
            moved_ref.at[block, :], expert_out.at[chip], at_plane(plane[step]), expert_slots[step]
        )
    block = pl.ds(pl.multiple_of(chip * rows_each, rows_each), rows_each)
    links.move(moved_ref.at[block, :], expert_out.at[chip])

    def to_mate(source, target):
        slot = links.slot()
        links.send(source, target.at[core], mate, slot)
        return lambda: links.land(target.at[1 - core], mate, slot)

    def parity_exchange(source, target):
        lands = []
        for c in range(4):
            cols = pl.ds(c * rows_each, rows_each)
            theirs = pl.ds(pl.multiple_of((2 * c + 1 - core) * rows_each, rows_each), rows_each)
            ours = pl.ds(pl.multiple_of((2 * c + core) * rows_each, rows_each), rows_each)
            slot = links.slot()
            links.send(source.at[:, theirs], target.at[core, :, cols], mate, slot)
            target[core, :, c * rows_each : (c + 1) * rows_each] = source[:, ours]
            lands.append((target.at[1 - core, :, cols], slot))
        return lambda: [links.land(block, mate, slot) for block, slot in lands]

    hidden_there = parity_exchange(hidden_ref, hidden_cat)
    att_cat[core] = att_ref[...]
    att_there = to_mate(att_ref, att_cat)

    stat = jnp.concatenate([stat_ref[...], jnp.zeros((120, token_count), F32)], 0).T
    lane_at = lax.broadcasted_iota(jnp.int32, (token_count, 128), 1)
    scale_second = lax.rsqrt(stat[:, 4:5] * (1.0 / full) + NORM_EPS)
    logits = stat * scale_second
    hot_first = lane_at == cols_ref[:, 2:3].astype(jnp.int32)
    hot_second = lane_at == cols_ref[:, 3:4].astype(jnp.int32)
    logit_first = jnp.sum(jnp.where(hot_first, logits, 0.0), 1, keepdims=True)
    logit_second = jnp.sum(jnp.where(hot_second, logits, 0.0), 1, keepdims=True)
    apart = logit_first - logit_second
    share_first = 1.0 / (1.0 + jnp.exp(-apart))
    share_second = 1.0 / (1.0 + jnp.exp(apart))
    normed = middle_ref[...] * scale_second
    gain_second = tokens_ref[n, token_count + 1 : token_count + 2, :].astype(F32)
    hidden_second = (normed * gain_second).astype(BF)
    for load in loads:
        load.wait()
    router = qkvw[pl.ds(2 * n, 2), :, 1536:1664].reshape(part_width, 128)

    rows_mid = returned(0)
    rows_ext = returned(1)
    ext_first = cols_cols(picks_ref[0], rows_ext)
    ext_second = cols_cols(picks_ref[1], rows_ext)
    ext_both = ext_first + ext_second
    grad_share = ext_first[:, 0:1] + ext_first[:, 1:2] - ext_second[:, 0:1] - ext_second[:, 1:2]
    delta = (grad_share * share_first * share_second).astype(BF).astype(F32)
    grad_logits = jnp.where(hot_first, delta, jnp.where(hot_second, -delta, 0.0)).astype(BF)
    stat_total = ext_both[:, 2:3] + ext_both[:, 3:4] + delta * apart
    grad_hidden = cols_cols(picks_ref[0] + picks_ref[1], rows_mid) + rows_rows(grad_logits, router)
    grad_middle = cot_ref[...].astype(F32) + scale_second * (
        gain_second * grad_hidden - normed * (stat_total * (1.0 / full))
    )
    own_cols = pl.ds(pl.multiple_of(n * part_width, part_width), part_width)
    branch[:, own_cols] = grad_middle.astype(BF)
    branch_slots = [links.slot() for _ in range(NEAR)]
    for step in range(NEAR):
        links.send(
            branch.at[:, own_cols], branch.at[:, own_cols], {"narrow": to_z[step]},
            branch_slots[step],
        )

    links.land(exp_in, {"narrow": lax.rem(n + 1, 4)}, last_slot)
    exp_sum[...] = (exp_ref[...].astype(F32) + exp_in[...].astype(F32)).astype(BF)
    give_back(exp_sum, ret_exp)

    router_part = cols_cols(grad_logits, hidden_second)[0:8, :]
    gain_part = jnp.sum(grad_hidden * normed, 0, keepdims=True)
    kind_at = lax.broadcasted_iota(jnp.int32, (8, part_width), 0)
    small = jnp.where(kind_at == 4, gain_part, router_part)
    small_mate[core] = small
    small_there = to_mate(small_mate.at[core], small_mate)

    small_there()
    small = small_mate[0] + small_mate[1]
    small_sum[...] = small
    small_slots = [links.slot() for _ in range(NEAR)]
    for step in range(NEAR):
        links.send(small_sum, small_recv.at[step], at_plane(plane[step]), small_slots[step])

    for step in range(NEAR):
        cols = pl.ds(pl.multiple_of(from_z[step] * part_width, part_width), part_width)
        links.land(branch.at[:, cols], {"narrow": from_z[step]}, branch_slots[step])
    branch_there = parity_exchange(branch, branch_cat)
    grad_att = low_dot(branch[...], outw[...].reshape(full, part_width)).astype(BF)

    proj_sums = {
        part: PlaneSum(
            links, core, chip, plane, part % 2, proj_send.at[part], proj_recv.at[part]
        )
        for part in (3, 0, 1, 2)
    }

    branch_there()
    att_there()
    proj_send[3] = cols_cols(
        branch_cat[...].reshape(2 * token_count, half), att_cat[...].reshape(2 * token_count, part_width)
    ).astype(BF)
    proj_sums[3].start()
    cosines, sines = rope_ref[0], rope_ref[1]
    score_scale = HEAD_DIM ** (-0.5)
    stat_first = jnp.zeros((token_count, 1), F32)
    for head in range(heads):
        cols = slice(head * HEAD_DIM, (head + 1) * HEAD_DIM)
        query, key, value = (qkv_ref[i, :, cols] for i in range(3))
        grad_out = grad_att[:, cols]
        weights = prob_ref[head]
        grad_weights = rows_rows(grad_out, value)
        inner = jnp.sum(weights * grad_weights, 1, keepdims=True)
        grad_scores = (weights * (grad_weights - inner)).astype(BF)
        grad_query = low_dot(grad_scores, key) * score_scale
        grad_key = cols_cols(grad_scores, query) * score_scale
        grad_value = cols_cols(weights.astype(BF), grad_out)
        products = (
            grad_query * query.astype(F32)
            + grad_key * key.astype(F32)
            + grad_value * value.astype(F32)
        )
        stat_first = stat_first + jnp.sum(products, 1, keepdims=True)
        for part, grad in ((0, grad_query), (1, grad_key)):
            turned = grad * cosines - pltpu.roll(grad, HEAD_DIM // 2, 1) * sines
            proj_cat[core, :, part * 512 + head * 128 : part * 512 + (head + 1) * 128] = (
                turned.astype(BF)
            )
        proj_cat[core, :, 1024 + head * 128 : 1024 + (head + 1) * 128] = grad_value.astype(BF)
    proj_there = to_mate(proj_cat.at[core], proj_cat)
    high = stat_first.astype(BF)
    rest = (stat_first - high.astype(F32)).astype(BF)
    col_send[...] = jnp.where(
        lane_at == 0, high.astype(F32), jnp.where(lane_at == 1, rest.astype(F32), 0.0)
    ).astype(BF)
    col_slots = [links.slot() for _ in range(NEAR)]
    for step in range(NEAR):
        links.send(col_send, col_recv.at[step], {"narrow": to_z[step]}, col_slots[step])
    grads = proj_cat[core]

    def first_block(m):
        weight = qkvw[pl.ds(2 * m, 2), :, 0:1536].reshape(part_width, 1536)
        return rows_rows(grads, weight)

    first_slots = [links.slot() for _ in range(NEAR)]
    for step in range(NEAR):
        first_send[step] = first_block(to_z[step]).astype(BF)
        links.send(
            first_send.at[step], first_recv.at[step], {"narrow": to_z[step]}, first_slots[step]
        )

    hidden_there()
    proj_there()
    hidden_rows = hidden_cat[...].reshape(2 * token_count, half)
    proj_sums[3].turn()
    for part in range(3):
        cols = slice(part * 512, (part + 1) * 512)
        proj_send[part] = cols_cols(
            hidden_rows, proj_cat[:, :, cols].reshape(2 * token_count, part_width)
        ).astype(BF)
        proj_sums[part].start()

    rows_exp = returned(2)
    output_out[...] = (
        middle_ref[...]
        + share_first * cols_cols(picks_ref[0], rows_exp)
        + share_second * cols_cols(picks_ref[1], rows_exp)
    ).astype(BF)

    grad_first = first_block(n)
    stat_first = high.astype(F32) + rest.astype(F32)
    total = jnp.zeros((token_count, 1), F32)
    for m in range(4):
        part = tokens_ref[m, 0:token_count, :].astype(F32)
        total = total + jnp.sum(part * part, 1, keepdims=True)
    scale_first = lax.rsqrt(total * (1.0 / full) + NORM_EPS)
    normed_first = tok_ref[...].astype(F32) * scale_first
    gain_first = tokens_ref[n, token_count : token_count + 1, :].astype(F32)
    for step in range(NEAR):
        links.land(col_recv.at[step], {"narrow": from_z[step]}, col_slots[step])
        stat_first = stat_first + (
            col_recv[step, :, 0:1].astype(F32) + col_recv[step, :, 1:2].astype(F32)
        )
    for step in range(NEAR):
        links.land(first_recv.at[step], {"narrow": from_z[step]}, first_slots[step])
        grad_first = grad_first + first_recv[step].astype(F32)
    grad_tokens_out[...] = grad_middle + scale_first * (
        gain_first * grad_first - normed_first * (stat_first * (1.0 / full))
    )
    gain_part = jnp.sum(grad_first * normed_first, 0, keepdims=True)
    for part in range(3):
        proj_sums[part].turn()
    last_mate[core] = jnp.broadcast_to(gain_part, (8, part_width))
    last_there = to_mate(last_mate.at[core], last_mate)

    for step in range(NEAR):
        links.land(small_recv.at[step], at_plane(plane[step]), small_slots[step])
        small = small + small_recv[step]
    last_there()
    last = last_mate[0] + last_mate[1]
    last_sum[...] = last
    last_slots = [links.slot() for _ in range(NEAR)]
    for step in range(NEAR):
        links.send(last_sum, last_recv.at[step], at_plane(plane[step]), last_slots[step])
    router_all[:, own_cols] = small
    router_slots = [links.slot() for _ in range(NEAR)]
    for step in range(NEAR):
        links.send(
            router_all.at[:, own_cols], router_all.at[:, own_cols], {"narrow": to_z[step]},
            router_slots[step],
        )
    for step in range(NEAR):
        links.land(last_recv.at[step], at_plane(plane[step]), last_slots[step])
        last = last + last_recv[step]
    small_out[...] = jnp.where(kind_at == 5, last, small)
    for step in range(NEAR):
        cols = pl.ds(pl.multiple_of(from_z[step] * part_width, part_width), part_width)
        links.land(router_all.at[:, cols], {"narrow": from_z[step]}, router_slots[step])

    router_out[...] = router_all[:, pl.ds(pl.multiple_of(w * rows_each, rows_each), rows_each)]
    for part in range(4):
        summed_out[:, part * part_width : (part + 1) * part_width] = proj_sums[part].total()
    for step in range(NEAR):
        links.land(expert_out.at[plane[step]], at_plane(plane[step]), expert_slots[step])
    links.finish()


def tail_call(*args):
    slots, part_width = args[0].shape
    half, hidden_width = args[4].shape
    token_count = args[10].shape[0]
    full, rows_each = 2 * half, half // 4
    vmem = pl.BlockSpec(memory_space=pltpu.VMEM)
    hbm = pl.BlockSpec(memory_space=pl.ANY)

    def arr(shape, dtype):
        return jax.ShapeDtypeStruct(shape, dtype)

    own = (token_count, part_width)
    return pl.pallas_call(
        tail_body,
        out_shape=(
            arr(own, BF),
            arr(own, F32),
            arr((rows_each, full), F32),
            arr((8, part_width), F32),
            arr((8, rows_each), F32),
            arr((4, rows_each, hidden_width), BF),
        ),
        in_specs=[vmem] * 4 + [hbm] + [vmem] * 12 + [hbm] * 2,
        out_specs=(vmem,) * 5 + (hbm,),
        scratch_shapes=[
            pltpu.VMEM((slots, part_width), BF),
            pltpu.VMEM((slots, part_width), BF),
            pltpu.VMEM((8, full), F32),
            pltpu.VMEM((8, rows_each, 1664), BF),
            pltpu.VMEM((8, rows_each, part_width), BF),
            pltpu.VMEM((slots, part_width), BF),
            pltpu.VMEM((slots, part_width), BF),
            pltpu.VMEM((slots, 128), BF),
            pltpu.VMEM((token_count, full), BF),
            pltpu.VMEM((2, token_count, half), BF),
            pltpu.VMEM((2, token_count, half), BF),
            pltpu.VMEM((2, token_count, part_width), BF),
            pltpu.VMEM((2, token_count, 1536), BF),
            pltpu.VMEM((4, half, part_width), BF),
            pltpu.VMEM((4, NEAR, rows_each, part_width), BF),
            pltpu.VMEM((NEAR,) + own, BF),
            pltpu.VMEM((NEAR,) + own, BF),
            pltpu.VMEM((token_count, 128), BF),
            pltpu.VMEM((NEAR, token_count, 128), BF),
            pltpu.VMEM((2, 8, part_width), F32),
            pltpu.VMEM((8, part_width), F32),
            pltpu.VMEM((NEAR, 8, part_width), F32),
            pltpu.VMEM((2, 8, part_width), F32),
            pltpu.VMEM((8, part_width), F32),
            pltpu.VMEM((NEAR, 8, part_width), F32),
            pltpu.SemaphoreType.DMA((TAIL_SLOTS,)),
            pltpu.SemaphoreType.DMA((TAIL_SLOTS,)),
            pltpu.SemaphoreType.DMA((16,)),
        ],
        compiler_params=pltpu.CompilerParams(
            collective_id=2, has_side_effects=True, vmem_limit_bytes=60 * 1024 * 1024
        ),
        cost_estimate=pl.CostEstimate(
            flops=6_000_000_000, bytes_accessed=60_000_000, transcendentals=1_000
        ),
        name="tail",
    )(*args)


def finish_body(
    down_ref, gate_ref, up_ref, output_ref, tokens_ref, summed_ref,
    gate_out, up_out, down_out, output_out, tokens_out, *proj_outs,
):
    for source, target in ((gate_ref, gate_out), (up_ref, up_out), (down_ref, down_out)):
        for expert in range(EXPERTS):
            target[:, expert, :] = source[expert].astype(F32)
    output_out[...] = output_ref[...]
    tokens_out[...] = tokens_ref[...]
    width = tokens_ref.shape[1]
    for part, target in enumerate(proj_outs):
        target[...] = summed_ref[:, part * width : (part + 1) * width].astype(F32)


def finish_call(early, late, output, grad_tokens, summed):
    _, rows_each, hidden_width = late.shape
    token_count, part_width = output.shape
    step = 32

    def flat(width):
        return pl.BlockSpec((step, width), lambda i: (i, 0))

    def cube(which):
        return pl.BlockSpec((None, EXPERTS, step, hidden_width), lambda i: (which, 0, i, 0))

    spread = pl.BlockSpec((step, EXPERTS, hidden_width), lambda i: (i, 0, 0))

    def arr(shape, dtype):
        return jax.ShapeDtypeStruct(shape, dtype)

    return pl.pallas_call(
        finish_body,
        grid=(rows_each // step,),
        out_shape=(arr((rows_each, EXPERTS, hidden_width), F32),) * 3
        + (arr(output.shape, BF), arr(output.shape, F32))
        + (arr((rows_each, part_width), F32),) * 4,
        in_specs=[
            cube(0), cube(1),
            pl.BlockSpec((EXPERTS, step, hidden_width), lambda i: (0, i, 0)),
            flat(part_width), flat(part_width), flat(4 * part_width),
        ],
        out_specs=(spread,) * 3 + (flat(part_width),) * 6,
        name="finish",
    )(early, early, late, output, grad_tokens, summed)


def plain_device(
    tokens, gain_attn, w_query, w_key, w_value, w_out, gain_ffn, w_router,
    w_gate, w_up, w_down, segment, parents, expert_ids, slot_order, cotangent,
):
    narrow_count = lax.axis_size("narrow")
    wide_count = lax.axis_size("wide")
    narrow_at = lax.axis_index("narrow")
    token_count, part_width = tokens.shape
    full_width = part_width * narrow_count
    hidden_width = w_gate.shape[2]
    rows_each = w_gate.shape[0]
    blocks = wide_count // 8
    quads = [
        [8 * block + 2 * chip + core for chip in range(4)]
        for block in range(blocks)
        for core in range(2)
    ]
    mates = [
        [8 * block + 2 * chip + core for block in range(blocks) for core in range(2)]
        for chip in range(4)
    ]

    def quad_swap(array):
        return lax.all_to_all(array, "wide", 0, 0, axis_index_groups=quads, tiled=True)

    def own_rows(weight):
        moved = quad_swap(jnp.transpose(weight, (1, 0, 2)))
        joined = lax.all_gather(moved, "wide", axis=0, axis_index_groups=mates, tiled=True)
        joined = joined.reshape(blocks, 2, 4, rows_each, hidden_width).transpose(0, 2, 1, 3, 4)
        return joined.reshape(full_width, hidden_width)

    def share_rows(grad):
        parts = grad.astype(BF).reshape(blocks, 4, 2, rows_each, hidden_width)
        parts = parts.transpose(0, 2, 1, 3, 4).reshape(blocks * 2, 4, rows_each, hidden_width)
        summed = lax.psum_scatter(
            parts, "wide", scatter_dimension=0, axis_index_groups=mates, tiled=True
        )[0]
        return jnp.transpose(quad_swap(summed), (1, 0, 2)).astype(F32)

    def head_cols(array, head):
        return array[:, head * HEAD_DIM : (head + 1) * HEAD_DIM]

    heads = part_width // HEAD_DIM
    half_dim = HEAD_DIM // 2
    freqs = ROPE_BASE ** (-2.0 * jnp.arange(half_dim, dtype=F32) / HEAD_DIM)
    score_scale = HEAD_DIM ** (-0.5)
    gains = jnp.stack([gain_attn, gain_ffn])
    gain_first_loc = gain_attn.astype(F32)
    gain_second_loc = gain_ffn.astype(F32)
    hot_first, hot_second, kept, pick_first, pick_second = route(expert_ids, slot_order[0])

    gate_w, up_w, down_w = own_rows(w_gate), own_rows(w_up), own_rows(w_down)
    attn_w = lax.all_gather(
        jnp.stack([w_query, w_key, w_value, w_out], 1), "wide", axis=0, tiled=True
    )
    query_w, key_w, value_w, out_w = (attn_w[:, i] for i in range(4))
    router_w = lax.all_gather(w_router, "wide", axis=0, tiled=True)
    tokens_full = lax.all_gather(tokens, "narrow", axis=1, tiled=True)
    grad_full = lax.all_gather(cotangent, "narrow", axis=1, tiled=True)
    gains_full = lax.all_gather(gains, "narrow", axis=1, tiled=True)
    gain_first = gains_full[0].astype(F32)
    gain_second = gains_full[1].astype(F32)

    seen, places = tree_layout(segment[0], parents[0])
    pick_first_low = pick_first.astype(BF)
    pick_second_low = pick_second.astype(BF)
    pick_both_low = (pick_first | pick_second).astype(BF)

    inputs_full = tokens_full.astype(F32)
    scale_first = lax.rsqrt(jnp.mean(inputs_full * inputs_full, -1, keepdims=True) + NORM_EPS)
    normed_first = inputs_full * scale_first
    hidden_first = (normed_first * gain_first).astype(BF)
    angles = places[:, None] * freqs[None, :]
    cosines, sines = jnp.cos(angles), jnp.sin(angles)
    query_raw = rows_cols(hidden_first, query_w)
    key_raw = rows_cols(hidden_first, key_w)
    value_low = rows_cols(hidden_first, value_w).astype(BF)

    saved = []
    outs = []
    for head in range(heads):
        query = rotate(head_cols(query_raw, head), cosines, sines).astype(BF)
        key = rotate(head_cols(key_raw, head), cosines, sines).astype(BF)
        value = head_cols(value_low, head)
        scores = jnp.where(seen, rows_rows(query, key) * score_scale, NEG_FILL)
        exps = jnp.exp(scores - jnp.max(scores, -1, keepdims=True))
        weights = exps / jnp.sum(exps, -1, keepdims=True)
        saved.append((query, key, value, weights))
        outs.append(rows_cols(weights.astype(BF), value).astype(BF))
    attended = jnp.concatenate(outs, 1)
    branch_part = rows_rows(attended, out_w).astype(BF)
    branch_loc = lax.psum_scatter(
        branch_part, "narrow", scatter_dimension=1, tiled=True
    ).astype(F32)
    middle = tokens.astype(F32) + branch_loc
    middle_full = lax.all_gather(middle.astype(BF), "narrow", axis=1, tiled=True).astype(F32)
    scale_second = lax.rsqrt(jnp.mean(middle_full * middle_full, -1, keepdims=True) + NORM_EPS)
    normed_second = middle_full * scale_second
    hidden_second = (normed_second * gain_second).astype(BF)
    logits = rows_cols(hidden_second, router_w)
    share_first, share_second = gate_pair(logits, hot_first, hot_second)
    weight_first = kept[:, 0] * share_first
    weight_second = kept[:, 1] * share_second

    slot_weight = jnp.sum(
        pick_first * weight_first[:, None] + pick_second * weight_second[:, None], 0
    )
    weight_high, weight_low = two_parts(slot_weight)
    pads = jnp.stack([weight_high, weight_low], 1)
    pads = jnp.pad(pads, ((0, 0), (0, 126)))
    sent_hidden = cols_cols(pick_both_low, hidden_second).astype(BF)
    sent_grad = cols_cols(pick_both_low, grad_full).astype(BF)
    sent = jnp.concatenate([sent_hidden, sent_grad, pads], 1)
    got = quad_swap(sent.reshape(EXPERTS, CAP, -1)).reshape(SLOTS, -1)
    slot_hidden = got[:, :full_width]
    slot_grad = got[:, full_width : 2 * full_width]
    slot_gate = got[:, 2 * full_width : 2 * full_width + 2].astype(F32)
    slot_gate = slot_gate[:, 0:1] + slot_gate[:, 1:2]

    gate_pre = rows_cols(slot_hidden, gate_w)
    up_pre = rows_cols(slot_hidden, up_w)
    sigmoid_gate = jax.nn.sigmoid(gate_pre)
    silu_gate = gate_pre * sigmoid_gate
    activated = (silu_gate * up_pre).astype(BF)
    expert_part = rows_rows(activated, down_w)
    act_raw = rows_cols(slot_grad, down_w)
    share_part = jnp.sum(act_raw * activated.astype(F32), 1, keepdims=True)
    grad_act = act_raw * slot_gate
    grad_gate_pre = (
        grad_act * up_pre * sigmoid_gate * (1.0 + gate_pre * (1.0 - sigmoid_gate))
    ).astype(BF)
    grad_up_pre = (grad_act * silu_gate).astype(BF)
    grad_slot = rows_rows(grad_gate_pre, gate_w) + rows_rows(grad_up_pre, up_w)
    stat_part = jnp.sum(slot_hidden.astype(F32) * grad_slot, 1, keepdims=True)
    extras = jnp.concatenate([*two_parts(share_part), *two_parts(stat_part)], 1)
    extras = jnp.pad(extras, ((0, 0), (0, 124)))
    back_parts = []
    expert_plain = expert_part.astype(BF)
    slot_plain = grad_slot.astype(BF)
    for part in range(narrow_count):
        cols = slice(part * part_width, (part + 1) * part_width)
        back_parts += [expert_plain[:, cols], slot_plain[:, cols], extras]
    back = lax.psum_scatter(
        jnp.concatenate(back_parts, 1), "narrow", scatter_dimension=1, tiled=True
    )
    back = quad_swap(back.reshape(EXPERTS, CAP, -1)).reshape(SLOTS, -1)
    picked_first = rows_cols(pick_first_low, back)
    picked_second = rows_cols(pick_second_low, back)
    output = (
        middle
        + weight_first[:, None] * picked_first[:, :part_width]
        + weight_second[:, None] * picked_second[:, :part_width]
    ).astype(BF)

    grad_weight = (slot_grad.astype(F32) * slot_gate).astype(BF)
    gate_out = share_rows(cols_cols(slot_hidden, grad_gate_pre))
    up_out = share_rows(cols_cols(slot_hidden, grad_up_pre))
    down_out = share_rows(cols_cols(grad_weight, activated))

    tail = 2 * part_width
    share_first_grad = picked_first[:, tail] + picked_first[:, tail + 1]
    share_second_grad = picked_second[:, tail] + picked_second[:, tail + 1]
    both = picked_first + picked_second
    stat_second = both[:, tail + 2] + both[:, tail + 3]
    grad_hidden_loc = both[:, part_width:tail]
    grad_local = cotangent.astype(F32)
    _, pull_gates = jax.vjp(lambda given: gate_pair(given, hot_first, hot_second), logits)
    (grad_logits,) = pull_gates((kept[:, 0] * share_first_grad, kept[:, 1] * share_second_grad))
    grad_logits_low = grad_logits.astype(BF)
    grad_router_rows = rows_rows(grad_logits_low, router_w)
    stat_total = stat_second + jnp.sum(normed_second * gain_second * grad_router_rows, 1)

    def take_cols(full_rows):
        return lax.dynamic_slice_in_dim(full_rows, narrow_at * part_width, part_width, 1)

    grad_hidden_loc = grad_hidden_loc + take_cols(grad_router_rows)
    normed_second_loc = take_cols(normed_second)
    grad_gain_second = jnp.sum(grad_hidden_loc * normed_second_loc, 0)
    grad_middle = grad_local + scale_second * (
        gain_second_loc * grad_hidden_loc - normed_second_loc * stat_total[:, None] / full_width
    )
    grad_router_w = cols_cols(hidden_second, grad_logits_low)
    grad_branch = lax.all_gather(grad_middle.astype(BF), "narrow", axis=1, tiled=True)
    grad_attended = rows_cols(grad_branch, out_w).astype(BF)
    grad_out_w = cols_cols(grad_branch, attended)
    grad_qs, grad_ks, grad_vs = [], [], []
    for head in range(heads):
        query, key, value, weights = saved[head]
        grad_out = head_cols(grad_attended, head)
        grad_weights = rows_rows(grad_out, value)
        inner = jnp.sum(weights * grad_weights, -1, keepdims=True)
        grad_scores = (weights * (grad_weights - inner)).astype(BF)
        grad_q = rows_cols(grad_scores, key) * score_scale
        grad_k = cols_cols(grad_scores, query) * score_scale
        grad_qs.append(rotate(grad_q, cosines, -sines).astype(BF))
        grad_ks.append(rotate(grad_k, cosines, -sines).astype(BF))
        grad_vs.append(cols_cols(weights.astype(BF), grad_out).astype(BF))
    grad_query_raw = jnp.concatenate(grad_qs, 1)
    grad_key_raw = jnp.concatenate(grad_ks, 1)
    grad_value_raw = jnp.concatenate(grad_vs, 1)
    grad_hidden_first = (
        rows_rows(grad_query_raw, query_w)
        + rows_rows(grad_key_raw, key_w)
        + rows_rows(grad_value_raw, value_w)
    )
    stat_first = jnp.sum(normed_first * gain_first * grad_hidden_first, 1, keepdims=True)
    extras = jnp.pad(jnp.concatenate(two_parts(stat_first), 1), ((0, 0), (0, 126)))
    grad_hidden_low = grad_hidden_first.astype(BF)
    first_parts = []
    for part in range(narrow_count):
        first_parts += [grad_hidden_low[:, part * part_width : (part + 1) * part_width], extras]
    first_back = lax.psum_scatter(
        jnp.concatenate(first_parts, 1), "narrow", scatter_dimension=1, tiled=True
    ).astype(F32)
    grad_first_loc = first_back[:, :part_width]
    stat_first = first_back[:, part_width : part_width + 1]
    stat_first = stat_first + first_back[:, part_width + 1 : part_width + 2]
    normed_first_loc = take_cols(normed_first)
    grad_gain_first = jnp.sum(grad_first_loc * normed_first_loc, 0)
    grad_tokens = grad_middle + scale_first * (
        gain_first_loc * grad_first_loc - normed_first_loc * stat_first / full_width
    )
    grad_attn_w = jnp.concatenate(
        [
            cols_cols(hidden_first, grad_query_raw).astype(BF),
            cols_cols(hidden_first, grad_key_raw).astype(BF),
            cols_cols(hidden_first, grad_value_raw).astype(BF),
            grad_out_w.astype(BF),
        ],
        1,
    )
    attn_summed = lax.psum_scatter(
        grad_attn_w, "wide", scatter_dimension=0, tiled=True
    ).astype(F32)
    router_summed = lax.psum_scatter(grad_router_w, "wide", scatter_dimension=0, tiled=True)
    gains_summed = lax.psum(jnp.stack([grad_gain_first, grad_gain_second]), "wide")
    return (
        output,
        grad_tokens,
        gains_summed[0],
        attn_summed[:, :part_width],
        attn_summed[:, part_width : 2 * part_width],
        attn_summed[:, 2 * part_width : 3 * part_width],
        attn_summed[:, 3 * part_width :],
        gains_summed[1],
        router_summed,
        gate_out,
        up_out,
        down_out,
    )


def per_device(
    tokens, gain_attn, w_query, w_key, w_value, w_out, gain_ffn, w_router,
    w_gate, w_up, w_down, segment, parents, expert_ids, slot_order, cotangent,
):
    if lax.axis_size("wide") != 8 or lax.axis_size("narrow") != 4:
        return plain_device(
            tokens, gain_attn, w_query, w_key, w_value, w_out, gain_ffn, w_router,
            w_gate, w_up, w_down, segment, parents, expert_ids, slot_order, cotangent,
        )
    (
        in_w, out_w, expert_w, slot_mid, slot_grad, slot_gate, middle, hidden_first,
        token_parts, qkv, probs, attended, stat, rope, picks, columns,
    ) = front_call(
        tokens, cotangent, jnp.stack([gain_attn, gain_ffn]), (w_query, w_key, w_value, w_out),
        w_router.T, (w_gate, w_up, w_down), segment, parents, expert_ids.T, slot_order,
    )
    back_mid, back_exp, last_exp, back_ext, grads, early_experts = mid_call(
        slot_mid, slot_grad, slot_gate, token_parts, expert_w
    )
    (
        output, grad_tokens, summed, small, router, experts,
    ) = tail_call(
        back_mid, back_exp, last_exp, back_ext, grads, picks, stat, columns, middle, cotangent, tokens,
        token_parts, qkv, probs, attended, rope, hidden_first, in_w, out_w,
    )
    gate_out, up_out, down_out, output, grad_tokens, grad_q, grad_k, grad_v, grad_o = finish_call(
        early_experts, experts, output, grad_tokens, summed
    )
    return (
        output, grad_tokens, small[5], grad_q, grad_k, grad_v, grad_o, small[4],
        router[:EXPERTS].T, gate_out, up_out, down_out,
    )


def solution(mesh):
    pair = P("wide", "narrow")
    part = P("narrow")
    rows = P("wide", None)
    cube = P("wide", None, "narrow")
    return jax.shard_map(
        per_device,
        mesh=mesh,
        in_specs=(
            pair, part, pair, pair, pair, pair, part, rows, cube, cube, cube,
            rows, rows, rows, rows, pair,
        ),
        out_specs=(
            pair, pair, part, pair, pair, pair, pair, part, rows, cube, cube, cube,
        ),
        check_vma=False,
    )
```

```python
import math

import jax
import jax.numpy as jnp
from jax import lax
from jax.experimental import pallas as pl
from jax.experimental.pallas import tpu as pltpu
from jax.sharding import PartitionSpec as P

HEAD_DIM = 128
EXPERTS = 4
SEGS = 13
CAP = 144
SLOTS = EXPERTS * CAP
NORM_EPS = 1e-05
NEG_FILL = -1e30
ROPE_BASE = 10000.0
BF = jnp.bfloat16
F32 = jnp.float32


def mm(left, right, dims):
    return lax.dot_general(left, right, (dims, ((), ())), preferred_element_type=F32)


def rows_cols(left, right):
    return mm(left, right, ((1,), (0,)))


def rows_rows(left, right):
    return mm(left, right, ((1,), (1,)))


def cols_cols(left, right):
    return mm(left, right, ((0,), (0,)))


def tree_layout(segment_row, parent_row):
    seg_ids = jnp.arange(SEGS, dtype=jnp.int32)
    member = segment_row[:, None] == seg_ids[None, :]
    parent_of = (parent_row[:, None] == seg_ids[None, :]) & (seg_ids[:, None] != 0)
    itself = seg_ids[:, None] == seg_ids[None, :]
    reach = itself
    for _ in range(3):
        reach = itself | jnp.any(parent_of[:, :, None] & reach[None, :, :], axis=1)
    counts = member.astype(jnp.int32)
    lengths = jnp.sum(counts, 0)
    starts = jnp.sum(jnp.where(seg_ids[None, :] < seg_ids[:, None], lengths[None, :], 0), 1)
    before = jnp.sum(jnp.where(reach, lengths[None, :], 0), 1) - lengths
    row_at = jnp.arange(segment_row.shape[0], dtype=jnp.int32)
    places = jnp.sum(counts * (before - starts)[None, :], 1) + row_at
    member_low = member.astype(BF)
    lineage = rows_cols(member_low, reach.astype(BF)).astype(BF)
    shared = rows_rows(lineage, member_low) > 0.5
    seen = shared & (row_at[None, :] <= row_at[:, None])
    return seen, places.astype(F32)


def route(expert_row, slot_rank):
    expert_range = jnp.arange(EXPERTS, dtype=jnp.int32)
    hot_first = (expert_row[:, 0:1] == expert_range[None, :]).astype(F32)
    hot_second = (expert_row[:, 1:2] == expert_range[None, :]).astype(F32)
    earlier = (slot_rank[None, :] < slot_rank[:, None]).astype(BF)
    count_first = rows_cols(earlier, hot_first.astype(BF))
    count_second = rows_cols(earlier, hot_second.astype(BF))
    ahead_first = jnp.sum(count_first * hot_first, 1)
    ahead_second = jnp.sum((count_second + jnp.sum(hot_first, 0)[None, :]) * hot_second, 1)
    slot_index = jnp.stack([ahead_first, ahead_second], 1).astype(jnp.int32)
    kept = slot_index < CAP
    flat_slot = jnp.where(kept, expert_row * CAP + slot_index, SLOTS)
    slot_range = jnp.arange(SLOTS, dtype=jnp.int32)
    pick_first = flat_slot[:, 0:1] == slot_range[None, :]
    pick_second = flat_slot[:, 1:2] == slot_range[None, :]
    return hot_first, hot_second, kept.astype(F32), pick_first, pick_second


def rotate(vectors, cosines, sines):
    half_dim = HEAD_DIM // 2
    first_half = vectors[..., :half_dim]
    second_half = vectors[..., half_dim:]
    return jnp.concatenate(
        [
            first_half * cosines - second_half * sines,
            second_half * cosines + first_half * sines,
        ],
        -1,
    )


def gate_pair(logits, hot_first, hot_second):
    chances = jax.nn.softmax(logits, axis=-1)
    first_share = jnp.sum(chances * hot_first, 1)
    second_share = jnp.sum(chances * hot_second, 1)
    pair_total = first_share + second_share
    return (first_share / pair_total, second_share / pair_total)


def two_parts(column):
    high = column.astype(BF)
    return high, (column - high.astype(F32)).astype(BF)


MESH = pl.DeviceIdType.MESH
NEAR = 3


def low_dot(left, right):
    return jnp.dot(left, right, preferred_element_type=F32)


def places_of(n):
    return [lax.rem(n + step, 4) for step in (1, 2, 3)], [lax.rem(n + 4 - step, 4) for step in (1, 2, 3)]


def plane_of(chip):
    x, y = lax.rem(chip, 2), chip // 2
    return [2 * y + 1 - x, 2 * (1 - y) + x, 2 * (1 - y) + 1 - x]


def greet(narrow_peers, plane_peers, chip, core, mate):
    barrier = pltpu.get_barrier_semaphore()
    count = 0
    for peer in narrow_peers:
        pl.semaphore_signal(barrier, inc=1, device_id={"narrow": peer}, device_id_type=MESH)
        count += 1
    for peer in plane_peers:
        pl.semaphore_signal(
            barrier, inc=1, device_id={"wide": 2 * peer + core}, device_id_type=MESH
        )
        count += 1
    if mate:
        pl.semaphore_signal(
            barrier, inc=1, device_id={"wide": 2 * chip + 1 - core}, device_id_type=MESH
        )
        count += 1
    pl.semaphore_wait(barrier, count)


class Links:
    def __init__(self, sent, landed, local):
        self.sent, self.landed, self.local = sent, landed, local
        self.used, self.local_used = 0, 0
        self.waits = []

    def slot(self):
        self.used += 1
        return self.used - 1

    def send(self, source, target, device, slot, when=None):
        copy = pltpu.make_async_remote_copy(
            src_ref=source,
            dst_ref=target,
            send_sem=self.sent.at[slot],
            recv_sem=self.landed.at[slot],
            device_id=device,
            device_id_type=MESH,
        )
        if when is None:
            copy.start()
        else:
            pl.when(when)(copy.start)
        self.waits.append((copy, when))

    def land(self, target, device, slot, when=None):
        copy = pltpu.make_async_remote_copy(
            src_ref=target,
            dst_ref=target,
            send_sem=self.sent.at[slot],
            recv_sem=self.landed.at[slot],
            device_id=device,
            device_id_type=MESH,
        )
        if when is None:
            copy.wait_recv()
        else:
            pl.when(when)(copy.wait_recv)

    def move(self, source, target):
        copy = pltpu.make_async_copy(source, target, self.local.at[self.local_used])
        self.local_used += 1
        copy.start()
        self.waits.append((copy, "local"))
        return copy

    def finish(self):
        for copy, when in self.waits:
            if when == "local":
                copy.wait()
            elif when is None:
                copy.wait_send()
            else:
                pl.when(when)(copy.wait_send)


class Chain:
    def __init__(self, links, n, block):
        self.links, self.n, self.block = links, n, block
        self.slots = [(links.slot(), links.slot()) for _ in range(3)]

    def start(self, step):
        n, links = self.n, self.links
        right, left = self.slots[step]
        block = self.block(lax.rem(n + 4 - step, 4))
        links.send(
            block, block, {"narrow": lax.rem(n + 1, 4)}, right,
            (n < 3) & (n >= step),
        )
        block = self.block(lax.rem(n + step, 4))
        links.send(
            block, block, {"narrow": lax.rem(n + 3, 4)}, left,
            (n > 0) & (n + step <= 3),
        )

    def land(self, step):
        n, links = self.n, self.links
        right, left = self.slots[step]
        links.land(
            self.block(lax.rem(n + 7 - step, 4)), {"narrow": lax.rem(n + 3, 4)}, right,
            n >= step + 1,
        )
        links.land(
            self.block(lax.rem(n + 1 + step, 4)), {"narrow": lax.rem(n + 1, 4)}, left,
            n + 1 + step <= 3,
        )


class LineSum:
    def __init__(self, links, n, outbox, inbox):
        self.links, self.n, self.outbox, self.inbox = links, n, outbox, inbox
        self.inner = (n == 1) | (n == 2)
        self.outer = (n == 0) | (n == 3)
        self.targets = [self.owner(step) for step in range(NEAR)]
        self.next = 1 + lax.rem(n, 2)
        self.slots = [links.slot() for _ in range(6)]

    def owner(self, step):
        return lax.rem((4 - step) * self.n + (3 - step), 5)

    def put(self, step, part):
        self.outbox[step] = part.astype(BF)
        self.set_out(step)

    def set_out(self, step):
        links, outbox, inbox = self.links, self.outbox, self.inbox
        goal = {"narrow": self.next if step == 0 else self.targets[step]}
        far, near = self.slots[2 * step], self.slots[2 * step + 1]
        if step == 0:
            links.send(outbox.at[0], inbox.at[3], goal, far, self.outer)
            links.send(outbox.at[0], inbox.at[0], goal, near, self.inner)
        elif step == 1:
            links.send(outbox.at[1], inbox.at[1], goal, far, self.outer)
            links.send(outbox.at[1], inbox.at[0], goal, near, self.inner)
        else:
            links.send(outbox.at[2], inbox.at[2], goal, far, self.outer)

    def join(self):
        links, outbox, inbox = self.links, self.outbox, self.inbox
        home = {"narrow": 3 * (self.n // 2)}
        links.land(inbox.at[3], home, self.slots[0], self.inner)

        @pl.when(self.inner)
        def _():
            outbox[2] = (outbox[2].astype(F32) + inbox[3].astype(F32)).astype(BF)

    def relay(self):
        self.join()
        goal = {"narrow": self.targets[2]}
        self.links.send(
            self.outbox.at[2], self.inbox.at[1], goal, self.slots[5], self.inner
        )

    def early(self, own):
        links, inbox = self.links, self.inbox
        other = {"narrow": lax.rem(self.n + 1, 4)}
        links.land(inbox.at[0], other, self.slots[1], self.inner)
        links.land(inbox.at[0], other, self.slots[3], self.outer)
        links.land(inbox.at[1], other, self.slots[2], self.inner)

        @pl.when(self.outer)
        def _():
            inbox[1] = jnp.zeros(inbox.shape[1:], BF)

        return own + inbox[0].astype(F32) + inbox[1].astype(F32)

    def total(self, own):
        links, inbox = self.links, self.inbox
        outer, inner = self.outer, self.inner
        other = {"narrow": lax.rem(self.n + 1, 4)}
        links.land(inbox.at[0], other, self.slots[1], inner)
        links.land(inbox.at[0], other, self.slots[3], outer)
        links.land(inbox.at[1], other, self.slots[2], inner)
        links.land(inbox.at[1], other, self.slots[5], outer)
        links.land(inbox.at[2], other, self.slots[4], inner)

        @pl.when(outer)
        def _():
            inbox[2] = jnp.zeros(inbox.shape[1:], BF)

        for index in range(3):
            own = own + inbox[index].astype(F32)
        return own


class PlaneGather:
    def __init__(self, links, chip, core, plane, mate, source, blocks):
        self.links, self.chip, self.core, self.plane, self.mate = links, chip, core, plane, mate
        self.blocks = blocks
        self.slots = [links.slot() for _ in range(4)]
        self.mate_slots = [links.slot() for _ in range(4)]
        own = 2 * chip + core
        for side in range(2):
            links.send(source, blocks.at[own], self.at_plane(plane[side]), self.slots[side])
        links.send(source, blocks.at[own], mate, self.mate_slots[3])

    def at_plane(self, peer):
        return {"wide": 2 * peer + self.core}

    def half(self, peer, side):
        rows = self.blocks.shape[1] // 2
        return self.blocks.at[2 * peer + self.core, pl.ds(side * rows, rows), :]

    def pass_on(self):
        links, plane = self.links, self.plane
        for side in range(2):
            block = self.blocks.at[2 * plane[side] + self.core]
            links.land(block, self.at_plane(plane[side]), self.slots[side])
            part = self.half(plane[side], side)
            links.send(part, part, self.at_plane(plane[1 - side]), self.slots[2 + side])
            links.send(block, block, self.mate, self.mate_slots[side])

    def far(self):
        links, plane = self.links, self.plane
        for side in range(2):
            links.land(
                self.half(plane[2], side), self.at_plane(plane[1 - side]), self.slots[2 + side]
            )
        block = self.blocks.at[2 * plane[2] + self.core]
        links.send(block, block, self.mate, self.mate_slots[2])

    def finish(self):
        links, plane = self.links, self.plane
        for step in range(NEAR):
            block = self.blocks.at[2 * plane[step] + 1 - self.core]
            links.land(block, self.mate, self.mate_slots[step])
        links.land(self.blocks.at[2 * self.chip + 1 - self.core], self.mate, self.mate_slots[3])


FRONT_SLOTS = 104


def front_body(
    tok_ref, cot_ref, gains_ref, wq_ref, wk_ref, wv_ref, wo_ref, router_ref, gate_ref, up_ref,
    down_ref, segment_ref, parents_ref, ids_ref, rank_ref,
    qkvw_out, outw_out, expert_out, x_out, dy_out, gate_out, middle_out, hidden_out,
    tokens_out, qkv_out, prob_out, att_out, stat_out, rope_out, pick_out, cols_out,
    raw_proj, seen_at, raw, moved_ref, pack, tok_pack, qkvw, outw, cot_send, y_send, br_send, br_recv, stat_send, stat_recv,
    gate_send, sent, landed, local,
):
    n = lax.axis_index("narrow")
    w = lax.axis_index("wide")
    chip, core = w // 2, lax.rem(w, 2)
    to_z, from_z = places_of(n)
    plane = plane_of(chip)
    links = Links(sent, landed, local)
    mate = {"wide": 2 * chip + 1 - core}

    def at_plane(peer):
        return {"wide": 2 * peer + core}

    token_count, part_width = tok_ref.shape
    rows_each = raw.shape[1]
    raw_loads = [
        links.move(source, raw.at[kind_at]) for kind_at, source in enumerate((gate_ref, up_ref, down_ref))
    ]
    links.waits = []
    greet(to_z, plane, chip, core, True)

    def by_expert(kind_at):
        raw_loads[kind_at].wait()

        def some_rows(index, value):
            rows = pl.ds(pl.multiple_of(index * 32, 32), 32)
            for expert in range(EXPERTS):
                moved_ref[kind_at, expert, rows, :] = raw[kind_at, rows, expert, :]
            return value

        lax.fori_loop(0, rows_each // 32, some_rows, 0)

    tok_pack[0:token_count, :] = tok_ref[...]
    tok_pack[token_count : token_count + 2, :] = gains_ref[...]
    tokens_out[n] = tok_pack[...]
    tok_chain = Chain(links, n, lambda m: tokens_out.at[m])
    tok_chain.start(0)
    wide_shape = (token_count, token_count)
    row_at = lax.broadcasted_iota(jnp.int32, wide_shape, 0)
    col_at = lax.broadcasted_iota(jnp.int32, wide_shape, 1)
    seg_row, rank_row = segment_ref[...], rank_ref[...]
    first_row, second_row = ids_ref[0:1, :], ids_ref[1:2, :]
    stacked = [item.astype(F32) for item in (seg_row, rank_row, first_row, second_row)]
    columns = jnp.concatenate(stacked + [jnp.zeros((124, token_count), F32)], 0).T
    cols_out[...] = columns
    columns = columns.astype(jnp.int32)
    seg_col, rank_col = columns[:, 0:1], columns[:, 1:2]
    segs = parents_ref.shape[1]
    of_seg = lax.broadcasted_iota(jnp.int32, (token_count, segs), 1) == seg_col
    par_col = jnp.sum(
        jnp.where(of_seg, parents_ref[...].astype(F32), 0.0), 1, keepdims=True
    ).astype(jnp.int32)
    seen = ((seg_row == seg_col) | (seg_row == par_col) | (seg_row == 0)) & (col_at <= row_at)
    spots = jnp.sum(jnp.where(seen, 1.0, 0.0), 1, keepdims=True) - 1.0
    lane_at = lax.broadcasted_iota(jnp.int32, (token_count, HEAD_DIM), 1)
    turn = lax.rem(lane_at, HEAD_DIM // 2).astype(F32) * (-2.0 / HEAD_DIM * math.log(ROPE_BASE))
    angles = spots * jnp.exp(turn)
    cosines = jnp.cos(angles)
    sines = jnp.sin(angles) * jnp.where(lane_at < HEAD_DIM // 2, -1.0, 1.0)
    rope_out[0] = cosines
    rope_out[1] = sines
    kind = lax.broadcasted_iota(jnp.int32, (8, token_count), 0)
    hot_first = jnp.where(kind == first_row, 1.0, 0.0)
    hot_second = jnp.where(kind == second_row, 1.0, 0.0)
    earlier = jnp.where(rank_col < rank_row, 1.0, 0.0).astype(BF)
    count_first = low_dot(hot_first.astype(BF), earlier)
    count_second = low_dot(hot_second.astype(BF), earlier)
    count_second = count_second + jnp.sum(hot_first, 1, keepdims=True)
    slot_first = jnp.sum(count_first * hot_first, 0, keepdims=True)
    slot_second = jnp.sum(count_second * hot_second, 0, keepdims=True)
    kept_first = jnp.where(slot_first < CAP, 1.0, 0.0)
    kept_second = jnp.where(slot_second < CAP, 1.0, 0.0)
    flat_first = jnp.where(slot_first < CAP, first_row * CAP + slot_first.astype(jnp.int32), SLOTS)
    flat_second = jnp.where(
        slot_second < CAP, second_row * CAP + slot_second.astype(jnp.int32), SLOTS
    )
    slot_at = lax.broadcasted_iota(jnp.int32, (SLOTS, token_count), 0)
    pick_first = jnp.where(slot_at == flat_first, 1.0, 0.0)
    pick_second = jnp.where(slot_at == flat_second, 1.0, 0.0)
    pick_out[0] = pick_first.astype(BF)
    pick_out[1] = pick_second.astype(BF)
    pick_both = (pick_first + pick_second).astype(BF)

    def column_block(array):
        return lambda m: array.at[:, pl.ds(pl.multiple_of(m * part_width, part_width), part_width)]

    def slot_block(array, owner):
        return array.at[
            pl.ds(pl.multiple_of(owner * CAP, 16), CAP),
            pl.ds(pl.multiple_of(n * part_width, part_width), part_width),
        ]

    def dispatch(rows, buffer, array):
        slots = [links.slot() for _ in range(NEAR)]
        buffer[...] = low_dot(pick_both, rows).astype(BF)
        for step in range(NEAR):
            links.send(
                buffer.at[pl.ds(pl.multiple_of(plane[step] * CAP, 16), CAP), :],
                slot_block(array, chip), at_plane(plane[step]), slots[step],
            )
        own = links.move(
            buffer.at[pl.ds(pl.multiple_of(chip * CAP, 16), CAP), :], slot_block(array, chip)
        )
        return slots, own

    def arrive(array, state):
        slots, own = state
        for step in range(NEAR):
            links.land(slot_block(array, plane[step]), at_plane(plane[step]), slots[step])
        own.wait()
        links.waits = [item for item in links.waits if item[0] is not own]

    dy_state = dispatch(cot_ref[...], cot_send, dy_out)
    dy_chain = Chain(links, n, column_block(dy_out))

    pack[:, 0:512] = wq_ref[...]
    pack[:, 512:1024] = wk_ref[...]
    pack[:, 1024:1536] = wv_ref[...]
    router_rows = jnp.concatenate(
        [router_ref[...].astype(F32), jnp.zeros((128 - EXPERTS, rows_each), F32)], 0
    )
    pack[:, 1536:1664] = router_rows.T.astype(BF)
    in_gather = PlaneGather(links, chip, core, plane, mate, pack, qkvw)
    qkvw[w] = pack[...]
    outw[w] = wo_ref[...]

    tok_chain.land(0)
    tok_chain.start(1)
    by_expert(0)
    tok_chain.land(1)
    tok_chain.start(2)
    arrive(dy_out, dy_state)
    dy_chain.start(0)
    tok_chain.land(2)
    in_gather.pass_on()
    out_gather = PlaneGather(links, chip, core, plane, mate, wo_ref, outw)
    total = jnp.zeros((token_count, 1), F32)
    for m in range(4):
        part = tokens_out[m, 0:token_count, :].astype(F32)
        total = total + jnp.sum(part * part, 1, keepdims=True)
    scale_first = lax.rsqrt(total * (1.0 / (4 * part_width)) + NORM_EPS)
    for m in range(4):
        part = tokens_out[m, 0:token_count, :].astype(F32)
        gain = tokens_out[m, token_count : token_count + 1, :].astype(F32)
        hidden_out[:, m * part_width : (m + 1) * part_width] = (part * scale_first * gain).astype(BF)

    by_expert(1)

    in_gather.far()
    out_gather.pass_on()
    in_gather.finish()
    saved_in = links.move(qkvw, qkvw_out)

    expert_slots = [[links.slot() for _ in range(NEAR)] for _ in range(3)]
    expert_mate = [[links.slot() for _ in range(4)] for _ in range(3)]
    def set_out(kind_at):
        for step in range(NEAR):
            links.send(
                moved_ref.at[kind_at, plane[step]], expert_out.at[kind_at, chip, core],
                at_plane(plane[step]), expert_slots[kind_at][step],
            )
        links.send(
            moved_ref.at[kind_at, chip], expert_out.at[kind_at, chip, core], mate,
            expert_mate[kind_at][3],
        )
        links.move(moved_ref.at[kind_at, chip], expert_out.at[kind_at, chip, core])

    set_out(0)
    set_out(1)

    def pass_on(kind_at):
        for step in range(NEAR):
            block = expert_out.at[kind_at, plane[step], core]
            links.land(block, at_plane(plane[step]), expert_slots[kind_at][step])
            links.send(block, block, mate, expert_mate[kind_at][step])

    def all_there(kind_at):
        for step in range(NEAR):
            links.land(
                expert_out.at[kind_at, plane[step], 1 - core], mate, expert_mate[kind_at][step]
            )
        links.land(expert_out.at[kind_at, chip, 1 - core], mate, expert_mate[kind_at][3])

    dy_chain.land(0)
    dy_chain.start(1)
    by_expert(2)

    score_scale = HEAD_DIM ** (-0.5)

    def one_projection(part, value):
        cols = pl.ds(pl.multiple_of(part * part_width, part_width), part_width)
        weight = qkvw[:, :, cols].reshape(4 * part_width, part_width)
        raw_proj[part] = low_dot(hidden_out[...], weight)
        return value

    lax.fori_loop(0, 3, one_projection, 0)
    seen_at[...] = jnp.where(seen, 1.0, 0.0)

    def one_head(head, value):
        cols = pl.ds(pl.multiple_of(head * HEAD_DIM, HEAD_DIM), HEAD_DIM)
        turned = []
        for part in range(2):
            proj = raw_proj[part, :, cols]
            turned.append(
                (proj * rope_out[0] + pltpu.roll(proj, HEAD_DIM // 2, 1) * rope_out[1]).astype(BF)
            )
            qkv_out[part, :, cols] = turned[part]
        values = raw_proj[2, :, cols].astype(BF)
        qkv_out[2, :, cols] = values
        scores = rows_rows(turned[0], turned[1]) * score_scale
        scores = jnp.where(seen_at[...] > 0.5, scores, NEG_FILL)
        exps = jnp.exp(scores - jnp.max(scores, 1, keepdims=True))
        weights = exps / jnp.sum(exps, 1, keepdims=True)
        prob_out[head] = weights
        att_out[:, cols] = low_dot(weights.astype(BF), values).astype(BF)
        return value

    lax.fori_loop(0, part_width // HEAD_DIM, one_head, 0)

    dy_chain.land(1)
    dy_chain.start(2)
    out_gather.far()

    out_gather.finish()
    links.move(outw, outw_out)

    attended = att_out[...]

    def branch(m):
        weight = outw[pl.ds(2 * m, 2)].reshape(part_width, part_width)
        return rows_rows(attended, weight)

    branch_sum = LineSum(links, n, br_send, br_recv)
    for step in range(NEAR):
        branch_sum.put(step, branch(branch_sum.targets[step]))
    middle = tok_ref[...].astype(F32) + branch(n)
    branch_sum.relay()
    middle = branch_sum.total(middle)
    middle_out[...] = middle
    x_state = dispatch(middle.astype(BF), y_send, x_out)

    def cap_block(owner):
        return lambda m: x_out.at[
            pl.ds(pl.multiple_of(owner * CAP, 16), CAP),
            pl.ds(pl.multiple_of(m * part_width, part_width), part_width),
        ]

    x_chains = [Chain(links, n, cap_block(owner)) for owner in (chip, *plane)]
    x_slots, x_own = x_state
    x_own.wait()
    links.waits = [item for item in links.waits if item[0] is not x_own]
    x_chains[0].start(0)

    set_out(2)

    gain_second = gains_ref[1:2, :].astype(F32)
    router = qkvw[pl.ds(2 * n, 2), :, 1536:1664].reshape(part_width, 128)
    logit_part = mm(router, (middle * gain_second).astype(BF), ((0,), (1,)))[0:8, :]
    square = middle * middle
    square_high = square.astype(BF)
    square_low = (square - square_high.astype(F32)).astype(BF)
    ones = jnp.ones((8, part_width), BF)
    square_sum = rows_rows(ones, square_high) + rows_rows(ones, square_low)
    stat = jnp.where(kind == 4, square_sum, logit_part)
    stat_send[...] = stat
    stat_slots = [links.slot() for _ in range(NEAR)]
    for step in range(NEAR):
        links.send(stat_send, stat_recv.at[step], {"narrow": to_z[step]}, stat_slots[step])

    for step in range(NEAR):
        links.land(slot_block(x_out, plane[step]), at_plane(plane[step]), x_slots[step])
        x_chains[1 + step].start(0)
    for step in range(NEAR):
        links.land(stat_recv.at[step], {"narrow": from_z[step]}, stat_slots[step])
        stat = stat + stat_recv[step]
    stat_out[...] = stat
    scale_row = lax.rsqrt(stat[4:5, :] * (1.0 / (4 * part_width)) + NORM_EPS)
    logits = jnp.where(kind < EXPERTS, stat * scale_row, NEG_FILL)
    chances = jnp.exp(logits - jnp.max(logits, 0, keepdims=True))
    chances = chances / jnp.sum(chances, 0, keepdims=True)
    share_first = jnp.sum(chances * hot_first, 0, keepdims=True)
    share_second = jnp.sum(chances * hot_second, 0, keepdims=True)
    both = share_first + share_second
    weighted = pick_first * (share_first / both) + pick_second * (share_second / both)
    slot_gate = jnp.sum(weighted, 1, keepdims=True)
    gate_send[...] = jnp.broadcast_to(slot_gate, (SLOTS, 128))

    def gate_rows(array, owner):
        return array.at[pl.ds(pl.multiple_of(owner * CAP, 16), CAP), :]

    gate_slots = [links.slot() for _ in range(NEAR)]
    for step in range(NEAR):
        links.send(
            gate_rows(gate_send, plane[step]), gate_rows(gate_out, chip),
            at_plane(plane[step]), gate_slots[step],
        )
    links.move(gate_rows(gate_send, chip), gate_rows(gate_out, chip))

    for step in range(2):
        for chain in x_chains:
            chain.land(step)
            chain.start(step + 1)
        pass_on(step)
    for chain in x_chains:
        chain.land(2)
    dy_chain.land(2)
    for step in range(NEAR):
        links.land(gate_rows(gate_out, plane[step]), at_plane(plane[step]), gate_slots[step])
    pass_on(2)
    for kind_at in range(3):
        all_there(kind_at)
    links.finish()


def front_call(tokens, cotangent, gains, weights, router, experts, segment, parents, ids, rank):
    token_count, part_width = tokens.shape
    full = 4 * part_width
    rows_each, _, hidden_width = experts[0].shape
    heads = part_width // HEAD_DIM
    vmem = pl.BlockSpec(memory_space=pltpu.VMEM)
    hbm = pl.BlockSpec(memory_space=pl.ANY)

    def arr(shape, dtype):
        return jax.ShapeDtypeStruct(shape, dtype)

    return pl.pallas_call(
        front_body,
        out_shape=(
            arr((8, rows_each, 1664), BF),
            arr((8, rows_each, part_width), BF),
            arr((3, 4, 2, rows_each, hidden_width), BF),
            arr((SLOTS, full), BF),
            arr((SLOTS, full), BF),
            arr((SLOTS, 128), F32),
            arr((token_count, part_width), F32),
            arr((token_count, full), BF),
            arr((4, token_count + 16, part_width), BF),
            arr((3, token_count, part_width), BF),
            arr((heads, token_count, token_count), F32),
            arr((token_count, part_width), BF),
            arr((8, token_count), F32),
            arr((2, token_count, HEAD_DIM), F32),
            arr((2, SLOTS, token_count), BF),
            arr((token_count, 128), F32),
        ),
        in_specs=[vmem] * 8 + [hbm] * 3 + [vmem] * 4,
        out_specs=(hbm, hbm, hbm) + (vmem,) * 13,
        scratch_shapes=[
            pltpu.VMEM((3, token_count, part_width), F32),
            pltpu.VMEM((token_count, token_count), F32),
            pltpu.VMEM((3, rows_each, EXPERTS, hidden_width), BF),
            pltpu.VMEM((3, EXPERTS, rows_each, hidden_width), BF),
            pltpu.VMEM((rows_each, 1664), BF),
            pltpu.VMEM((token_count + 16, part_width), BF),
            pltpu.VMEM((8, rows_each, 1664), BF),
            pltpu.VMEM((8, rows_each, part_width), BF),
            pltpu.VMEM((SLOTS, part_width), BF),
            pltpu.VMEM((SLOTS, part_width), BF),
            pltpu.VMEM((NEAR, token_count, part_width), BF),
            pltpu.VMEM((NEAR + 1, token_count, part_width), BF),
            pltpu.VMEM((8, token_count), F32),
            pltpu.VMEM((NEAR, 8, token_count), F32),
            pltpu.VMEM((SLOTS, 128), F32),
            pltpu.SemaphoreType.DMA((FRONT_SLOTS,)),
            pltpu.SemaphoreType.DMA((FRONT_SLOTS,)),
            pltpu.SemaphoreType.DMA((16,)),
        ],
        compiler_params=pltpu.CompilerParams(
            collective_id=0, has_side_effects=True, vmem_limit_bytes=60 * 1024 * 1024
        ),
        cost_estimate=pl.CostEstimate(
            flops=6_000_000_000, bytes_accessed=60_000_000, transcendentals=400_000
        ),
        name="front",
    )(tokens, cotangent, gains, *weights, router, *experts, segment, parents, ids, rank)


MID_SLOTS = 48


TILE = 512


def mid_body(
    x_ref, dy_ref, gate_ref, tokens_ref, w_ref,
    back_mid_out, back_exp_out, last_exp_out, extra_out, grads_out, expert_out,
    weights, hidden, graded_send, hidden_cat, graded_cat, act_cat, gate_cat, up_cat,
    turned, down_grad, rs_send, rs_recv, ext_send, ext_recv, sent, landed, local,
):
    n = lax.axis_index("narrow")
    w = lax.axis_index("wide")
    chip, core = w // 2, lax.rem(w, 2)
    to_z, from_z = places_of(n)
    plane = plane_of(chip)
    links = Links(sent, landed, local)
    mate = {"wide": 2 * chip + 1 - core}
    slots, full = hidden.shape
    part_width = full // 4
    rows_each = full // 8
    half = full // 2
    hidden_width = weights.shape[2]

    x_load = links.move(x_ref, hidden)
    loads = [
        links.move(
            w_ref.at[kind, c, k],
            weights.at[kind, pl.ds((2 * c + k) * rows_each, rows_each), :],
        )
        for kind in range(3)
        for c in range(4)
        for k in range(2)
    ]
    links.waits = []
    greet(to_z, plane, chip, core, True)

    slot_gate = gate_ref[:, 0:1]
    for c in range(4):
        theirs = pl.ds(pl.multiple_of((2 * c + 1 - core) * rows_each, rows_each), rows_each)
        ours = pl.ds(pl.multiple_of((2 * c + core) * rows_each, rows_each), rows_each)
        cols = slice(c * rows_each, (c + 1) * rows_each)
        graded_cat[core, :, cols] = (dy_ref[:, ours].astype(F32) * slot_gate).astype(BF)
        graded_send[:, cols] = (dy_ref[:, theirs].astype(F32) * slot_gate).astype(BF)

    def to_mate(source, target):
        slot = links.slot()
        links.send(source, target.at[core], mate, slot)
        return lambda: links.land(target.at[1 - core], mate, slot)

    graded_there = to_mate(graded_send, graded_cat)
    x_load.wait()
    total = jnp.zeros((slots, 1), F32)
    for m in range(4):
        part = hidden[:, m * part_width : (m + 1) * part_width].astype(F32)
        total = total + jnp.sum(part * part, 1, keepdims=True)
    scale = lax.rsqrt(total * (1.0 / full) + NORM_EPS)
    gain_row = tokens_ref.shape[1] - 15
    for m in range(4):
        cols = slice(m * part_width, (m + 1) * part_width)
        gain = tokens_ref[m, gain_row : gain_row + 1, :].astype(F32)
        hidden[:, cols] = (hidden[:, cols].astype(F32) * scale * gain).astype(BF)
    hidden_slots = [links.slot() for _ in range(4)]
    for c in range(4):
        cols = pl.ds(c * rows_each, rows_each)
        theirs = pl.ds(pl.multiple_of((2 * c + 1 - core) * rows_each, rows_each), rows_each)
        ours = pl.ds(pl.multiple_of((2 * c + core) * rows_each, rows_each), rows_each)
        links.send(hidden.at[:, theirs], hidden_cat.at[core, :, cols], mate, hidden_slots[c])
        hidden_cat[core, :, c * rows_each : (c + 1) * rows_each] = hidden[:, ours]
    for load in loads:
        load.wait()

    def one_tile(cols, rows):
        gate_pre = low_dot(hidden[rows, :], weights[0, :, cols])
        up_pre = low_dot(hidden[rows, :], weights[1, :, cols])
        act_raw = low_dot(dy_ref[rows, :], weights[2, :, cols])
        sigmoid = 1.0 / (1.0 + jnp.exp(-gate_pre))
        silu = gate_pre * sigmoid
        activated = (silu * up_pre).astype(BF)
        grad_act = act_raw * gate_ref[rows, 0:1]
        act_cat[core, rows, cols] = activated
        gate_cat[core, rows, cols] = (
            grad_act * up_pre * (sigmoid * (1.0 + gate_pre * (1.0 - sigmoid)))
        ).astype(BF)
        up_cat[core, rows, cols] = (grad_act * silu).astype(BF)
        return jnp.sum(act_raw * activated.astype(F32), 1, keepdims=True)

    def over_tiles(tile, body, carry):
        whole = hidden_width // tile
        carry = lax.fori_loop(
            0, whole, lambda t, value: body(pl.ds(pl.multiple_of(t * tile, tile), tile), value), carry
        )
        if hidden_width % tile:
            carry = body(pl.ds(whole * tile, hidden_width % tile), carry)
        return carry

    share = over_tiles(
        TILE,
        lambda cols, value: tuple(
            value[index] + one_tile(cols, pl.ds(index * (slots // 2), slots // 2))
            for index in range(2)
        ),
        (jnp.zeros((slots // 2, 1), F32),) * 2,
    )
    share = jnp.concatenate(share, 0)
    acts_there = [to_mate(item.at[core], item) for item in (act_cat, gate_cat, up_cat)]

    grad_gate, grad_up = gate_cat.at[core], up_cat.at[core]
    mid_sum = LineSum(links, n, rs_send.at[0], rs_recv.at[0])

    def mid_part(owner):
        rows = pl.ds(pl.multiple_of(owner * part_width, part_width), part_width)
        block = rows_rows(grad_gate[...], weights[0, rows, :])
        block = block + rows_rows(grad_up[...], weights[1, rows, :])
        return block, jnp.sum(hidden[:, rows].astype(F32) * block, 1, keepdims=True)

    stat = jnp.zeros((slots, 1), F32)
    block, part = mid_part(mid_sum.targets[0])
    mid_sum.put(0, block)
    stat = stat + part

    expert_slots = {}

    def weight_grad(right, target):
        def body(cols, value):
            right_rows = right[:, :, cols].reshape(2 * slots, cols.size)
            target[:, cols] = low_dot(turned[...], right_rows).astype(BF)
            return value

        over_tiles(TILE, body, 0)

    def share_out(index, source):
        expert_slots[index] = [links.slot() for _ in range(NEAR)]

        def block(owner):
            first = pl.multiple_of(owner * rows_each, rows_each)
            return source.at[pl.ds(first, rows_each), :]

        for step in range(NEAR):
            links.send(
                block(plane[step]), expert_out.at[index, chip],
                {"wide": 2 * plane[step] + core}, expert_slots[index][step],
            )
        links.move(block(chip), expert_out.at[index, chip])

    graded_there()
    acts_there[0]()
    turned[...] = graded_cat[...].reshape(2 * slots, half).T
    weight_grad(act_cat, down_grad)
    share_out(0, down_grad)

    def other_part(step, stat):
        block, part = mid_part(mid_sum.owner(step))
        rs_send[0, step] = block.astype(BF)
        return stat + part

    stat = lax.fori_loop(1, 4, other_part, stat)
    mid_sum.set_out(1)
    mid_sum.set_out(2)
    lane_at = lax.broadcasted_iota(jnp.int32, (slots, 128), 1)
    columns = jnp.where(lane_at == 0, share, jnp.where(lane_at == 1, stat, 0.0))
    high = columns.astype(BF)
    rest = (columns - high.astype(F32)).astype(BF)
    pick = jnp.where(
        lax.broadcasted_iota(jnp.int32, (8, 128), 0) == lax.broadcasted_iota(jnp.int32, (8, 128), 1),
        1.0, 0.0,
    ).astype(BF)
    extra = rows_rows(pick, high) + rows_rows(pick, rest)
    ext_send[...] = extra
    ext_slots = [links.slot() for _ in range(NEAR)]
    for step in range(NEAR):
        links.send(ext_send, ext_recv.at[step], {"narrow": to_z[step]}, ext_slots[step])

    mid_sum.relay()

    activated = act_cat.at[core]
    exp_sum = LineSum(links, n, rs_send.at[1], rs_recv.at[1])

    def exp_part(owner):
        rows = pl.ds(pl.multiple_of(owner * part_width, part_width), part_width)
        return rows_rows(activated[...], weights[2, rows, :])

    def expert_part(step, value):
        rs_send[1, step] = exp_part(exp_sum.owner(step)).astype(BF)
        return value

    lax.fori_loop(0, 4, expert_part, 0)
    exp_sum.set_out(0)
    exp_sum.set_out(1)
    for slot in hidden_slots:
        index = hidden_slots.index(slot)
        links.land(
            hidden_cat.at[1 - core, :, pl.ds(index * rows_each, rows_each)], mate, slot
        )
    for there in acts_there[1:]:
        there()
    turned[...] = hidden_cat[...].reshape(2 * slots, half).T
    gate_grad = weights.at[0, pl.ds(0, half), :]
    weight_grad(gate_cat, gate_grad)
    share_out(1, gate_grad)
    up_grad = weights.at[1, pl.ds(0, half), :]
    weight_grad(up_cat, up_grad)
    links.move(up_grad, grads_out)

    for step in range(NEAR):
        links.land(ext_recv.at[step], {"narrow": from_z[step]}, ext_slots[step])
        extra = extra + ext_recv[step]
    high = extra.astype(BF)
    rest = (extra - high.astype(F32)).astype(BF)
    place = lax.broadcasted_iota(jnp.int32, (8, 128), 0) * 2
    lanes = lax.broadcasted_iota(jnp.int32, (8, 128), 1)
    spread_high = jnp.where(place == lanes, 1.0, 0.0).astype(BF)
    spread_low = jnp.where(place + 1 == lanes, 1.0, 0.0).astype(BF)
    columns = mm(high, spread_high, ((0,), (0,))) + mm(rest, spread_low, ((0,), (0,)))
    extra_out[...] = jnp.where(lane_at == 4, 1.0, columns).astype(BF)
    back_mid_out[...] = mid_sum.total(rs_send[0, 3].astype(F32)).astype(BF)
    exp_sum.join()
    last_exp_out[...] = rs_send[1, 2]
    back_exp_out[...] = exp_sum.early(rs_send[1, 3].astype(F32)).astype(BF)
    for index in range(2):
        for step in range(NEAR):
            links.land(
                expert_out.at[index, plane[step]], {"wide": 2 * plane[step] + core},
                expert_slots[index][step],
            )
    links.finish()


def mid_call(slot_mid, slot_grad, slot_gate, token_parts, expert_w):
    slots, full = slot_mid.shape
    part_width = full // 4
    rows_each, hidden_width = expert_w.shape[3:]
    vmem = pl.BlockSpec(memory_space=pltpu.VMEM)
    hbm = pl.BlockSpec(memory_space=pl.ANY)

    def arr(shape, dtype):
        return jax.ShapeDtypeStruct(shape, dtype)

    return pl.pallas_call(
        mid_body,
        out_shape=(
            arr((slots, part_width), BF),
            arr((slots, part_width), BF),
            arr((slots, part_width), BF),
            arr((slots, 128), BF),
            arr((full // 2, hidden_width), BF),
            arr((2, 4, rows_each, hidden_width), BF),
        ),
        in_specs=[hbm] + [vmem] * 3 + [hbm],
        out_specs=(vmem,) * 4 + (hbm, hbm),
        scratch_shapes=[
            pltpu.VMEM((3, full, hidden_width), BF),
            pltpu.VMEM((slots, full), BF),
            pltpu.VMEM((slots, full // 2), BF),
            pltpu.VMEM((2, slots, full // 2), BF),
            pltpu.VMEM((2, slots, full // 2), BF),
            pltpu.VMEM((2, slots, hidden_width), BF),
            pltpu.VMEM((2, slots, hidden_width), BF),
            pltpu.VMEM((2, slots, hidden_width), BF),
            pltpu.VMEM((full // 2, 2 * slots), BF),
            pltpu.VMEM((full // 2, hidden_width), BF),
            pltpu.VMEM((2, NEAR + 1, slots, part_width), BF),
            pltpu.VMEM((2, NEAR + 1, slots, part_width), BF),
            pltpu.VMEM((8, slots), F32),
            pltpu.VMEM((NEAR, 8, slots), F32),
            pltpu.SemaphoreType.DMA((MID_SLOTS,)),
            pltpu.SemaphoreType.DMA((MID_SLOTS,)),
            pltpu.SemaphoreType.DMA((32,)),
        ],
        compiler_params=pltpu.CompilerParams(
            collective_id=1, has_side_effects=True, vmem_limit_bytes=62 * 1024 * 1024
        ),
        cost_estimate=pl.CostEstimate(
            flops=30_000_000_000, bytes_accessed=40_000_000, transcendentals=800_000
        ),
        name="mid",
    )(slot_mid, slot_grad, slot_gate, token_parts, expert_w)


class PlaneSum:
    def __init__(self, links, core, chip, plane, first, send, inbox):
        self.links, self.core, self.chip = links, core, chip
        self.near, self.next, self.far = plane[first], plane[1 - first], plane[2]
        self.send, self.inbox = send, inbox
        self.slots = [links.slot() for _ in range(3)]

    def at(self, peer):
        return {"wide": 2 * peer + self.core}

    def block(self, owner):
        rows = self.inbox.shape[1]
        return self.send.at[pl.ds(pl.multiple_of(owner * rows, rows), rows), :]

    def start(self):
        links = self.links
        links.send(self.block(self.far), self.inbox.at[1], self.at(self.near), self.slots[1])
        links.send(self.block(self.near), self.inbox.at[0], self.at(self.near), self.slots[0])

    def turn(self):
        links = self.links
        links.land(self.inbox.at[1], self.at(self.near), self.slots[1])
        block = self.block(self.next)
        block[...] = (block[...].astype(F32) + self.inbox[1].astype(F32)).astype(BF)
        links.send(block, self.inbox.at[2], self.at(self.next), self.slots[2])

    def total(self):
        links = self.links
        links.land(self.inbox.at[0], self.at(self.near), self.slots[0])
        links.land(self.inbox.at[2], self.at(self.next), self.slots[2])
        own = self.block(self.chip)[...].astype(F32)
        return own + self.inbox[0].astype(F32) + self.inbox[2].astype(F32)


TAIL_SLOTS = 72


def tail_body(
    mid_ref, exp_ref, last_ref, ext_ref, moved_ref, picks_ref, stat_ref, cols_ref, middle_ref, cot_ref,
    tok_ref, tokens_ref, qkv_ref, prob_ref, att_ref, rope_ref, hidden_ref, qkvw_ref, outw_ref,
    output_out, grad_tokens_out, summed_out, small_out,
    router_out, expert_out,
    grad_att_at, exp_in, exp_sum, router_all, qkvw, outw, ret_mid, ret_exp, ret_ext, branch, hidden_cat, branch_cat, att_cat, proj_cat,
    proj_send, proj_recv, first_send, first_recv, col_send, col_recv, small_mate, small_sum,
    small_recv, last_mate, last_sum, last_recv, sent, landed, local,
):
    n = lax.axis_index("narrow")
    w = lax.axis_index("wide")
    chip, core = w // 2, lax.rem(w, 2)
    to_z, from_z = places_of(n)
    plane = plane_of(chip)
    links = Links(sent, landed, local)
    mate = {"wide": 2 * chip + 1 - core}
    token_count, part_width = tok_ref.shape
    full = 4 * part_width
    rows_each = full // 8
    heads = part_width // HEAD_DIM
    half = full // 2

    def at_plane(peer):
        return {"wide": 2 * peer + core}

    def cap_rows(array, owner):
        return array.at[pl.ds(pl.multiple_of(owner * CAP, 16), CAP), :]

    loads = [links.move(qkvw_ref, qkvw), links.move(outw_ref, outw)]
    links.waits = []
    greet(to_z, plane, chip, core, True)

    last_slot = links.slot()
    links.send(last_ref, exp_in, {"narrow": lax.rem(2 * n + 1, 5)}, last_slot)

    back_slots = []

    def give_back(source, target):
        slots = [links.slot() for _ in range(NEAR)]
        for step in range(NEAR):
            links.send(
                cap_rows(source, plane[step]), cap_rows(target, chip), at_plane(plane[step]),
                slots[step],
            )
        own = links.move(cap_rows(source, chip), cap_rows(target, chip))
        links.waits.pop()
        back_slots.append((target, slots, own))

    give_back(mid_ref, ret_mid)
    give_back(ext_ref, ret_ext)

    def returned(which):
        target, slots, own = back_slots[which]
        for step in range(NEAR):
            links.land(cap_rows(target, plane[step]), at_plane(plane[step]), slots[step])
        own.wait()
        return target[...]

    expert_slots = [links.slot() for _ in range(NEAR)]
    for step in range(NEAR):
        block = pl.ds(pl.multiple_of(plane[step] * rows_each, rows_each), rows_each)
        links.send(
            moved_ref.at[block, :], expert_out.at[chip], at_plane(plane[step]), expert_slots[step]
        )
    block = pl.ds(pl.multiple_of(chip * rows_each, rows_each), rows_each)
    links.move(moved_ref.at[block, :], expert_out.at[chip])

    def to_mate(source, target):
        slot = links.slot()
        links.send(source, target.at[core], mate, slot)
        return lambda: links.land(target.at[1 - core], mate, slot)

    def parity_exchange(source, target):
        lands = []
        for c in range(4):
            cols = pl.ds(c * rows_each, rows_each)
            theirs = pl.ds(pl.multiple_of((2 * c + 1 - core) * rows_each, rows_each), rows_each)
            ours = pl.ds(pl.multiple_of((2 * c + core) * rows_each, rows_each), rows_each)
            slot = links.slot()
            links.send(source.at[:, theirs], target.at[core, :, cols], mate, slot)
            target[core, :, c * rows_each : (c + 1) * rows_each] = source[:, ours]
            lands.append((target.at[1 - core, :, cols], slot))
        return lambda: [links.land(block, mate, slot) for block, slot in lands]

    hidden_there = parity_exchange(hidden_ref, hidden_cat)
    att_cat[core] = att_ref[...]
    att_there = to_mate(att_ref, att_cat)

    stat = jnp.concatenate([stat_ref[...], jnp.zeros((120, token_count), F32)], 0).T
    lane_at = lax.broadcasted_iota(jnp.int32, (token_count, 128), 1)
    scale_second = lax.rsqrt(stat[:, 4:5] * (1.0 / full) + NORM_EPS)
    logits = stat * scale_second
    hot_first = lane_at == cols_ref[:, 2:3].astype(jnp.int32)
    hot_second = lane_at == cols_ref[:, 3:4].astype(jnp.int32)
    logit_first = jnp.sum(jnp.where(hot_first, logits, 0.0), 1, keepdims=True)
    logit_second = jnp.sum(jnp.where(hot_second, logits, 0.0), 1, keepdims=True)
    apart = logit_first - logit_second
    share_first = 1.0 / (1.0 + jnp.exp(-apart))
    share_second = 1.0 / (1.0 + jnp.exp(apart))
    normed = middle_ref[...] * scale_second
    gain_second = tokens_ref[n, token_count + 1 : token_count + 2, :].astype(F32)
    hidden_second = (normed * gain_second).astype(BF)
    for load in loads:
        load.wait()
    router = qkvw[pl.ds(2 * n, 2), :, 1536:1664].reshape(part_width, 128)

    rows_mid = returned(0)
    rows_ext = returned(1)
    ext_first = cols_cols(picks_ref[0], rows_ext)
    ext_second = cols_cols(picks_ref[1], rows_ext)
    ext_both = ext_first + ext_second
    grad_share = ext_first[:, 0:1] + ext_first[:, 1:2] - ext_second[:, 0:1] - ext_second[:, 1:2]
    delta = (grad_share * share_first * share_second).astype(BF).astype(F32)
    grad_logits = jnp.where(hot_first, delta, jnp.where(hot_second, -delta, 0.0)).astype(BF)
    stat_total = ext_both[:, 2:3] + ext_both[:, 3:4] + delta * apart
    grad_hidden = cols_cols(picks_ref[0] + picks_ref[1], rows_mid) + rows_rows(grad_logits, router)
    grad_middle = cot_ref[...].astype(F32) + scale_second * (
        gain_second * grad_hidden - normed * (stat_total * (1.0 / full))
    )
    own_cols = pl.ds(pl.multiple_of(n * part_width, part_width), part_width)
    branch[:, own_cols] = grad_middle.astype(BF)
    branch_slots = [links.slot() for _ in range(NEAR)]
    for step in range(NEAR):
        links.send(
            branch.at[:, own_cols], branch.at[:, own_cols], {"narrow": to_z[step]},
            branch_slots[step],
        )

    links.land(exp_in, {"narrow": lax.rem(n + 1, 4)}, last_slot)
    exp_sum[...] = (exp_ref[...].astype(F32) + exp_in[...].astype(F32)).astype(BF)
    give_back(exp_sum, ret_exp)

    router_part = cols_cols(grad_logits, hidden_second)[0:8, :]
    gain_part = jnp.sum(grad_hidden * normed, 0, keepdims=True)
    kind_at = lax.broadcasted_iota(jnp.int32, (8, part_width), 0)
    small = jnp.where(kind_at == 4, gain_part, router_part)
    small_mate[core] = small
    small_there = to_mate(small_mate.at[core], small_mate)

    small_there()
    small = small_mate[0] + small_mate[1]
    small_sum[...] = small
    small_slots = [links.slot() for _ in range(NEAR)]
    for step in range(NEAR):
        links.send(small_sum, small_recv.at[step], at_plane(plane[step]), small_slots[step])

    for step in range(NEAR):
        cols = pl.ds(pl.multiple_of(from_z[step] * part_width, part_width), part_width)
        links.land(branch.at[:, cols], {"narrow": from_z[step]}, branch_slots[step])
    branch_there = parity_exchange(branch, branch_cat)
    grad_att = low_dot(branch[...], outw[...].reshape(full, part_width)).astype(BF)

    proj_sums = {
        part: PlaneSum(
            links, core, chip, plane, part % 2, proj_send.at[part], proj_recv.at[part]
        )
        for part in (3, 0, 1, 2)
    }

    branch_there()
    att_there()
    proj_send[3] = cols_cols(
        branch_cat[...].reshape(2 * token_count, half), att_cat[...].reshape(2 * token_count, part_width)
    ).astype(BF)
    proj_sums[3].start()
    score_scale = HEAD_DIM ** (-0.5)
    grad_att_at[...] = grad_att

    def one_head(head, stat_first):
        def lanes(start):
            return pl.ds(pl.multiple_of(start + head * HEAD_DIM, HEAD_DIM), HEAD_DIM)

        query, key, value = (qkv_ref[i, :, lanes(0)] for i in range(3))
        grad_out = grad_att_at[:, lanes(0)]
        weights = prob_ref[head]
        grad_weights = rows_rows(grad_out, value)
        inner = jnp.sum(weights * grad_weights, 1, keepdims=True)
        grad_scores = (weights * (grad_weights - inner)).astype(BF)
        grad_query = low_dot(grad_scores, key) * score_scale
        grad_key = cols_cols(grad_scores, query) * score_scale
        grad_value = cols_cols(weights.astype(BF), grad_out)
        products = (
            grad_query * query.astype(F32)
            + grad_key * key.astype(F32)
            + grad_value * value.astype(F32)
        )
        for part, grad in ((0, grad_query), (1, grad_key)):
            turned = grad * rope_ref[0] - pltpu.roll(grad, HEAD_DIM // 2, 1) * rope_ref[1]
            proj_cat[core, :, lanes(part * part_width)] = turned.astype(BF)
        proj_cat[core, :, lanes(2 * part_width)] = grad_value.astype(BF)
        return stat_first + jnp.sum(products, 1, keepdims=True)

    stat_first = lax.fori_loop(0, heads, one_head, jnp.zeros((token_count, 1), F32))
    proj_there = to_mate(proj_cat.at[core], proj_cat)
    high = stat_first.astype(BF)
    rest = (stat_first - high.astype(F32)).astype(BF)
    col_send[...] = jnp.where(
        lane_at == 0, high.astype(F32), jnp.where(lane_at == 1, rest.astype(F32), 0.0)
    ).astype(BF)
    col_slots = [links.slot() for _ in range(NEAR)]
    for step in range(NEAR):
        links.send(col_send, col_recv.at[step], {"narrow": to_z[step]}, col_slots[step])
    grads = proj_cat[core]

    def first_block(m):
        weight = qkvw[pl.ds(2 * m, 2), :, 0:1536].reshape(part_width, 1536)
        return rows_rows(grads, weight)

    def fill_first(step, value):
        first_send[step] = first_block(lax.rem(n + 1 + step, 4)).astype(BF)
        return value

    lax.fori_loop(0, NEAR, fill_first, 0)
    first_slots = [links.slot() for _ in range(NEAR)]
    for step in range(NEAR):
        links.send(
            first_send.at[step], first_recv.at[step], {"narrow": to_z[step]}, first_slots[step]
        )

    hidden_there()
    proj_there()
    hidden_rows = hidden_cat[...].reshape(2 * token_count, half)
    proj_sums[3].turn()
    for part in range(3):
        cols = slice(part * 512, (part + 1) * 512)
        proj_send[part] = cols_cols(
            hidden_rows, proj_cat[:, :, cols].reshape(2 * token_count, part_width)
        ).astype(BF)
        proj_sums[part].start()

    rows_exp = returned(2)
    output_out[...] = (
        middle_ref[...]
        + share_first * cols_cols(picks_ref[0], rows_exp)
        + share_second * cols_cols(picks_ref[1], rows_exp)
    ).astype(BF)

    grad_first = first_block(n)
    stat_first = high.astype(F32) + rest.astype(F32)
    total = jnp.zeros((token_count, 1), F32)
    for m in range(4):
        part = tokens_ref[m, 0:token_count, :].astype(F32)
        total = total + jnp.sum(part * part, 1, keepdims=True)
    scale_first = lax.rsqrt(total * (1.0 / full) + NORM_EPS)
    normed_first = tok_ref[...].astype(F32) * scale_first
    gain_first = tokens_ref[n, token_count : token_count + 1, :].astype(F32)
    for step in range(NEAR):
        links.land(col_recv.at[step], {"narrow": from_z[step]}, col_slots[step])
        stat_first = stat_first + (
            col_recv[step, :, 0:1].astype(F32) + col_recv[step, :, 1:2].astype(F32)
        )
    for step in range(NEAR):
        links.land(first_recv.at[step], {"narrow": from_z[step]}, first_slots[step])
        grad_first = grad_first + first_recv[step].astype(F32)
    grad_tokens_out[...] = grad_middle + scale_first * (
        gain_first * grad_first - normed_first * (stat_first * (1.0 / full))
    )
    gain_part = jnp.sum(grad_first * normed_first, 0, keepdims=True)
    for part in range(3):
        proj_sums[part].turn()
    last_mate[core] = jnp.broadcast_to(gain_part, (8, part_width))
    last_there = to_mate(last_mate.at[core], last_mate)

    for step in range(NEAR):
        links.land(small_recv.at[step], at_plane(plane[step]), small_slots[step])
        small = small + small_recv[step]
    last_there()
    last = last_mate[0] + last_mate[1]
    last_sum[...] = last
    last_slots = [links.slot() for _ in range(NEAR)]
    for step in range(NEAR):
        links.send(last_sum, last_recv.at[step], at_plane(plane[step]), last_slots[step])
    router_all[:, own_cols] = small
    router_slots = [links.slot() for _ in range(NEAR)]
    for step in range(NEAR):
        links.send(
            router_all.at[:, own_cols], router_all.at[:, own_cols], {"narrow": to_z[step]},
            router_slots[step],
        )
    for step in range(NEAR):
        links.land(last_recv.at[step], at_plane(plane[step]), last_slots[step])
        last = last + last_recv[step]
    small_out[...] = jnp.where(kind_at == 5, last, small)
    for step in range(NEAR):
        cols = pl.ds(pl.multiple_of(from_z[step] * part_width, part_width), part_width)
        links.land(router_all.at[:, cols], {"narrow": from_z[step]}, router_slots[step])

    router_out[...] = router_all[:, pl.ds(pl.multiple_of(w * rows_each, rows_each), rows_each)]
    for part in range(4):
        summed_out[:, part * part_width : (part + 1) * part_width] = proj_sums[part].total()
    for step in range(NEAR):
        links.land(expert_out.at[plane[step]], at_plane(plane[step]), expert_slots[step])
    links.finish()


def tail_call(*args):
    slots, part_width = args[0].shape
    half, hidden_width = args[4].shape
    token_count = args[10].shape[0]
    full, rows_each = 2 * half, half // 4
    vmem = pl.BlockSpec(memory_space=pltpu.VMEM)
    hbm = pl.BlockSpec(memory_space=pl.ANY)

    def arr(shape, dtype):
        return jax.ShapeDtypeStruct(shape, dtype)

    own = (token_count, part_width)
    return pl.pallas_call(
        tail_body,
        out_shape=(
            arr(own, BF),
            arr(own, F32),
            arr((rows_each, full), F32),
            arr((8, part_width), F32),
            arr((8, rows_each), F32),
            arr((4, rows_each, hidden_width), BF),
        ),
        in_specs=[vmem] * 4 + [hbm] + [vmem] * 12 + [hbm] * 2,
        out_specs=(vmem,) * 5 + (hbm,),
        scratch_shapes=[
            pltpu.VMEM(own, BF),
            pltpu.VMEM((slots, part_width), BF),
            pltpu.VMEM((slots, part_width), BF),
            pltpu.VMEM((8, full), F32),
            pltpu.VMEM((8, rows_each, 1664), BF),
            pltpu.VMEM((8, rows_each, part_width), BF),
            pltpu.VMEM((slots, part_width), BF),
            pltpu.VMEM((slots, part_width), BF),
            pltpu.VMEM((slots, 128), BF),
            pltpu.VMEM((token_count, full), BF),
            pltpu.VMEM((2, token_count, half), BF),
            pltpu.VMEM((2, token_count, half), BF),
            pltpu.VMEM((2, token_count, part_width), BF),
            pltpu.VMEM((2, token_count, 1536), BF),
            pltpu.VMEM((4, half, part_width), BF),
            pltpu.VMEM((4, NEAR, rows_each, part_width), BF),
            pltpu.VMEM((NEAR,) + own, BF),
            pltpu.VMEM((NEAR,) + own, BF),
            pltpu.VMEM((token_count, 128), BF),
            pltpu.VMEM((NEAR, token_count, 128), BF),
            pltpu.VMEM((2, 8, part_width), F32),
            pltpu.VMEM((8, part_width), F32),
            pltpu.VMEM((NEAR, 8, part_width), F32),
            pltpu.VMEM((2, 8, part_width), F32),
            pltpu.VMEM((8, part_width), F32),
            pltpu.VMEM((NEAR, 8, part_width), F32),
            pltpu.SemaphoreType.DMA((TAIL_SLOTS,)),
            pltpu.SemaphoreType.DMA((TAIL_SLOTS,)),
            pltpu.SemaphoreType.DMA((16,)),
        ],
        compiler_params=pltpu.CompilerParams(
            collective_id=2, has_side_effects=True, vmem_limit_bytes=60 * 1024 * 1024
        ),
        cost_estimate=pl.CostEstimate(
            flops=6_000_000_000, bytes_accessed=60_000_000, transcendentals=1_000
        ),
        name="tail",
    )(*args)


def finish_body(
    down_ref, gate_ref, up_ref, output_ref, tokens_ref, summed_ref,
    gate_out, up_out, down_out, output_out, tokens_out, *proj_outs,
):
    def some_rows(index, value):
        rows = pl.ds(pl.multiple_of(index * 16, 16), 16)
        for source, target in ((gate_ref, gate_out), (up_ref, up_out), (down_ref, down_out)):
            for expert in range(EXPERTS):
                target[rows, expert, :] = source[expert, rows, :].astype(F32)
        return value

    lax.fori_loop(0, tokens_ref.shape[0] // 16, some_rows, 0)
    output_out[...] = output_ref[...]
    tokens_out[...] = tokens_ref[...]
    width = tokens_ref.shape[1]
    for part, target in enumerate(proj_outs):
        target[...] = summed_ref[:, part * width : (part + 1) * width].astype(F32)


def finish_call(early, late, output, grad_tokens, summed):
    _, rows_each, hidden_width = late.shape
    token_count, part_width = output.shape
    step = 32

    def flat(width):
        return pl.BlockSpec((step, width), lambda i: (i, 0))

    def cube(which):
        return pl.BlockSpec((None, EXPERTS, step, hidden_width), lambda i: (which, 0, i, 0))

    spread = pl.BlockSpec((step, EXPERTS, hidden_width), lambda i: (i, 0, 0))

    def arr(shape, dtype):
        return jax.ShapeDtypeStruct(shape, dtype)

    return pl.pallas_call(
        finish_body,
        grid=(rows_each // step,),
        out_shape=(arr((rows_each, EXPERTS, hidden_width), F32),) * 3
        + (arr(output.shape, BF), arr(output.shape, F32))
        + (arr((rows_each, part_width), F32),) * 4,
        in_specs=[
            cube(0), cube(1),
            pl.BlockSpec((EXPERTS, step, hidden_width), lambda i: (0, i, 0)),
            flat(part_width), flat(part_width), flat(4 * part_width),
        ],
        out_specs=(spread,) * 3 + (flat(part_width),) * 6,
        name="finish",
    )(early, early, late, output, grad_tokens, summed)


def plain_device(
    tokens, gain_attn, w_query, w_key, w_value, w_out, gain_ffn, w_router,
    w_gate, w_up, w_down, segment, parents, expert_ids, slot_order, cotangent,
):
    narrow_count = lax.axis_size("narrow")
    wide_count = lax.axis_size("wide")
    narrow_at = lax.axis_index("narrow")
    token_count, part_width = tokens.shape
    full_width = part_width * narrow_count
    hidden_width = w_gate.shape[2]
    rows_each = w_gate.shape[0]
    blocks = wide_count // 8
    quads = [
        [8 * block + 2 * chip + core for chip in range(4)]
        for block in range(blocks)
        for core in range(2)
    ]
    mates = [
        [8 * block + 2 * chip + core for block in range(blocks) for core in range(2)]
        for chip in range(4)
    ]

    def quad_swap(array):
        return lax.all_to_all(array, "wide", 0, 0, axis_index_groups=quads, tiled=True)

    def own_rows(weight):
        moved = quad_swap(jnp.transpose(weight, (1, 0, 2)))
        joined = lax.all_gather(moved, "wide", axis=0, axis_index_groups=mates, tiled=True)
        joined = joined.reshape(blocks, 2, 4, rows_each, hidden_width).transpose(0, 2, 1, 3, 4)
        return joined.reshape(full_width, hidden_width)

    def share_rows(grad):
        parts = grad.astype(BF).reshape(blocks, 4, 2, rows_each, hidden_width)
        parts = parts.transpose(0, 2, 1, 3, 4).reshape(blocks * 2, 4, rows_each, hidden_width)
        summed = lax.psum_scatter(
            parts, "wide", scatter_dimension=0, axis_index_groups=mates, tiled=True
        )[0]
        return jnp.transpose(quad_swap(summed), (1, 0, 2)).astype(F32)

    def head_cols(array, head):
        return array[:, head * HEAD_DIM : (head + 1) * HEAD_DIM]

    heads = part_width // HEAD_DIM
    half_dim = HEAD_DIM // 2
    freqs = ROPE_BASE ** (-2.0 * jnp.arange(half_dim, dtype=F32) / HEAD_DIM)
    score_scale = HEAD_DIM ** (-0.5)
    gains = jnp.stack([gain_attn, gain_ffn])
    gain_first_loc = gain_attn.astype(F32)
    gain_second_loc = gain_ffn.astype(F32)
    hot_first, hot_second, kept, pick_first, pick_second = route(expert_ids, slot_order[0])

    gate_w, up_w, down_w = own_rows(w_gate), own_rows(w_up), own_rows(w_down)
    attn_w = lax.all_gather(
        jnp.stack([w_query, w_key, w_value, w_out], 1), "wide", axis=0, tiled=True
    )
    query_w, key_w, value_w, out_w = (attn_w[:, i] for i in range(4))
    router_w = lax.all_gather(w_router, "wide", axis=0, tiled=True)
    tokens_full = lax.all_gather(tokens, "narrow", axis=1, tiled=True)
    grad_full = lax.all_gather(cotangent, "narrow", axis=1, tiled=True)
    gains_full = lax.all_gather(gains, "narrow", axis=1, tiled=True)
    gain_first = gains_full[0].astype(F32)
    gain_second = gains_full[1].astype(F32)

    seen, places = tree_layout(segment[0], parents[0])
    pick_first_low = pick_first.astype(BF)
    pick_second_low = pick_second.astype(BF)
    pick_both_low = (pick_first | pick_second).astype(BF)

    inputs_full = tokens_full.astype(F32)
    scale_first = lax.rsqrt(jnp.mean(inputs_full * inputs_full, -1, keepdims=True) + NORM_EPS)
    normed_first = inputs_full * scale_first
    hidden_first = (normed_first * gain_first).astype(BF)
    angles = places[:, None] * freqs[None, :]
    cosines, sines = jnp.cos(angles), jnp.sin(angles)
    query_raw = rows_cols(hidden_first, query_w)
    key_raw = rows_cols(hidden_first, key_w)
    value_low = rows_cols(hidden_first, value_w).astype(BF)

    saved = []
    outs = []
    for head in range(heads):
        query = rotate(head_cols(query_raw, head), cosines, sines).astype(BF)
        key = rotate(head_cols(key_raw, head), cosines, sines).astype(BF)
        value = head_cols(value_low, head)
        scores = jnp.where(seen, rows_rows(query, key) * score_scale, NEG_FILL)
        exps = jnp.exp(scores - jnp.max(scores, -1, keepdims=True))
        weights = exps / jnp.sum(exps, -1, keepdims=True)
        saved.append((query, key, value, weights))
        outs.append(rows_cols(weights.astype(BF), value).astype(BF))
    attended = jnp.concatenate(outs, 1)
    branch_part = rows_rows(attended, out_w).astype(BF)
    branch_loc = lax.psum_scatter(
        branch_part, "narrow", scatter_dimension=1, tiled=True
    ).astype(F32)
    middle = tokens.astype(F32) + branch_loc
    middle_full = lax.all_gather(middle.astype(BF), "narrow", axis=1, tiled=True).astype(F32)
    scale_second = lax.rsqrt(jnp.mean(middle_full * middle_full, -1, keepdims=True) + NORM_EPS)
    normed_second = middle_full * scale_second
    hidden_second = (normed_second * gain_second).astype(BF)
    logits = rows_cols(hidden_second, router_w)
    share_first, share_second = gate_pair(logits, hot_first, hot_second)
    weight_first = kept[:, 0] * share_first
    weight_second = kept[:, 1] * share_second

    slot_weight = jnp.sum(
        pick_first * weight_first[:, None] + pick_second * weight_second[:, None], 0
    )
    weight_high, weight_low = two_parts(slot_weight)
    pads = jnp.stack([weight_high, weight_low], 1)
    pads = jnp.pad(pads, ((0, 0), (0, 126)))
    sent_hidden = cols_cols(pick_both_low, hidden_second).astype(BF)
    sent_grad = cols_cols(pick_both_low, grad_full).astype(BF)
    sent = jnp.concatenate([sent_hidden, sent_grad, pads], 1)
    got = quad_swap(sent.reshape(EXPERTS, CAP, -1)).reshape(SLOTS, -1)
    slot_hidden = got[:, :full_width]
    slot_grad = got[:, full_width : 2 * full_width]
    slot_gate = got[:, 2 * full_width : 2 * full_width + 2].astype(F32)
    slot_gate = slot_gate[:, 0:1] + slot_gate[:, 1:2]

    gate_pre = rows_cols(slot_hidden, gate_w)
    up_pre = rows_cols(slot_hidden, up_w)
    sigmoid_gate = jax.nn.sigmoid(gate_pre)
    silu_gate = gate_pre * sigmoid_gate
    activated = (silu_gate * up_pre).astype(BF)
    expert_part = rows_rows(activated, down_w)
    act_raw = rows_cols(slot_grad, down_w)
    share_part = jnp.sum(act_raw * activated.astype(F32), 1, keepdims=True)
    grad_act = act_raw * slot_gate
    grad_gate_pre = (
        grad_act * up_pre * sigmoid_gate * (1.0 + gate_pre * (1.0 - sigmoid_gate))
    ).astype(BF)
    grad_up_pre = (grad_act * silu_gate).astype(BF)
    grad_slot = rows_rows(grad_gate_pre, gate_w) + rows_rows(grad_up_pre, up_w)
    stat_part = jnp.sum(slot_hidden.astype(F32) * grad_slot, 1, keepdims=True)
    extras = jnp.concatenate([*two_parts(share_part), *two_parts(stat_part)], 1)
    extras = jnp.pad(extras, ((0, 0), (0, 124)))
    back_parts = []
    expert_plain = expert_part.astype(BF)
    slot_plain = grad_slot.astype(BF)
    for part in range(narrow_count):
        cols = slice(part * part_width, (part + 1) * part_width)
        back_parts += [expert_plain[:, cols], slot_plain[:, cols], extras]
    back = lax.psum_scatter(
        jnp.concatenate(back_parts, 1), "narrow", scatter_dimension=1, tiled=True
    )
    back = quad_swap(back.reshape(EXPERTS, CAP, -1)).reshape(SLOTS, -1)
    picked_first = rows_cols(pick_first_low, back)
    picked_second = rows_cols(pick_second_low, back)
    output = (
        middle
        + weight_first[:, None] * picked_first[:, :part_width]
        + weight_second[:, None] * picked_second[:, :part_width]
    ).astype(BF)

    grad_weight = (slot_grad.astype(F32) * slot_gate).astype(BF)
    gate_out = share_rows(cols_cols(slot_hidden, grad_gate_pre))
    up_out = share_rows(cols_cols(slot_hidden, grad_up_pre))
    down_out = share_rows(cols_cols(grad_weight, activated))

    tail = 2 * part_width
    share_first_grad = picked_first[:, tail] + picked_first[:, tail + 1]
    share_second_grad = picked_second[:, tail] + picked_second[:, tail + 1]
    both = picked_first + picked_second
    stat_second = both[:, tail + 2] + both[:, tail + 3]
    grad_hidden_loc = both[:, part_width:tail]
    grad_local = cotangent.astype(F32)
    _, pull_gates = jax.vjp(lambda given: gate_pair(given, hot_first, hot_second), logits)
    (grad_logits,) = pull_gates((kept[:, 0] * share_first_grad, kept[:, 1] * share_second_grad))
    grad_logits_low = grad_logits.astype(BF)
    grad_router_rows = rows_rows(grad_logits_low, router_w)
    stat_total = stat_second + jnp.sum(normed_second * gain_second * grad_router_rows, 1)

    def take_cols(full_rows):
        return lax.dynamic_slice_in_dim(full_rows, narrow_at * part_width, part_width, 1)

    grad_hidden_loc = grad_hidden_loc + take_cols(grad_router_rows)
    normed_second_loc = take_cols(normed_second)
    grad_gain_second = jnp.sum(grad_hidden_loc * normed_second_loc, 0)
    grad_middle = grad_local + scale_second * (
        gain_second_loc * grad_hidden_loc - normed_second_loc * stat_total[:, None] / full_width
    )
    grad_router_w = cols_cols(hidden_second, grad_logits_low)
    grad_branch = lax.all_gather(grad_middle.astype(BF), "narrow", axis=1, tiled=True)
    grad_attended = rows_cols(grad_branch, out_w).astype(BF)
    grad_out_w = cols_cols(grad_branch, attended)
    grad_qs, grad_ks, grad_vs = [], [], []
    for head in range(heads):
        query, key, value, weights = saved[head]
        grad_out = head_cols(grad_attended, head)
        grad_weights = rows_rows(grad_out, value)
        inner = jnp.sum(weights * grad_weights, -1, keepdims=True)
        grad_scores = (weights * (grad_weights - inner)).astype(BF)
        grad_q = rows_cols(grad_scores, key) * score_scale
        grad_k = cols_cols(grad_scores, query) * score_scale
        grad_qs.append(rotate(grad_q, cosines, -sines).astype(BF))
        grad_ks.append(rotate(grad_k, cosines, -sines).astype(BF))
        grad_vs.append(cols_cols(weights.astype(BF), grad_out).astype(BF))
    grad_query_raw = jnp.concatenate(grad_qs, 1)
    grad_key_raw = jnp.concatenate(grad_ks, 1)
    grad_value_raw = jnp.concatenate(grad_vs, 1)
    grad_hidden_first = (
        rows_rows(grad_query_raw, query_w)
        + rows_rows(grad_key_raw, key_w)
        + rows_rows(grad_value_raw, value_w)
    )
    stat_first = jnp.sum(normed_first * gain_first * grad_hidden_first, 1, keepdims=True)
    extras = jnp.pad(jnp.concatenate(two_parts(stat_first), 1), ((0, 0), (0, 126)))
    grad_hidden_low = grad_hidden_first.astype(BF)
    first_parts = []
    for part in range(narrow_count):
        first_parts += [grad_hidden_low[:, part * part_width : (part + 1) * part_width], extras]
    first_back = lax.psum_scatter(
        jnp.concatenate(first_parts, 1), "narrow", scatter_dimension=1, tiled=True
    ).astype(F32)
    grad_first_loc = first_back[:, :part_width]
    stat_first = first_back[:, part_width : part_width + 1]
    stat_first = stat_first + first_back[:, part_width + 1 : part_width + 2]
    normed_first_loc = take_cols(normed_first)
    grad_gain_first = jnp.sum(grad_first_loc * normed_first_loc, 0)
    grad_tokens = grad_middle + scale_first * (
        gain_first_loc * grad_first_loc - normed_first_loc * stat_first / full_width
    )
    grad_attn_w = jnp.concatenate(
        [
            cols_cols(hidden_first, grad_query_raw).astype(BF),
            cols_cols(hidden_first, grad_key_raw).astype(BF),
            cols_cols(hidden_first, grad_value_raw).astype(BF),
            grad_out_w.astype(BF),
        ],
        1,
    )
    attn_summed = lax.psum_scatter(
        grad_attn_w, "wide", scatter_dimension=0, tiled=True
    ).astype(F32)
    router_summed = lax.psum_scatter(grad_router_w, "wide", scatter_dimension=0, tiled=True)
    gains_summed = lax.psum(jnp.stack([grad_gain_first, grad_gain_second]), "wide")
    return (
        output,
        grad_tokens,
        gains_summed[0],
        attn_summed[:, :part_width],
        attn_summed[:, part_width : 2 * part_width],
        attn_summed[:, 2 * part_width : 3 * part_width],
        attn_summed[:, 3 * part_width :],
        gains_summed[1],
        router_summed,
        gate_out,
        up_out,
        down_out,
    )


def per_device(
    tokens, gain_attn, w_query, w_key, w_value, w_out, gain_ffn, w_router,
    w_gate, w_up, w_down, segment, parents, expert_ids, slot_order, cotangent,
):
    if lax.axis_size("wide") != 8 or lax.axis_size("narrow") != 4:
        return plain_device(
            tokens, gain_attn, w_query, w_key, w_value, w_out, gain_ffn, w_router,
            w_gate, w_up, w_down, segment, parents, expert_ids, slot_order, cotangent,
        )
    (
        in_w, out_w, expert_w, slot_mid, slot_grad, slot_gate, middle, hidden_first,
        token_parts, qkv, probs, attended, stat, rope, picks, columns,
    ) = front_call(
        tokens, cotangent, jnp.stack([gain_attn, gain_ffn]), (w_query, w_key, w_value, w_out),
        w_router.T, (w_gate, w_up, w_down), segment, parents, expert_ids.T, slot_order,
    )
    back_mid, back_exp, last_exp, back_ext, grads, early_experts = mid_call(
        slot_mid, slot_grad, slot_gate, token_parts, expert_w
    )
    (
        output, grad_tokens, summed, small, router, experts,
    ) = tail_call(
        back_mid, back_exp, last_exp, back_ext, grads, picks, stat, columns, middle, cotangent, tokens,
        token_parts, qkv, probs, attended, rope, hidden_first, in_w, out_w,
    )
    gate_out, up_out, down_out, output, grad_tokens, grad_q, grad_k, grad_v, grad_o = finish_call(
        early_experts, experts, output, grad_tokens, summed
    )
    return (
        output, grad_tokens, small[5], grad_q, grad_k, grad_v, grad_o, small[4],
        router[:EXPERTS].T, gate_out, up_out, down_out,
    )


def solution(mesh):
    pair = P("wide", "narrow")
    part = P("narrow")
    rows = P("wide", None)
    cube = P("wide", None, "narrow")
    return jax.shard_map(
        per_device,
        mesh=mesh,
        in_specs=(
            pair, part, pair, pair, pair, pair, part, rows, cube, cube, cube,
            rows, rows, rows, rows, pair,
        ),
        out_specs=(
            pair, pair, part, pair, pair, pair, pair, part, rows, cube, cube, cube,
        ),
        check_vma=False,
    )
```

```python
import math

import jax
import jax.numpy as jnp
from jax import lax
from jax.experimental import pallas as pl
from jax.experimental.pallas import tpu as pltpu
from jax.sharding import PartitionSpec as P

HEAD_DIM = 128
EXPERTS = 4
SEGS = 13
CAP = 144
SLOTS = EXPERTS * CAP
NORM_EPS = 1e-05
NEG_FILL = -1e30
ROPE_BASE = 10000.0
BF = jnp.bfloat16
F32 = jnp.float32


def mm(left, right, dims):
    return lax.dot_general(left, right, (dims, ((), ())), preferred_element_type=F32)


def rows_cols(left, right):
    return mm(left, right, ((1,), (0,)))


def rows_rows(left, right):
    return mm(left, right, ((1,), (1,)))


def cols_cols(left, right):
    return mm(left, right, ((0,), (0,)))


def tree_layout(segment_row, parent_row):
    seg_ids = jnp.arange(SEGS, dtype=jnp.int32)
    member = segment_row[:, None] == seg_ids[None, :]
    parent_of = (parent_row[:, None] == seg_ids[None, :]) & (seg_ids[:, None] != 0)
    itself = seg_ids[:, None] == seg_ids[None, :]
    reach = itself
    for _ in range(3):
        reach = itself | jnp.any(parent_of[:, :, None] & reach[None, :, :], axis=1)
    counts = member.astype(jnp.int32)
    lengths = jnp.sum(counts, 0)
    starts = jnp.sum(jnp.where(seg_ids[None, :] < seg_ids[:, None], lengths[None, :], 0), 1)
    before = jnp.sum(jnp.where(reach, lengths[None, :], 0), 1) - lengths
    row_at = jnp.arange(segment_row.shape[0], dtype=jnp.int32)
    places = jnp.sum(counts * (before - starts)[None, :], 1) + row_at
    member_low = member.astype(BF)
    lineage = rows_cols(member_low, reach.astype(BF)).astype(BF)
    shared = rows_rows(lineage, member_low) > 0.5
    seen = shared & (row_at[None, :] <= row_at[:, None])
    return seen, places.astype(F32)


def route(expert_row, slot_rank):
    expert_range = jnp.arange(EXPERTS, dtype=jnp.int32)
    hot_first = (expert_row[:, 0:1] == expert_range[None, :]).astype(F32)
    hot_second = (expert_row[:, 1:2] == expert_range[None, :]).astype(F32)
    earlier = (slot_rank[None, :] < slot_rank[:, None]).astype(BF)
    count_first = rows_cols(earlier, hot_first.astype(BF))
    count_second = rows_cols(earlier, hot_second.astype(BF))
    ahead_first = jnp.sum(count_first * hot_first, 1)
    ahead_second = jnp.sum((count_second + jnp.sum(hot_first, 0)[None, :]) * hot_second, 1)
    slot_index = jnp.stack([ahead_first, ahead_second], 1).astype(jnp.int32)
    kept = slot_index < CAP
    flat_slot = jnp.where(kept, expert_row * CAP + slot_index, SLOTS)
    slot_range = jnp.arange(SLOTS, dtype=jnp.int32)
    pick_first = flat_slot[:, 0:1] == slot_range[None, :]
    pick_second = flat_slot[:, 1:2] == slot_range[None, :]
    return hot_first, hot_second, kept.astype(F32), pick_first, pick_second


def rotate(vectors, cosines, sines):
    half_dim = HEAD_DIM // 2
    first_half = vectors[..., :half_dim]
    second_half = vectors[..., half_dim:]
    return jnp.concatenate(
        [
            first_half * cosines - second_half * sines,
            second_half * cosines + first_half * sines,
        ],
        -1,
    )


def gate_pair(logits, hot_first, hot_second):
    chances = jax.nn.softmax(logits, axis=-1)
    first_share = jnp.sum(chances * hot_first, 1)
    second_share = jnp.sum(chances * hot_second, 1)
    pair_total = first_share + second_share
    return (first_share / pair_total, second_share / pair_total)


def two_parts(column):
    high = column.astype(BF)
    return high, (column - high.astype(F32)).astype(BF)


MESH = pl.DeviceIdType.MESH
NEAR = 3


def low_dot(left, right):
    return jnp.dot(left, right, preferred_element_type=F32)


def places_of(n):
    return [lax.rem(n + step, 4) for step in (1, 2, 3)], [lax.rem(n + 4 - step, 4) for step in (1, 2, 3)]


def plane_of(chip):
    x, y = lax.rem(chip, 2), chip // 2
    return [2 * y + 1 - x, 2 * (1 - y) + x, 2 * (1 - y) + 1 - x]


def greet(narrow_peers, plane_peers, chip, core, mate):
    barrier = pltpu.get_barrier_semaphore()
    count = 0
    for peer in narrow_peers:
        pl.semaphore_signal(barrier, inc=1, device_id={"narrow": peer}, device_id_type=MESH)
        count += 1
    for peer in plane_peers:
        pl.semaphore_signal(
            barrier, inc=1, device_id={"wide": 2 * peer + core}, device_id_type=MESH
        )
        count += 1
    if mate:
        pl.semaphore_signal(
            barrier, inc=1, device_id={"wide": 2 * chip + 1 - core}, device_id_type=MESH
        )
        count += 1
    pl.semaphore_wait(barrier, count)


class Links:
    def __init__(self, sent, landed, local):
        self.sent, self.landed, self.local = sent, landed, local
        self.used, self.local_used = 0, 0
        self.waits = []

    def slot(self):
        self.used += 1
        return self.used - 1

    def send(self, source, target, device, slot, when=None):
        copy = pltpu.make_async_remote_copy(
            src_ref=source,
            dst_ref=target,
            send_sem=self.sent.at[slot],
            recv_sem=self.landed.at[slot],
            device_id=device,
            device_id_type=MESH,
        )
        if when is None:
            copy.start()
        else:
            pl.when(when)(copy.start)
        self.waits.append((copy, when))

    def land(self, target, device, slot, when=None):
        copy = pltpu.make_async_remote_copy(
            src_ref=target,
            dst_ref=target,
            send_sem=self.sent.at[slot],
            recv_sem=self.landed.at[slot],
            device_id=device,
            device_id_type=MESH,
        )
        if when is None:
            copy.wait_recv()
        else:
            pl.when(when)(copy.wait_recv)

    def move(self, source, target):
        copy = pltpu.make_async_copy(source, target, self.local.at[self.local_used])
        self.local_used += 1
        copy.start()
        self.waits.append((copy, "local"))
        return copy

    def finish(self):
        for copy, when in self.waits:
            if when == "local":
                copy.wait()
            elif when is None:
                copy.wait_send()
            else:
                pl.when(when)(copy.wait_send)


class Chain:
    def __init__(self, links, n, block):
        self.links, self.n, self.block = links, n, block
        self.slots = [(links.slot(), links.slot()) for _ in range(3)]

    def start(self, step):
        n, links = self.n, self.links
        right, left = self.slots[step]
        block = self.block(lax.rem(n + 4 - step, 4))
        links.send(
            block, block, {"narrow": lax.rem(n + 1, 4)}, right,
            (n < 3) & (n >= step),
        )
        block = self.block(lax.rem(n + step, 4))
        links.send(
            block, block, {"narrow": lax.rem(n + 3, 4)}, left,
            (n > 0) & (n + step <= 3),
        )

    def land(self, step):
        n, links = self.n, self.links
        right, left = self.slots[step]
        links.land(
            self.block(lax.rem(n + 7 - step, 4)), {"narrow": lax.rem(n + 3, 4)}, right,
            n >= step + 1,
        )
        links.land(
            self.block(lax.rem(n + 1 + step, 4)), {"narrow": lax.rem(n + 1, 4)}, left,
            n + 1 + step <= 3,
        )


class LineSum:
    def __init__(self, links, n, outbox, inbox):
        self.links, self.n, self.outbox, self.inbox = links, n, outbox, inbox
        self.inner = (n == 1) | (n == 2)
        self.outer = (n == 0) | (n == 3)
        self.targets = [self.owner(step) for step in range(NEAR)]
        self.next = 1 + lax.rem(n, 2)
        self.slots = [links.slot() for _ in range(6)]

    def owner(self, step):
        return lax.rem((4 - step) * self.n + (3 - step), 5)

    def put(self, step, part):
        self.outbox[step] = part.astype(BF)
        self.set_out(step)

    def set_out(self, step):
        links, outbox, inbox = self.links, self.outbox, self.inbox
        goal = {"narrow": self.next if step == 0 else self.targets[step]}
        far, near = self.slots[2 * step], self.slots[2 * step + 1]
        if step == 0:
            links.send(outbox.at[0], inbox.at[3], goal, far, self.outer)
            links.send(outbox.at[0], inbox.at[0], goal, near, self.inner)
        elif step == 1:
            links.send(outbox.at[1], inbox.at[1], goal, far, self.outer)
            links.send(outbox.at[1], inbox.at[0], goal, near, self.inner)
        else:
            links.send(outbox.at[2], inbox.at[2], goal, far, self.outer)

    def join(self):
        links, outbox, inbox = self.links, self.outbox, self.inbox
        home = {"narrow": 3 * (self.n // 2)}
        links.land(inbox.at[3], home, self.slots[0], self.inner)

        @pl.when(self.inner)
        def _():
            outbox[2] = (outbox[2].astype(F32) + inbox[3].astype(F32)).astype(BF)

    def relay(self):
        self.join()
        goal = {"narrow": self.targets[2]}
        self.links.send(
            self.outbox.at[2], self.inbox.at[1], goal, self.slots[5], self.inner
        )

    def early(self, own):
        links, inbox = self.links, self.inbox
        other = {"narrow": lax.rem(self.n + 1, 4)}
        links.land(inbox.at[0], other, self.slots[1], self.inner)
        links.land(inbox.at[0], other, self.slots[3], self.outer)
        links.land(inbox.at[1], other, self.slots[2], self.inner)

        @pl.when(self.outer)
        def _():
            inbox[1] = jnp.zeros(inbox.shape[1:], BF)

        return own + inbox[0].astype(F32) + inbox[1].astype(F32)

    def total(self, own):
        links, inbox = self.links, self.inbox
        outer, inner = self.outer, self.inner
        other = {"narrow": lax.rem(self.n + 1, 4)}
        links.land(inbox.at[0], other, self.slots[1], inner)
        links.land(inbox.at[0], other, self.slots[3], outer)
        links.land(inbox.at[1], other, self.slots[2], inner)
        links.land(inbox.at[1], other, self.slots[5], outer)
        links.land(inbox.at[2], other, self.slots[4], inner)

        @pl.when(outer)
        def _():
            inbox[2] = jnp.zeros(inbox.shape[1:], BF)

        for index in range(3):
            own = own + inbox[index].astype(F32)
        return own


class PlaneGather:
    def __init__(self, links, chip, core, plane, mate, source, blocks):
        self.links, self.chip, self.core, self.plane, self.mate = links, chip, core, plane, mate
        self.blocks = blocks
        self.slots = [links.slot() for _ in range(4)]
        self.mate_slots = [links.slot() for _ in range(4)]
        own = 2 * chip + core
        for side in range(2):
            links.send(source, blocks.at[own], self.at_plane(plane[side]), self.slots[side])
        links.send(source, blocks.at[own], mate, self.mate_slots[3])

    def at_plane(self, peer):
        return {"wide": 2 * peer + self.core}

    def half(self, peer, side):
        rows = self.blocks.shape[1] // 2
        return self.blocks.at[2 * peer + self.core, pl.ds(side * rows, rows), :]

    def pass_on(self):
        links, plane = self.links, self.plane
        for side in range(2):
            block = self.blocks.at[2 * plane[side] + self.core]
            links.land(block, self.at_plane(plane[side]), self.slots[side])
            part = self.half(plane[side], side)
            links.send(part, part, self.at_plane(plane[1 - side]), self.slots[2 + side])
            links.send(block, block, self.mate, self.mate_slots[side])

    def far(self):
        links, plane = self.links, self.plane
        for side in range(2):
            links.land(
                self.half(plane[2], side), self.at_plane(plane[1 - side]), self.slots[2 + side]
            )
        block = self.blocks.at[2 * plane[2] + self.core]
        links.send(block, block, self.mate, self.mate_slots[2])

    def finish(self):
        links, plane = self.links, self.plane
        for step in range(NEAR):
            block = self.blocks.at[2 * plane[step] + 1 - self.core]
            links.land(block, self.mate, self.mate_slots[step])
        links.land(self.blocks.at[2 * self.chip + 1 - self.core], self.mate, self.mate_slots[3])


FRONT_SLOTS = 112


def front_body(
    tok_ref, cot_ref, gain_first_ref, gain_second_ref, wq_ref, wk_ref, wv_ref, wo_ref, router_ref, gate_ref, up_ref,
    down_ref, segment_ref, parents_ref, ids_ref, rank_ref,
    qkvw_out, outw_out, expert_out, x_out, dy_out, gate_out, middle_out, hidden_hbm,
    tokens_hbm, qkv_hbm, prob_hbm, att_out, stat_out, rope_out, pick_hbm, cols_out,
    hidden_out, tokens_out, qkv_out, prob_out, pick_out,
    raw_proj, seen_at, raw, moved_ref, pack, tok_pack, qkvw, outw, cot_send, y_send, br_send,
    br_recv, stat_send, stat_recv, gate_send, sent, landed, local,
):
    n = lax.axis_index("narrow")
    w = lax.axis_index("wide")
    chip, core = w // 2, lax.rem(w, 2)
    to_z, from_z = places_of(n)
    plane = plane_of(chip)
    links = Links(sent, landed, local)
    mate = {"wide": 2 * chip + 1 - core}

    def at_plane(peer):
        return {"wide": 2 * peer + core}

    token_count, part_width = tok_ref.shape
    rows_each = raw.shape[1]
    raw_loads = [
        links.move(source, raw.at[kind_at]) for kind_at, source in enumerate((gate_ref, up_ref, down_ref))
    ]
    links.waits = []
    greet(to_z, plane, chip, core, True)

    def by_expert(kind_at):
        raw_loads[kind_at].wait()

        def some_rows(index, value):
            rows = pl.ds(pl.multiple_of(index * 32, 32), 32)
            for expert in range(EXPERTS):
                moved_ref[kind_at, expert, rows, :] = raw[kind_at, rows, expert, :]
            return value

        lax.fori_loop(0, rows_each // 32, some_rows, 0)

    tok_pack[0:token_count, :] = tok_ref[...]
    for index, gain_ref in enumerate((gain_first_ref, gain_second_ref)):
        for row in range(part_width // 128):
            tok_pack[
                token_count + index : token_count + index + 1, row * 128 : (row + 1) * 128
            ] = gain_ref[row : row + 1, :]
    tokens_out[n] = tok_pack[...]
    tok_chain = Chain(links, n, lambda m: tokens_out.at[m])
    tok_chain.start(0)
    wide_shape = (token_count, token_count)
    row_at = lax.broadcasted_iota(jnp.int32, wide_shape, 0)
    col_at = lax.broadcasted_iota(jnp.int32, wide_shape, 1)
    seg_row, rank_row = segment_ref[...], rank_ref[...]
    first_row, second_row = ids_ref[0:1, :], ids_ref[1:2, :]
    stacked = [item.astype(F32) for item in (seg_row, rank_row, first_row, second_row)]
    columns = jnp.concatenate(stacked + [jnp.zeros((124, token_count), F32)], 0).T
    cols_out[...] = columns
    columns = columns.astype(jnp.int32)
    seg_col, rank_col = columns[:, 0:1], columns[:, 1:2]
    segs = parents_ref.shape[1]
    of_seg = lax.broadcasted_iota(jnp.int32, (token_count, segs), 1) == seg_col
    par_col = jnp.sum(
        jnp.where(of_seg, parents_ref[...].astype(F32), 0.0), 1, keepdims=True
    ).astype(jnp.int32)
    seen = ((seg_row == seg_col) | (seg_row == par_col) | (seg_row == 0)) & (col_at <= row_at)
    spots = jnp.sum(jnp.where(seen, 1.0, 0.0), 1, keepdims=True) - 1.0
    lane_at = lax.broadcasted_iota(jnp.int32, (token_count, HEAD_DIM), 1)
    turn = lax.rem(lane_at, HEAD_DIM // 2).astype(F32) * (-2.0 / HEAD_DIM * math.log(ROPE_BASE))
    angles = spots * jnp.exp(turn)
    cosines = jnp.cos(angles)
    sines = jnp.sin(angles) * jnp.where(lane_at < HEAD_DIM // 2, -1.0, 1.0)
    rope_out[0] = cosines
    rope_out[1] = sines
    kind = lax.broadcasted_iota(jnp.int32, (8, token_count), 0)
    hot_first = jnp.where(kind == first_row, 1.0, 0.0)
    hot_second = jnp.where(kind == second_row, 1.0, 0.0)
    earlier = jnp.where(rank_col < rank_row, 1.0, 0.0).astype(BF)
    count_first = low_dot(hot_first.astype(BF), earlier)
    count_second = low_dot(hot_second.astype(BF), earlier)
    count_second = count_second + jnp.sum(hot_first, 1, keepdims=True)
    slot_first = jnp.sum(count_first * hot_first, 0, keepdims=True)
    slot_second = jnp.sum(count_second * hot_second, 0, keepdims=True)
    kept_first = jnp.where(slot_first < CAP, 1.0, 0.0)
    kept_second = jnp.where(slot_second < CAP, 1.0, 0.0)
    flat_first = jnp.where(slot_first < CAP, first_row * CAP + slot_first.astype(jnp.int32), SLOTS)
    flat_second = jnp.where(
        slot_second < CAP, second_row * CAP + slot_second.astype(jnp.int32), SLOTS
    )
    slot_at = lax.broadcasted_iota(jnp.int32, (SLOTS, token_count), 0)
    pick_first = jnp.where(slot_at == flat_first, 1.0, 0.0)
    pick_second = jnp.where(slot_at == flat_second, 1.0, 0.0)
    pick_out[0] = pick_first.astype(BF)
    pick_out[1] = pick_second.astype(BF)
    pick_both = (pick_first + pick_second).astype(BF)

    def column_block(array):
        return lambda m: array.at[:, pl.ds(pl.multiple_of(m * part_width, part_width), part_width)]

    def slot_block(array, owner):
        return array.at[
            pl.ds(pl.multiple_of(owner * CAP, 16), CAP),
            pl.ds(pl.multiple_of(n * part_width, part_width), part_width),
        ]

    def dispatch(rows, buffer, array):
        slots = [links.slot() for _ in range(NEAR)]
        buffer[...] = low_dot(pick_both, rows).astype(BF)
        for step in range(NEAR):
            links.send(
                buffer.at[pl.ds(pl.multiple_of(plane[step] * CAP, 16), CAP), :],
                slot_block(array, chip), at_plane(plane[step]), slots[step],
            )
        own = links.move(
            buffer.at[pl.ds(pl.multiple_of(chip * CAP, 16), CAP), :], slot_block(array, chip)
        )
        return slots, own

    def arrive(array, state):
        slots, own = state
        for step in range(NEAR):
            links.land(slot_block(array, plane[step]), at_plane(plane[step]), slots[step])
        own.wait()
        links.waits = [item for item in links.waits if item[0] is not own]

    dy_state = dispatch(cot_ref[...], cot_send, dy_out)
    dy_chain = Chain(links, n, column_block(dy_out))

    pack[:, 0:512] = wq_ref[...]
    pack[:, 512:1024] = wk_ref[...]
    pack[:, 1024:1536] = wv_ref[...]
    router_rows = jnp.concatenate(
        [router_ref[...].astype(F32), jnp.zeros((128 - EXPERTS, rows_each), F32)], 0
    )
    pack[:, 1536:1664] = router_rows.T.astype(BF)
    in_gather = PlaneGather(links, chip, core, plane, mate, pack, qkvw)
    qkvw[w] = pack[...]
    outw[w] = wo_ref[...]

    tok_chain.land(0)
    tok_chain.start(1)
    by_expert(0)
    tok_chain.land(1)
    tok_chain.start(2)
    arrive(dy_out, dy_state)
    dy_chain.start(0)
    tok_chain.land(2)
    in_gather.pass_on()
    out_gather = PlaneGather(links, chip, core, plane, mate, wo_ref, outw)
    total = jnp.zeros((token_count, 1), F32)
    for m in range(4):
        part = tokens_out[m, 0:token_count, :].astype(F32)
        total = total + jnp.sum(part * part, 1, keepdims=True)
    scale_first = lax.rsqrt(total * (1.0 / (4 * part_width)) + NORM_EPS)
    for m in range(4):
        part = tokens_out[m, 0:token_count, :].astype(F32)
        gain = tokens_out[m, token_count : token_count + 1, :].astype(F32)
        hidden_out[:, m * part_width : (m + 1) * part_width] = (part * scale_first * gain).astype(BF)

    by_expert(1)

    in_gather.far()
    out_gather.pass_on()
    in_gather.finish()
    saved_in = links.move(qkvw, qkvw_out)

    pieces = ((0, 0, rows_each), (1, 0, rows_each)) + tuple(
        (2, half * rows_each // 2, rows_each // 2) for half in range(2)
    )
    expert_slots = [[links.slot() for _ in range(NEAR)] for _ in pieces]
    expert_mate = [[links.slot() for _ in range(4)] for _ in pieces]

    def piece_of(array, index):
        return array.at[pl.ds(pieces[index][1], pieces[index][2]), :]

    def landing(index, owner, side):
        return piece_of(expert_out.at[pieces[index][0], owner, side], index)

    def set_out(index):
        kind_at = pieces[index][0]
        for step in range(NEAR):
            links.send(
                piece_of(moved_ref.at[kind_at, plane[step]], index), landing(index, chip, core),
                at_plane(plane[step]), expert_slots[index][step],
            )
        own = piece_of(moved_ref.at[kind_at, chip], index)
        links.send(own, landing(index, chip, core), mate, expert_mate[index][3])
        links.move(own, landing(index, chip, core))

    set_out(0)
    set_out(1)

    def pass_on(index):
        for step in range(NEAR):
            block = landing(index, plane[step], core)
            links.land(block, at_plane(plane[step]), expert_slots[index][step])
            links.send(block, block, mate, expert_mate[index][step])

    def all_there(index):
        for step in range(NEAR):
            links.land(landing(index, plane[step], 1 - core), mate, expert_mate[index][step])
        links.land(landing(index, chip, 1 - core), mate, expert_mate[index][3])

    dy_chain.land(0)
    dy_chain.start(1)
    by_expert(2)

    score_scale = HEAD_DIM ** (-0.5)

    def one_projection(part, value):
        cols = pl.ds(pl.multiple_of(part * part_width, part_width), part_width)
        weight = qkvw[:, :, cols].reshape(4 * part_width, part_width)
        raw_proj[part] = low_dot(hidden_out[...], weight)
        return value

    lax.fori_loop(0, 3, one_projection, 0)
    seen_at[...] = jnp.where(seen, 1.0, 0.0)

    def one_head(head, value):
        cols = pl.ds(pl.multiple_of(head * HEAD_DIM, HEAD_DIM), HEAD_DIM)
        turned = []
        for part in range(2):
            proj = raw_proj[part, :, cols]
            turned.append(
                (proj * rope_out[0] + pltpu.roll(proj, HEAD_DIM // 2, 1) * rope_out[1]).astype(BF)
            )
            qkv_out[part, :, cols] = turned[part]
        values = raw_proj[2, :, cols].astype(BF)
        qkv_out[2, :, cols] = values
        scores = rows_rows(turned[0], turned[1]) * score_scale
        scores = jnp.where(seen_at[...] > 0.5, scores, NEG_FILL)
        exps = jnp.exp(scores - jnp.max(scores, 1, keepdims=True))
        weights = exps / jnp.sum(exps, 1, keepdims=True)
        prob_out[head] = weights
        att_out[:, cols] = low_dot(weights.astype(BF), values).astype(BF)
        return value

    lax.fori_loop(0, part_width // HEAD_DIM, one_head, 0)
    for source, target in (
        (hidden_out, hidden_hbm), (tokens_out, tokens_hbm), (qkv_out, qkv_hbm),
        (prob_out, prob_hbm), (pick_out, pick_hbm),
    ):
        links.move(source, target)

    dy_chain.land(1)
    dy_chain.start(2)
    out_gather.far()

    out_gather.finish()
    links.move(outw, outw_out)

    attended = att_out[...]

    def branch(m):
        weight = outw[pl.ds(2 * m, 2)].reshape(part_width, part_width)
        return rows_rows(attended, weight)

    branch_sum = LineSum(links, n, br_send, br_recv)
    for step in range(NEAR):
        branch_sum.put(step, branch(branch_sum.targets[step]))
    middle = tok_ref[...].astype(F32) + branch(n)
    branch_sum.relay()
    middle = branch_sum.total(middle)
    middle_out[...] = middle
    x_state = dispatch(middle.astype(BF), y_send, x_out)

    def cap_block(owner):
        return lambda m: x_out.at[
            pl.ds(pl.multiple_of(owner * CAP, 16), CAP),
            pl.ds(pl.multiple_of(m * part_width, part_width), part_width),
        ]

    x_chains = [Chain(links, n, cap_block(owner)) for owner in (chip, *plane)]
    x_slots, x_own = x_state
    x_own.wait()
    links.waits = [item for item in links.waits if item[0] is not x_own]
    x_chains[0].start(0)

    set_out(2)
    set_out(3)

    gain_second = tok_pack[token_count + 1 : token_count + 2, :].astype(F32)
    router = qkvw[pl.ds(2 * n, 2), :, 1536:1664].reshape(part_width, 128)
    logit_part = mm(router, (middle * gain_second).astype(BF), ((0,), (1,)))[0:8, :]
    square = middle * middle
    square_high = square.astype(BF)
    square_low = (square - square_high.astype(F32)).astype(BF)
    ones = jnp.ones((8, part_width), BF)
    square_sum = rows_rows(ones, square_high) + rows_rows(ones, square_low)
    stat = jnp.where(kind == 4, square_sum, logit_part)
    stat_send[...] = stat
    stat_slots = [links.slot() for _ in range(NEAR)]
    for step in range(NEAR):
        links.send(stat_send, stat_recv.at[step], {"narrow": to_z[step]}, stat_slots[step])

    for step in range(NEAR):
        links.land(slot_block(x_out, plane[step]), at_plane(plane[step]), x_slots[step])
        x_chains[1 + step].start(0)
    for step in range(NEAR):
        links.land(stat_recv.at[step], {"narrow": from_z[step]}, stat_slots[step])
        stat = stat + stat_recv[step]
    stat_out[...] = stat
    scale_row = lax.rsqrt(stat[4:5, :] * (1.0 / (4 * part_width)) + NORM_EPS)
    logits = jnp.where(kind < EXPERTS, stat * scale_row, NEG_FILL)
    chances = jnp.exp(logits - jnp.max(logits, 0, keepdims=True))
    chances = chances / jnp.sum(chances, 0, keepdims=True)
    share_first = jnp.sum(chances * hot_first, 0, keepdims=True)
    share_second = jnp.sum(chances * hot_second, 0, keepdims=True)
    both = share_first + share_second
    weighted = pick_first * (share_first / both) + pick_second * (share_second / both)
    slot_gate = jnp.sum(weighted, 1, keepdims=True)
    gate_send[...] = jnp.broadcast_to(slot_gate, (SLOTS, 128))

    def gate_rows(array, owner):
        return array.at[pl.ds(pl.multiple_of(owner * CAP, 16), CAP), :]

    gate_slots = [links.slot() for _ in range(NEAR)]
    for step in range(NEAR):
        links.send(
            gate_rows(gate_send, plane[step]), gate_rows(gate_out, chip),
            at_plane(plane[step]), gate_slots[step],
        )
    links.move(gate_rows(gate_send, chip), gate_rows(gate_out, chip))

    for step in range(2):
        for chain in x_chains:
            chain.land(step)
            chain.start(step + 1)
        pass_on(step)
    for chain in x_chains:
        chain.land(2)
    dy_chain.land(2)
    for step in range(NEAR):
        links.land(gate_rows(gate_out, plane[step]), at_plane(plane[step]), gate_slots[step])
    pass_on(2)
    pass_on(3)
    for index in range(len(pieces)):
        all_there(index)
    links.finish()


def front_call(tokens, cotangent, gain_attn, gain_ffn, weights, router, experts, segment, parents, ids, rank):
    token_count, part_width = tokens.shape
    full = 4 * part_width
    rows_each, _, hidden_width = experts[0].shape
    heads = part_width // HEAD_DIM
    vmem = pl.BlockSpec(memory_space=pltpu.VMEM)
    hbm = pl.BlockSpec(memory_space=pl.ANY)

    def arr(shape, dtype):
        return jax.ShapeDtypeStruct(shape, dtype)

    return pl.pallas_call(
        front_body,
        out_shape=(
            arr((8, rows_each, 1664), BF),
            arr((8, rows_each, part_width), BF),
            arr((3, 4, 2, rows_each, hidden_width), BF),
            arr((SLOTS, full), BF),
            arr((SLOTS, full), BF),
            arr((SLOTS, 128), F32),
            arr((token_count, part_width), F32),
            arr((token_count, full), BF),
            arr((4, token_count + 16, part_width), BF),
            arr((3, token_count, part_width), BF),
            arr((heads, token_count, token_count), F32),
            arr((token_count, part_width), BF),
            arr((8, token_count), F32),
            arr((2, token_count, HEAD_DIM), F32),
            arr((2, SLOTS, token_count), BF),
            arr((token_count, 128), F32),
        ),
        in_specs=[vmem] * 9 + [hbm] * 3 + [vmem] * 4,
        out_specs=(hbm,) * 5 + (vmem, vmem) + (hbm,) * 4 + (vmem,) * 3 + (hbm, vmem),
        scratch_shapes=[
            pltpu.VMEM((token_count, full), BF),
            pltpu.VMEM((4, token_count + 16, part_width), BF),
            pltpu.VMEM((3, token_count, part_width), BF),
            pltpu.VMEM((heads, token_count, token_count), F32),
            pltpu.VMEM((2, SLOTS, token_count), BF),
            pltpu.VMEM((3, token_count, part_width), F32),
            pltpu.VMEM((token_count, token_count), F32),
            pltpu.VMEM((3, rows_each, EXPERTS, hidden_width), BF),
            pltpu.VMEM((3, EXPERTS, rows_each, hidden_width), BF),
            pltpu.VMEM((rows_each, 1664), BF),
            pltpu.VMEM((token_count + 16, part_width), BF),
            pltpu.VMEM((8, rows_each, 1664), BF),
            pltpu.VMEM((8, rows_each, part_width), BF),
            pltpu.VMEM((SLOTS, part_width), BF),
            pltpu.VMEM((SLOTS, part_width), BF),
            pltpu.VMEM((NEAR, token_count, part_width), BF),
            pltpu.VMEM((NEAR + 1, token_count, part_width), BF),
            pltpu.VMEM((8, token_count), F32),
            pltpu.VMEM((NEAR, 8, token_count), F32),
            pltpu.VMEM((SLOTS, 128), F32),
            pltpu.SemaphoreType.DMA((FRONT_SLOTS,)),
            pltpu.SemaphoreType.DMA((FRONT_SLOTS,)),
            pltpu.SemaphoreType.DMA((24,)),
        ],
        compiler_params=pltpu.CompilerParams(
            collective_id=0, has_side_effects=True, vmem_limit_bytes=60 * 1024 * 1024
        ),
        cost_estimate=pl.CostEstimate(
            flops=6_000_000_000, bytes_accessed=60_000_000, transcendentals=400_000
        ),
        name="front",
    )(
        tokens, cotangent, gain_attn.reshape(-1, 128), gain_ffn.reshape(-1, 128), *weights,
        router, *experts, segment, parents, ids, rank,
    )


MID_SLOTS = 48


TILE = 512


def mid_body(
    x_ref, dy_hbm, gate_ref, tokens_ref, w_ref,
    back_mid_out, back_exp_out, last_exp_out, extra_out, grads_out, expert_out,
    dy_ref, weights, hidden, graded_send, hidden_cat, graded_cat, act_cat, gate_cat, up_cat,
    turned, down_grad, rs_send, rs_recv, ext_send, ext_recv, sent, landed, local,
):
    n = lax.axis_index("narrow")
    w = lax.axis_index("wide")
    chip, core = w // 2, lax.rem(w, 2)
    to_z, from_z = places_of(n)
    plane = plane_of(chip)
    links = Links(sent, landed, local)
    mate = {"wide": 2 * chip + 1 - core}
    slots, full = hidden.shape
    part_width = full // 4
    rows_each = full // 8
    half = full // 2
    hidden_width = weights.shape[2]

    dy_load = links.move(dy_hbm, dy_ref)
    x_load = links.move(x_ref, hidden)
    loads = [
        links.move(
            w_ref.at[kind, c, k],
            weights.at[kind, pl.ds((2 * c + k) * rows_each, rows_each), :],
        )
        for kind in range(3)
        for c in range(4)
        for k in range(2)
    ]
    links.waits = []
    greet(to_z, plane, chip, core, True)

    slot_gate = gate_ref[:, 0:1]
    dy_load.wait()
    for c in range(4):
        theirs = pl.ds(pl.multiple_of((2 * c + 1 - core) * rows_each, rows_each), rows_each)
        ours = pl.ds(pl.multiple_of((2 * c + core) * rows_each, rows_each), rows_each)
        cols = slice(c * rows_each, (c + 1) * rows_each)
        graded_cat[core, :, cols] = (dy_ref[:, ours].astype(F32) * slot_gate).astype(BF)
        graded_send[:, cols] = (dy_ref[:, theirs].astype(F32) * slot_gate).astype(BF)

    def to_mate(source, target):
        slot = links.slot()
        links.send(source, target.at[core], mate, slot)
        return lambda: links.land(target.at[1 - core], mate, slot)

    graded_there = to_mate(graded_send, graded_cat)
    x_load.wait()
    total = jnp.zeros((slots, 1), F32)
    for m in range(4):
        part = hidden[:, m * part_width : (m + 1) * part_width].astype(F32)
        total = total + jnp.sum(part * part, 1, keepdims=True)
    scale = lax.rsqrt(total * (1.0 / full) + NORM_EPS)
    gain_row = tokens_ref.shape[1] - 15
    for m in range(4):
        cols = slice(m * part_width, (m + 1) * part_width)
        gain = tokens_ref[m, gain_row : gain_row + 1, :].astype(F32)
        hidden[:, cols] = (hidden[:, cols].astype(F32) * scale * gain).astype(BF)
    hidden_slots = [links.slot() for _ in range(4)]
    for c in range(4):
        cols = pl.ds(c * rows_each, rows_each)
        theirs = pl.ds(pl.multiple_of((2 * c + 1 - core) * rows_each, rows_each), rows_each)
        ours = pl.ds(pl.multiple_of((2 * c + core) * rows_each, rows_each), rows_each)
        links.send(hidden.at[:, theirs], hidden_cat.at[core, :, cols], mate, hidden_slots[c])
        hidden_cat[core, :, c * rows_each : (c + 1) * rows_each] = hidden[:, ours]
    for load in loads:
        load.wait()

    def one_tile(cols, rows):
        gate_pre = low_dot(hidden[rows, :], weights[0, :, cols])
        up_pre = low_dot(hidden[rows, :], weights[1, :, cols])
        act_raw = low_dot(dy_ref[rows, :], weights[2, :, cols])
        sigmoid = 1.0 / (1.0 + jnp.exp(-gate_pre))
        silu = gate_pre * sigmoid
        activated = (silu * up_pre).astype(BF)
        grad_act = act_raw * gate_ref[rows, 0:1]
        act_cat[core, rows, cols] = activated
        gate_cat[core, rows, cols] = (
            grad_act * up_pre * (sigmoid * (1.0 + gate_pre * (1.0 - sigmoid)))
        ).astype(BF)
        up_cat[core, rows, cols] = (grad_act * silu).astype(BF)
        return jnp.sum(act_raw * activated.astype(F32), 1, keepdims=True)

    def over_tiles(tile, body, carry):
        whole = hidden_width // tile
        carry = lax.fori_loop(
            0, whole, lambda t, value: body(pl.ds(pl.multiple_of(t * tile, tile), tile), value), carry
        )
        if hidden_width % tile:
            carry = body(pl.ds(whole * tile, hidden_width % tile), carry)
        return carry

    share = over_tiles(
        TILE,
        lambda cols, value: tuple(
            value[index] + one_tile(cols, pl.ds(index * (slots // 2), slots // 2))
            for index in range(2)
        ),
        (jnp.zeros((slots // 2, 1), F32),) * 2,
    )
    share = jnp.concatenate(share, 0)
    acts_there = [to_mate(item.at[core], item) for item in (act_cat, gate_cat, up_cat)]

    grad_gate, grad_up = gate_cat.at[core], up_cat.at[core]
    mid_sum = LineSum(links, n, rs_send.at[0], rs_recv.at[0])

    def mid_part(owner):
        rows = pl.ds(pl.multiple_of(owner * part_width, part_width), part_width)
        block = rows_rows(grad_gate[...], weights[0, rows, :])
        block = block + rows_rows(grad_up[...], weights[1, rows, :])
        return block, jnp.sum(hidden[:, rows].astype(F32) * block, 1, keepdims=True)

    stat = jnp.zeros((slots, 1), F32)
    block, part = mid_part(mid_sum.targets[0])
    mid_sum.put(0, block)
    stat = stat + part

    expert_slots = {}

    def weight_grad(right, target):
        def body(cols, value):
            right_rows = right[:, :, cols].reshape(2 * slots, cols.size)
            target[:, cols] = low_dot(turned[...], right_rows).astype(BF)
            return value

        over_tiles(TILE, body, 0)

    def share_out(index, source):
        expert_slots[index] = [links.slot() for _ in range(NEAR)]

        def block(owner):
            first = pl.multiple_of(owner * rows_each, rows_each)
            return source.at[pl.ds(first, rows_each), :]

        for step in range(NEAR):
            links.send(
                block(plane[step]), expert_out.at[index, chip],
                {"wide": 2 * plane[step] + core}, expert_slots[index][step],
            )
        links.move(block(chip), expert_out.at[index, chip])

    graded_there()
    acts_there[0]()
    turned[...] = graded_cat[...].reshape(2 * slots, half).T
    weight_grad(act_cat, down_grad)
    share_out(0, down_grad)

    def other_part(step, stat):
        block, part = mid_part(mid_sum.owner(step))
        rs_send[0, step] = block.astype(BF)
        return stat + part

    stat = lax.fori_loop(1, 4, other_part, stat)
    mid_sum.set_out(1)
    mid_sum.set_out(2)
    lane_at = lax.broadcasted_iota(jnp.int32, (slots, 128), 1)
    columns = jnp.where(lane_at == 0, share, jnp.where(lane_at == 1, stat, 0.0))
    high = columns.astype(BF)
    rest = (columns - high.astype(F32)).astype(BF)
    pick = jnp.where(
        lax.broadcasted_iota(jnp.int32, (8, 128), 0) == lax.broadcasted_iota(jnp.int32, (8, 128), 1),
        1.0, 0.0,
    ).astype(BF)
    extra = rows_rows(pick, high) + rows_rows(pick, rest)
    ext_send[...] = extra
    ext_slots = [links.slot() for _ in range(NEAR)]
    for step in range(NEAR):
        links.send(ext_send, ext_recv.at[step], {"narrow": to_z[step]}, ext_slots[step])

    mid_sum.relay()

    activated = act_cat.at[core]
    exp_sum = LineSum(links, n, rs_send.at[1], rs_recv.at[1])

    def exp_part(owner):
        rows = pl.ds(pl.multiple_of(owner * part_width, part_width), part_width)
        return rows_rows(activated[...], weights[2, rows, :])

    def expert_part(step, value):
        rs_send[1, step] = exp_part(exp_sum.owner(step)).astype(BF)
        return value

    lax.fori_loop(0, 4, expert_part, 0)
    exp_sum.set_out(0)
    exp_sum.set_out(1)
    for slot in hidden_slots:
        index = hidden_slots.index(slot)
        links.land(
            hidden_cat.at[1 - core, :, pl.ds(index * rows_each, rows_each)], mate, slot
        )
    for there in acts_there[1:]:
        there()
    turned[...] = hidden_cat[...].reshape(2 * slots, half).T
    gate_grad = weights.at[0, pl.ds(0, half), :]
    weight_grad(gate_cat, gate_grad)
    share_out(1, gate_grad)
    up_grad = weights.at[1, pl.ds(0, half), :]
    weight_grad(up_cat, up_grad)
    links.move(up_grad, grads_out)

    for step in range(NEAR):
        links.land(ext_recv.at[step], {"narrow": from_z[step]}, ext_slots[step])
        extra = extra + ext_recv[step]
    high = extra.astype(BF)
    rest = (extra - high.astype(F32)).astype(BF)
    place = lax.broadcasted_iota(jnp.int32, (8, 128), 0) * 2
    lanes = lax.broadcasted_iota(jnp.int32, (8, 128), 1)
    spread_high = jnp.where(place == lanes, 1.0, 0.0).astype(BF)
    spread_low = jnp.where(place + 1 == lanes, 1.0, 0.0).astype(BF)
    columns = mm(high, spread_high, ((0,), (0,))) + mm(rest, spread_low, ((0,), (0,)))
    extra_out[...] = jnp.where(lane_at == 4, 1.0, columns).astype(BF)
    back_mid_out[...] = mid_sum.total(rs_send[0, 3].astype(F32)).astype(BF)
    exp_sum.join()
    last_exp_out[...] = rs_send[1, 2]
    back_exp_out[...] = exp_sum.early(rs_send[1, 3].astype(F32)).astype(BF)
    for index in range(2):
        for step in range(NEAR):
            links.land(
                expert_out.at[index, plane[step]], {"wide": 2 * plane[step] + core},
                expert_slots[index][step],
            )
    links.finish()


def mid_call(slot_mid, slot_grad, slot_gate, token_parts, expert_w):
    slots, full = slot_mid.shape
    part_width = full // 4
    rows_each, hidden_width = expert_w.shape[3:]
    vmem = pl.BlockSpec(memory_space=pltpu.VMEM)
    hbm = pl.BlockSpec(memory_space=pl.ANY)

    def arr(shape, dtype):
        return jax.ShapeDtypeStruct(shape, dtype)

    return pl.pallas_call(
        mid_body,
        out_shape=(
            arr((slots, part_width), BF),
            arr((slots, part_width), BF),
            arr((slots, part_width), BF),
            arr((slots, 128), BF),
            arr((full // 2, hidden_width), BF),
            arr((2, 4, rows_each, hidden_width), BF),
        ),
        in_specs=[hbm] * 2 + [vmem] * 2 + [hbm],
        out_specs=(vmem,) * 4 + (hbm, hbm),
        scratch_shapes=[
            pltpu.VMEM((slots, full), BF),
            pltpu.VMEM((3, full, hidden_width), BF),
            pltpu.VMEM((slots, full), BF),
            pltpu.VMEM((slots, full // 2), BF),
            pltpu.VMEM((2, slots, full // 2), BF),
            pltpu.VMEM((2, slots, full // 2), BF),
            pltpu.VMEM((2, slots, hidden_width), BF),
            pltpu.VMEM((2, slots, hidden_width), BF),
            pltpu.VMEM((2, slots, hidden_width), BF),
            pltpu.VMEM((full // 2, 2 * slots), BF),
            pltpu.VMEM((full // 2, hidden_width), BF),
            pltpu.VMEM((2, NEAR + 1, slots, part_width), BF),
            pltpu.VMEM((2, NEAR + 1, slots, part_width), BF),
            pltpu.VMEM((8, slots), F32),
            pltpu.VMEM((NEAR, 8, slots), F32),
            pltpu.SemaphoreType.DMA((MID_SLOTS,)),
            pltpu.SemaphoreType.DMA((MID_SLOTS,)),
            pltpu.SemaphoreType.DMA((32,)),
        ],
        compiler_params=pltpu.CompilerParams(
            collective_id=1, has_side_effects=True, vmem_limit_bytes=62 * 1024 * 1024
        ),
        cost_estimate=pl.CostEstimate(
            flops=30_000_000_000, bytes_accessed=40_000_000, transcendentals=800_000
        ),
        name="mid",
    )(slot_mid, slot_grad, slot_gate, token_parts, expert_w)


class PlaneSum:
    def __init__(self, links, core, chip, plane, first, send, inbox):
        self.links, self.core, self.chip = links, core, chip
        self.near, self.next, self.far = plane[first], plane[1 - first], plane[2]
        self.send, self.inbox = send, inbox
        self.slots = [links.slot() for _ in range(3)]

    def at(self, peer):
        return {"wide": 2 * peer + self.core}

    def block(self, owner):
        rows = self.inbox.shape[1]
        return self.send.at[pl.ds(pl.multiple_of(owner * rows, rows), rows), :]

    def start(self):
        links = self.links
        links.send(self.block(self.far), self.inbox.at[1], self.at(self.near), self.slots[1])
        links.send(self.block(self.near), self.inbox.at[0], self.at(self.near), self.slots[0])

    def turn(self):
        links = self.links
        links.land(self.inbox.at[1], self.at(self.near), self.slots[1])
        block = self.block(self.next)
        block[...] = (block[...].astype(F32) + self.inbox[1].astype(F32)).astype(BF)
        links.send(block, self.inbox.at[2], self.at(self.next), self.slots[2])

    def total(self):
        links = self.links
        links.land(self.inbox.at[0], self.at(self.near), self.slots[0])
        links.land(self.inbox.at[2], self.at(self.next), self.slots[2])
        own = self.block(self.chip)[...].astype(F32)
        return own + self.inbox[0].astype(F32) + self.inbox[2].astype(F32)


TAIL_SLOTS = 72


def tail_body(
    mid_ref, exp_ref, last_ref, ext_ref, moved_ref, picks_hbm, stat_ref, cols_ref, middle_ref,
    cot_ref, tok_ref, tokens_hbm, qkv_hbm, prob_hbm, att_ref, rope_ref, hidden_hbm, qkvw_ref,
    outw_ref,
    output_out, grad_tokens_out, summed_out, small_out,
    router_out, expert_out,
    picks_ref, tokens_ref, qkv_ref, prob_ref, hidden_ref, grad_att_at, exp_in, exp_sum, router_all, qkvw, outw, ret_mid, ret_exp, ret_ext, branch, hidden_cat, branch_cat, att_cat, proj_cat,
    proj_send, proj_recv, first_send, first_recv, col_send, col_recv, small_mate, small_sum,
    small_recv, last_mate, last_sum, last_recv, sent, landed, local,
):
    n = lax.axis_index("narrow")
    w = lax.axis_index("wide")
    chip, core = w // 2, lax.rem(w, 2)
    to_z, from_z = places_of(n)
    plane = plane_of(chip)
    links = Links(sent, landed, local)
    mate = {"wide": 2 * chip + 1 - core}
    token_count, part_width = tok_ref.shape
    full = 4 * part_width
    rows_each = full // 8
    heads = part_width // HEAD_DIM
    half = full // 2

    def at_plane(peer):
        return {"wide": 2 * peer + core}

    def cap_rows(array, owner):
        return array.at[pl.ds(pl.multiple_of(owner * CAP, 16), CAP), :]

    first_loads = [
        links.move(source, target)
        for source, target in (
            (hidden_hbm, hidden_ref), (picks_hbm, picks_ref), (tokens_hbm, tokens_ref),
            (qkv_hbm, qkv_ref), (prob_hbm, prob_ref),
        )
    ]
    loads = [links.move(qkvw_ref, qkvw), links.move(outw_ref, outw)]
    links.waits = []
    greet(to_z, plane, chip, core, True)

    last_slot = links.slot()
    links.send(last_ref, exp_in, {"narrow": lax.rem(2 * n + 1, 5)}, last_slot)

    back_slots = []

    def give_back(source, target):
        slots = [links.slot() for _ in range(NEAR)]
        for step in range(NEAR):
            links.send(
                cap_rows(source, plane[step]), cap_rows(target, chip), at_plane(plane[step]),
                slots[step],
            )
        own = links.move(cap_rows(source, chip), cap_rows(target, chip))
        links.waits.pop()
        back_slots.append((target, slots, own))

    give_back(mid_ref, ret_mid)
    give_back(ext_ref, ret_ext)

    def returned(which):
        target, slots, own = back_slots[which]
        for step in range(NEAR):
            links.land(cap_rows(target, plane[step]), at_plane(plane[step]), slots[step])
        own.wait()
        return target[...]

    expert_slots = [links.slot() for _ in range(NEAR)]
    for step in range(NEAR):
        block = pl.ds(pl.multiple_of(plane[step] * rows_each, rows_each), rows_each)
        links.send(
            moved_ref.at[block, :], expert_out.at[chip], at_plane(plane[step]), expert_slots[step]
        )
    block = pl.ds(pl.multiple_of(chip * rows_each, rows_each), rows_each)
    links.move(moved_ref.at[block, :], expert_out.at[chip])

    def to_mate(source, target):
        slot = links.slot()
        links.send(source, target.at[core], mate, slot)
        return lambda: links.land(target.at[1 - core], mate, slot)

    def parity_exchange(source, target):
        lands = []
        for c in range(4):
            cols = pl.ds(c * rows_each, rows_each)
            theirs = pl.ds(pl.multiple_of((2 * c + 1 - core) * rows_each, rows_each), rows_each)
            ours = pl.ds(pl.multiple_of((2 * c + core) * rows_each, rows_each), rows_each)
            slot = links.slot()
            links.send(source.at[:, theirs], target.at[core, :, cols], mate, slot)
            target[core, :, c * rows_each : (c + 1) * rows_each] = source[:, ours]
            lands.append((target.at[1 - core, :, cols], slot))
        return lambda: [links.land(block, mate, slot) for block, slot in lands]

    for load in first_loads:
        load.wait()
    hidden_there = parity_exchange(hidden_ref, hidden_cat)
    att_cat[core] = att_ref[...]
    att_there = to_mate(att_ref, att_cat)

    stat = jnp.concatenate([stat_ref[...], jnp.zeros((120, token_count), F32)], 0).T
    lane_at = lax.broadcasted_iota(jnp.int32, (token_count, 128), 1)
    scale_second = lax.rsqrt(stat[:, 4:5] * (1.0 / full) + NORM_EPS)
    logits = stat * scale_second
    hot_first = lane_at == cols_ref[:, 2:3].astype(jnp.int32)
    hot_second = lane_at == cols_ref[:, 3:4].astype(jnp.int32)
    logit_first = jnp.sum(jnp.where(hot_first, logits, 0.0), 1, keepdims=True)
    logit_second = jnp.sum(jnp.where(hot_second, logits, 0.0), 1, keepdims=True)
    apart = logit_first - logit_second
    share_first = 1.0 / (1.0 + jnp.exp(-apart))
    share_second = 1.0 / (1.0 + jnp.exp(apart))
    normed = middle_ref[...] * scale_second
    gain_second = tokens_ref[n, token_count + 1 : token_count + 2, :].astype(F32)
    hidden_second = (normed * gain_second).astype(BF)
    for load in loads:
        load.wait()
    router = qkvw[pl.ds(2 * n, 2), :, 1536:1664].reshape(part_width, 128)

    rows_mid = returned(0)
    rows_ext = returned(1)
    ext_first = cols_cols(picks_ref[0], rows_ext)
    ext_second = cols_cols(picks_ref[1], rows_ext)
    ext_both = ext_first + ext_second
    grad_share = ext_first[:, 0:1] + ext_first[:, 1:2] - ext_second[:, 0:1] - ext_second[:, 1:2]
    delta = (grad_share * share_first * share_second).astype(BF).astype(F32)
    grad_logits = jnp.where(hot_first, delta, jnp.where(hot_second, -delta, 0.0)).astype(BF)
    stat_total = ext_both[:, 2:3] + ext_both[:, 3:4] + delta * apart
    grad_hidden = cols_cols(picks_ref[0] + picks_ref[1], rows_mid) + rows_rows(grad_logits, router)
    grad_middle = cot_ref[...].astype(F32) + scale_second * (
        gain_second * grad_hidden - normed * (stat_total * (1.0 / full))
    )
    own_cols = pl.ds(pl.multiple_of(n * part_width, part_width), part_width)
    branch[:, own_cols] = grad_middle.astype(BF)
    branch_slots = [links.slot() for _ in range(NEAR)]
    for step in range(NEAR):
        links.send(
            branch.at[:, own_cols], branch.at[:, own_cols], {"narrow": to_z[step]},
            branch_slots[step],
        )

    links.land(exp_in, {"narrow": lax.rem(n + 1, 4)}, last_slot)
    exp_sum[...] = (exp_ref[...].astype(F32) + exp_in[...].astype(F32)).astype(BF)
    give_back(exp_sum, ret_exp)

    router_part = cols_cols(grad_logits, hidden_second)[0:8, :]
    gain_part = jnp.sum(grad_hidden * normed, 0, keepdims=True)
    kind_at = lax.broadcasted_iota(jnp.int32, (8, part_width), 0)
    small = jnp.where(kind_at == 4, gain_part, router_part)
    small_mate[core] = small
    small_there = to_mate(small_mate.at[core], small_mate)

    small_there()
    small = small_mate[0] + small_mate[1]
    small_sum[...] = small
    small_slots = [links.slot() for _ in range(NEAR)]
    for step in range(NEAR):
        links.send(small_sum, small_recv.at[step], at_plane(plane[step]), small_slots[step])

    for step in range(NEAR):
        cols = pl.ds(pl.multiple_of(from_z[step] * part_width, part_width), part_width)
        links.land(branch.at[:, cols], {"narrow": from_z[step]}, branch_slots[step])
    branch_there = parity_exchange(branch, branch_cat)
    grad_att = low_dot(branch[...], outw[...].reshape(full, part_width)).astype(BF)

    proj_sums = {
        part: PlaneSum(
            links, core, chip, plane, part % 2, proj_send.at[part], proj_recv.at[part]
        )
        for part in (3, 0, 1, 2)
    }

    branch_there()
    att_there()
    proj_send[3] = cols_cols(
        branch_cat[...].reshape(2 * token_count, half), att_cat[...].reshape(2 * token_count, part_width)
    ).astype(BF)
    proj_sums[3].start()
    score_scale = HEAD_DIM ** (-0.5)
    grad_att_at[...] = grad_att

    def one_head(head, stat_first):
        def lanes(start):
            return pl.ds(pl.multiple_of(start + head * HEAD_DIM, HEAD_DIM), HEAD_DIM)

        query, key, value = (qkv_ref[i, :, lanes(0)] for i in range(3))
        grad_out = grad_att_at[:, lanes(0)]
        weights = prob_ref[head]
        grad_weights = rows_rows(grad_out, value)
        inner = jnp.sum(weights * grad_weights, 1, keepdims=True)
        grad_scores = (weights * (grad_weights - inner)).astype(BF)
        grad_query = low_dot(grad_scores, key) * score_scale
        grad_key = cols_cols(grad_scores, query) * score_scale
        grad_value = cols_cols(weights.astype(BF), grad_out)
        products = (
            grad_query * query.astype(F32)
            + grad_key * key.astype(F32)
            + grad_value * value.astype(F32)
        )
        for part, grad in ((0, grad_query), (1, grad_key)):
            turned = grad * rope_ref[0] - pltpu.roll(grad, HEAD_DIM // 2, 1) * rope_ref[1]
            proj_cat[core, :, lanes(part * part_width)] = turned.astype(BF)
        proj_cat[core, :, lanes(2 * part_width)] = grad_value.astype(BF)
        return stat_first + jnp.sum(products, 1, keepdims=True)

    stat_first = lax.fori_loop(0, heads, one_head, jnp.zeros((token_count, 1), F32))
    proj_there = to_mate(proj_cat.at[core], proj_cat)
    high = stat_first.astype(BF)
    rest = (stat_first - high.astype(F32)).astype(BF)
    col_send[...] = jnp.where(
        lane_at == 0, high.astype(F32), jnp.where(lane_at == 1, rest.astype(F32), 0.0)
    ).astype(BF)
    col_slots = [links.slot() for _ in range(NEAR)]
    for step in range(NEAR):
        links.send(col_send, col_recv.at[step], {"narrow": to_z[step]}, col_slots[step])
    grads = proj_cat[core]

    def first_block(m):
        weight = qkvw[pl.ds(2 * m, 2), :, 0:1536].reshape(part_width, 1536)
        return rows_rows(grads, weight)

    def fill_first(step, value):
        first_send[step] = first_block(lax.rem(n + 1 + step, 4)).astype(BF)
        return value

    lax.fori_loop(0, NEAR, fill_first, 0)
    first_slots = [links.slot() for _ in range(NEAR)]
    for step in range(NEAR):
        links.send(
            first_send.at[step], first_recv.at[step], {"narrow": to_z[step]}, first_slots[step]
        )

    hidden_there()
    proj_there()
    hidden_rows = hidden_cat[...].reshape(2 * token_count, half)
    proj_sums[3].turn()
    for part in range(3):
        cols = slice(part * 512, (part + 1) * 512)
        proj_send[part] = cols_cols(
            hidden_rows, proj_cat[:, :, cols].reshape(2 * token_count, part_width)
        ).astype(BF)
        proj_sums[part].start()

    rows_exp = returned(2)
    output_out[...] = (
        middle_ref[...]
        + share_first * cols_cols(picks_ref[0], rows_exp)
        + share_second * cols_cols(picks_ref[1], rows_exp)
    ).astype(BF)

    grad_first = first_block(n)
    stat_first = high.astype(F32) + rest.astype(F32)
    total = jnp.zeros((token_count, 1), F32)
    for m in range(4):
        part = tokens_ref[m, 0:token_count, :].astype(F32)
        total = total + jnp.sum(part * part, 1, keepdims=True)
    scale_first = lax.rsqrt(total * (1.0 / full) + NORM_EPS)
    normed_first = tok_ref[...].astype(F32) * scale_first
    gain_first = tokens_ref[n, token_count : token_count + 1, :].astype(F32)
    for step in range(NEAR):
        links.land(col_recv.at[step], {"narrow": from_z[step]}, col_slots[step])
        stat_first = stat_first + (
            col_recv[step, :, 0:1].astype(F32) + col_recv[step, :, 1:2].astype(F32)
        )
    for step in range(NEAR):
        links.land(first_recv.at[step], {"narrow": from_z[step]}, first_slots[step])
        grad_first = grad_first + first_recv[step].astype(F32)
    grad_tokens_out[...] = grad_middle + scale_first * (
        gain_first * grad_first - normed_first * (stat_first * (1.0 / full))
    )
    gain_part = jnp.sum(grad_first * normed_first, 0, keepdims=True)
    for part in range(3):
        proj_sums[part].turn()
    last_mate[core] = jnp.broadcast_to(gain_part, (8, part_width))
    last_there = to_mate(last_mate.at[core], last_mate)

    for step in range(NEAR):
        links.land(small_recv.at[step], at_plane(plane[step]), small_slots[step])
        small = small + small_recv[step]
    last_there()
    last = last_mate[0] + last_mate[1]
    last_sum[...] = last
    last_slots = [links.slot() for _ in range(NEAR)]
    for step in range(NEAR):
        links.send(last_sum, last_recv.at[step], at_plane(plane[step]), last_slots[step])
    router_all[:, own_cols] = small
    router_slots = [links.slot() for _ in range(NEAR)]
    for step in range(NEAR):
        links.send(
            router_all.at[:, own_cols], router_all.at[:, own_cols], {"narrow": to_z[step]},
            router_slots[step],
        )
    for step in range(NEAR):
        links.land(last_recv.at[step], at_plane(plane[step]), last_slots[step])
        last = last + last_recv[step]
    small_out[...] = jnp.where(kind_at == 5, last, small)
    for step in range(NEAR):
        cols = pl.ds(pl.multiple_of(from_z[step] * part_width, part_width), part_width)
        links.land(router_all.at[:, cols], {"narrow": from_z[step]}, router_slots[step])

    router_out[...] = router_all[:, pl.ds(pl.multiple_of(w * rows_each, rows_each), rows_each)]
    for part in range(4):
        summed_out[:, part * part_width : (part + 1) * part_width] = proj_sums[part].total()
    for step in range(NEAR):
        links.land(expert_out.at[plane[step]], at_plane(plane[step]), expert_slots[step])
    links.finish()


def tail_call(*args):
    slots, part_width = args[0].shape
    half, hidden_width = args[4].shape
    token_count = args[10].shape[0]
    full, rows_each = 2 * half, half // 4
    vmem = pl.BlockSpec(memory_space=pltpu.VMEM)
    hbm = pl.BlockSpec(memory_space=pl.ANY)

    def arr(shape, dtype):
        return jax.ShapeDtypeStruct(shape, dtype)

    own = (token_count, part_width)
    return pl.pallas_call(
        tail_body,
        out_shape=(
            arr(own, BF),
            arr(own, F32),
            arr((rows_each, full), F32),
            arr((8, part_width), F32),
            arr((8, rows_each), F32),
            arr((4, rows_each, hidden_width), BF),
        ),
        in_specs=[vmem] * 4 + [hbm] * 2 + [vmem] * 5 + [hbm] * 3 + [vmem] * 2 + [hbm] * 3,
        out_specs=(vmem,) * 5 + (hbm,),
        scratch_shapes=[
            pltpu.VMEM((2, slots, token_count), BF),
            pltpu.VMEM((4, token_count + 16, part_width), BF),
            pltpu.VMEM((3,) + own, BF),
            pltpu.VMEM((part_width // HEAD_DIM, token_count, token_count), F32),
            pltpu.VMEM((token_count, full), BF),
            pltpu.VMEM(own, BF),
            pltpu.VMEM((slots, part_width), BF),
            pltpu.VMEM((slots, part_width), BF),
            pltpu.VMEM((8, full), F32),
            pltpu.VMEM((8, rows_each, 1664), BF),
            pltpu.VMEM((8, rows_each, part_width), BF),
            pltpu.VMEM((slots, part_width), BF),
            pltpu.VMEM((slots, part_width), BF),
            pltpu.VMEM((slots, 128), BF),
            pltpu.VMEM((token_count, full), BF),
            pltpu.VMEM((2, token_count, half), BF),
            pltpu.VMEM((2, token_count, half), BF),
            pltpu.VMEM((2, token_count, part_width), BF),
            pltpu.VMEM((2, token_count, 1536), BF),
            pltpu.VMEM((4, half, part_width), BF),
            pltpu.VMEM((4, NEAR, rows_each, part_width), BF),
            pltpu.VMEM((NEAR,) + own, BF),
            pltpu.VMEM((NEAR,) + own, BF),
            pltpu.VMEM((token_count, 128), BF),
            pltpu.VMEM((NEAR, token_count, 128), BF),
            pltpu.VMEM((2, 8, part_width), F32),
            pltpu.VMEM((8, part_width), F32),
            pltpu.VMEM((NEAR, 8, part_width), F32),
            pltpu.VMEM((2, 8, part_width), F32),
            pltpu.VMEM((8, part_width), F32),
            pltpu.VMEM((NEAR, 8, part_width), F32),
            pltpu.SemaphoreType.DMA((TAIL_SLOTS,)),
            pltpu.SemaphoreType.DMA((TAIL_SLOTS,)),
            pltpu.SemaphoreType.DMA((24,)),
        ],
        compiler_params=pltpu.CompilerParams(
            collective_id=2, has_side_effects=True, vmem_limit_bytes=60 * 1024 * 1024
        ),
        cost_estimate=pl.CostEstimate(
            flops=6_000_000_000, bytes_accessed=60_000_000, transcendentals=1_000
        ),
        name="tail",
    )(*args)


def finish_body(
    down_ref, gate_ref, up_ref, output_ref, tokens_ref, summed_ref, small_ref, router_ref,
    gate_out, up_out, down_out, output_out, tokens_out, q_out, k_out, v_out, o_out,
    gain_first_out, gain_second_out, router_out,
):
    def some_rows(index, value):
        rows = pl.ds(pl.multiple_of(index * 16, 16), 16)
        for source, target in ((gate_ref, gate_out), (up_ref, up_out), (down_ref, down_out)):
            for expert in range(EXPERTS):
                target[rows, expert, :] = source[expert, rows, :].astype(F32)
        return value

    lax.fori_loop(0, tokens_ref.shape[0] // 16, some_rows, 0)
    output_out[...] = output_ref[...]
    tokens_out[...] = tokens_ref[...]
    width = tokens_ref.shape[1]
    for part, target in enumerate((q_out, k_out, v_out, o_out)):
        target[...] = summed_ref[:, part * width : (part + 1) * width].astype(F32)
    for row, target in ((5, gain_first_out), (4, gain_second_out)):
        for index in range(width // 128):
            target[index : index + 1, :] = small_ref[
                row : row + 1, index * 128 : (index + 1) * 128
            ]
    router_out[...] = router_ref[0:EXPERTS, :]


def finish_call(early, late, output, grad_tokens, summed, small, router):
    _, rows_each, hidden_width = late.shape
    token_count, part_width = output.shape
    step = 32

    def flat(width):
        return pl.BlockSpec((step, width), lambda i: (i, 0))

    def cube(which):
        return pl.BlockSpec((None, EXPERTS, step, hidden_width), lambda i: (which, 0, i, 0))

    def same(shape):
        return pl.BlockSpec(shape, lambda i: (0, 0))

    spread = pl.BlockSpec((step, EXPERTS, hidden_width), lambda i: (i, 0, 0))

    def arr(shape, dtype):
        return jax.ShapeDtypeStruct(shape, dtype)

    return pl.pallas_call(
        finish_body,
        grid=(rows_each // step,),
        out_shape=(arr((rows_each, EXPERTS, hidden_width), F32),) * 3
        + (arr(output.shape, BF), arr(output.shape, F32))
        + (arr((rows_each, part_width), F32),) * 4
        + (arr((part_width // 128, 128), F32),) * 2
        + (arr((EXPERTS, rows_each), F32),),
        in_specs=[
            cube(0), cube(1),
            pl.BlockSpec((EXPERTS, step, hidden_width), lambda i: (0, i, 0)),
            flat(part_width), flat(part_width), flat(4 * part_width), same(small.shape),
            same(router.shape),
        ],
        out_specs=(spread,) * 3
        + (flat(part_width),) * 6
        + (same((part_width // 128, 128)),) * 2
        + (same((EXPERTS, rows_each)),),
        name="finish",
    )(early, early, late, output, grad_tokens, summed, small, router)


def plain_device(
    tokens, gain_attn, w_query, w_key, w_value, w_out, gain_ffn, w_router,
    w_gate, w_up, w_down, segment, parents, expert_ids, slot_order, cotangent,
):
    narrow_count = lax.axis_size("narrow")
    wide_count = lax.axis_size("wide")
    narrow_at = lax.axis_index("narrow")
    token_count, part_width = tokens.shape
    full_width = part_width * narrow_count
    hidden_width = w_gate.shape[2]
    rows_each = w_gate.shape[0]
    blocks = wide_count // 8
    quads = [
        [8 * block + 2 * chip + core for chip in range(4)]
        for block in range(blocks)
        for core in range(2)
    ]
    mates = [
        [8 * block + 2 * chip + core for block in range(blocks) for core in range(2)]
        for chip in range(4)
    ]

    def quad_swap(array):
        return lax.all_to_all(array, "wide", 0, 0, axis_index_groups=quads, tiled=True)

    def own_rows(weight):
        moved = quad_swap(jnp.transpose(weight, (1, 0, 2)))
        joined = lax.all_gather(moved, "wide", axis=0, axis_index_groups=mates, tiled=True)
        joined = joined.reshape(blocks, 2, 4, rows_each, hidden_width).transpose(0, 2, 1, 3, 4)
        return joined.reshape(full_width, hidden_width)

    def share_rows(grad):
        parts = grad.astype(BF).reshape(blocks, 4, 2, rows_each, hidden_width)
        parts = parts.transpose(0, 2, 1, 3, 4).reshape(blocks * 2, 4, rows_each, hidden_width)
        summed = lax.psum_scatter(
            parts, "wide", scatter_dimension=0, axis_index_groups=mates, tiled=True
        )[0]
        return jnp.transpose(quad_swap(summed), (1, 0, 2)).astype(F32)

    def head_cols(array, head):
        return array[:, head * HEAD_DIM : (head + 1) * HEAD_DIM]

    heads = part_width // HEAD_DIM
    half_dim = HEAD_DIM // 2
    freqs = ROPE_BASE ** (-2.0 * jnp.arange(half_dim, dtype=F32) / HEAD_DIM)
    score_scale = HEAD_DIM ** (-0.5)
    gains = jnp.stack([gain_attn, gain_ffn])
    gain_first_loc = gain_attn.astype(F32)
    gain_second_loc = gain_ffn.astype(F32)
    hot_first, hot_second, kept, pick_first, pick_second = route(expert_ids, slot_order[0])

    gate_w, up_w, down_w = own_rows(w_gate), own_rows(w_up), own_rows(w_down)
    attn_w = lax.all_gather(
        jnp.stack([w_query, w_key, w_value, w_out], 1), "wide", axis=0, tiled=True
    )
    query_w, key_w, value_w, out_w = (attn_w[:, i] for i in range(4))
    router_w = lax.all_gather(w_router, "wide", axis=0, tiled=True)
    tokens_full = lax.all_gather(tokens, "narrow", axis=1, tiled=True)
    grad_full = lax.all_gather(cotangent, "narrow", axis=1, tiled=True)
    gains_full = lax.all_gather(gains, "narrow", axis=1, tiled=True)
    gain_first = gains_full[0].astype(F32)
    gain_second = gains_full[1].astype(F32)

    seen, places = tree_layout(segment[0], parents[0])
    pick_first_low = pick_first.astype(BF)
    pick_second_low = pick_second.astype(BF)
    pick_both_low = (pick_first | pick_second).astype(BF)

    inputs_full = tokens_full.astype(F32)
    scale_first = lax.rsqrt(jnp.mean(inputs_full * inputs_full, -1, keepdims=True) + NORM_EPS)
    normed_first = inputs_full * scale_first
    hidden_first = (normed_first * gain_first).astype(BF)
    angles = places[:, None] * freqs[None, :]
    cosines, sines = jnp.cos(angles), jnp.sin(angles)
    query_raw = rows_cols(hidden_first, query_w)
    key_raw = rows_cols(hidden_first, key_w)
    value_low = rows_cols(hidden_first, value_w).astype(BF)

    saved = []
    outs = []
    for head in range(heads):
        query = rotate(head_cols(query_raw, head), cosines, sines).astype(BF)
        key = rotate(head_cols(key_raw, head), cosines, sines).astype(BF)
        value = head_cols(value_low, head)
        scores = jnp.where(seen, rows_rows(query, key) * score_scale, NEG_FILL)
        exps = jnp.exp(scores - jnp.max(scores, -1, keepdims=True))
        weights = exps / jnp.sum(exps, -1, keepdims=True)
        saved.append((query, key, value, weights))
        outs.append(rows_cols(weights.astype(BF), value).astype(BF))
    attended = jnp.concatenate(outs, 1)
    branch_part = rows_rows(attended, out_w).astype(BF)
    branch_loc = lax.psum_scatter(
        branch_part, "narrow", scatter_dimension=1, tiled=True
    ).astype(F32)
    middle = tokens.astype(F32) + branch_loc
    middle_full = lax.all_gather(middle.astype(BF), "narrow", axis=1, tiled=True).astype(F32)
    scale_second = lax.rsqrt(jnp.mean(middle_full * middle_full, -1, keepdims=True) + NORM_EPS)
    normed_second = middle_full * scale_second
    hidden_second = (normed_second * gain_second).astype(BF)
    logits = rows_cols(hidden_second, router_w)
    share_first, share_second = gate_pair(logits, hot_first, hot_second)
    weight_first = kept[:, 0] * share_first
    weight_second = kept[:, 1] * share_second

    slot_weight = jnp.sum(
        pick_first * weight_first[:, None] + pick_second * weight_second[:, None], 0
    )
    weight_high, weight_low = two_parts(slot_weight)
    pads = jnp.stack([weight_high, weight_low], 1)
    pads = jnp.pad(pads, ((0, 0), (0, 126)))
    sent_hidden = cols_cols(pick_both_low, hidden_second).astype(BF)
    sent_grad = cols_cols(pick_both_low, grad_full).astype(BF)
    sent = jnp.concatenate([sent_hidden, sent_grad, pads], 1)
    got = quad_swap(sent.reshape(EXPERTS, CAP, -1)).reshape(SLOTS, -1)
    slot_hidden = got[:, :full_width]
    slot_grad = got[:, full_width : 2 * full_width]
    slot_gate = got[:, 2 * full_width : 2 * full_width + 2].astype(F32)
    slot_gate = slot_gate[:, 0:1] + slot_gate[:, 1:2]

    gate_pre = rows_cols(slot_hidden, gate_w)
    up_pre = rows_cols(slot_hidden, up_w)
    sigmoid_gate = jax.nn.sigmoid(gate_pre)
    silu_gate = gate_pre * sigmoid_gate
    activated = (silu_gate * up_pre).astype(BF)
    expert_part = rows_rows(activated, down_w)
    act_raw = rows_cols(slot_grad, down_w)
    share_part = jnp.sum(act_raw * activated.astype(F32), 1, keepdims=True)
    grad_act = act_raw * slot_gate
    grad_gate_pre = (
        grad_act * up_pre * sigmoid_gate * (1.0 + gate_pre * (1.0 - sigmoid_gate))
    ).astype(BF)
    grad_up_pre = (grad_act * silu_gate).astype(BF)
    grad_slot = rows_rows(grad_gate_pre, gate_w) + rows_rows(grad_up_pre, up_w)
    stat_part = jnp.sum(slot_hidden.astype(F32) * grad_slot, 1, keepdims=True)
    extras = jnp.concatenate([*two_parts(share_part), *two_parts(stat_part)], 1)
    extras = jnp.pad(extras, ((0, 0), (0, 124)))
    back_parts = []
    expert_plain = expert_part.astype(BF)
    slot_plain = grad_slot.astype(BF)
    for part in range(narrow_count):
        cols = slice(part * part_width, (part + 1) * part_width)
        back_parts += [expert_plain[:, cols], slot_plain[:, cols], extras]
    back = lax.psum_scatter(
        jnp.concatenate(back_parts, 1), "narrow", scatter_dimension=1, tiled=True
    )
    back = quad_swap(back.reshape(EXPERTS, CAP, -1)).reshape(SLOTS, -1)
    picked_first = rows_cols(pick_first_low, back)
    picked_second = rows_cols(pick_second_low, back)
    output = (
        middle
        + weight_first[:, None] * picked_first[:, :part_width]
        + weight_second[:, None] * picked_second[:, :part_width]
    ).astype(BF)

    grad_weight = (slot_grad.astype(F32) * slot_gate).astype(BF)
    gate_out = share_rows(cols_cols(slot_hidden, grad_gate_pre))
    up_out = share_rows(cols_cols(slot_hidden, grad_up_pre))
    down_out = share_rows(cols_cols(grad_weight, activated))

    tail = 2 * part_width
    share_first_grad = picked_first[:, tail] + picked_first[:, tail + 1]
    share_second_grad = picked_second[:, tail] + picked_second[:, tail + 1]
    both = picked_first + picked_second
    stat_second = both[:, tail + 2] + both[:, tail + 3]
    grad_hidden_loc = both[:, part_width:tail]
    grad_local = cotangent.astype(F32)
    _, pull_gates = jax.vjp(lambda given: gate_pair(given, hot_first, hot_second), logits)
    (grad_logits,) = pull_gates((kept[:, 0] * share_first_grad, kept[:, 1] * share_second_grad))
    grad_logits_low = grad_logits.astype(BF)
    grad_router_rows = rows_rows(grad_logits_low, router_w)
    stat_total = stat_second + jnp.sum(normed_second * gain_second * grad_router_rows, 1)

    def take_cols(full_rows):
        return lax.dynamic_slice_in_dim(full_rows, narrow_at * part_width, part_width, 1)

    grad_hidden_loc = grad_hidden_loc + take_cols(grad_router_rows)
    normed_second_loc = take_cols(normed_second)
    grad_gain_second = jnp.sum(grad_hidden_loc * normed_second_loc, 0)
    grad_middle = grad_local + scale_second * (
        gain_second_loc * grad_hidden_loc - normed_second_loc * stat_total[:, None] / full_width
    )
    grad_router_w = cols_cols(hidden_second, grad_logits_low)
    grad_branch = lax.all_gather(grad_middle.astype(BF), "narrow", axis=1, tiled=True)
    grad_attended = rows_cols(grad_branch, out_w).astype(BF)
    grad_out_w = cols_cols(grad_branch, attended)
    grad_qs, grad_ks, grad_vs = [], [], []
    for head in range(heads):
        query, key, value, weights = saved[head]
        grad_out = head_cols(grad_attended, head)
        grad_weights = rows_rows(grad_out, value)
        inner = jnp.sum(weights * grad_weights, -1, keepdims=True)
        grad_scores = (weights * (grad_weights - inner)).astype(BF)
        grad_q = rows_cols(grad_scores, key) * score_scale
        grad_k = cols_cols(grad_scores, query) * score_scale
        grad_qs.append(rotate(grad_q, cosines, -sines).astype(BF))
        grad_ks.append(rotate(grad_k, cosines, -sines).astype(BF))
        grad_vs.append(cols_cols(weights.astype(BF), grad_out).astype(BF))
    grad_query_raw = jnp.concatenate(grad_qs, 1)
    grad_key_raw = jnp.concatenate(grad_ks, 1)
    grad_value_raw = jnp.concatenate(grad_vs, 1)
    grad_hidden_first = (
        rows_rows(grad_query_raw, query_w)
        + rows_rows(grad_key_raw, key_w)
        + rows_rows(grad_value_raw, value_w)
    )
    stat_first = jnp.sum(normed_first * gain_first * grad_hidden_first, 1, keepdims=True)
    extras = jnp.pad(jnp.concatenate(two_parts(stat_first), 1), ((0, 0), (0, 126)))
    grad_hidden_low = grad_hidden_first.astype(BF)
    first_parts = []
    for part in range(narrow_count):
        first_parts += [grad_hidden_low[:, part * part_width : (part + 1) * part_width], extras]
    first_back = lax.psum_scatter(
        jnp.concatenate(first_parts, 1), "narrow", scatter_dimension=1, tiled=True
    ).astype(F32)
    grad_first_loc = first_back[:, :part_width]
    stat_first = first_back[:, part_width : part_width + 1]
    stat_first = stat_first + first_back[:, part_width + 1 : part_width + 2]
    normed_first_loc = take_cols(normed_first)
    grad_gain_first = jnp.sum(grad_first_loc * normed_first_loc, 0)
    grad_tokens = grad_middle + scale_first * (
        gain_first_loc * grad_first_loc - normed_first_loc * stat_first / full_width
    )
    grad_attn_w = jnp.concatenate(
        [
            cols_cols(hidden_first, grad_query_raw).astype(BF),
            cols_cols(hidden_first, grad_key_raw).astype(BF),
            cols_cols(hidden_first, grad_value_raw).astype(BF),
            grad_out_w.astype(BF),
        ],
        1,
    )
    attn_summed = lax.psum_scatter(
        grad_attn_w, "wide", scatter_dimension=0, tiled=True
    ).astype(F32)
    router_summed = lax.psum_scatter(grad_router_w, "wide", scatter_dimension=0, tiled=True)
    gains_summed = lax.psum(jnp.stack([grad_gain_first, grad_gain_second]), "wide")
    return (
        output,
        grad_tokens,
        gains_summed[0],
        attn_summed[:, :part_width],
        attn_summed[:, part_width : 2 * part_width],
        attn_summed[:, 2 * part_width : 3 * part_width],
        attn_summed[:, 3 * part_width :],
        gains_summed[1],
        router_summed,
        gate_out,
        up_out,
        down_out,
    )


def per_device(
    tokens, gain_attn, w_query, w_key, w_value, w_out, gain_ffn, w_router,
    w_gate, w_up, w_down, segment, parents, expert_ids, slot_order, cotangent,
):
    if lax.axis_size("wide") != 8 or lax.axis_size("narrow") != 4:
        return plain_device(
            tokens, gain_attn, w_query, w_key, w_value, w_out, gain_ffn, w_router,
            w_gate, w_up, w_down, segment, parents, expert_ids, slot_order, cotangent,
        )
    (
        in_w, out_w, expert_w, slot_mid, slot_grad, slot_gate, middle, hidden_first,
        token_parts, qkv, probs, attended, stat, rope, picks, columns,
    ) = front_call(
        tokens, cotangent, gain_attn, gain_ffn, (w_query, w_key, w_value, w_out),
        w_router.T, (w_gate, w_up, w_down), segment, parents, expert_ids.T, slot_order,
    )
    back_mid, back_exp, last_exp, back_ext, grads, early_experts = mid_call(
        slot_mid, slot_grad, slot_gate, token_parts, expert_w
    )
    (
        output, grad_tokens, summed, small, router, experts,
    ) = tail_call(
        back_mid, back_exp, last_exp, back_ext, grads, picks, stat, columns, middle, cotangent, tokens,
        token_parts, qkv, probs, attended, rope, hidden_first, in_w, out_w,
    )
    (
        gate_out, up_out, down_out, output, grad_tokens, grad_q, grad_k, grad_v, grad_o,
        grad_gain_first, grad_gain_second, router,
    ) = finish_call(early_experts, experts, output, grad_tokens, summed, small, router)
    return (
        output, grad_tokens, grad_gain_first.reshape(-1), grad_q, grad_k, grad_v, grad_o,
        grad_gain_second.reshape(-1), router.T, gate_out, up_out, down_out,
    )


def solution(mesh):
    pair = P("wide", "narrow")
    part = P("narrow")
    rows = P("wide", None)
    cube = P("wide", None, "narrow")
    return jax.shard_map(
        per_device,
        mesh=mesh,
        in_specs=(
            pair, part, pair, pair, pair, pair, part, rows, cube, cube, cube,
            rows, rows, rows, rows, pair,
        ),
        out_specs=(
            pair, pair, part, pair, pair, pair, pair, part, rows, cube, cube, cube,
        ),
        check_vma=False,
    )
```

```python
import math

import jax
import jax.numpy as jnp
from jax import lax
from jax.experimental import pallas as pl
from jax.experimental.pallas import tpu as pltpu
from jax.sharding import PartitionSpec as P

HEAD_DIM = 128
EXPERTS = 4
SEGS = 13
CAP = 144
SLOTS = EXPERTS * CAP
NORM_EPS = 1e-05
NEG_FILL = -1e30
ROPE_BASE = 10000.0
BF = jnp.bfloat16
F32 = jnp.float32


def mm(left, right, dims):
    return lax.dot_general(left, right, (dims, ((), ())), preferred_element_type=F32)


def rows_cols(left, right):
    return mm(left, right, ((1,), (0,)))


def rows_rows(left, right):
    return mm(left, right, ((1,), (1,)))


def cols_cols(left, right):
    return mm(left, right, ((0,), (0,)))


def tree_layout(segment_row, parent_row):
    seg_ids = jnp.arange(SEGS, dtype=jnp.int32)
    member = segment_row[:, None] == seg_ids[None, :]
    parent_of = (parent_row[:, None] == seg_ids[None, :]) & (seg_ids[:, None] != 0)
    itself = seg_ids[:, None] == seg_ids[None, :]
    reach = itself
    for _ in range(3):
        reach = itself | jnp.any(parent_of[:, :, None] & reach[None, :, :], axis=1)
    counts = member.astype(jnp.int32)
    lengths = jnp.sum(counts, 0)
    starts = jnp.sum(jnp.where(seg_ids[None, :] < seg_ids[:, None], lengths[None, :], 0), 1)
    before = jnp.sum(jnp.where(reach, lengths[None, :], 0), 1) - lengths
    row_at = jnp.arange(segment_row.shape[0], dtype=jnp.int32)
    places = jnp.sum(counts * (before - starts)[None, :], 1) + row_at
    member_low = member.astype(BF)
    lineage = rows_cols(member_low, reach.astype(BF)).astype(BF)
    shared = rows_rows(lineage, member_low) > 0.5
    seen = shared & (row_at[None, :] <= row_at[:, None])
    return seen, places.astype(F32)


def route(expert_row, slot_rank):
    expert_range = jnp.arange(EXPERTS, dtype=jnp.int32)
    hot_first = (expert_row[:, 0:1] == expert_range[None, :]).astype(F32)
    hot_second = (expert_row[:, 1:2] == expert_range[None, :]).astype(F32)
    earlier = (slot_rank[None, :] < slot_rank[:, None]).astype(BF)
    count_first = rows_cols(earlier, hot_first.astype(BF))
    count_second = rows_cols(earlier, hot_second.astype(BF))
    ahead_first = jnp.sum(count_first * hot_first, 1)
    ahead_second = jnp.sum((count_second + jnp.sum(hot_first, 0)[None, :]) * hot_second, 1)
    slot_index = jnp.stack([ahead_first, ahead_second], 1).astype(jnp.int32)
    kept = slot_index < CAP
    flat_slot = jnp.where(kept, expert_row * CAP + slot_index, SLOTS)
    slot_range = jnp.arange(SLOTS, dtype=jnp.int32)
    pick_first = flat_slot[:, 0:1] == slot_range[None, :]
    pick_second = flat_slot[:, 1:2] == slot_range[None, :]
    return hot_first, hot_second, kept.astype(F32), pick_first, pick_second


def rotate(vectors, cosines, sines):
    half_dim = HEAD_DIM // 2
    first_half = vectors[..., :half_dim]
    second_half = vectors[..., half_dim:]
    return jnp.concatenate(
        [
            first_half * cosines - second_half * sines,
            second_half * cosines + first_half * sines,
        ],
        -1,
    )


def gate_pair(logits, hot_first, hot_second):
    chances = jax.nn.softmax(logits, axis=-1)
    first_share = jnp.sum(chances * hot_first, 1)
    second_share = jnp.sum(chances * hot_second, 1)
    pair_total = first_share + second_share
    return (first_share / pair_total, second_share / pair_total)


def two_parts(column):
    high = column.astype(BF)
    return high, (column - high.astype(F32)).astype(BF)


MESH = pl.DeviceIdType.MESH
NEAR = 3


def low_dot(left, right):
    return jnp.dot(left, right, preferred_element_type=F32)


def places_of(n):
    return [lax.rem(n + step, 4) for step in (1, 2, 3)], [lax.rem(n + 4 - step, 4) for step in (1, 2, 3)]


def plane_of(chip):
    x, y = lax.rem(chip, 2), chip // 2
    return [2 * y + 1 - x, 2 * (1 - y) + x, 2 * (1 - y) + 1 - x]


def greet(narrow_peers, plane_peers, chip, core, mate):
    barrier = pltpu.get_barrier_semaphore()
    count = 0
    for peer in narrow_peers:
        pl.semaphore_signal(barrier, inc=1, device_id={"narrow": peer}, device_id_type=MESH)
        count += 1
    for peer in plane_peers:
        pl.semaphore_signal(
            barrier, inc=1, device_id={"wide": 2 * peer + core}, device_id_type=MESH
        )
        count += 1
    if mate:
        pl.semaphore_signal(
            barrier, inc=1, device_id={"wide": 2 * chip + 1 - core}, device_id_type=MESH
        )
        count += 1
    pl.semaphore_wait(barrier, count)


class Links:
    def __init__(self, sent, landed, local):
        self.sent, self.landed, self.local = sent, landed, local
        self.used, self.local_used = 0, 0
        self.waits = []

    def slot(self):
        self.used += 1
        return self.used - 1

    def send(self, source, target, device, slot, when=None):
        copy = pltpu.make_async_remote_copy(
            src_ref=source,
            dst_ref=target,
            send_sem=self.sent.at[slot],
            recv_sem=self.landed.at[slot],
            device_id=device,
            device_id_type=MESH,
        )
        if when is None:
            copy.start()
        else:
            pl.when(when)(copy.start)
        self.waits.append((copy, when))

    def land(self, target, device, slot, when=None):
        copy = pltpu.make_async_remote_copy(
            src_ref=target,
            dst_ref=target,
            send_sem=self.sent.at[slot],
            recv_sem=self.landed.at[slot],
            device_id=device,
            device_id_type=MESH,
        )
        if when is None:
            copy.wait_recv()
        else:
            pl.when(when)(copy.wait_recv)

    def move(self, source, target):
        copy = pltpu.make_async_copy(source, target, self.local.at[self.local_used])
        self.local_used += 1
        copy.start()
        self.waits.append((copy, "local"))
        return copy

    def finish(self):
        for copy, when in self.waits:
            if when == "local":
                copy.wait()
            elif when is None:
                copy.wait_send()
            else:
                pl.when(when)(copy.wait_send)


class Chain:
    def __init__(self, links, n, block):
        self.links, self.n, self.block = links, n, block
        self.slots = [(links.slot(), links.slot()) for _ in range(3)]

    def start(self, step):
        n, links = self.n, self.links
        right, left = self.slots[step]
        block = self.block(lax.rem(n + 4 - step, 4))
        links.send(
            block, block, {"narrow": lax.rem(n + 1, 4)}, right,
            (n < 3) & (n >= step),
        )
        block = self.block(lax.rem(n + step, 4))
        links.send(
            block, block, {"narrow": lax.rem(n + 3, 4)}, left,
            (n > 0) & (n + step <= 3),
        )

    def land(self, step):
        n, links = self.n, self.links
        right, left = self.slots[step]
        links.land(
            self.block(lax.rem(n + 7 - step, 4)), {"narrow": lax.rem(n + 3, 4)}, right,
            n >= step + 1,
        )
        links.land(
            self.block(lax.rem(n + 1 + step, 4)), {"narrow": lax.rem(n + 1, 4)}, left,
            n + 1 + step <= 3,
        )


class LineSum:
    def __init__(self, links, n, outbox, inbox):
        self.links, self.n, self.outbox, self.inbox = links, n, outbox, inbox
        self.inner = (n == 1) | (n == 2)
        self.outer = (n == 0) | (n == 3)
        self.targets = [self.owner(step) for step in range(NEAR)]
        self.next = 1 + lax.rem(n, 2)
        self.slots = [links.slot() for _ in range(6)]

    def owner(self, step):
        return lax.rem((4 - step) * self.n + (3 - step), 5)

    def put(self, step, part):
        self.outbox[step] = part.astype(BF)
        self.set_out(step)

    def set_out(self, step):
        links, outbox, inbox = self.links, self.outbox, self.inbox
        goal = {"narrow": self.next if step == 0 else self.targets[step]}
        far, near = self.slots[2 * step], self.slots[2 * step + 1]
        if step == 0:
            links.send(outbox.at[0], inbox.at[3], goal, far, self.outer)
            links.send(outbox.at[0], inbox.at[0], goal, near, self.inner)
        elif step == 1:
            links.send(outbox.at[1], inbox.at[1], goal, far, self.outer)
            links.send(outbox.at[1], inbox.at[0], goal, near, self.inner)
        else:
            links.send(outbox.at[2], inbox.at[2], goal, far, self.outer)

    def join(self):
        links, outbox, inbox = self.links, self.outbox, self.inbox
        home = {"narrow": 3 * (self.n // 2)}
        links.land(inbox.at[3], home, self.slots[0], self.inner)

        @pl.when(self.inner)
        def _():
            outbox[2] = (outbox[2].astype(F32) + inbox[3].astype(F32)).astype(BF)

    def relay(self):
        self.join()
        goal = {"narrow": self.targets[2]}
        self.links.send(
            self.outbox.at[2], self.inbox.at[1], goal, self.slots[5], self.inner
        )

    def early(self, own):
        links, inbox = self.links, self.inbox
        other = {"narrow": lax.rem(self.n + 1, 4)}
        links.land(inbox.at[0], other, self.slots[1], self.inner)
        links.land(inbox.at[0], other, self.slots[3], self.outer)
        links.land(inbox.at[1], other, self.slots[2], self.inner)

        @pl.when(self.outer)
        def _():
            inbox[1] = jnp.zeros(inbox.shape[1:], BF)

        return own + inbox[0].astype(F32) + inbox[1].astype(F32)

    def total(self, own):
        links, inbox = self.links, self.inbox
        outer, inner = self.outer, self.inner
        other = {"narrow": lax.rem(self.n + 1, 4)}
        links.land(inbox.at[0], other, self.slots[1], inner)
        links.land(inbox.at[0], other, self.slots[3], outer)
        links.land(inbox.at[1], other, self.slots[2], inner)
        links.land(inbox.at[1], other, self.slots[5], outer)
        links.land(inbox.at[2], other, self.slots[4], inner)

        @pl.when(outer)
        def _():
            inbox[2] = jnp.zeros(inbox.shape[1:], BF)

        for index in range(3):
            own = own + inbox[index].astype(F32)
        return own


class PlaneGather:
    def __init__(self, links, chip, core, plane, mate, source, blocks):
        self.links, self.chip, self.core, self.plane, self.mate = links, chip, core, plane, mate
        self.blocks = blocks
        self.slots = [links.slot() for _ in range(4)]
        self.mate_slots = [links.slot() for _ in range(4)]
        own = 2 * chip + core
        for side in range(2):
            links.send(source, blocks.at[own], self.at_plane(plane[side]), self.slots[side])
        links.send(source, blocks.at[own], mate, self.mate_slots[3])

    def at_plane(self, peer):
        return {"wide": 2 * peer + self.core}

    def half(self, peer, side):
        rows = self.blocks.shape[1] // 2
        return self.blocks.at[2 * peer + self.core, pl.ds(side * rows, rows), :]

    def pass_on(self):
        links, plane = self.links, self.plane
        for side in range(2):
            block = self.blocks.at[2 * plane[side] + self.core]
            links.land(block, self.at_plane(plane[side]), self.slots[side])
            part = self.half(plane[side], side)
            links.send(part, part, self.at_plane(plane[1 - side]), self.slots[2 + side])
            links.send(block, block, self.mate, self.mate_slots[side])

    def far(self):
        links, plane = self.links, self.plane
        for side in range(2):
            links.land(
                self.half(plane[2], side), self.at_plane(plane[1 - side]), self.slots[2 + side]
            )
        block = self.blocks.at[2 * plane[2] + self.core]
        links.send(block, block, self.mate, self.mate_slots[2])

    def finish(self):
        links, plane = self.links, self.plane
        for step in range(NEAR):
            block = self.blocks.at[2 * plane[step] + 1 - self.core]
            links.land(block, self.mate, self.mate_slots[step])
        links.land(self.blocks.at[2 * self.chip + 1 - self.core], self.mate, self.mate_slots[3])


FRONT_SLOTS = 112


def front_body(
    tok_ref, cot_ref, gain_first_ref, gain_second_ref, wq_ref, wk_ref, wv_ref, wo_ref, router_ref, gate_ref, up_ref,
    down_ref, segment_ref, parents_ref, ids_ref, rank_ref,
    qkvw_out, outw_out, expert_out, x_out, dy_out, gate_out, middle_out, hidden_hbm,
    tokens_hbm, qkv_hbm, prob_hbm, att_out, stat_out, rope_out, pick_hbm, cols_out,
    hidden_out, tokens_out, qkv_out, prob_out, pick_out,
    raw_proj, seen_at, raw, moved_ref, pack, tok_pack, qkvw, outw, cot_send, y_send, br_send,
    br_recv, stat_send, stat_recv, gate_send, sent, landed, local,
):
    n = lax.axis_index("narrow")
    w = lax.axis_index("wide")
    chip, core = w // 2, lax.rem(w, 2)
    to_z, from_z = places_of(n)
    plane = plane_of(chip)
    links = Links(sent, landed, local)
    mate = {"wide": 2 * chip + 1 - core}

    def at_plane(peer):
        return {"wide": 2 * peer + core}

    token_count, part_width = tok_ref.shape
    rows_each = raw.shape[1]
    raw_loads = [
        links.move(source, raw.at[kind_at]) for kind_at, source in enumerate((gate_ref, up_ref, down_ref))
    ]
    links.waits = []
    greet(to_z, plane, chip, core, True)

    def by_expert(kind_at):
        raw_loads[kind_at].wait()

        def some_rows(index, value):
            rows = pl.ds(pl.multiple_of(index * 32, 32), 32)
            for expert in range(EXPERTS):
                moved_ref[kind_at, expert, rows, :] = raw[kind_at, rows, expert, :]
            return value

        lax.fori_loop(0, rows_each // 32, some_rows, 0)

    tok_pack[0:token_count, :] = tok_ref[...]
    for index, gain_ref in enumerate((gain_first_ref, gain_second_ref)):
        for row in range(part_width // 128):
            tok_pack[
                token_count + index : token_count + index + 1, row * 128 : (row + 1) * 128
            ] = gain_ref[row : row + 1, :]
    tokens_out[n] = tok_pack[...]
    tok_chain = Chain(links, n, lambda m: tokens_out.at[m])
    tok_chain.start(0)
    wide_shape = (token_count, token_count)
    row_at = lax.broadcasted_iota(jnp.int32, wide_shape, 0)
    col_at = lax.broadcasted_iota(jnp.int32, wide_shape, 1)
    seg_row, rank_row = segment_ref[...], rank_ref[...]
    first_row, second_row = ids_ref[0:1, :], ids_ref[1:2, :]
    stacked = [item.astype(F32) for item in (seg_row, rank_row, first_row, second_row)]
    columns = jnp.concatenate(stacked + [jnp.zeros((124, token_count), F32)], 0).T
    cols_out[...] = columns
    columns = columns.astype(jnp.int32)
    seg_col, rank_col = columns[:, 0:1], columns[:, 1:2]
    segs = parents_ref.shape[1]
    of_seg = lax.broadcasted_iota(jnp.int32, (token_count, segs), 1) == seg_col
    par_col = jnp.sum(
        jnp.where(of_seg, parents_ref[...].astype(F32), 0.0), 1, keepdims=True
    ).astype(jnp.int32)
    seen = ((seg_row == seg_col) | (seg_row == par_col) | (seg_row == 0)) & (col_at <= row_at)
    spots = jnp.sum(jnp.where(seen, 1.0, 0.0), 1, keepdims=True) - 1.0
    lane_at = lax.broadcasted_iota(jnp.int32, (token_count, HEAD_DIM), 1)
    turn = lax.rem(lane_at, HEAD_DIM // 2).astype(F32) * (-2.0 / HEAD_DIM * math.log(ROPE_BASE))
    angles = spots * jnp.exp(turn)
    cosines = jnp.cos(angles)
    sines = jnp.sin(angles) * jnp.where(lane_at < HEAD_DIM // 2, -1.0, 1.0)
    rope_out[0] = cosines
    rope_out[1] = sines
    kind = lax.broadcasted_iota(jnp.int32, (8, token_count), 0)
    hot_first = jnp.where(kind == first_row, 1.0, 0.0)
    hot_second = jnp.where(kind == second_row, 1.0, 0.0)
    earlier = jnp.where(rank_col < rank_row, 1.0, 0.0).astype(BF)
    count_first = low_dot(hot_first.astype(BF), earlier)
    count_second = low_dot(hot_second.astype(BF), earlier)
    count_second = count_second + jnp.sum(hot_first, 1, keepdims=True)
    slot_first = jnp.sum(count_first * hot_first, 0, keepdims=True)
    slot_second = jnp.sum(count_second * hot_second, 0, keepdims=True)
    kept_first = jnp.where(slot_first < CAP, 1.0, 0.0)
    kept_second = jnp.where(slot_second < CAP, 1.0, 0.0)
    flat_first = jnp.where(slot_first < CAP, first_row * CAP + slot_first.astype(jnp.int32), SLOTS)
    flat_second = jnp.where(
        slot_second < CAP, second_row * CAP + slot_second.astype(jnp.int32), SLOTS
    )
    slot_at = lax.broadcasted_iota(jnp.int32, (SLOTS, token_count), 0)
    pick_first = jnp.where(slot_at == flat_first, 1.0, 0.0)
    pick_second = jnp.where(slot_at == flat_second, 1.0, 0.0)
    pick_out[0] = pick_first.astype(BF)
    pick_out[1] = pick_second.astype(BF)
    pick_both = (pick_first + pick_second).astype(BF)

    def column_block(array):
        return lambda m: array.at[:, pl.ds(pl.multiple_of(m * part_width, part_width), part_width)]

    def slot_block(array, owner):
        return array.at[
            pl.ds(pl.multiple_of(owner * CAP, 16), CAP),
            pl.ds(pl.multiple_of(n * part_width, part_width), part_width),
        ]

    def dispatch(rows, buffer, array):
        slots = [links.slot() for _ in range(NEAR)]
        buffer[...] = low_dot(pick_both, rows).astype(BF)
        for step in range(NEAR):
            links.send(
                buffer.at[pl.ds(pl.multiple_of(plane[step] * CAP, 16), CAP), :],
                slot_block(array, chip), at_plane(plane[step]), slots[step],
            )
        own = links.move(
            buffer.at[pl.ds(pl.multiple_of(chip * CAP, 16), CAP), :], slot_block(array, chip)
        )
        return slots, own

    def arrive(array, state):
        slots, own = state
        for step in range(NEAR):
            links.land(slot_block(array, plane[step]), at_plane(plane[step]), slots[step])
        own.wait()
        links.waits = [item for item in links.waits if item[0] is not own]

    dy_state = dispatch(cot_ref[...], cot_send, dy_out)
    dy_chain = Chain(links, n, column_block(dy_out))

    pack[:, 0:512] = wq_ref[...]
    pack[:, 512:1024] = wk_ref[...]
    pack[:, 1024:1536] = wv_ref[...]
    router_rows = jnp.concatenate(
        [router_ref[...].astype(F32), jnp.zeros((128 - EXPERTS, rows_each), F32)], 0
    )
    pack[:, 1536:1664] = router_rows.T.astype(BF)
    in_gather = PlaneGather(links, chip, core, plane, mate, pack, qkvw)
    qkvw[w] = pack[...]
    outw[w] = wo_ref[...]

    tok_chain.land(0)
    tok_chain.start(1)
    by_expert(0)
    tok_chain.land(1)
    tok_chain.start(2)
    arrive(dy_out, dy_state)
    dy_chain.start(0)
    tok_chain.land(2)
    in_gather.pass_on()
    out_gather = PlaneGather(links, chip, core, plane, mate, wo_ref, outw)
    total = jnp.zeros((token_count, 1), F32)
    for m in range(4):
        part = tokens_out[m, 0:token_count, :].astype(F32)
        total = total + jnp.sum(part * part, 1, keepdims=True)
    scale_first = lax.rsqrt(total * (1.0 / (4 * part_width)) + NORM_EPS)
    for m in range(4):
        part = tokens_out[m, 0:token_count, :].astype(F32)
        gain = tokens_out[m, token_count : token_count + 1, :].astype(F32)
        hidden_out[:, m * part_width : (m + 1) * part_width] = (part * scale_first * gain).astype(BF)

    by_expert(1)

    in_gather.far()
    out_gather.pass_on()
    in_gather.finish()
    saved_in = links.move(qkvw, qkvw_out)

    pieces = ((0, 0, rows_each), (1, 0, rows_each)) + tuple(
        (2, half * rows_each // 2, rows_each // 2) for half in range(2)
    )
    expert_slots = [[links.slot() for _ in range(NEAR)] for _ in pieces]
    expert_mate = [[links.slot() for _ in range(4)] for _ in pieces]

    def piece_of(array, index):
        return array.at[pl.ds(pieces[index][1], pieces[index][2]), :]

    def landing(index, owner, side):
        return piece_of(expert_out.at[pieces[index][0], owner, side], index)

    def set_out(index):
        kind_at = pieces[index][0]
        for step in range(NEAR):
            links.send(
                piece_of(moved_ref.at[kind_at, plane[step]], index), landing(index, chip, core),
                at_plane(plane[step]), expert_slots[index][step],
            )
        own = piece_of(moved_ref.at[kind_at, chip], index)
        links.send(own, landing(index, chip, core), mate, expert_mate[index][3])
        links.move(own, landing(index, chip, core))

    set_out(0)
    set_out(1)

    def pass_on(index):
        for step in range(NEAR):
            block = landing(index, plane[step], core)
            links.land(block, at_plane(plane[step]), expert_slots[index][step])
            links.send(block, block, mate, expert_mate[index][step])

    def all_there(index):
        for step in range(NEAR):
            links.land(landing(index, plane[step], 1 - core), mate, expert_mate[index][step])
        links.land(landing(index, chip, 1 - core), mate, expert_mate[index][3])

    dy_chain.land(0)
    dy_chain.start(1)
    by_expert(2)

    score_scale = HEAD_DIM ** (-0.5)

    def one_projection(part, value):
        cols = pl.ds(pl.multiple_of(part * part_width, part_width), part_width)
        weight = qkvw[:, :, cols].reshape(4 * part_width, part_width)
        raw_proj[part] = low_dot(hidden_out[...], weight)
        return value

    lax.fori_loop(0, 3, one_projection, 0)
    seen_at[...] = jnp.where(seen, 1.0, 0.0)

    def one_head(head, value):
        cols = pl.ds(pl.multiple_of(head * HEAD_DIM, HEAD_DIM), HEAD_DIM)
        turned = []
        for part in range(2):
            proj = raw_proj[part, :, cols]
            turned.append(
                (proj * rope_out[0] + pltpu.roll(proj, HEAD_DIM // 2, 1) * rope_out[1]).astype(BF)
            )
            qkv_out[part, :, cols] = turned[part]
        values = raw_proj[2, :, cols].astype(BF)
        qkv_out[2, :, cols] = values
        scores = rows_rows(turned[0], turned[1]) * score_scale
        scores = jnp.where(seen_at[...] > 0.5, scores, NEG_FILL)
        exps = jnp.exp(scores - jnp.max(scores, 1, keepdims=True))
        weights = exps / jnp.sum(exps, 1, keepdims=True)
        prob_out[head] = weights
        att_out[:, cols] = low_dot(weights.astype(BF), values).astype(BF)
        return value

    lax.fori_loop(0, part_width // HEAD_DIM, one_head, 0)
    for source, target in (
        (hidden_out, hidden_hbm), (tokens_out, tokens_hbm), (qkv_out, qkv_hbm),
        (prob_out, prob_hbm), (pick_out, pick_hbm),
    ):
        links.move(source, target)

    dy_chain.land(1)
    dy_chain.start(2)
    out_gather.far()

    out_gather.finish()
    links.move(outw, outw_out)

    attended = att_out[...]

    def branch(m):
        weight = outw[pl.ds(2 * m, 2)].reshape(part_width, part_width)
        return rows_rows(attended, weight)

    branch_sum = LineSum(links, n, br_send, br_recv)
    for step in range(NEAR):
        branch_sum.put(step, branch(branch_sum.targets[step]))
    middle = tok_ref[...].astype(F32) + branch(n)
    branch_sum.relay()
    middle = branch_sum.total(middle)
    middle_out[...] = middle
    x_state = dispatch(middle.astype(BF), y_send, x_out)

    def cap_block(owner):
        return lambda m: x_out.at[
            pl.ds(pl.multiple_of(owner * CAP, 16), CAP),
            pl.ds(pl.multiple_of(m * part_width, part_width), part_width),
        ]

    x_chains = [Chain(links, n, cap_block(owner)) for owner in (chip, *plane)]
    x_slots, x_own = x_state
    x_own.wait()
    links.waits = [item for item in links.waits if item[0] is not x_own]
    x_chains[0].start(0)

    set_out(2)
    set_out(3)

    gain_second = tok_pack[token_count + 1 : token_count + 2, :].astype(F32)
    router = qkvw[pl.ds(2 * n, 2), :, 1536:1664].reshape(part_width, 128)
    logit_part = mm(router, (middle * gain_second).astype(BF), ((0,), (1,)))[0:8, :]
    square = middle * middle
    square_high = square.astype(BF)
    square_low = (square - square_high.astype(F32)).astype(BF)
    ones = jnp.ones((8, part_width), BF)
    square_sum = rows_rows(ones, square_high) + rows_rows(ones, square_low)
    stat = jnp.where(kind == 4, square_sum, logit_part)
    stat_send[...] = stat
    stat_slots = [links.slot() for _ in range(NEAR)]
    for step in range(NEAR):
        links.send(stat_send, stat_recv.at[step], {"narrow": to_z[step]}, stat_slots[step])

    for step in range(NEAR):
        links.land(slot_block(x_out, plane[step]), at_plane(plane[step]), x_slots[step])
        x_chains[1 + step].start(0)
    for step in range(NEAR):
        links.land(stat_recv.at[step], {"narrow": from_z[step]}, stat_slots[step])
        stat = stat + stat_recv[step]
    stat_out[...] = stat
    scale_row = lax.rsqrt(stat[4:5, :] * (1.0 / (4 * part_width)) + NORM_EPS)
    logits = jnp.where(kind < EXPERTS, stat * scale_row, NEG_FILL)
    chances = jnp.exp(logits - jnp.max(logits, 0, keepdims=True))
    chances = chances / jnp.sum(chances, 0, keepdims=True)
    share_first = jnp.sum(chances * hot_first, 0, keepdims=True)
    share_second = jnp.sum(chances * hot_second, 0, keepdims=True)
    both = share_first + share_second
    weighted = pick_first * (share_first / both) + pick_second * (share_second / both)
    slot_gate = jnp.sum(weighted, 1, keepdims=True)
    gate_send[...] = jnp.broadcast_to(slot_gate, (SLOTS, 128))

    def gate_rows(array, owner):
        return array.at[pl.ds(pl.multiple_of(owner * CAP, 16), CAP), :]

    gate_slots = [links.slot() for _ in range(NEAR)]
    for step in range(NEAR):
        links.send(
            gate_rows(gate_send, plane[step]), gate_rows(gate_out, chip),
            at_plane(plane[step]), gate_slots[step],
        )
    links.move(gate_rows(gate_send, chip), gate_rows(gate_out, chip))

    for step in range(2):
        for chain in x_chains:
            chain.land(step)
            chain.start(step + 1)
        pass_on(step)
    for chain in x_chains:
        chain.land(2)
    dy_chain.land(2)
    for step in range(NEAR):
        links.land(gate_rows(gate_out, plane[step]), at_plane(plane[step]), gate_slots[step])
    pass_on(2)
    pass_on(3)
    for index in range(len(pieces)):
        all_there(index)
    links.finish()


def front_call(tokens, cotangent, gain_attn, gain_ffn, weights, router, experts, segment, parents, ids, rank):
    token_count, part_width = tokens.shape
    full = 4 * part_width
    rows_each, _, hidden_width = experts[0].shape
    heads = part_width // HEAD_DIM
    vmem = pl.BlockSpec(memory_space=pltpu.VMEM)
    hbm = pl.BlockSpec(memory_space=pl.ANY)

    def arr(shape, dtype):
        return jax.ShapeDtypeStruct(shape, dtype)

    return pl.pallas_call(
        front_body,
        out_shape=(
            arr((8, rows_each, 1664), BF),
            arr((8, rows_each, part_width), BF),
            arr((3, 4, 2, rows_each, hidden_width), BF),
            arr((SLOTS, full), BF),
            arr((SLOTS, full), BF),
            arr((SLOTS, 128), F32),
            arr((token_count, part_width), F32),
            arr((token_count, full), BF),
            arr((4, token_count + 16, part_width), BF),
            arr((3, token_count, part_width), BF),
            arr((heads, token_count, token_count), F32),
            arr((token_count, part_width), BF),
            arr((8, token_count), F32),
            arr((2, token_count, HEAD_DIM), F32),
            arr((2, SLOTS, token_count), BF),
            arr((token_count, 128), F32),
        ),
        in_specs=[vmem] * 9 + [hbm] * 3 + [vmem] * 4,
        out_specs=(hbm,) * 5 + (vmem, vmem) + (hbm,) * 4 + (vmem,) * 3 + (hbm, vmem),
        scratch_shapes=[
            pltpu.VMEM((token_count, full), BF),
            pltpu.VMEM((4, token_count + 16, part_width), BF),
            pltpu.VMEM((3, token_count, part_width), BF),
            pltpu.VMEM((heads, token_count, token_count), F32),
            pltpu.VMEM((2, SLOTS, token_count), BF),
            pltpu.VMEM((3, token_count, part_width), F32),
            pltpu.VMEM((token_count, token_count), F32),
            pltpu.VMEM((3, rows_each, EXPERTS, hidden_width), BF),
            pltpu.VMEM((3, EXPERTS, rows_each, hidden_width), BF),
            pltpu.VMEM((rows_each, 1664), BF),
            pltpu.VMEM((token_count + 16, part_width), BF),
            pltpu.VMEM((8, rows_each, 1664), BF),
            pltpu.VMEM((8, rows_each, part_width), BF),
            pltpu.VMEM((SLOTS, part_width), BF),
            pltpu.VMEM((SLOTS, part_width), BF),
            pltpu.VMEM((NEAR, token_count, part_width), BF),
            pltpu.VMEM((NEAR + 1, token_count, part_width), BF),
            pltpu.VMEM((8, token_count), F32),
            pltpu.VMEM((NEAR, 8, token_count), F32),
            pltpu.VMEM((SLOTS, 128), F32),
            pltpu.SemaphoreType.DMA((FRONT_SLOTS,)),
            pltpu.SemaphoreType.DMA((FRONT_SLOTS,)),
            pltpu.SemaphoreType.DMA((24,)),
        ],
        compiler_params=pltpu.CompilerParams(
            collective_id=0, has_side_effects=True, vmem_limit_bytes=60 * 1024 * 1024
        ),
        cost_estimate=pl.CostEstimate(
            flops=6_000_000_000, bytes_accessed=60_000_000, transcendentals=400_000
        ),
        name="front",
    )(
        tokens, cotangent, gain_attn.reshape(-1, 128), gain_ffn.reshape(-1, 128), *weights,
        router, *experts, segment, parents, ids, rank,
    )


MID_SLOTS = 48


TILE = 512


def mid_body(
    x_ref, dy_hbm, gate_ref, tokens_ref, w_ref,
    back_mid_out, back_exp_out, last_exp_out, extra_out, grads_out, expert_out,
    dy_ref, weights, hidden, graded_send, hidden_cat, graded_cat, act_cat, gate_cat, up_cat,
    turned, down_grad, rs_send, rs_recv, ext_send, ext_recv, sent, landed, local,
):
    n = lax.axis_index("narrow")
    w = lax.axis_index("wide")
    chip, core = w // 2, lax.rem(w, 2)
    to_z, from_z = places_of(n)
    plane = plane_of(chip)
    links = Links(sent, landed, local)
    mate = {"wide": 2 * chip + 1 - core}
    slots, full = hidden.shape
    part_width = full // 4
    rows_each = full // 8
    half = full // 2
    hidden_width = weights.shape[2]

    dy_load = links.move(dy_hbm, dy_ref)
    x_load = links.move(x_ref, hidden)
    loads = [
        links.move(
            w_ref.at[kind, c, k],
            weights.at[kind, pl.ds((2 * c + k) * rows_each, rows_each), :],
        )
        for kind in range(3)
        for c in range(4)
        for k in range(2)
    ]
    links.waits = []
    greet(to_z, plane, chip, core, True)

    slot_gate = gate_ref[:, 0:1]
    dy_load.wait()
    for c in range(4):
        theirs = pl.ds(pl.multiple_of((2 * c + 1 - core) * rows_each, rows_each), rows_each)
        ours = pl.ds(pl.multiple_of((2 * c + core) * rows_each, rows_each), rows_each)
        cols = slice(c * rows_each, (c + 1) * rows_each)
        graded_cat[core, :, cols] = (dy_ref[:, ours].astype(F32) * slot_gate).astype(BF)
        graded_send[:, cols] = (dy_ref[:, theirs].astype(F32) * slot_gate).astype(BF)

    def to_mate(source, target):
        slot = links.slot()
        links.send(source, target.at[core], mate, slot)
        return lambda: links.land(target.at[1 - core], mate, slot)

    graded_there = to_mate(graded_send, graded_cat)
    x_load.wait()
    total = jnp.zeros((slots, 1), F32)
    for m in range(4):
        part = hidden[:, m * part_width : (m + 1) * part_width].astype(F32)
        total = total + jnp.sum(part * part, 1, keepdims=True)
    scale = lax.rsqrt(total * (1.0 / full) + NORM_EPS)
    gain_row = tokens_ref.shape[1] - 15
    for m in range(4):
        cols = slice(m * part_width, (m + 1) * part_width)
        gain = tokens_ref[m, gain_row : gain_row + 1, :].astype(F32)
        hidden[:, cols] = (hidden[:, cols].astype(F32) * scale * gain).astype(BF)
    hidden_slots = [links.slot() for _ in range(4)]
    for c in range(4):
        cols = pl.ds(c * rows_each, rows_each)
        theirs = pl.ds(pl.multiple_of((2 * c + 1 - core) * rows_each, rows_each), rows_each)
        ours = pl.ds(pl.multiple_of((2 * c + core) * rows_each, rows_each), rows_each)
        links.send(hidden.at[:, theirs], hidden_cat.at[core, :, cols], mate, hidden_slots[c])
        hidden_cat[core, :, c * rows_each : (c + 1) * rows_each] = hidden[:, ours]
    for load in loads:
        load.wait()

    def one_tile(cols, rows):
        gate_pre = low_dot(hidden[rows, :], weights[0, :, cols])
        up_pre = low_dot(hidden[rows, :], weights[1, :, cols])
        act_raw = low_dot(dy_ref[rows, :], weights[2, :, cols])
        sigmoid = 1.0 / (1.0 + jnp.exp(-gate_pre))
        silu = gate_pre * sigmoid
        activated = (silu * up_pre).astype(BF)
        grad_act = act_raw * gate_ref[rows, 0:1]
        act_cat[core, rows, cols] = activated
        gate_cat[core, rows, cols] = (
            grad_act * up_pre * (sigmoid * (1.0 + gate_pre * (1.0 - sigmoid)))
        ).astype(BF)
        up_cat[core, rows, cols] = (grad_act * silu).astype(BF)
        return jnp.sum(act_raw * activated.astype(F32), 1, keepdims=True)

    def over_tiles(tile, body, carry):
        whole = hidden_width // tile
        carry = lax.fori_loop(
            0, whole, lambda t, value: body(pl.ds(pl.multiple_of(t * tile, tile), tile), value), carry
        )
        if hidden_width % tile:
            carry = body(pl.ds(whole * tile, hidden_width % tile), carry)
        return carry

    share = over_tiles(
        TILE,
        lambda cols, value: tuple(
            value[index] + one_tile(cols, pl.ds(index * (slots // 2), slots // 2))
            for index in range(2)
        ),
        (jnp.zeros((slots // 2, 1), F32),) * 2,
    )
    share = jnp.concatenate(share, 0)
    acts_there = [to_mate(item.at[core], item) for item in (act_cat, gate_cat, up_cat)]

    grad_gate, grad_up = gate_cat.at[core], up_cat.at[core]
    mid_sum = LineSum(links, n, rs_send.at[0], rs_recv.at[0])

    def mid_part(owner):
        rows = pl.ds(pl.multiple_of(owner * part_width, part_width), part_width)
        block = rows_rows(grad_gate[...], weights[0, rows, :])
        block = block + rows_rows(grad_up[...], weights[1, rows, :])
        return block, jnp.sum(hidden[:, rows].astype(F32) * block, 1, keepdims=True)

    stat = jnp.zeros((slots, 1), F32)
    block, part = mid_part(mid_sum.targets[0])
    mid_sum.put(0, block)
    stat = stat + part

    expert_slots = {}

    def weight_grad(right, target):
        def body(cols, value):
            right_rows = right[:, :, cols].reshape(2 * slots, cols.size)
            target[:, cols] = low_dot(turned[...], right_rows).astype(BF)
            return value

        over_tiles(TILE, body, 0)

    def share_out(index, source):
        expert_slots[index] = [links.slot() for _ in range(NEAR)]

        def block(owner):
            first = pl.multiple_of(owner * rows_each, rows_each)
            return source.at[pl.ds(first, rows_each), :]

        for step in range(NEAR):
            links.send(
                block(plane[step]), expert_out.at[index, chip],
                {"wide": 2 * plane[step] + core}, expert_slots[index][step],
            )
        links.move(block(chip), expert_out.at[index, chip])

    graded_there()
    acts_there[0]()
    turned[...] = graded_cat[...].reshape(2 * slots, half).T
    weight_grad(act_cat, down_grad)
    share_out(0, down_grad)

    def other_part(step, stat):
        block, part = mid_part(mid_sum.owner(step))
        rs_send[0, step] = block.astype(BF)
        return stat + part

    stat = lax.fori_loop(1, 4, other_part, stat)
    mid_sum.set_out(1)
    mid_sum.set_out(2)
    lane_at = lax.broadcasted_iota(jnp.int32, (slots, 128), 1)
    columns = jnp.where(lane_at == 0, share, jnp.where(lane_at == 1, stat, 0.0))
    high = columns.astype(BF)
    rest = (columns - high.astype(F32)).astype(BF)
    pick = jnp.where(
        lax.broadcasted_iota(jnp.int32, (8, 128), 0) == lax.broadcasted_iota(jnp.int32, (8, 128), 1),
        1.0, 0.0,
    ).astype(BF)
    extra = rows_rows(pick, high) + rows_rows(pick, rest)
    ext_send[...] = extra
    ext_slots = [links.slot() for _ in range(NEAR)]
    for step in range(NEAR):
        links.send(ext_send, ext_recv.at[step], {"narrow": to_z[step]}, ext_slots[step])

    mid_sum.relay()

    activated = act_cat.at[core]
    exp_sum = LineSum(links, n, rs_send.at[1], rs_recv.at[1])

    def exp_part(owner):
        rows = pl.ds(pl.multiple_of(owner * part_width, part_width), part_width)
        return rows_rows(activated[...], weights[2, rows, :])

    def expert_part(step, value):
        rs_send[1, step] = exp_part(exp_sum.owner(step)).astype(BF)
        return value

    lax.fori_loop(0, 4, expert_part, 0)
    exp_sum.set_out(0)
    exp_sum.set_out(1)
    for slot in hidden_slots:
        index = hidden_slots.index(slot)
        links.land(
            hidden_cat.at[1 - core, :, pl.ds(index * rows_each, rows_each)], mate, slot
        )
    for there in acts_there[1:]:
        there()
    turned[...] = hidden_cat[...].reshape(2 * slots, half).T
    gate_grad = weights.at[0, pl.ds(0, half), :]
    weight_grad(gate_cat, gate_grad)
    share_out(1, gate_grad)
    up_grad = weights.at[1, pl.ds(0, half), :]
    weight_grad(up_cat, up_grad)
    links.move(up_grad, grads_out)

    for step in range(NEAR):
        links.land(ext_recv.at[step], {"narrow": from_z[step]}, ext_slots[step])
        extra = extra + ext_recv[step]
    high = extra.astype(BF)
    rest = (extra - high.astype(F32)).astype(BF)
    place = lax.broadcasted_iota(jnp.int32, (8, 128), 0) * 2
    lanes = lax.broadcasted_iota(jnp.int32, (8, 128), 1)
    spread_high = jnp.where(place == lanes, 1.0, 0.0).astype(BF)
    spread_low = jnp.where(place + 1 == lanes, 1.0, 0.0).astype(BF)
    columns = mm(high, spread_high, ((0,), (0,))) + mm(rest, spread_low, ((0,), (0,)))
    extra_out[...] = jnp.where(lane_at == 4, 1.0, columns).astype(BF)
    back_mid_out[...] = mid_sum.total(rs_send[0, 3].astype(F32)).astype(BF)
    exp_sum.join()
    last_exp_out[...] = rs_send[1, 2]
    back_exp_out[...] = exp_sum.early(rs_send[1, 3].astype(F32)).astype(BF)
    for index in range(2):
        for step in range(NEAR):
            links.land(
                expert_out.at[index, plane[step]], {"wide": 2 * plane[step] + core},
                expert_slots[index][step],
            )
    links.finish()


def mid_call(slot_mid, slot_grad, slot_gate, token_parts, expert_w):
    slots, full = slot_mid.shape
    part_width = full // 4
    rows_each, hidden_width = expert_w.shape[3:]
    vmem = pl.BlockSpec(memory_space=pltpu.VMEM)
    hbm = pl.BlockSpec(memory_space=pl.ANY)

    def arr(shape, dtype):
        return jax.ShapeDtypeStruct(shape, dtype)

    return pl.pallas_call(
        mid_body,
        out_shape=(
            arr((slots, part_width), BF),
            arr((slots, part_width), BF),
            arr((slots, part_width), BF),
            arr((slots, 128), BF),
            arr((full // 2, hidden_width), BF),
            arr((2, 4, rows_each, hidden_width), BF),
        ),
        in_specs=[hbm] * 2 + [vmem] * 2 + [hbm],
        out_specs=(vmem,) * 4 + (hbm, hbm),
        scratch_shapes=[
            pltpu.VMEM((slots, full), BF),
            pltpu.VMEM((3, full, hidden_width), BF),
            pltpu.VMEM((slots, full), BF),
            pltpu.VMEM((slots, full // 2), BF),
            pltpu.VMEM((2, slots, full // 2), BF),
            pltpu.VMEM((2, slots, full // 2), BF),
            pltpu.VMEM((2, slots, hidden_width), BF),
            pltpu.VMEM((2, slots, hidden_width), BF),
            pltpu.VMEM((2, slots, hidden_width), BF),
            pltpu.VMEM((full // 2, 2 * slots), BF),
            pltpu.VMEM((full // 2, hidden_width), BF),
            pltpu.VMEM((2, NEAR + 1, slots, part_width), BF),
            pltpu.VMEM((2, NEAR + 1, slots, part_width), BF),
            pltpu.VMEM((8, slots), F32),
            pltpu.VMEM((NEAR, 8, slots), F32),
            pltpu.SemaphoreType.DMA((MID_SLOTS,)),
            pltpu.SemaphoreType.DMA((MID_SLOTS,)),
            pltpu.SemaphoreType.DMA((32,)),
        ],
        compiler_params=pltpu.CompilerParams(
            collective_id=1, has_side_effects=True, vmem_limit_bytes=62 * 1024 * 1024
        ),
        cost_estimate=pl.CostEstimate(
            flops=30_000_000_000, bytes_accessed=40_000_000, transcendentals=800_000
        ),
        name="mid",
    )(slot_mid, slot_grad, slot_gate, token_parts, expert_w)


class PlaneSum:
    def __init__(self, links, core, chip, plane, first, send, inbox):
        self.links, self.core, self.chip = links, core, chip
        self.near, self.next, self.far = plane[first], plane[1 - first], plane[2]
        self.send, self.inbox = send, inbox
        self.slots = [links.slot() for _ in range(3)]

    def at(self, peer):
        return {"wide": 2 * peer + self.core}

    def block(self, owner):
        rows = self.inbox.shape[1]
        return self.send.at[pl.ds(pl.multiple_of(owner * rows, rows), rows), :]

    def start(self):
        links = self.links
        links.send(self.block(self.far), self.inbox.at[1], self.at(self.near), self.slots[1])
        links.send(self.block(self.near), self.inbox.at[0], self.at(self.near), self.slots[0])

    def turn(self):
        links = self.links
        links.land(self.inbox.at[1], self.at(self.near), self.slots[1])
        block = self.block(self.next)
        block[...] = (block[...].astype(F32) + self.inbox[1].astype(F32)).astype(BF)
        links.send(block, self.inbox.at[2], self.at(self.next), self.slots[2])

    def total(self):
        links = self.links
        links.land(self.inbox.at[0], self.at(self.near), self.slots[0])
        links.land(self.inbox.at[2], self.at(self.next), self.slots[2])
        own = self.block(self.chip)[...].astype(F32)
        return own + self.inbox[0].astype(F32) + self.inbox[2].astype(F32)


TAIL_SLOTS = 72


def tail_body(
    mid_ref, exp_ref, last_ref, ext_ref, moved_ref, picks_hbm, stat_ref, cols_ref, middle_ref,
    cot_ref, tok_ref, tokens_hbm, qkv_hbm, prob_hbm, att_ref, rope_ref, hidden_hbm, qkvw_ref,
    outw_ref,
    output_out, grad_tokens_out, summed_out, small_out,
    router_out, expert_out,
    picks_ref, tokens_ref, qkv_ref, prob_ref, hidden_ref, grad_att_at, exp_in, exp_sum, router_all, qkvw, outw, ret_mid, ret_exp, ret_ext, branch, hidden_cat, branch_cat, att_cat, proj_cat,
    proj_send, proj_recv, first_send, first_recv, col_send, col_recv, small_mate, small_sum,
    small_recv, last_mate, last_sum, last_recv, sent, landed, local,
):
    n = lax.axis_index("narrow")
    w = lax.axis_index("wide")
    chip, core = w // 2, lax.rem(w, 2)
    to_z, from_z = places_of(n)
    plane = plane_of(chip)
    links = Links(sent, landed, local)
    mate = {"wide": 2 * chip + 1 - core}
    token_count, part_width = tok_ref.shape
    full = 4 * part_width
    rows_each = full // 8
    heads = part_width // HEAD_DIM
    half = full // 2

    def at_plane(peer):
        return {"wide": 2 * peer + core}

    def cap_rows(array, owner):
        return array.at[pl.ds(pl.multiple_of(owner * CAP, 16), CAP), :]

    first_loads = [
        links.move(source, target)
        for source, target in (
            (hidden_hbm, hidden_ref), (picks_hbm, picks_ref), (tokens_hbm, tokens_ref),
            (qkv_hbm, qkv_ref), (prob_hbm, prob_ref),
        )
    ]
    loads = [links.move(qkvw_ref, qkvw), links.move(outw_ref, outw)]
    links.waits = []
    greet(to_z, plane, chip, core, True)

    last_slot = links.slot()
    links.send(last_ref, exp_in, {"narrow": lax.rem(2 * n + 1, 5)}, last_slot)

    back_slots = []

    def give_back(source, target):
        slots = [links.slot() for _ in range(NEAR)]
        for step in range(NEAR):
            links.send(
                cap_rows(source, plane[step]), cap_rows(target, chip), at_plane(plane[step]),
                slots[step],
            )
        own = links.move(cap_rows(source, chip), cap_rows(target, chip))
        links.waits.pop()
        back_slots.append((target, slots, own))

    give_back(mid_ref, ret_mid)
    give_back(ext_ref, ret_ext)

    def returned(which):
        target, slots, own = back_slots[which]
        for step in range(NEAR):
            links.land(cap_rows(target, plane[step]), at_plane(plane[step]), slots[step])
        own.wait()
        return target[...]

    expert_slots = [links.slot() for _ in range(NEAR)]
    for step in range(NEAR):
        block = pl.ds(pl.multiple_of(plane[step] * rows_each, rows_each), rows_each)
        links.send(
            moved_ref.at[block, :], expert_out.at[chip], at_plane(plane[step]), expert_slots[step]
        )
    block = pl.ds(pl.multiple_of(chip * rows_each, rows_each), rows_each)
    links.move(moved_ref.at[block, :], expert_out.at[chip])

    def to_mate(source, target):
        slot = links.slot()
        links.send(source, target.at[core], mate, slot)
        return lambda: links.land(target.at[1 - core], mate, slot)

    def parity_exchange(source, target):
        lands = []
        for c in range(4):
            cols = pl.ds(c * rows_each, rows_each)
            theirs = pl.ds(pl.multiple_of((2 * c + 1 - core) * rows_each, rows_each), rows_each)
            ours = pl.ds(pl.multiple_of((2 * c + core) * rows_each, rows_each), rows_each)
            slot = links.slot()
            links.send(source.at[:, theirs], target.at[core, :, cols], mate, slot)
            target[core, :, c * rows_each : (c + 1) * rows_each] = source[:, ours]
            lands.append((target.at[1 - core, :, cols], slot))
        return lambda: [links.land(block, mate, slot) for block, slot in lands]

    for load in first_loads:
        load.wait()
    hidden_there = parity_exchange(hidden_ref, hidden_cat)
    att_cat[core] = att_ref[...]
    att_there = to_mate(att_ref, att_cat)

    stat = jnp.concatenate([stat_ref[...], jnp.zeros((120, token_count), F32)], 0).T
    lane_at = lax.broadcasted_iota(jnp.int32, (token_count, 128), 1)
    scale_second = lax.rsqrt(stat[:, 4:5] * (1.0 / full) + NORM_EPS)
    logits = stat * scale_second
    hot_first = lane_at == cols_ref[:, 2:3].astype(jnp.int32)
    hot_second = lane_at == cols_ref[:, 3:4].astype(jnp.int32)
    logit_first = jnp.sum(jnp.where(hot_first, logits, 0.0), 1, keepdims=True)
    logit_second = jnp.sum(jnp.where(hot_second, logits, 0.0), 1, keepdims=True)
    apart = logit_first - logit_second
    share_first = 1.0 / (1.0 + jnp.exp(-apart))
    share_second = 1.0 / (1.0 + jnp.exp(apart))
    normed = middle_ref[...] * scale_second
    gain_second = tokens_ref[n, token_count + 1 : token_count + 2, :].astype(F32)
    hidden_second = (normed * gain_second).astype(BF)
    for load in loads:
        load.wait()
    router = qkvw[pl.ds(2 * n, 2), :, 1536:1664].reshape(part_width, 128)

    rows_mid = returned(0)
    rows_ext = returned(1)
    ext_first = cols_cols(picks_ref[0], rows_ext)
    ext_second = cols_cols(picks_ref[1], rows_ext)
    ext_both = ext_first + ext_second
    grad_share = ext_first[:, 0:1] + ext_first[:, 1:2] - ext_second[:, 0:1] - ext_second[:, 1:2]
    delta = (grad_share * share_first * share_second).astype(BF).astype(F32)
    grad_logits = jnp.where(hot_first, delta, jnp.where(hot_second, -delta, 0.0)).astype(BF)
    stat_total = ext_both[:, 2:3] + ext_both[:, 3:4] + delta * apart
    grad_hidden = cols_cols(picks_ref[0] + picks_ref[1], rows_mid) + rows_rows(grad_logits, router)
    grad_middle = cot_ref[...].astype(F32) + scale_second * (
        gain_second * grad_hidden - normed * (stat_total * (1.0 / full))
    )
    own_cols = pl.ds(pl.multiple_of(n * part_width, part_width), part_width)
    branch[:, own_cols] = grad_middle.astype(BF)
    branch_slots = [links.slot() for _ in range(NEAR)]
    for step in range(NEAR):
        links.send(
            branch.at[:, own_cols], branch.at[:, own_cols], {"narrow": to_z[step]},
            branch_slots[step],
        )

    links.land(exp_in, {"narrow": lax.rem(n + 1, 4)}, last_slot)
    exp_sum[...] = (exp_ref[...].astype(F32) + exp_in[...].astype(F32)).astype(BF)
    give_back(exp_sum, ret_exp)

    router_part = cols_cols(grad_logits, hidden_second)[0:8, :]
    gain_part = jnp.sum(grad_hidden * normed, 0, keepdims=True)
    kind_at = lax.broadcasted_iota(jnp.int32, (8, part_width), 0)
    small = jnp.where(kind_at == 4, gain_part, router_part)
    small_mate[core] = small
    small_there = to_mate(small_mate.at[core], small_mate)

    small_there()
    small = small_mate[0] + small_mate[1]
    small_sum[...] = small
    small_slots = [links.slot() for _ in range(NEAR)]
    for step in range(NEAR):
        links.send(small_sum, small_recv.at[step], at_plane(plane[step]), small_slots[step])

    for step in range(NEAR):
        cols = pl.ds(pl.multiple_of(from_z[step] * part_width, part_width), part_width)
        links.land(branch.at[:, cols], {"narrow": from_z[step]}, branch_slots[step])
    branch_there = parity_exchange(branch, branch_cat)
    grad_att = low_dot(branch[...], outw[...].reshape(full, part_width)).astype(BF)

    proj_sums = {
        part: PlaneSum(
            links, core, chip, plane, part % 2, proj_send.at[part], proj_recv.at[part]
        )
        for part in (3, 0, 1, 2)
    }

    branch_there()
    att_there()
    proj_send[3] = cols_cols(
        branch_cat[...].reshape(2 * token_count, half), att_cat[...].reshape(2 * token_count, part_width)
    ).astype(BF)
    proj_sums[3].start()
    score_scale = HEAD_DIM ** (-0.5)
    grad_att_at[...] = grad_att

    def one_head(head, stat_first):
        def lanes(start):
            return pl.ds(pl.multiple_of(start + head * HEAD_DIM, HEAD_DIM), HEAD_DIM)

        query, key, value = (qkv_ref[i, :, lanes(0)] for i in range(3))
        grad_out = grad_att_at[:, lanes(0)]
        weights = prob_ref[head]
        grad_weights = rows_rows(grad_out, value)
        inner = jnp.sum(weights * grad_weights, 1, keepdims=True)
        grad_scores = (weights * (grad_weights - inner)).astype(BF)
        grad_query = low_dot(grad_scores, key) * score_scale
        grad_key = cols_cols(grad_scores, query) * score_scale
        grad_value = cols_cols(weights.astype(BF), grad_out)
        products = (
            grad_query * query.astype(F32)
            + grad_key * key.astype(F32)
            + grad_value * value.astype(F32)
        )
        for part, grad in ((0, grad_query), (1, grad_key)):
            turned = grad * rope_ref[0] - pltpu.roll(grad, HEAD_DIM // 2, 1) * rope_ref[1]
            proj_cat[core, :, lanes(part * part_width)] = turned.astype(BF)
        proj_cat[core, :, lanes(2 * part_width)] = grad_value.astype(BF)
        return stat_first + jnp.sum(products, 1, keepdims=True)

    stat_first = lax.fori_loop(0, heads, one_head, jnp.zeros((token_count, 1), F32))
    proj_there = to_mate(proj_cat.at[core], proj_cat)
    high = stat_first.astype(BF)
    rest = (stat_first - high.astype(F32)).astype(BF)
    col_send[...] = jnp.where(
        lane_at == 0, high.astype(F32), jnp.where(lane_at == 1, rest.astype(F32), 0.0)
    ).astype(BF)
    col_slots = [links.slot() for _ in range(NEAR)]
    for step in range(NEAR):
        links.send(col_send, col_recv.at[step], {"narrow": to_z[step]}, col_slots[step])
    grads = proj_cat[core]

    def first_block(m):
        weight = qkvw[pl.ds(2 * m, 2), :, 0:1536].reshape(part_width, 1536)
        return rows_rows(grads, weight)

    def fill_first(step, value):
        first_send[step] = first_block(lax.rem(n + 1 + step, 4)).astype(BF)
        return value

    lax.fori_loop(0, NEAR, fill_first, 0)
    first_slots = [links.slot() for _ in range(NEAR)]
    for step in range(NEAR):
        links.send(
            first_send.at[step], first_recv.at[step], {"narrow": to_z[step]}, first_slots[step]
        )

    hidden_there()
    proj_there()
    hidden_rows = hidden_cat[...].reshape(2 * token_count, half)
    proj_sums[3].turn()
    for part in range(3):
        cols = slice(part * 512, (part + 1) * 512)
        proj_send[part] = cols_cols(
            hidden_rows, proj_cat[:, :, cols].reshape(2 * token_count, part_width)
        ).astype(BF)
        proj_sums[part].start()

    rows_exp = returned(2)
    output_out[...] = (
        middle_ref[...]
        + share_first * cols_cols(picks_ref[0], rows_exp)
        + share_second * cols_cols(picks_ref[1], rows_exp)
    ).astype(BF)

    grad_first = first_block(n)
    stat_first = high.astype(F32) + rest.astype(F32)
    total = jnp.zeros((token_count, 1), F32)
    for m in range(4):
        part = tokens_ref[m, 0:token_count, :].astype(F32)
        total = total + jnp.sum(part * part, 1, keepdims=True)
    scale_first = lax.rsqrt(total * (1.0 / full) + NORM_EPS)
    normed_first = tok_ref[...].astype(F32) * scale_first
    gain_first = tokens_ref[n, token_count : token_count + 1, :].astype(F32)
    for step in range(NEAR):
        links.land(col_recv.at[step], {"narrow": from_z[step]}, col_slots[step])
        stat_first = stat_first + (
            col_recv[step, :, 0:1].astype(F32) + col_recv[step, :, 1:2].astype(F32)
        )
    for step in range(NEAR):
        links.land(first_recv.at[step], {"narrow": from_z[step]}, first_slots[step])
        grad_first = grad_first + first_recv[step].astype(F32)
    grad_tokens_out[...] = grad_middle + scale_first * (
        gain_first * grad_first - normed_first * (stat_first * (1.0 / full))
    )
    gain_part = jnp.sum(grad_first * normed_first, 0, keepdims=True)
    for part in range(3):
        proj_sums[part].turn()
    last_mate[core] = jnp.broadcast_to(gain_part, (8, part_width))
    last_there = to_mate(last_mate.at[core], last_mate)

    for step in range(NEAR):
        links.land(small_recv.at[step], at_plane(plane[step]), small_slots[step])
        small = small + small_recv[step]
    last_there()
    last = last_mate[0] + last_mate[1]
    last_sum[...] = last
    last_slots = [links.slot() for _ in range(NEAR)]
    for step in range(NEAR):
        links.send(last_sum, last_recv.at[step], at_plane(plane[step]), last_slots[step])
    router_all[:, own_cols] = small
    router_slots = [links.slot() for _ in range(NEAR)]
    for step in range(NEAR):
        links.send(
            router_all.at[:, own_cols], router_all.at[:, own_cols], {"narrow": to_z[step]},
            router_slots[step],
        )
    for step in range(NEAR):
        links.land(last_recv.at[step], at_plane(plane[step]), last_slots[step])
        last = last + last_recv[step]
    small_out[...] = jnp.where(kind_at == 5, last, small)
    for step in range(NEAR):
        cols = pl.ds(pl.multiple_of(from_z[step] * part_width, part_width), part_width)
        links.land(router_all.at[:, cols], {"narrow": from_z[step]}, router_slots[step])

    router_out[...] = router_all[:, pl.ds(pl.multiple_of(w * rows_each, rows_each), rows_each)]
    for part in range(4):
        summed_out[:, part * part_width : (part + 1) * part_width] = proj_sums[part].total()
    for step in range(NEAR):
        links.land(expert_out.at[plane[step]], at_plane(plane[step]), expert_slots[step])
    links.finish()


def tail_call(*args):
    slots, part_width = args[0].shape
    half, hidden_width = args[4].shape
    token_count = args[10].shape[0]
    full, rows_each = 2 * half, half // 4
    vmem = pl.BlockSpec(memory_space=pltpu.VMEM)
    hbm = pl.BlockSpec(memory_space=pl.ANY)

    def arr(shape, dtype):
        return jax.ShapeDtypeStruct(shape, dtype)

    own = (token_count, part_width)
    return pl.pallas_call(
        tail_body,
        out_shape=(
            arr(own, BF),
            arr(own, F32),
            arr((rows_each, full), F32),
            arr((8, part_width), F32),
            arr((8, rows_each), F32),
            arr((4, rows_each, hidden_width), BF),
        ),
        in_specs=[vmem] * 4 + [hbm] * 2 + [vmem] * 5 + [hbm] * 3 + [vmem] * 2 + [hbm] * 3,
        out_specs=(vmem,) * 5 + (hbm,),
        scratch_shapes=[
            pltpu.VMEM((2, slots, token_count), BF),
            pltpu.VMEM((4, token_count + 16, part_width), BF),
            pltpu.VMEM((3,) + own, BF),
            pltpu.VMEM((part_width // HEAD_DIM, token_count, token_count), F32),
            pltpu.VMEM((token_count, full), BF),
            pltpu.VMEM(own, BF),
            pltpu.VMEM((slots, part_width), BF),
            pltpu.VMEM((slots, part_width), BF),
            pltpu.VMEM((8, full), F32),
            pltpu.VMEM((8, rows_each, 1664), BF),
            pltpu.VMEM((8, rows_each, part_width), BF),
            pltpu.VMEM((slots, part_width), BF),
            pltpu.VMEM((slots, part_width), BF),
            pltpu.VMEM((slots, 128), BF),
            pltpu.VMEM((token_count, full), BF),
            pltpu.VMEM((2, token_count, half), BF),
            pltpu.VMEM((2, token_count, half), BF),
            pltpu.VMEM((2, token_count, part_width), BF),
            pltpu.VMEM((2, token_count, 1536), BF),
            pltpu.VMEM((4, half, part_width), BF),
            pltpu.VMEM((4, NEAR, rows_each, part_width), BF),
            pltpu.VMEM((NEAR,) + own, BF),
            pltpu.VMEM((NEAR,) + own, BF),
            pltpu.VMEM((token_count, 128), BF),
            pltpu.VMEM((NEAR, token_count, 128), BF),
            pltpu.VMEM((2, 8, part_width), F32),
            pltpu.VMEM((8, part_width), F32),
            pltpu.VMEM((NEAR, 8, part_width), F32),
            pltpu.VMEM((2, 8, part_width), F32),
            pltpu.VMEM((8, part_width), F32),
            pltpu.VMEM((NEAR, 8, part_width), F32),
            pltpu.SemaphoreType.DMA((TAIL_SLOTS,)),
            pltpu.SemaphoreType.DMA((TAIL_SLOTS,)),
            pltpu.SemaphoreType.DMA((24,)),
        ],
        compiler_params=pltpu.CompilerParams(
            collective_id=2, has_side_effects=True, vmem_limit_bytes=60 * 1024 * 1024
        ),
        cost_estimate=pl.CostEstimate(
            flops=6_000_000_000, bytes_accessed=60_000_000, transcendentals=1_000
        ),
        name="tail",
    )(*args)


FINISH_ROWS = 64


def finish_body(
    early_ref, late_ref, output_ref, tokens_ref, summed_ref, small_ref, router_ref,
    gate_out, up_out, down_out, output_out, tokens_out, q_out, k_out, v_out, o_out,
    gain_first_out, gain_second_out, router_out,
    packed, spread, incoming, outgoing, passing,
):
    rows_each = packed.shape[2]
    width = tokens_ref.shape[1]
    sources = (early_ref.at[0], early_ref.at[1], late_ref)
    targets = (down_out, gate_out, up_out)
    loads = {}
    for kind in range(3):
        for part in range(rows_each // FINISH_ROWS):
            rows = pl.ds(part * FINISH_ROWS, FINISH_ROWS)
            loads[kind, part] = pltpu.make_async_copy(
                sources[kind].at[:, rows, :], packed.at[kind, :, rows, :], incoming.at[kind, part]
            )
            loads[kind, part].start()
    whole = [(output_ref, output_out), (tokens_ref, tokens_out)]
    for part, target in enumerate((q_out, k_out, v_out, o_out)):
        whole.append((summed_ref.at[:, pl.ds(part * width, width)], target))
    copies = [
        pltpu.make_async_copy(source, target, passing.at[index])
        for index, (source, target) in enumerate(whole)
    ]
    stores = []
    for (kind, part), load in loads.items():
        load.wait()

        def some_rows(index, value):
            first = pl.multiple_of(part * FINISH_ROWS + index * 16, 16)
            rows = pl.ds(first, 16)
            for expert in range(EXPERTS):
                spread[kind, rows, expert, :] = packed[kind, expert, rows, :].astype(F32)
            return value

        lax.fori_loop(0, FINISH_ROWS // 16, some_rows, 0)
        rows = pl.ds(part * FINISH_ROWS, FINISH_ROWS)
        stores.append(
            pltpu.make_async_copy(
                spread.at[kind, rows], targets[kind].at[rows], outgoing.at[kind, part]
            )
        )
        stores[-1].start()
        if kind == 0 and part == 0:
            for copy in copies:
                copy.start()
    for row, target in ((5, gain_first_out), (4, gain_second_out)):
        for index in range(width // 128):
            target[index : index + 1, :] = small_ref[
                row : row + 1, index * 128 : (index + 1) * 128
            ]
    router_out[...] = router_ref[0:EXPERTS, :]
    for copy in stores + copies:
        copy.wait()


def finish_call(early, late, output, grad_tokens, summed, small, router):
    _, rows_each, hidden_width = late.shape
    part_width = output.shape[1]
    vmem = pl.BlockSpec(memory_space=pltpu.VMEM)
    hbm = pl.BlockSpec(memory_space=pl.ANY)
    parts = rows_each // FINISH_ROWS

    def arr(shape, dtype):
        return jax.ShapeDtypeStruct(shape, dtype)

    return pl.pallas_call(
        finish_body,
        out_shape=(arr((rows_each, EXPERTS, hidden_width), F32),) * 3
        + (arr(output.shape, BF), arr(output.shape, F32))
        + (arr((rows_each, part_width), F32),) * 4
        + (arr((part_width // 128, 128), F32),) * 2
        + (arr((EXPERTS, rows_each), F32),),
        in_specs=[hbm] * 2 + [vmem] * 5,
        out_specs=(hbm,) * 9 + (vmem,) * 3,
        scratch_shapes=[
            pltpu.VMEM((3, EXPERTS, rows_each, hidden_width), BF),
            pltpu.VMEM((3, rows_each, EXPERTS, hidden_width), F32),
            pltpu.SemaphoreType.DMA((3, parts)),
            pltpu.SemaphoreType.DMA((3, parts)),
            pltpu.SemaphoreType.DMA((6,)),
        ],
        compiler_params=pltpu.CompilerParams(vmem_limit_bytes=56 * 1024 * 1024),
        name="finish",
    )(early, late, output, grad_tokens, summed, small, router)


def plain_device(
    tokens, gain_attn, w_query, w_key, w_value, w_out, gain_ffn, w_router,
    w_gate, w_up, w_down, segment, parents, expert_ids, slot_order, cotangent,
):
    narrow_count = lax.axis_size("narrow")
    wide_count = lax.axis_size("wide")
    narrow_at = lax.axis_index("narrow")
    token_count, part_width = tokens.shape
    full_width = part_width * narrow_count
    hidden_width = w_gate.shape[2]
    rows_each = w_gate.shape[0]
    blocks = wide_count // 8
    quads = [
        [8 * block + 2 * chip + core for chip in range(4)]
        for block in range(blocks)
        for core in range(2)
    ]
    mates = [
        [8 * block + 2 * chip + core for block in range(blocks) for core in range(2)]
        for chip in range(4)
    ]

    def quad_swap(array):
        return lax.all_to_all(array, "wide", 0, 0, axis_index_groups=quads, tiled=True)

    def own_rows(weight):
        moved = quad_swap(jnp.transpose(weight, (1, 0, 2)))
        joined = lax.all_gather(moved, "wide", axis=0, axis_index_groups=mates, tiled=True)
        joined = joined.reshape(blocks, 2, 4, rows_each, hidden_width).transpose(0, 2, 1, 3, 4)
        return joined.reshape(full_width, hidden_width)

    def share_rows(grad):
        parts = grad.astype(BF).reshape(blocks, 4, 2, rows_each, hidden_width)
        parts = parts.transpose(0, 2, 1, 3, 4).reshape(blocks * 2, 4, rows_each, hidden_width)
        summed = lax.psum_scatter(
            parts, "wide", scatter_dimension=0, axis_index_groups=mates, tiled=True
        )[0]
        return jnp.transpose(quad_swap(summed), (1, 0, 2)).astype(F32)

    def head_cols(array, head):
        return array[:, head * HEAD_DIM : (head + 1) * HEAD_DIM]

    heads = part_width // HEAD_DIM
    half_dim = HEAD_DIM // 2
    freqs = ROPE_BASE ** (-2.0 * jnp.arange(half_dim, dtype=F32) / HEAD_DIM)
    score_scale = HEAD_DIM ** (-0.5)
    gains = jnp.stack([gain_attn, gain_ffn])
    gain_first_loc = gain_attn.astype(F32)
    gain_second_loc = gain_ffn.astype(F32)
    hot_first, hot_second, kept, pick_first, pick_second = route(expert_ids, slot_order[0])

    gate_w, up_w, down_w = own_rows(w_gate), own_rows(w_up), own_rows(w_down)
    attn_w = lax.all_gather(
        jnp.stack([w_query, w_key, w_value, w_out], 1), "wide", axis=0, tiled=True
    )
    query_w, key_w, value_w, out_w = (attn_w[:, i] for i in range(4))
    router_w = lax.all_gather(w_router, "wide", axis=0, tiled=True)
    tokens_full = lax.all_gather(tokens, "narrow", axis=1, tiled=True)
    grad_full = lax.all_gather(cotangent, "narrow", axis=1, tiled=True)
    gains_full = lax.all_gather(gains, "narrow", axis=1, tiled=True)
    gain_first = gains_full[0].astype(F32)
    gain_second = gains_full[1].astype(F32)

    seen, places = tree_layout(segment[0], parents[0])
    pick_first_low = pick_first.astype(BF)
    pick_second_low = pick_second.astype(BF)
    pick_both_low = (pick_first | pick_second).astype(BF)

    inputs_full = tokens_full.astype(F32)
    scale_first = lax.rsqrt(jnp.mean(inputs_full * inputs_full, -1, keepdims=True) + NORM_EPS)
    normed_first = inputs_full * scale_first
    hidden_first = (normed_first * gain_first).astype(BF)
    angles = places[:, None] * freqs[None, :]
    cosines, sines = jnp.cos(angles), jnp.sin(angles)
    query_raw = rows_cols(hidden_first, query_w)
    key_raw = rows_cols(hidden_first, key_w)
    value_low = rows_cols(hidden_first, value_w).astype(BF)

    saved = []
    outs = []
    for head in range(heads):
        query = rotate(head_cols(query_raw, head), cosines, sines).astype(BF)
        key = rotate(head_cols(key_raw, head), cosines, sines).astype(BF)
        value = head_cols(value_low, head)
        scores = jnp.where(seen, rows_rows(query, key) * score_scale, NEG_FILL)
        exps = jnp.exp(scores - jnp.max(scores, -1, keepdims=True))
        weights = exps / jnp.sum(exps, -1, keepdims=True)
        saved.append((query, key, value, weights))
        outs.append(rows_cols(weights.astype(BF), value).astype(BF))
    attended = jnp.concatenate(outs, 1)
    branch_part = rows_rows(attended, out_w).astype(BF)
    branch_loc = lax.psum_scatter(
        branch_part, "narrow", scatter_dimension=1, tiled=True
    ).astype(F32)
    middle = tokens.astype(F32) + branch_loc
    middle_full = lax.all_gather(middle.astype(BF), "narrow", axis=1, tiled=True).astype(F32)
    scale_second = lax.rsqrt(jnp.mean(middle_full * middle_full, -1, keepdims=True) + NORM_EPS)
    normed_second = middle_full * scale_second
    hidden_second = (normed_second * gain_second).astype(BF)
    logits = rows_cols(hidden_second, router_w)
    share_first, share_second = gate_pair(logits, hot_first, hot_second)
    weight_first = kept[:, 0] * share_first
    weight_second = kept[:, 1] * share_second

    slot_weight = jnp.sum(
        pick_first * weight_first[:, None] + pick_second * weight_second[:, None], 0
    )
    weight_high, weight_low = two_parts(slot_weight)
    pads = jnp.stack([weight_high, weight_low], 1)
    pads = jnp.pad(pads, ((0, 0), (0, 126)))
    sent_hidden = cols_cols(pick_both_low, hidden_second).astype(BF)
    sent_grad = cols_cols(pick_both_low, grad_full).astype(BF)
    sent = jnp.concatenate([sent_hidden, sent_grad, pads], 1)
    got = quad_swap(sent.reshape(EXPERTS, CAP, -1)).reshape(SLOTS, -1)
    slot_hidden = got[:, :full_width]
    slot_grad = got[:, full_width : 2 * full_width]
    slot_gate = got[:, 2 * full_width : 2 * full_width + 2].astype(F32)
    slot_gate = slot_gate[:, 0:1] + slot_gate[:, 1:2]

    gate_pre = rows_cols(slot_hidden, gate_w)
    up_pre = rows_cols(slot_hidden, up_w)
    sigmoid_gate = jax.nn.sigmoid(gate_pre)
    silu_gate = gate_pre * sigmoid_gate
    activated = (silu_gate * up_pre).astype(BF)
    expert_part = rows_rows(activated, down_w)
    act_raw = rows_cols(slot_grad, down_w)
    share_part = jnp.sum(act_raw * activated.astype(F32), 1, keepdims=True)
    grad_act = act_raw * slot_gate
    grad_gate_pre = (
        grad_act * up_pre * sigmoid_gate * (1.0 + gate_pre * (1.0 - sigmoid_gate))
    ).astype(BF)
    grad_up_pre = (grad_act * silu_gate).astype(BF)
    grad_slot = rows_rows(grad_gate_pre, gate_w) + rows_rows(grad_up_pre, up_w)
    stat_part = jnp.sum(slot_hidden.astype(F32) * grad_slot, 1, keepdims=True)
    extras = jnp.concatenate([*two_parts(share_part), *two_parts(stat_part)], 1)
    extras = jnp.pad(extras, ((0, 0), (0, 124)))
    back_parts = []
    expert_plain = expert_part.astype(BF)
    slot_plain = grad_slot.astype(BF)
    for part in range(narrow_count):
        cols = slice(part * part_width, (part + 1) * part_width)
        back_parts += [expert_plain[:, cols], slot_plain[:, cols], extras]
    back = lax.psum_scatter(
        jnp.concatenate(back_parts, 1), "narrow", scatter_dimension=1, tiled=True
    )
    back = quad_swap(back.reshape(EXPERTS, CAP, -1)).reshape(SLOTS, -1)
    picked_first = rows_cols(pick_first_low, back)
    picked_second = rows_cols(pick_second_low, back)
    output = (
        middle
        + weight_first[:, None] * picked_first[:, :part_width]
        + weight_second[:, None] * picked_second[:, :part_width]
    ).astype(BF)

    grad_weight = (slot_grad.astype(F32) * slot_gate).astype(BF)
    gate_out = share_rows(cols_cols(slot_hidden, grad_gate_pre))
    up_out = share_rows(cols_cols(slot_hidden, grad_up_pre))
    down_out = share_rows(cols_cols(grad_weight, activated))

    tail = 2 * part_width
    share_first_grad = picked_first[:, tail] + picked_first[:, tail + 1]
    share_second_grad = picked_second[:, tail] + picked_second[:, tail + 1]
    both = picked_first + picked_second
    stat_second = both[:, tail + 2] + both[:, tail + 3]
    grad_hidden_loc = both[:, part_width:tail]
    grad_local = cotangent.astype(F32)
    _, pull_gates = jax.vjp(lambda given: gate_pair(given, hot_first, hot_second), logits)
    (grad_logits,) = pull_gates((kept[:, 0] * share_first_grad, kept[:, 1] * share_second_grad))
    grad_logits_low = grad_logits.astype(BF)
    grad_router_rows = rows_rows(grad_logits_low, router_w)
    stat_total = stat_second + jnp.sum(normed_second * gain_second * grad_router_rows, 1)

    def take_cols(full_rows):
        return lax.dynamic_slice_in_dim(full_rows, narrow_at * part_width, part_width, 1)

    grad_hidden_loc = grad_hidden_loc + take_cols(grad_router_rows)
    normed_second_loc = take_cols(normed_second)
    grad_gain_second = jnp.sum(grad_hidden_loc * normed_second_loc, 0)
    grad_middle = grad_local + scale_second * (
        gain_second_loc * grad_hidden_loc - normed_second_loc * stat_total[:, None] / full_width
    )
    grad_router_w = cols_cols(hidden_second, grad_logits_low)
    grad_branch = lax.all_gather(grad_middle.astype(BF), "narrow", axis=1, tiled=True)
    grad_attended = rows_cols(grad_branch, out_w).astype(BF)
    grad_out_w = cols_cols(grad_branch, attended)
    grad_qs, grad_ks, grad_vs = [], [], []
    for head in range(heads):
        query, key, value, weights = saved[head]
        grad_out = head_cols(grad_attended, head)
        grad_weights = rows_rows(grad_out, value)
        inner = jnp.sum(weights * grad_weights, -1, keepdims=True)
        grad_scores = (weights * (grad_weights - inner)).astype(BF)
        grad_q = rows_cols(grad_scores, key) * score_scale
        grad_k = cols_cols(grad_scores, query) * score_scale
        grad_qs.append(rotate(grad_q, cosines, -sines).astype(BF))
        grad_ks.append(rotate(grad_k, cosines, -sines).astype(BF))
        grad_vs.append(cols_cols(weights.astype(BF), grad_out).astype(BF))
    grad_query_raw = jnp.concatenate(grad_qs, 1)
    grad_key_raw = jnp.concatenate(grad_ks, 1)
    grad_value_raw = jnp.concatenate(grad_vs, 1)
    grad_hidden_first = (
        rows_rows(grad_query_raw, query_w)
        + rows_rows(grad_key_raw, key_w)
        + rows_rows(grad_value_raw, value_w)
    )
    stat_first = jnp.sum(normed_first * gain_first * grad_hidden_first, 1, keepdims=True)
    extras = jnp.pad(jnp.concatenate(two_parts(stat_first), 1), ((0, 0), (0, 126)))
    grad_hidden_low = grad_hidden_first.astype(BF)
    first_parts = []
    for part in range(narrow_count):
        first_parts += [grad_hidden_low[:, part * part_width : (part + 1) * part_width], extras]
    first_back = lax.psum_scatter(
        jnp.concatenate(first_parts, 1), "narrow", scatter_dimension=1, tiled=True
    ).astype(F32)
    grad_first_loc = first_back[:, :part_width]
    stat_first = first_back[:, part_width : part_width + 1]
    stat_first = stat_first + first_back[:, part_width + 1 : part_width + 2]
    normed_first_loc = take_cols(normed_first)
    grad_gain_first = jnp.sum(grad_first_loc * normed_first_loc, 0)
    grad_tokens = grad_middle + scale_first * (
        gain_first_loc * grad_first_loc - normed_first_loc * stat_first / full_width
    )
    grad_attn_w = jnp.concatenate(
        [
            cols_cols(hidden_first, grad_query_raw).astype(BF),
            cols_cols(hidden_first, grad_key_raw).astype(BF),
            cols_cols(hidden_first, grad_value_raw).astype(BF),
            grad_out_w.astype(BF),
        ],
        1,
    )
    attn_summed = lax.psum_scatter(
        grad_attn_w, "wide", scatter_dimension=0, tiled=True
    ).astype(F32)
    router_summed = lax.psum_scatter(grad_router_w, "wide", scatter_dimension=0, tiled=True)
    gains_summed = lax.psum(jnp.stack([grad_gain_first, grad_gain_second]), "wide")
    return (
        output,
        grad_tokens,
        gains_summed[0],
        attn_summed[:, :part_width],
        attn_summed[:, part_width : 2 * part_width],
        attn_summed[:, 2 * part_width : 3 * part_width],
        attn_summed[:, 3 * part_width :],
        gains_summed[1],
        router_summed,
        gate_out,
        up_out,
        down_out,
    )


def per_device(
    tokens, gain_attn, w_query, w_key, w_value, w_out, gain_ffn, w_router,
    w_gate, w_up, w_down, segment, parents, expert_ids, slot_order, cotangent,
):
    if lax.axis_size("wide") != 8 or lax.axis_size("narrow") != 4:
        return plain_device(
            tokens, gain_attn, w_query, w_key, w_value, w_out, gain_ffn, w_router,
            w_gate, w_up, w_down, segment, parents, expert_ids, slot_order, cotangent,
        )
    (
        in_w, out_w, expert_w, slot_mid, slot_grad, slot_gate, middle, hidden_first,
        token_parts, qkv, probs, attended, stat, rope, picks, columns,
    ) = front_call(
        tokens, cotangent, gain_attn, gain_ffn, (w_query, w_key, w_value, w_out),
        w_router.T, (w_gate, w_up, w_down), segment, parents, expert_ids.T, slot_order,
    )
    back_mid, back_exp, last_exp, back_ext, grads, early_experts = mid_call(
        slot_mid, slot_grad, slot_gate, token_parts, expert_w
    )
    (
        output, grad_tokens, summed, small, router, experts,
    ) = tail_call(
        back_mid, back_exp, last_exp, back_ext, grads, picks, stat, columns, middle, cotangent, tokens,
        token_parts, qkv, probs, attended, rope, hidden_first, in_w, out_w,
    )
    (
        gate_out, up_out, down_out, output, grad_tokens, grad_q, grad_k, grad_v, grad_o,
        grad_gain_first, grad_gain_second, router,
    ) = finish_call(early_experts, experts, output, grad_tokens, summed, small, router)
    return (
        output, grad_tokens, grad_gain_first.reshape(-1), grad_q, grad_k, grad_v, grad_o,
        grad_gain_second.reshape(-1), router.T, gate_out, up_out, down_out,
    )


def solution(mesh):
    pair = P("wide", "narrow")
    part = P("narrow")
    rows = P("wide", None)
    cube = P("wide", None, "narrow")
    return jax.shard_map(
        per_device,
        mesh=mesh,
        in_specs=(
            pair, part, pair, pair, pair, pair, part, rows, cube, cube, cube,
            rows, rows, rows, rows, pair,
        ),
        out_specs=(
            pair, pair, part, pair, pair, pair, pair, part, rows, cube, cube, cube,
        ),
        check_vma=False,
    )
```

```python
import math

import jax
import jax.numpy as jnp
from jax import lax
from jax.experimental import pallas as pl
from jax.experimental.pallas import tpu as pltpu
from jax.sharding import PartitionSpec as P

HEAD_DIM = 128
EXPERTS = 4
SEGS = 13
CAP = 144
SLOTS = EXPERTS * CAP
NORM_EPS = 1e-05
NEG_FILL = -1e30
ROPE_BASE = 10000.0
BF = jnp.bfloat16
F32 = jnp.float32


def mm(left, right, dims):
    return lax.dot_general(left, right, (dims, ((), ())), preferred_element_type=F32)


def rows_cols(left, right):
    return mm(left, right, ((1,), (0,)))


def rows_rows(left, right):
    return mm(left, right, ((1,), (1,)))


def cols_cols(left, right):
    return mm(left, right, ((0,), (0,)))


def tree_layout(segment_row, parent_row):
    seg_ids = jnp.arange(SEGS, dtype=jnp.int32)
    member = segment_row[:, None] == seg_ids[None, :]
    parent_of = (parent_row[:, None] == seg_ids[None, :]) & (seg_ids[:, None] != 0)
    itself = seg_ids[:, None] == seg_ids[None, :]
    reach = itself
    for _ in range(3):
        reach = itself | jnp.any(parent_of[:, :, None] & reach[None, :, :], axis=1)
    counts = member.astype(jnp.int32)
    lengths = jnp.sum(counts, 0)
    starts = jnp.sum(jnp.where(seg_ids[None, :] < seg_ids[:, None], lengths[None, :], 0), 1)
    before = jnp.sum(jnp.where(reach, lengths[None, :], 0), 1) - lengths
    row_at = jnp.arange(segment_row.shape[0], dtype=jnp.int32)
    places = jnp.sum(counts * (before - starts)[None, :], 1) + row_at
    member_low = member.astype(BF)
    lineage = rows_cols(member_low, reach.astype(BF)).astype(BF)
    shared = rows_rows(lineage, member_low) > 0.5
    seen = shared & (row_at[None, :] <= row_at[:, None])
    return seen, places.astype(F32)


def route(expert_row, slot_rank):
    expert_range = jnp.arange(EXPERTS, dtype=jnp.int32)
    hot_first = (expert_row[:, 0:1] == expert_range[None, :]).astype(F32)
    hot_second = (expert_row[:, 1:2] == expert_range[None, :]).astype(F32)
    earlier = (slot_rank[None, :] < slot_rank[:, None]).astype(BF)
    count_first = rows_cols(earlier, hot_first.astype(BF))
    count_second = rows_cols(earlier, hot_second.astype(BF))
    ahead_first = jnp.sum(count_first * hot_first, 1)
    ahead_second = jnp.sum((count_second + jnp.sum(hot_first, 0)[None, :]) * hot_second, 1)
    slot_index = jnp.stack([ahead_first, ahead_second], 1).astype(jnp.int32)
    kept = slot_index < CAP
    flat_slot = jnp.where(kept, expert_row * CAP + slot_index, SLOTS)
    slot_range = jnp.arange(SLOTS, dtype=jnp.int32)
    pick_first = flat_slot[:, 0:1] == slot_range[None, :]
    pick_second = flat_slot[:, 1:2] == slot_range[None, :]
    return hot_first, hot_second, kept.astype(F32), pick_first, pick_second


def rotate(vectors, cosines, sines):
    half_dim = HEAD_DIM // 2
    first_half = vectors[..., :half_dim]
    second_half = vectors[..., half_dim:]
    return jnp.concatenate(
        [
            first_half * cosines - second_half * sines,
            second_half * cosines + first_half * sines,
        ],
        -1,
    )


def gate_pair(logits, hot_first, hot_second):
    chances = jax.nn.softmax(logits, axis=-1)
    first_share = jnp.sum(chances * hot_first, 1)
    second_share = jnp.sum(chances * hot_second, 1)
    pair_total = first_share + second_share
    return (first_share / pair_total, second_share / pair_total)


def two_parts(column):
    high = column.astype(BF)
    return high, (column - high.astype(F32)).astype(BF)


MESH = pl.DeviceIdType.MESH
NEAR = 3


def low_dot(left, right):
    return jnp.dot(left, right, preferred_element_type=F32)


def places_of(n):
    return [lax.rem(n + step, 4) for step in (1, 2, 3)], [lax.rem(n + 4 - step, 4) for step in (1, 2, 3)]


def plane_of(chip):
    x, y = lax.rem(chip, 2), chip // 2
    return [2 * y + 1 - x, 2 * (1 - y) + x, 2 * (1 - y) + 1 - x]


def greet(narrow_peers, plane_peers, chip, core, mate):
    barrier = pltpu.get_barrier_semaphore()
    count = 0
    for peer in narrow_peers:
        pl.semaphore_signal(barrier, inc=1, device_id={"narrow": peer}, device_id_type=MESH)
        count += 1
    for peer in plane_peers:
        pl.semaphore_signal(
            barrier, inc=1, device_id={"wide": 2 * peer + core}, device_id_type=MESH
        )
        count += 1
    if mate:
        pl.semaphore_signal(
            barrier, inc=1, device_id={"wide": 2 * chip + 1 - core}, device_id_type=MESH
        )
        count += 1
    pl.semaphore_wait(barrier, count)


class Links:
    def __init__(self, sent, landed, local):
        self.sent, self.landed, self.local = sent, landed, local
        self.used, self.local_used = 0, 0
        self.waits = []

    def slot(self):
        self.used += 1
        return self.used - 1

    def send(self, source, target, device, slot, when=None):
        copy = pltpu.make_async_remote_copy(
            src_ref=source,
            dst_ref=target,
            send_sem=self.sent.at[slot],
            recv_sem=self.landed.at[slot],
            device_id=device,
            device_id_type=MESH,
        )
        if when is None:
            copy.start()
        else:
            pl.when(when)(copy.start)
        self.waits.append((copy, when))

    def land(self, target, device, slot, when=None):
        copy = pltpu.make_async_remote_copy(
            src_ref=target,
            dst_ref=target,
            send_sem=self.sent.at[slot],
            recv_sem=self.landed.at[slot],
            device_id=device,
            device_id_type=MESH,
        )
        if when is None:
            copy.wait_recv()
        else:
            pl.when(when)(copy.wait_recv)

    def move(self, source, target):
        copy = pltpu.make_async_copy(source, target, self.local.at[self.local_used])
        self.local_used += 1
        copy.start()
        self.waits.append((copy, "local"))
        return copy

    def finish(self):
        for copy, when in self.waits:
            if when == "local":
                copy.wait()
            elif when is None:
                copy.wait_send()
            else:
                pl.when(when)(copy.wait_send)


class Chain:
    def __init__(self, links, n, block):
        self.links, self.n, self.block = links, n, block
        self.slots = [(links.slot(), links.slot()) for _ in range(3)]

    def start(self, step):
        n, links = self.n, self.links
        right, left = self.slots[step]
        block = self.block(lax.rem(n + 4 - step, 4))
        links.send(
            block, block, {"narrow": lax.rem(n + 1, 4)}, right,
            (n < 3) & (n >= step),
        )
        block = self.block(lax.rem(n + step, 4))
        links.send(
            block, block, {"narrow": lax.rem(n + 3, 4)}, left,
            (n > 0) & (n + step <= 3),
        )

    def land(self, step):
        n, links = self.n, self.links
        right, left = self.slots[step]
        links.land(
            self.block(lax.rem(n + 7 - step, 4)), {"narrow": lax.rem(n + 3, 4)}, right,
            n >= step + 1,
        )
        links.land(
            self.block(lax.rem(n + 1 + step, 4)), {"narrow": lax.rem(n + 1, 4)}, left,
            n + 1 + step <= 3,
        )


class LineSum:
    def __init__(self, links, n, outbox, inbox):
        self.links, self.n, self.outbox, self.inbox = links, n, outbox, inbox
        self.inner = (n == 1) | (n == 2)
        self.outer = (n == 0) | (n == 3)
        self.targets = [self.owner(step) for step in range(NEAR)]
        self.next = 1 + lax.rem(n, 2)
        self.slots = [links.slot() for _ in range(6)]

    def owner(self, step):
        return lax.rem((4 - step) * self.n + (3 - step), 5)

    def put(self, step, part):
        self.outbox[step] = part.astype(BF)
        self.set_out(step)

    def set_out(self, step):
        links, outbox, inbox = self.links, self.outbox, self.inbox
        goal = {"narrow": self.next if step == 0 else self.targets[step]}
        far, near = self.slots[2 * step], self.slots[2 * step + 1]
        if step == 0:
            links.send(outbox.at[0], inbox.at[3], goal, far, self.outer)
            links.send(outbox.at[0], inbox.at[0], goal, near, self.inner)
        elif step == 1:
            links.send(outbox.at[1], inbox.at[1], goal, far, self.outer)
            links.send(outbox.at[1], inbox.at[0], goal, near, self.inner)
        else:
            links.send(outbox.at[2], inbox.at[2], goal, far, self.outer)

    def join(self):
        links, outbox, inbox = self.links, self.outbox, self.inbox
        home = {"narrow": 3 * (self.n // 2)}
        links.land(inbox.at[3], home, self.slots[0], self.inner)

        @pl.when(self.inner)
        def _():
            outbox[2] = (outbox[2].astype(F32) + inbox[3].astype(F32)).astype(BF)

    def relay(self):
        self.join()
        goal = {"narrow": self.targets[2]}
        self.links.send(
            self.outbox.at[2], self.inbox.at[1], goal, self.slots[5], self.inner
        )

    def early(self, own):
        links, inbox = self.links, self.inbox
        other = {"narrow": lax.rem(self.n + 1, 4)}
        links.land(inbox.at[0], other, self.slots[1], self.inner)
        links.land(inbox.at[0], other, self.slots[3], self.outer)
        links.land(inbox.at[1], other, self.slots[2], self.inner)

        @pl.when(self.outer)
        def _():
            inbox[1] = jnp.zeros(inbox.shape[1:], BF)

        return own + inbox[0].astype(F32) + inbox[1].astype(F32)

    def total(self, own):
        links, inbox = self.links, self.inbox
        outer, inner = self.outer, self.inner
        other = {"narrow": lax.rem(self.n + 1, 4)}
        links.land(inbox.at[0], other, self.slots[1], inner)
        links.land(inbox.at[0], other, self.slots[3], outer)
        links.land(inbox.at[1], other, self.slots[2], inner)
        links.land(inbox.at[1], other, self.slots[5], outer)
        links.land(inbox.at[2], other, self.slots[4], inner)

        @pl.when(outer)
        def _():
            inbox[2] = jnp.zeros(inbox.shape[1:], BF)

        for index in range(3):
            own = own + inbox[index].astype(F32)
        return own


class PlaneGather:
    def __init__(self, links, chip, core, plane, mate, source, blocks):
        self.links, self.chip, self.core, self.plane, self.mate = links, chip, core, plane, mate
        self.blocks = blocks
        self.slots = [links.slot() for _ in range(4)]
        self.mate_slots = [links.slot() for _ in range(4)]
        own = 2 * chip + core
        for side in range(2):
            links.send(source, blocks.at[own], self.at_plane(plane[side]), self.slots[side])
        links.send(source, blocks.at[own], mate, self.mate_slots[3])

    def at_plane(self, peer):
        return {"wide": 2 * peer + self.core}

    def half(self, peer, side):
        rows = self.blocks.shape[1] // 2
        return self.blocks.at[2 * peer + self.core, pl.ds(side * rows, rows), :]

    def pass_on(self):
        links, plane = self.links, self.plane
        for side in range(2):
            block = self.blocks.at[2 * plane[side] + self.core]
            links.land(block, self.at_plane(plane[side]), self.slots[side])
            part = self.half(plane[side], side)
            links.send(part, part, self.at_plane(plane[1 - side]), self.slots[2 + side])
            links.send(block, block, self.mate, self.mate_slots[side])

    def far(self):
        links, plane = self.links, self.plane
        for side in range(2):
            links.land(
                self.half(plane[2], side), self.at_plane(plane[1 - side]), self.slots[2 + side]
            )
        block = self.blocks.at[2 * plane[2] + self.core]
        links.send(block, block, self.mate, self.mate_slots[2])

    def finish(self):
        links, plane = self.links, self.plane
        for step in range(NEAR):
            block = self.blocks.at[2 * plane[step] + 1 - self.core]
            links.land(block, self.mate, self.mate_slots[step])
        links.land(self.blocks.at[2 * self.chip + 1 - self.core], self.mate, self.mate_slots[3])


FRONT_SLOTS = 112


def front_body(
    tok_ref, cot_ref, gain_first_ref, gain_second_ref, wq_ref, wk_ref, wv_ref, wo_ref, router_ref, gate_ref, up_ref,
    down_ref, segment_ref, parents_ref, ids_ref, rank_ref,
    qkvw_out, outw_out, expert_out, x_out, dy_out, gate_out, middle_out, hidden_hbm,
    tokens_hbm, qkv_hbm, prob_hbm, att_out, stat_out, rope_out, pick_hbm, cols_out,
    hidden_out, tokens_out, qkv_out, prob_out, pick_out,
    raw_proj, seen_at, raw, moved_ref, pack, tok_pack, qkvw, outw, cot_send, y_send, br_send,
    br_recv, stat_send, stat_recv, gate_send, sent, landed, local,
):
    n = lax.axis_index("narrow")
    w = lax.axis_index("wide")
    chip, core = w // 2, lax.rem(w, 2)
    to_z, from_z = places_of(n)
    plane = plane_of(chip)
    links = Links(sent, landed, local)
    mate = {"wide": 2 * chip + 1 - core}

    def at_plane(peer):
        return {"wide": 2 * peer + core}

    token_count, part_width = tok_ref.shape
    rows_each = raw.shape[1]
    raw_loads = [
        links.move(source, raw.at[kind_at]) for kind_at, source in enumerate((gate_ref, up_ref, down_ref))
    ]
    links.waits = []
    greet(to_z, plane, chip, core, True)

    def by_expert(kind_at):
        raw_loads[kind_at].wait()

        def some_rows(index, value):
            rows = pl.ds(pl.multiple_of(index * 32, 32), 32)
            for expert in range(EXPERTS):
                moved_ref[kind_at, expert, rows, :] = raw[kind_at, rows, expert, :]
            return value

        lax.fori_loop(0, rows_each // 32, some_rows, 0)

    tok_pack[0:token_count, :] = tok_ref[...]
    for index, gain_ref in enumerate((gain_first_ref, gain_second_ref)):
        for row in range(part_width // 128):
            tok_pack[
                token_count + index : token_count + index + 1, row * 128 : (row + 1) * 128
            ] = gain_ref[row : row + 1, :]
    tokens_out[n] = tok_pack[...]
    tok_chain = Chain(links, n, lambda m: tokens_out.at[m])
    tok_chain.start(0)
    wide_shape = (token_count, token_count)
    row_at = lax.broadcasted_iota(jnp.int32, wide_shape, 0)
    col_at = lax.broadcasted_iota(jnp.int32, wide_shape, 1)
    seg_row, rank_row = segment_ref[...], rank_ref[...]
    first_row, second_row = ids_ref[0:1, :], ids_ref[1:2, :]
    stacked = [item.astype(F32) for item in (seg_row, rank_row, first_row, second_row)]
    columns = jnp.concatenate(stacked + [jnp.zeros((124, token_count), F32)], 0).T
    cols_out[...] = columns
    columns = columns.astype(jnp.int32)
    seg_col, rank_col = columns[:, 0:1], columns[:, 1:2]
    segs = parents_ref.shape[1]
    of_seg = lax.broadcasted_iota(jnp.int32, (token_count, segs), 1) == seg_col
    par_col = jnp.sum(
        jnp.where(of_seg, parents_ref[...].astype(F32), 0.0), 1, keepdims=True
    ).astype(jnp.int32)
    seen = ((seg_row == seg_col) | (seg_row == par_col) | (seg_row == 0)) & (col_at <= row_at)
    spots = jnp.sum(jnp.where(seen, 1.0, 0.0), 1, keepdims=True) - 1.0
    lane_at = lax.broadcasted_iota(jnp.int32, (token_count, HEAD_DIM), 1)
    turn = lax.rem(lane_at, HEAD_DIM // 2).astype(F32) * (-2.0 / HEAD_DIM * math.log(ROPE_BASE))
    angles = spots * jnp.exp(turn)
    cosines = jnp.cos(angles)
    sines = jnp.sin(angles) * jnp.where(lane_at < HEAD_DIM // 2, -1.0, 1.0)
    rope_out[0] = cosines
    rope_out[1] = sines
    kind = lax.broadcasted_iota(jnp.int32, (8, token_count), 0)
    hot_first = jnp.where(kind == first_row, 1.0, 0.0)
    hot_second = jnp.where(kind == second_row, 1.0, 0.0)
    earlier = jnp.where(rank_col < rank_row, 1.0, 0.0).astype(BF)
    count_first = low_dot(hot_first.astype(BF), earlier)
    count_second = low_dot(hot_second.astype(BF), earlier)
    count_second = count_second + jnp.sum(hot_first, 1, keepdims=True)
    slot_first = jnp.sum(count_first * hot_first, 0, keepdims=True)
    slot_second = jnp.sum(count_second * hot_second, 0, keepdims=True)
    kept_first = jnp.where(slot_first < CAP, 1.0, 0.0)
    kept_second = jnp.where(slot_second < CAP, 1.0, 0.0)
    flat_first = jnp.where(slot_first < CAP, first_row * CAP + slot_first.astype(jnp.int32), SLOTS)
    flat_second = jnp.where(
        slot_second < CAP, second_row * CAP + slot_second.astype(jnp.int32), SLOTS
    )
    slot_at = lax.broadcasted_iota(jnp.int32, (SLOTS, token_count), 0)
    pick_first = jnp.where(slot_at == flat_first, 1.0, 0.0)
    pick_second = jnp.where(slot_at == flat_second, 1.0, 0.0)
    pick_out[0] = pick_first.astype(BF)
    pick_out[1] = pick_second.astype(BF)
    pick_both = (pick_first + pick_second).astype(BF)

    def column_block(array):
        return lambda m: array.at[:, pl.ds(pl.multiple_of(m * part_width, part_width), part_width)]

    def slot_block(array, owner):
        return array.at[
            pl.ds(pl.multiple_of(owner * CAP, 16), CAP),
            pl.ds(pl.multiple_of(n * part_width, part_width), part_width),
        ]

    def dispatch(rows, buffer, array):
        slots = [links.slot() for _ in range(NEAR)]
        buffer[...] = low_dot(pick_both, rows).astype(BF)
        for step in range(NEAR):
            links.send(
                buffer.at[pl.ds(pl.multiple_of(plane[step] * CAP, 16), CAP), :],
                slot_block(array, chip), at_plane(plane[step]), slots[step],
            )
        own = links.move(
            buffer.at[pl.ds(pl.multiple_of(chip * CAP, 16), CAP), :], slot_block(array, chip)
        )
        return slots, own

    def arrive(array, state):
        slots, own = state
        for step in range(NEAR):
            links.land(slot_block(array, plane[step]), at_plane(plane[step]), slots[step])
        own.wait()
        links.waits = [item for item in links.waits if item[0] is not own]

    dy_state = dispatch(cot_ref[...], cot_send, dy_out)
    dy_chain = Chain(links, n, column_block(dy_out))

    pack[:, 0:512] = wq_ref[...]
    pack[:, 512:1024] = wk_ref[...]
    pack[:, 1024:1536] = wv_ref[...]
    router_rows = jnp.concatenate(
        [router_ref[...].astype(F32), jnp.zeros((128 - EXPERTS, rows_each), F32)], 0
    )
    pack[:, 1536:1664] = router_rows.T.astype(BF)
    in_gather = PlaneGather(links, chip, core, plane, mate, pack, qkvw)
    qkvw[w] = pack[...]
    outw[w] = wo_ref[...]

    tok_chain.land(0)
    tok_chain.start(1)
    by_expert(0)
    tok_chain.land(1)
    tok_chain.start(2)
    arrive(dy_out, dy_state)
    dy_chain.start(0)
    tok_chain.land(2)
    in_gather.pass_on()
    out_gather = PlaneGather(links, chip, core, plane, mate, wo_ref, outw)
    total = jnp.zeros((token_count, 1), F32)
    for m in range(4):
        part = tokens_out[m, 0:token_count, :].astype(F32)
        total = total + jnp.sum(part * part, 1, keepdims=True)
    scale_first = lax.rsqrt(total * (1.0 / (4 * part_width)) + NORM_EPS)
    for m in range(4):
        part = tokens_out[m, 0:token_count, :].astype(F32)
        gain = tokens_out[m, token_count : token_count + 1, :].astype(F32)
        hidden_out[:, m * part_width : (m + 1) * part_width] = (part * scale_first * gain).astype(BF)

    by_expert(1)

    in_gather.far()
    out_gather.pass_on()
    in_gather.finish()
    saved_in = links.move(qkvw, qkvw_out)

    pieces = ((0, 0, rows_each), (1, 0, rows_each)) + tuple(
        (2, half * rows_each // 2, rows_each // 2) for half in range(2)
    )
    expert_slots = [[links.slot() for _ in range(NEAR)] for _ in pieces]
    expert_mate = [[links.slot() for _ in range(4)] for _ in pieces]

    def piece_of(array, index):
        return array.at[pl.ds(pieces[index][1], pieces[index][2]), :]

    def landing(index, owner, side):
        return piece_of(expert_out.at[pieces[index][0], owner, side], index)

    def set_out(index):
        kind_at = pieces[index][0]
        for step in range(NEAR):
            links.send(
                piece_of(moved_ref.at[kind_at, plane[step]], index), landing(index, chip, core),
                at_plane(plane[step]), expert_slots[index][step],
            )
        own = piece_of(moved_ref.at[kind_at, chip], index)
        links.send(own, landing(index, chip, core), mate, expert_mate[index][3])
        links.move(own, landing(index, chip, core))

    set_out(0)
    set_out(1)

    def pass_on(index):
        for step in range(NEAR):
            block = landing(index, plane[step], core)
            links.land(block, at_plane(plane[step]), expert_slots[index][step])
            links.send(block, block, mate, expert_mate[index][step])

    def all_there(index):
        for step in range(NEAR):
            links.land(landing(index, plane[step], 1 - core), mate, expert_mate[index][step])
        links.land(landing(index, chip, 1 - core), mate, expert_mate[index][3])

    dy_chain.land(0)
    dy_chain.start(1)
    by_expert(2)

    score_scale = HEAD_DIM ** (-0.5)

    def one_projection(part, value):
        cols = pl.ds(pl.multiple_of(part * part_width, part_width), part_width)
        weight = qkvw[:, :, cols].reshape(4 * part_width, part_width)
        raw_proj[part] = low_dot(hidden_out[...], weight)
        return value

    lax.fori_loop(0, 3, one_projection, 0)
    seen_at[...] = jnp.where(seen, 1.0, 0.0)

    def one_head(head, value):
        cols = pl.ds(pl.multiple_of(head * HEAD_DIM, HEAD_DIM), HEAD_DIM)
        turned = []
        for part in range(2):
            proj = raw_proj[part, :, cols]
            turned.append(
                (proj * rope_out[0] + pltpu.roll(proj, HEAD_DIM // 2, 1) * rope_out[1]).astype(BF)
            )
            qkv_out[part, :, cols] = turned[part]
        values = raw_proj[2, :, cols].astype(BF)
        qkv_out[2, :, cols] = values
        scores = rows_rows(turned[0], turned[1]) * score_scale
        scores = jnp.where(seen_at[...] > 0.5, scores, NEG_FILL)
        exps = jnp.exp(scores - jnp.max(scores, 1, keepdims=True))
        weights = exps / jnp.sum(exps, 1, keepdims=True)
        prob_out[head] = weights
        att_out[:, cols] = low_dot(weights.astype(BF), values).astype(BF)
        return value

    lax.fori_loop(0, part_width // HEAD_DIM, one_head, 0)
    for source, target in (
        (hidden_out, hidden_hbm), (tokens_out, tokens_hbm), (qkv_out, qkv_hbm),
        (prob_out, prob_hbm), (pick_out, pick_hbm),
    ):
        links.move(source, target)

    dy_chain.land(1)
    dy_chain.start(2)
    out_gather.far()

    out_gather.finish()
    links.move(outw, outw_out)

    attended = att_out[...]

    def branch(m):
        weight = outw[pl.ds(2 * m, 2)].reshape(part_width, part_width)
        return rows_rows(attended, weight)

    branch_sum = LineSum(links, n, br_send, br_recv)
    for step in range(NEAR):
        branch_sum.put(step, branch(branch_sum.targets[step]))
    middle = tok_ref[...].astype(F32) + branch(n)
    branch_sum.relay()
    middle = branch_sum.total(middle)
    middle_out[...] = middle
    x_state = dispatch(middle.astype(BF), y_send, x_out)

    def cap_block(owner):
        return lambda m: x_out.at[
            pl.ds(pl.multiple_of(owner * CAP, 16), CAP),
            pl.ds(pl.multiple_of(m * part_width, part_width), part_width),
        ]

    x_chains = [Chain(links, n, cap_block(owner)) for owner in (chip, *plane)]
    x_slots, x_own = x_state
    x_own.wait()
    links.waits = [item for item in links.waits if item[0] is not x_own]
    x_chains[0].start(0)

    set_out(2)
    set_out(3)

    gain_second = tok_pack[token_count + 1 : token_count + 2, :].astype(F32)
    router = qkvw[pl.ds(2 * n, 2), :, 1536:1664].reshape(part_width, 128)
    logit_part = mm(router, (middle * gain_second).astype(BF), ((0,), (1,)))[0:8, :]
    square = middle * middle
    square_high = square.astype(BF)
    square_low = (square - square_high.astype(F32)).astype(BF)
    ones = jnp.ones((8, part_width), BF)
    square_sum = rows_rows(ones, square_high) + rows_rows(ones, square_low)
    stat = jnp.where(kind == 4, square_sum, logit_part)
    stat_send[...] = stat
    stat_slots = [links.slot() for _ in range(NEAR)]
    for step in range(NEAR):
        links.send(stat_send, stat_recv.at[step], {"narrow": to_z[step]}, stat_slots[step])

    for step in range(NEAR):
        links.land(slot_block(x_out, plane[step]), at_plane(plane[step]), x_slots[step])
        x_chains[1 + step].start(0)
    for step in range(NEAR):
        links.land(stat_recv.at[step], {"narrow": from_z[step]}, stat_slots[step])
        stat = stat + stat_recv[step]
    stat_out[...] = stat
    scale_row = lax.rsqrt(stat[4:5, :] * (1.0 / (4 * part_width)) + NORM_EPS)
    logits = jnp.where(kind < EXPERTS, stat * scale_row, NEG_FILL)
    chances = jnp.exp(logits - jnp.max(logits, 0, keepdims=True))
    chances = chances / jnp.sum(chances, 0, keepdims=True)
    share_first = jnp.sum(chances * hot_first, 0, keepdims=True)
    share_second = jnp.sum(chances * hot_second, 0, keepdims=True)
    both = share_first + share_second
    weighted = pick_first * (share_first / both) + pick_second * (share_second / both)
    slot_gate = jnp.sum(weighted, 1, keepdims=True)
    gate_send[...] = jnp.broadcast_to(slot_gate, (SLOTS, 128))

    def gate_rows(array, owner):
        return array.at[pl.ds(pl.multiple_of(owner * CAP, 16), CAP), :]

    gate_slots = [links.slot() for _ in range(NEAR)]
    for step in range(NEAR):
        links.send(
            gate_rows(gate_send, plane[step]), gate_rows(gate_out, chip),
            at_plane(plane[step]), gate_slots[step],
        )
    links.move(gate_rows(gate_send, chip), gate_rows(gate_out, chip))

    for step in range(2):
        for chain in x_chains:
            chain.land(step)
            chain.start(step + 1)
        pass_on(step)
    for chain in x_chains:
        chain.land(2)
    dy_chain.land(2)
    for step in range(NEAR):
        links.land(gate_rows(gate_out, plane[step]), at_plane(plane[step]), gate_slots[step])
    pass_on(2)
    pass_on(3)
    for index in range(len(pieces)):
        all_there(index)
    links.finish()


def front_call(tokens, cotangent, gain_attn, gain_ffn, weights, router, experts, segment, parents, ids, rank):
    token_count, part_width = tokens.shape
    full = 4 * part_width
    rows_each, _, hidden_width = experts[0].shape
    heads = part_width // HEAD_DIM
    vmem = pl.BlockSpec(memory_space=pltpu.VMEM)
    hbm = pl.BlockSpec(memory_space=pl.ANY)

    def arr(shape, dtype):
        return jax.ShapeDtypeStruct(shape, dtype)

    return pl.pallas_call(
        front_body,
        out_shape=(
            arr((8, rows_each, 1664), BF),
            arr((8, rows_each, part_width), BF),
            arr((3, 4, 2, rows_each, hidden_width), BF),
            arr((SLOTS, full), BF),
            arr((SLOTS, full), BF),
            arr((SLOTS, 128), F32),
            arr((token_count, part_width), F32),
            arr((token_count, full), BF),
            arr((4, token_count + 16, part_width), BF),
            arr((3, token_count, part_width), BF),
            arr((heads, token_count, token_count), F32),
            arr((token_count, part_width), BF),
            arr((8, token_count), F32),
            arr((2, token_count, HEAD_DIM), F32),
            arr((2, SLOTS, token_count), BF),
            arr((token_count, 128), F32),
        ),
        in_specs=[vmem] * 9 + [hbm] * 3 + [vmem] * 4,
        out_specs=(hbm,) * 5 + (vmem, vmem) + (hbm,) * 4 + (vmem,) * 3 + (hbm, vmem),
        scratch_shapes=[
            pltpu.VMEM((token_count, full), BF),
            pltpu.VMEM((4, token_count + 16, part_width), BF),
            pltpu.VMEM((3, token_count, part_width), BF),
            pltpu.VMEM((heads, token_count, token_count), F32),
            pltpu.VMEM((2, SLOTS, token_count), BF),
            pltpu.VMEM((3, token_count, part_width), F32),
            pltpu.VMEM((token_count, token_count), F32),
            pltpu.VMEM((3, rows_each, EXPERTS, hidden_width), BF),
            pltpu.VMEM((3, EXPERTS, rows_each, hidden_width), BF),
            pltpu.VMEM((rows_each, 1664), BF),
            pltpu.VMEM((token_count + 16, part_width), BF),
            pltpu.VMEM((8, rows_each, 1664), BF),
            pltpu.VMEM((8, rows_each, part_width), BF),
            pltpu.VMEM((SLOTS, part_width), BF),
            pltpu.VMEM((SLOTS, part_width), BF),
            pltpu.VMEM((NEAR, token_count, part_width), BF),
            pltpu.VMEM((NEAR + 1, token_count, part_width), BF),
            pltpu.VMEM((8, token_count), F32),
            pltpu.VMEM((NEAR, 8, token_count), F32),
            pltpu.VMEM((SLOTS, 128), F32),
            pltpu.SemaphoreType.DMA((FRONT_SLOTS,)),
            pltpu.SemaphoreType.DMA((FRONT_SLOTS,)),
            pltpu.SemaphoreType.DMA((24,)),
        ],
        compiler_params=pltpu.CompilerParams(
            collective_id=0, has_side_effects=True, vmem_limit_bytes=60 * 1024 * 1024
        ),
        cost_estimate=pl.CostEstimate(
            flops=6_000_000_000, bytes_accessed=60_000_000, transcendentals=400_000
        ),
        name="front",
    )(
        tokens, cotangent, gain_attn.reshape(-1, 128), gain_ffn.reshape(-1, 128), *weights,
        router, *experts, segment, parents, ids, rank,
    )


MID_SLOTS = 48


TILE = 512


def mid_body(
    x_ref, dy_hbm, gate_ref, tokens_ref, w_ref,
    back_mid_out, back_exp_out, last_exp_out, extra_out, grads_out, expert_out,
    dy_ref, weights, hidden, graded_send, hidden_cat, graded_cat, act_cat, gate_cat, up_cat,
    turned, down_grad, rs_send, rs_recv, ext_send, ext_recv, sent, landed, local,
):
    n = lax.axis_index("narrow")
    w = lax.axis_index("wide")
    chip, core = w // 2, lax.rem(w, 2)
    to_z, from_z = places_of(n)
    plane = plane_of(chip)
    links = Links(sent, landed, local)
    mate = {"wide": 2 * chip + 1 - core}
    slots, full = hidden.shape
    part_width = full // 4
    rows_each = full // 8
    half = full // 2
    hidden_width = weights.shape[2]

    dy_load = links.move(dy_hbm, dy_ref)
    x_load = links.move(x_ref, hidden)
    loads = [
        links.move(
            w_ref.at[kind, c, k],
            weights.at[kind, pl.ds((2 * c + k) * rows_each, rows_each), :],
        )
        for kind in range(3)
        for c in range(4)
        for k in range(2)
    ]
    links.waits = []
    greet(to_z, plane, chip, core, True)

    slot_gate = gate_ref[:, 0:1]
    dy_load.wait()
    for c in range(4):
        theirs = pl.ds(pl.multiple_of((2 * c + 1 - core) * rows_each, rows_each), rows_each)
        ours = pl.ds(pl.multiple_of((2 * c + core) * rows_each, rows_each), rows_each)
        cols = slice(c * rows_each, (c + 1) * rows_each)
        graded_cat[core, :, cols] = (dy_ref[:, ours].astype(F32) * slot_gate).astype(BF)
        graded_send[:, cols] = (dy_ref[:, theirs].astype(F32) * slot_gate).astype(BF)

    def to_mate(source, target):
        slot = links.slot()
        links.send(source, target.at[core], mate, slot)
        return lambda: links.land(target.at[1 - core], mate, slot)

    graded_there = to_mate(graded_send, graded_cat)
    x_load.wait()
    total = jnp.zeros((slots, 1), F32)
    for m in range(4):
        part = hidden[:, m * part_width : (m + 1) * part_width].astype(F32)
        total = total + jnp.sum(part * part, 1, keepdims=True)
    scale = lax.rsqrt(total * (1.0 / full) + NORM_EPS)
    gain_row = tokens_ref.shape[1] - 15
    for m in range(4):
        cols = slice(m * part_width, (m + 1) * part_width)
        gain = tokens_ref[m, gain_row : gain_row + 1, :].astype(F32)
        hidden[:, cols] = (hidden[:, cols].astype(F32) * scale * gain).astype(BF)
    hidden_slots = [links.slot() for _ in range(4)]
    for c in range(4):
        cols = pl.ds(c * rows_each, rows_each)
        theirs = pl.ds(pl.multiple_of((2 * c + 1 - core) * rows_each, rows_each), rows_each)
        ours = pl.ds(pl.multiple_of((2 * c + core) * rows_each, rows_each), rows_each)
        links.send(hidden.at[:, theirs], hidden_cat.at[core, :, cols], mate, hidden_slots[c])
        hidden_cat[core, :, c * rows_each : (c + 1) * rows_each] = hidden[:, ours]
    for load in loads:
        load.wait()

    def one_tile(cols, rows):
        gate_pre = low_dot(hidden[rows, :], weights[0, :, cols])
        up_pre = low_dot(hidden[rows, :], weights[1, :, cols])
        act_raw = low_dot(dy_ref[rows, :], weights[2, :, cols])
        sigmoid = 1.0 / (1.0 + jnp.exp(-gate_pre))
        silu = gate_pre * sigmoid
        activated = (silu * up_pre).astype(BF)
        grad_act = act_raw * gate_ref[rows, 0:1]
        act_cat[core, rows, cols] = activated
        gate_cat[core, rows, cols] = (
            grad_act * up_pre * (sigmoid * (1.0 + gate_pre * (1.0 - sigmoid)))
        ).astype(BF)
        up_cat[core, rows, cols] = (grad_act * silu).astype(BF)
        return jnp.sum(act_raw * activated.astype(F32), 1, keepdims=True)

    def over_tiles(tile, body, carry):
        whole = hidden_width // tile
        carry = lax.fori_loop(
            0, whole, lambda t, value: body(pl.ds(pl.multiple_of(t * tile, tile), tile), value), carry
        )
        if hidden_width % tile:
            carry = body(pl.ds(whole * tile, hidden_width % tile), carry)
        return carry

    share = over_tiles(
        TILE,
        lambda cols, value: tuple(
            value[index] + one_tile(cols, pl.ds(index * (slots // 2), slots // 2))
            for index in range(2)
        ),
        (jnp.zeros((slots // 2, 1), F32),) * 2,
    )
    share = jnp.concatenate(share, 0)
    acts_there = [to_mate(item.at[core], item) for item in (act_cat, gate_cat, up_cat)]

    grad_gate, grad_up = gate_cat.at[core], up_cat.at[core]
    mid_sum = LineSum(links, n, rs_send.at[0], rs_recv.at[0])

    def mid_part(owner):
        rows = pl.ds(pl.multiple_of(owner * part_width, part_width), part_width)
        block = rows_rows(grad_gate[...], weights[0, rows, :])
        block = block + rows_rows(grad_up[...], weights[1, rows, :])
        return block, jnp.sum(hidden[:, rows].astype(F32) * block, 1, keepdims=True)

    stat = jnp.zeros((slots, 1), F32)
    block, part = mid_part(mid_sum.targets[0])
    mid_sum.put(0, block)
    stat = stat + part

    expert_slots = {}

    def weight_grad(right, target):
        def body(cols, value):
            right_rows = right[:, :, cols].reshape(2 * slots, cols.size)
            target[:, cols] = low_dot(turned[...], right_rows).astype(BF)
            return value

        over_tiles(TILE, body, 0)

    def share_out(index, source):
        expert_slots[index] = [links.slot() for _ in range(NEAR)]

        def block(owner):
            first = pl.multiple_of(owner * rows_each, rows_each)
            return source.at[pl.ds(first, rows_each), :]

        for step in range(NEAR):
            links.send(
                block(plane[step]), expert_out.at[index, chip],
                {"wide": 2 * plane[step] + core}, expert_slots[index][step],
            )
        links.move(block(chip), expert_out.at[index, chip])

    graded_there()
    acts_there[0]()
    turned[...] = graded_cat[...].reshape(2 * slots, half).T
    weight_grad(act_cat, down_grad)
    share_out(0, down_grad)

    def other_part(step, stat):
        block, part = mid_part(mid_sum.owner(step))
        rs_send[0, step] = block.astype(BF)
        return stat + part

    stat = lax.fori_loop(1, 4, other_part, stat)
    mid_sum.set_out(1)
    mid_sum.set_out(2)
    lane_at = lax.broadcasted_iota(jnp.int32, (slots, 128), 1)
    columns = jnp.where(lane_at == 0, share, jnp.where(lane_at == 1, stat, 0.0))
    high = columns.astype(BF)
    rest = (columns - high.astype(F32)).astype(BF)
    pick = jnp.where(
        lax.broadcasted_iota(jnp.int32, (8, 128), 0) == lax.broadcasted_iota(jnp.int32, (8, 128), 1),
        1.0, 0.0,
    ).astype(BF)
    extra = rows_rows(pick, high) + rows_rows(pick, rest)
    ext_send[...] = extra
    ext_slots = [links.slot() for _ in range(NEAR)]
    for step in range(NEAR):
        links.send(ext_send, ext_recv.at[step], {"narrow": to_z[step]}, ext_slots[step])

    mid_sum.relay()

    activated = act_cat.at[core]
    exp_sum = LineSum(links, n, rs_send.at[1], rs_recv.at[1])

    def exp_part(owner):
        rows = pl.ds(pl.multiple_of(owner * part_width, part_width), part_width)
        return rows_rows(activated[...], weights[2, rows, :])

    def expert_part(step, value):
        rs_send[1, step] = exp_part(exp_sum.owner(step)).astype(BF)
        return value

    lax.fori_loop(0, 4, expert_part, 0)
    exp_sum.set_out(0)
    exp_sum.set_out(1)
    for slot in hidden_slots:
        index = hidden_slots.index(slot)
        links.land(
            hidden_cat.at[1 - core, :, pl.ds(index * rows_each, rows_each)], mate, slot
        )
    for there in acts_there[1:]:
        there()
    turned[...] = hidden_cat[...].reshape(2 * slots, half).T
    gate_grad = weights.at[0, pl.ds(0, half), :]
    weight_grad(gate_cat, gate_grad)
    share_out(1, gate_grad)
    up_grad = weights.at[1, pl.ds(0, half), :]
    weight_grad(up_cat, up_grad)
    links.move(up_grad, grads_out)

    for step in range(NEAR):
        links.land(ext_recv.at[step], {"narrow": from_z[step]}, ext_slots[step])
        extra = extra + ext_recv[step]
    high = extra.astype(BF)
    rest = (extra - high.astype(F32)).astype(BF)
    place = lax.broadcasted_iota(jnp.int32, (8, 128), 0) * 2
    lanes = lax.broadcasted_iota(jnp.int32, (8, 128), 1)
    spread_high = jnp.where(place == lanes, 1.0, 0.0).astype(BF)
    spread_low = jnp.where(place + 1 == lanes, 1.0, 0.0).astype(BF)
    columns = mm(high, spread_high, ((0,), (0,))) + mm(rest, spread_low, ((0,), (0,)))
    extra_out[...] = jnp.where(lane_at == 4, 1.0, columns).astype(BF)
    back_mid_out[...] = mid_sum.total(rs_send[0, 3].astype(F32)).astype(BF)
    exp_sum.join()
    last_exp_out[...] = rs_send[1, 2]
    back_exp_out[...] = exp_sum.early(rs_send[1, 3].astype(F32)).astype(BF)
    for index in range(2):
        for step in range(NEAR):
            links.land(
                expert_out.at[index, plane[step]], {"wide": 2 * plane[step] + core},
                expert_slots[index][step],
            )
    links.finish()


def mid_call(slot_mid, slot_grad, slot_gate, token_parts, expert_w):
    slots, full = slot_mid.shape
    part_width = full // 4
    rows_each, hidden_width = expert_w.shape[3:]
    vmem = pl.BlockSpec(memory_space=pltpu.VMEM)
    hbm = pl.BlockSpec(memory_space=pl.ANY)

    def arr(shape, dtype):
        return jax.ShapeDtypeStruct(shape, dtype)

    return pl.pallas_call(
        mid_body,
        out_shape=(
            arr((slots, part_width), BF),
            arr((slots, part_width), BF),
            arr((slots, part_width), BF),
            arr((slots, 128), BF),
            arr((full // 2, hidden_width), BF),
            arr((2, 4, rows_each, hidden_width), BF),
        ),
        in_specs=[hbm] * 2 + [vmem] * 2 + [hbm],
        out_specs=(vmem,) * 4 + (hbm, hbm),
        scratch_shapes=[
            pltpu.VMEM((slots, full), BF),
            pltpu.VMEM((3, full, hidden_width), BF),
            pltpu.VMEM((slots, full), BF),
            pltpu.VMEM((slots, full // 2), BF),
            pltpu.VMEM((2, slots, full // 2), BF),
            pltpu.VMEM((2, slots, full // 2), BF),
            pltpu.VMEM((2, slots, hidden_width), BF),
            pltpu.VMEM((2, slots, hidden_width), BF),
            pltpu.VMEM((2, slots, hidden_width), BF),
            pltpu.VMEM((full // 2, 2 * slots), BF),
            pltpu.VMEM((full // 2, hidden_width), BF),
            pltpu.VMEM((2, NEAR + 1, slots, part_width), BF),
            pltpu.VMEM((2, NEAR + 1, slots, part_width), BF),
            pltpu.VMEM((8, slots), F32),
            pltpu.VMEM((NEAR, 8, slots), F32),
            pltpu.SemaphoreType.DMA((MID_SLOTS,)),
            pltpu.SemaphoreType.DMA((MID_SLOTS,)),
            pltpu.SemaphoreType.DMA((32,)),
        ],
        compiler_params=pltpu.CompilerParams(
            collective_id=1, has_side_effects=True, vmem_limit_bytes=62 * 1024 * 1024
        ),
        cost_estimate=pl.CostEstimate(
            flops=30_000_000_000, bytes_accessed=40_000_000, transcendentals=800_000
        ),
        name="mid",
    )(slot_mid, slot_grad, slot_gate, token_parts, expert_w)


class PlaneSum:
    def __init__(self, links, core, chip, plane, first, send, inbox):
        self.links, self.core, self.chip = links, core, chip
        self.near, self.next, self.far = plane[first], plane[1 - first], plane[2]
        self.send, self.inbox = send, inbox
        self.slots = [links.slot() for _ in range(3)]

    def at(self, peer):
        return {"wide": 2 * peer + self.core}

    def block(self, owner):
        rows = self.inbox.shape[1]
        return self.send.at[pl.ds(pl.multiple_of(owner * rows, rows), rows), :]

    def start(self):
        links = self.links
        links.send(self.block(self.far), self.inbox.at[1], self.at(self.near), self.slots[1])
        links.send(self.block(self.near), self.inbox.at[0], self.at(self.near), self.slots[0])

    def turn(self):
        links = self.links
        links.land(self.inbox.at[1], self.at(self.near), self.slots[1])
        block = self.block(self.next)
        block[...] = (block[...].astype(F32) + self.inbox[1].astype(F32)).astype(BF)
        links.send(block, self.inbox.at[2], self.at(self.next), self.slots[2])

    def total(self):
        links = self.links
        links.land(self.inbox.at[0], self.at(self.near), self.slots[0])
        links.land(self.inbox.at[2], self.at(self.next), self.slots[2])
        own = self.block(self.chip)[...].astype(F32)
        return own + self.inbox[0].astype(F32) + self.inbox[2].astype(F32)


TAIL_SLOTS = 72


def tail_body(
    mid_ref, exp_ref, last_ref, ext_ref, moved_ref, picks_hbm, stat_ref, cols_ref, middle_ref,
    cot_ref, tok_ref, tokens_hbm, qkv_hbm, prob_hbm, att_ref, rope_ref, hidden_hbm, qkvw_ref,
    outw_ref,
    output_out, grad_tokens_out, summed_out, small_out,
    router_out, expert_out,
    picks_ref, tokens_ref, qkv_ref, prob_ref, hidden_ref, grad_att_at, exp_in, exp_sum, router_all, qkvw, outw, ret_mid, ret_exp, ret_ext, branch, hidden_cat, branch_cat, att_cat, proj_cat,
    proj_send, proj_recv, first_send, first_recv, col_send, col_recv, small_mate, small_sum,
    small_recv, last_mate, last_sum, last_recv, sent, landed, local,
):
    n = lax.axis_index("narrow")
    w = lax.axis_index("wide")
    chip, core = w // 2, lax.rem(w, 2)
    to_z, from_z = places_of(n)
    plane = plane_of(chip)
    links = Links(sent, landed, local)
    mate = {"wide": 2 * chip + 1 - core}
    token_count, part_width = tok_ref.shape
    full = 4 * part_width
    rows_each = full // 8
    heads = part_width // HEAD_DIM
    half = full // 2

    def at_plane(peer):
        return {"wide": 2 * peer + core}

    def cap_rows(array, owner):
        return array.at[pl.ds(pl.multiple_of(owner * CAP, 16), CAP), :]

    first_loads = [
        links.move(source, target)
        for source, target in (
            (hidden_hbm, hidden_ref), (picks_hbm, picks_ref), (tokens_hbm, tokens_ref),
            (qkv_hbm, qkv_ref), (prob_hbm, prob_ref),
        )
    ]
    loads = [links.move(qkvw_ref, qkvw), links.move(outw_ref, outw)]
    links.waits = []
    greet(to_z, plane, chip, core, True)

    last_slot = links.slot()
    links.send(last_ref, exp_in, {"narrow": lax.rem(2 * n + 1, 5)}, last_slot)

    back_slots = []

    def give_back(source, target):
        slots = [links.slot() for _ in range(NEAR)]
        for step in range(NEAR):
            links.send(
                cap_rows(source, plane[step]), cap_rows(target, chip), at_plane(plane[step]),
                slots[step],
            )
        own = links.move(cap_rows(source, chip), cap_rows(target, chip))
        links.waits.pop()
        back_slots.append((target, slots, own))

    give_back(mid_ref, ret_mid)
    give_back(ext_ref, ret_ext)

    def returned(which):
        target, slots, own = back_slots[which]
        for step in range(NEAR):
            links.land(cap_rows(target, plane[step]), at_plane(plane[step]), slots[step])
        own.wait()
        return target[...]

    expert_slots = [links.slot() for _ in range(NEAR)]
    for step in range(NEAR):
        block = pl.ds(pl.multiple_of(plane[step] * rows_each, rows_each), rows_each)
        links.send(
            moved_ref.at[block, :], expert_out.at[chip], at_plane(plane[step]), expert_slots[step]
        )
    block = pl.ds(pl.multiple_of(chip * rows_each, rows_each), rows_each)
    links.move(moved_ref.at[block, :], expert_out.at[chip])

    def to_mate(source, target):
        slot = links.slot()
        links.send(source, target.at[core], mate, slot)
        return lambda: links.land(target.at[1 - core], mate, slot)

    def parity_exchange(source, target):
        lands = []
        for c in range(4):
            cols = pl.ds(c * rows_each, rows_each)
            theirs = pl.ds(pl.multiple_of((2 * c + 1 - core) * rows_each, rows_each), rows_each)
            ours = pl.ds(pl.multiple_of((2 * c + core) * rows_each, rows_each), rows_each)
            slot = links.slot()
            links.send(source.at[:, theirs], target.at[core, :, cols], mate, slot)
            target[core, :, c * rows_each : (c + 1) * rows_each] = source[:, ours]
            lands.append((target.at[1 - core, :, cols], slot))
        return lambda: [links.land(block, mate, slot) for block, slot in lands]

    for load in first_loads:
        load.wait()
    hidden_there = parity_exchange(hidden_ref, hidden_cat)
    att_cat[core] = att_ref[...]
    att_there = to_mate(att_ref, att_cat)

    stat = jnp.concatenate([stat_ref[...], jnp.zeros((120, token_count), F32)], 0).T
    lane_at = lax.broadcasted_iota(jnp.int32, (token_count, 128), 1)
    scale_second = lax.rsqrt(stat[:, 4:5] * (1.0 / full) + NORM_EPS)
    logits = stat * scale_second
    hot_first = lane_at == cols_ref[:, 2:3].astype(jnp.int32)
    hot_second = lane_at == cols_ref[:, 3:4].astype(jnp.int32)
    logit_first = jnp.sum(jnp.where(hot_first, logits, 0.0), 1, keepdims=True)
    logit_second = jnp.sum(jnp.where(hot_second, logits, 0.0), 1, keepdims=True)
    apart = logit_first - logit_second
    share_first = 1.0 / (1.0 + jnp.exp(-apart))
    share_second = 1.0 / (1.0 + jnp.exp(apart))
    normed = middle_ref[...] * scale_second
    gain_second = tokens_ref[n, token_count + 1 : token_count + 2, :].astype(F32)
    hidden_second = (normed * gain_second).astype(BF)
    for load in loads:
        load.wait()
    router = qkvw[pl.ds(2 * n, 2), :, 1536:1664].reshape(part_width, 128)

    rows_mid = returned(0)
    rows_ext = returned(1)
    ext_first = cols_cols(picks_ref[0], rows_ext)
    ext_second = cols_cols(picks_ref[1], rows_ext)
    ext_both = ext_first + ext_second
    grad_share = ext_first[:, 0:1] + ext_first[:, 1:2] - ext_second[:, 0:1] - ext_second[:, 1:2]
    delta = (grad_share * share_first * share_second).astype(BF).astype(F32)
    grad_logits = jnp.where(hot_first, delta, jnp.where(hot_second, -delta, 0.0)).astype(BF)
    stat_total = ext_both[:, 2:3] + ext_both[:, 3:4] + delta * apart
    grad_hidden = cols_cols(picks_ref[0] + picks_ref[1], rows_mid) + rows_rows(grad_logits, router)
    grad_middle = cot_ref[...].astype(F32) + scale_second * (
        gain_second * grad_hidden - normed * (stat_total * (1.0 / full))
    )
    own_cols = pl.ds(pl.multiple_of(n * part_width, part_width), part_width)
    branch[:, own_cols] = grad_middle.astype(BF)
    branch_slots = [links.slot() for _ in range(NEAR)]
    for step in range(NEAR):
        links.send(
            branch.at[:, own_cols], branch.at[:, own_cols], {"narrow": to_z[step]},
            branch_slots[step],
        )

    links.land(exp_in, {"narrow": lax.rem(n + 1, 4)}, last_slot)
    exp_sum[...] = (exp_ref[...].astype(F32) + exp_in[...].astype(F32)).astype(BF)
    give_back(exp_sum, ret_exp)

    router_part = cols_cols(grad_logits, hidden_second)[0:8, :]
    gain_part = jnp.sum(grad_hidden * normed, 0, keepdims=True)
    kind_at = lax.broadcasted_iota(jnp.int32, (8, part_width), 0)
    small = jnp.where(kind_at == 4, gain_part, router_part)
    small_mate[core] = small
    small_there = to_mate(small_mate.at[core], small_mate)

    small_there()
    small = small_mate[0] + small_mate[1]
    small_sum[...] = small
    small_slots = [links.slot() for _ in range(NEAR)]
    for step in range(NEAR):
        links.send(small_sum, small_recv.at[step], at_plane(plane[step]), small_slots[step])

    for step in range(NEAR):
        cols = pl.ds(pl.multiple_of(from_z[step] * part_width, part_width), part_width)
        links.land(branch.at[:, cols], {"narrow": from_z[step]}, branch_slots[step])
    branch_there = parity_exchange(branch, branch_cat)
    grad_att = low_dot(branch[...], outw[...].reshape(full, part_width)).astype(BF)

    proj_sums = {
        part: PlaneSum(
            links, core, chip, plane, part % 2, proj_send.at[part], proj_recv.at[part]
        )
        for part in (3, 0, 1, 2)
    }

    branch_there()
    att_there()
    proj_send[3] = cols_cols(
        branch_cat[...].reshape(2 * token_count, half), att_cat[...].reshape(2 * token_count, part_width)
    ).astype(BF)
    proj_sums[3].start()
    score_scale = HEAD_DIM ** (-0.5)
    grad_att_at[...] = grad_att

    def one_head(head, stat_first):
        def lanes(start):
            return pl.ds(pl.multiple_of(start + head * HEAD_DIM, HEAD_DIM), HEAD_DIM)

        query, key, value = (qkv_ref[i, :, lanes(0)] for i in range(3))
        grad_out = grad_att_at[:, lanes(0)]
        weights = prob_ref[head]
        grad_weights = rows_rows(grad_out, value)
        inner = jnp.sum(weights * grad_weights, 1, keepdims=True)
        grad_scores = (weights * (grad_weights - inner)).astype(BF)
        grad_query = low_dot(grad_scores, key) * score_scale
        grad_key = cols_cols(grad_scores, query) * score_scale
        grad_value = cols_cols(weights.astype(BF), grad_out)
        products = (
            grad_query * query.astype(F32)
            + grad_key * key.astype(F32)
            + grad_value * value.astype(F32)
        )
        for part, grad in ((0, grad_query), (1, grad_key)):
            turned = grad * rope_ref[0] - pltpu.roll(grad, HEAD_DIM // 2, 1) * rope_ref[1]
            proj_cat[core, :, lanes(part * part_width)] = turned.astype(BF)
        proj_cat[core, :, lanes(2 * part_width)] = grad_value.astype(BF)
        return stat_first + jnp.sum(products, 1, keepdims=True)

    stat_first = lax.fori_loop(0, heads, one_head, jnp.zeros((token_count, 1), F32))
    proj_there = to_mate(proj_cat.at[core], proj_cat)
    high = stat_first.astype(BF)
    rest = (stat_first - high.astype(F32)).astype(BF)
    col_send[...] = jnp.where(
        lane_at == 0, high.astype(F32), jnp.where(lane_at == 1, rest.astype(F32), 0.0)
    ).astype(BF)
    col_slots = [links.slot() for _ in range(NEAR)]
    for step in range(NEAR):
        links.send(col_send, col_recv.at[step], {"narrow": to_z[step]}, col_slots[step])
    grads = proj_cat[core]

    def first_block(m):
        weight = qkvw[pl.ds(2 * m, 2), :, 0:1536].reshape(part_width, 1536)
        return rows_rows(grads, weight)

    def fill_first(step, value):
        first_send[step] = first_block(lax.rem(n + 1 + step, 4)).astype(BF)
        return value

    lax.fori_loop(0, NEAR, fill_first, 0)
    first_slots = [links.slot() for _ in range(NEAR)]
    for step in range(NEAR):
        links.send(
            first_send.at[step], first_recv.at[step], {"narrow": to_z[step]}, first_slots[step]
        )

    hidden_there()
    proj_there()
    hidden_rows = hidden_cat[...].reshape(2 * token_count, half)
    proj_sums[3].turn()
    for part in range(3):
        cols = slice(part * 512, (part + 1) * 512)
        proj_send[part] = cols_cols(
            hidden_rows, proj_cat[:, :, cols].reshape(2 * token_count, part_width)
        ).astype(BF)
        proj_sums[part].start()

    rows_exp = returned(2)
    output_out[...] = (
        middle_ref[...]
        + share_first * cols_cols(picks_ref[0], rows_exp)
        + share_second * cols_cols(picks_ref[1], rows_exp)
    ).astype(BF)

    grad_first = first_block(n)
    stat_first = high.astype(F32) + rest.astype(F32)
    total = jnp.zeros((token_count, 1), F32)
    for m in range(4):
        part = tokens_ref[m, 0:token_count, :].astype(F32)
        total = total + jnp.sum(part * part, 1, keepdims=True)
    scale_first = lax.rsqrt(total * (1.0 / full) + NORM_EPS)
    normed_first = tok_ref[...].astype(F32) * scale_first
    gain_first = tokens_ref[n, token_count : token_count + 1, :].astype(F32)
    for step in range(NEAR):
        links.land(col_recv.at[step], {"narrow": from_z[step]}, col_slots[step])
        stat_first = stat_first + (
            col_recv[step, :, 0:1].astype(F32) + col_recv[step, :, 1:2].astype(F32)
        )
    for step in range(NEAR):
        links.land(first_recv.at[step], {"narrow": from_z[step]}, first_slots[step])
        grad_first = grad_first + first_recv[step].astype(F32)
    grad_tokens_out[...] = grad_middle + scale_first * (
        gain_first * grad_first - normed_first * (stat_first * (1.0 / full))
    )
    gain_part = jnp.sum(grad_first * normed_first, 0, keepdims=True)
    for part in range(3):
        proj_sums[part].turn()
    last_mate[core] = jnp.broadcast_to(gain_part, (8, part_width))
    last_there = to_mate(last_mate.at[core], last_mate)

    for step in range(NEAR):
        links.land(small_recv.at[step], at_plane(plane[step]), small_slots[step])
        small = small + small_recv[step]
    last_there()
    last = last_mate[0] + last_mate[1]
    last_sum[...] = last
    last_slots = [links.slot() for _ in range(NEAR)]
    for step in range(NEAR):
        links.send(last_sum, last_recv.at[step], at_plane(plane[step]), last_slots[step])
    router_all[:, own_cols] = small
    router_slots = [links.slot() for _ in range(NEAR)]
    for step in range(NEAR):
        links.send(
            router_all.at[:, own_cols], router_all.at[:, own_cols], {"narrow": to_z[step]},
            router_slots[step],
        )
    for step in range(NEAR):
        links.land(last_recv.at[step], at_plane(plane[step]), last_slots[step])
        last = last + last_recv[step]
    small_out[...] = jnp.where(kind_at == 5, last, small)
    for step in range(NEAR):
        cols = pl.ds(pl.multiple_of(from_z[step] * part_width, part_width), part_width)
        links.land(router_all.at[:, cols], {"narrow": from_z[step]}, router_slots[step])

    router_out[...] = router_all[:, pl.ds(pl.multiple_of(w * rows_each, rows_each), rows_each)]
    for part in range(4):
        summed_out[:, part * part_width : (part + 1) * part_width] = proj_sums[part].total()
    for step in range(NEAR):
        links.land(expert_out.at[plane[step]], at_plane(plane[step]), expert_slots[step])
    links.finish()


def tail_call(*args):
    slots, part_width = args[0].shape
    half, hidden_width = args[4].shape
    token_count = args[10].shape[0]
    full, rows_each = 2 * half, half // 4
    vmem = pl.BlockSpec(memory_space=pltpu.VMEM)
    hbm = pl.BlockSpec(memory_space=pl.ANY)

    def arr(shape, dtype):
        return jax.ShapeDtypeStruct(shape, dtype)

    own = (token_count, part_width)
    return pl.pallas_call(
        tail_body,
        out_shape=(
            arr(own, BF),
            arr(own, F32),
            arr((rows_each, full), F32),
            arr((8, part_width), F32),
            arr((8, rows_each), F32),
            arr((4, rows_each, hidden_width), BF),
        ),
        in_specs=[vmem] * 4 + [hbm] * 2 + [vmem] * 5 + [hbm] * 3 + [vmem] * 2 + [hbm] * 3,
        out_specs=(vmem,) * 5 + (hbm,),
        scratch_shapes=[
            pltpu.VMEM((2, slots, token_count), BF),
            pltpu.VMEM((4, token_count + 16, part_width), BF),
            pltpu.VMEM((3,) + own, BF),
            pltpu.VMEM((part_width // HEAD_DIM, token_count, token_count), F32),
            pltpu.VMEM((token_count, full), BF),
            pltpu.VMEM(own, BF),
            pltpu.VMEM((slots, part_width), BF),
            pltpu.VMEM((slots, part_width), BF),
            pltpu.VMEM((8, full), F32),
            pltpu.VMEM((8, rows_each, 1664), BF),
            pltpu.VMEM((8, rows_each, part_width), BF),
            pltpu.VMEM((slots, part_width), BF),
            pltpu.VMEM((slots, part_width), BF),
            pltpu.VMEM((slots, 128), BF),
            pltpu.VMEM((token_count, full), BF),
            pltpu.VMEM((2, token_count, half), BF),
            pltpu.VMEM((2, token_count, half), BF),
            pltpu.VMEM((2, token_count, part_width), BF),
            pltpu.VMEM((2, token_count, 1536), BF),
            pltpu.VMEM((4, half, part_width), BF),
            pltpu.VMEM((4, NEAR, rows_each, part_width), BF),
            pltpu.VMEM((NEAR,) + own, BF),
            pltpu.VMEM((NEAR,) + own, BF),
            pltpu.VMEM((token_count, 128), BF),
            pltpu.VMEM((NEAR, token_count, 128), BF),
            pltpu.VMEM((2, 8, part_width), F32),
            pltpu.VMEM((8, part_width), F32),
            pltpu.VMEM((NEAR, 8, part_width), F32),
            pltpu.VMEM((2, 8, part_width), F32),
            pltpu.VMEM((8, part_width), F32),
            pltpu.VMEM((NEAR, 8, part_width), F32),
            pltpu.SemaphoreType.DMA((TAIL_SLOTS,)),
            pltpu.SemaphoreType.DMA((TAIL_SLOTS,)),
            pltpu.SemaphoreType.DMA((24,)),
        ],
        compiler_params=pltpu.CompilerParams(
            collective_id=2, has_side_effects=True, vmem_limit_bytes=60 * 1024 * 1024
        ),
        cost_estimate=pl.CostEstimate(
            flops=6_000_000_000, bytes_accessed=60_000_000, transcendentals=1_000
        ),
        name="tail",
    )(*args)


FINISH_ROWS = 128


def finish_body(
    early_ref, late_ref, output_ref, tokens_ref, summed_ref, small_ref, router_ref,
    gate_out, up_out, down_out, output_out, tokens_out, q_out, k_out, v_out, o_out,
    gain_first_out, gain_second_out, router_out,
    packed, spread, incoming, outgoing, passing,
):
    rows_each = packed.shape[2]
    width = tokens_ref.shape[1]
    sources = (early_ref.at[0], early_ref.at[1], late_ref)
    targets = (down_out, gate_out, up_out)
    loads = {}
    for kind in range(3):
        for part in range(rows_each // FINISH_ROWS):
            rows = pl.ds(part * FINISH_ROWS, FINISH_ROWS)
            loads[kind, part] = pltpu.make_async_copy(
                sources[kind].at[:, rows, :], packed.at[kind, :, rows, :], incoming.at[kind, part]
            )
            loads[kind, part].start()
    whole = [(output_ref, output_out), (tokens_ref, tokens_out)]
    for part, target in enumerate((q_out, k_out, v_out, o_out)):
        whole.append((summed_ref.at[:, pl.ds(part * width, width)], target))
    copies = [
        pltpu.make_async_copy(source, target, passing.at[index])
        for index, (source, target) in enumerate(whole)
    ]
    stores = []
    for (kind, part), load in loads.items():
        load.wait()

        def some_rows(index, value):
            first = pl.multiple_of(part * FINISH_ROWS + index * 16, 16)
            rows = pl.ds(first, 16)
            for expert in range(EXPERTS):
                spread[kind, rows, expert, :] = packed[kind, expert, rows, :].astype(F32)
            return value

        lax.fori_loop(0, FINISH_ROWS // 16, some_rows, 0)
        rows = pl.ds(part * FINISH_ROWS, FINISH_ROWS)
        stores.append(
            pltpu.make_async_copy(
                spread.at[kind, rows], targets[kind].at[rows], outgoing.at[kind, part]
            )
        )
        stores[-1].start()
        if kind == 0 and part == 0:
            for copy in copies:
                copy.start()
    for row, target in ((5, gain_first_out), (4, gain_second_out)):
        for index in range(width // 128):
            target[index : index + 1, :] = small_ref[
                row : row + 1, index * 128 : (index + 1) * 128
            ]
    router_out[...] = router_ref[0:EXPERTS, :]
    for copy in stores + copies:
        copy.wait()


def finish_call(early, late, output, grad_tokens, summed, small, router):
    _, rows_each, hidden_width = late.shape
    part_width = output.shape[1]
    vmem = pl.BlockSpec(memory_space=pltpu.VMEM)
    hbm = pl.BlockSpec(memory_space=pl.ANY)
    parts = rows_each // FINISH_ROWS

    def arr(shape, dtype):
        return jax.ShapeDtypeStruct(shape, dtype)

    return pl.pallas_call(
        finish_body,
        out_shape=(arr((rows_each, EXPERTS, hidden_width), F32),) * 3
        + (arr(output.shape, BF), arr(output.shape, F32))
        + (arr((rows_each, part_width), F32),) * 4
        + (arr((part_width // 128, 128), F32),) * 2
        + (arr((EXPERTS, rows_each), F32),),
        in_specs=[hbm] * 2 + [vmem] * 5,
        out_specs=(hbm,) * 9 + (vmem,) * 3,
        scratch_shapes=[
            pltpu.VMEM((3, EXPERTS, rows_each, hidden_width), BF),
            pltpu.VMEM((3, rows_each, EXPERTS, hidden_width), F32),
            pltpu.SemaphoreType.DMA((3, parts)),
            pltpu.SemaphoreType.DMA((3, parts)),
            pltpu.SemaphoreType.DMA((6,)),
        ],
        compiler_params=pltpu.CompilerParams(vmem_limit_bytes=56 * 1024 * 1024),
        name="finish",
    )(early, late, output, grad_tokens, summed, small, router)


def plain_device(
    tokens, gain_attn, w_query, w_key, w_value, w_out, gain_ffn, w_router,
    w_gate, w_up, w_down, segment, parents, expert_ids, slot_order, cotangent,
):
    narrow_count = lax.axis_size("narrow")
    wide_count = lax.axis_size("wide")
    narrow_at = lax.axis_index("narrow")
    token_count, part_width = tokens.shape
    full_width = part_width * narrow_count
    hidden_width = w_gate.shape[2]
    rows_each = w_gate.shape[0]
    blocks = wide_count // 8
    quads = [
        [8 * block + 2 * chip + core for chip in range(4)]
        for block in range(blocks)
        for core in range(2)
    ]
    mates = [
        [8 * block + 2 * chip + core for block in range(blocks) for core in range(2)]
        for chip in range(4)
    ]

    def quad_swap(array):
        return lax.all_to_all(array, "wide", 0, 0, axis_index_groups=quads, tiled=True)

    def own_rows(weight):
        moved = quad_swap(jnp.transpose(weight, (1, 0, 2)))
        joined = lax.all_gather(moved, "wide", axis=0, axis_index_groups=mates, tiled=True)
        joined = joined.reshape(blocks, 2, 4, rows_each, hidden_width).transpose(0, 2, 1, 3, 4)
        return joined.reshape(full_width, hidden_width)

    def share_rows(grad):
        parts = grad.astype(BF).reshape(blocks, 4, 2, rows_each, hidden_width)
        parts = parts.transpose(0, 2, 1, 3, 4).reshape(blocks * 2, 4, rows_each, hidden_width)
        summed = lax.psum_scatter(
            parts, "wide", scatter_dimension=0, axis_index_groups=mates, tiled=True
        )[0]
        return jnp.transpose(quad_swap(summed), (1, 0, 2)).astype(F32)

    def head_cols(array, head):
        return array[:, head * HEAD_DIM : (head + 1) * HEAD_DIM]

    heads = part_width // HEAD_DIM
    half_dim = HEAD_DIM // 2
    freqs = ROPE_BASE ** (-2.0 * jnp.arange(half_dim, dtype=F32) / HEAD_DIM)
    score_scale = HEAD_DIM ** (-0.5)
    gains = jnp.stack([gain_attn, gain_ffn])
    gain_first_loc = gain_attn.astype(F32)
    gain_second_loc = gain_ffn.astype(F32)
    hot_first, hot_second, kept, pick_first, pick_second = route(expert_ids, slot_order[0])

    gate_w, up_w, down_w = own_rows(w_gate), own_rows(w_up), own_rows(w_down)
    attn_w = lax.all_gather(
        jnp.stack([w_query, w_key, w_value, w_out], 1), "wide", axis=0, tiled=True
    )
    query_w, key_w, value_w, out_w = (attn_w[:, i] for i in range(4))
    router_w = lax.all_gather(w_router, "wide", axis=0, tiled=True)
    tokens_full = lax.all_gather(tokens, "narrow", axis=1, tiled=True)
    grad_full = lax.all_gather(cotangent, "narrow", axis=1, tiled=True)
    gains_full = lax.all_gather(gains, "narrow", axis=1, tiled=True)
    gain_first = gains_full[0].astype(F32)
    gain_second = gains_full[1].astype(F32)

    seen, places = tree_layout(segment[0], parents[0])
    pick_first_low = pick_first.astype(BF)
    pick_second_low = pick_second.astype(BF)
    pick_both_low = (pick_first | pick_second).astype(BF)

    inputs_full = tokens_full.astype(F32)
    scale_first = lax.rsqrt(jnp.mean(inputs_full * inputs_full, -1, keepdims=True) + NORM_EPS)
    normed_first = inputs_full * scale_first
    hidden_first = (normed_first * gain_first).astype(BF)
    angles = places[:, None] * freqs[None, :]
    cosines, sines = jnp.cos(angles), jnp.sin(angles)
    query_raw = rows_cols(hidden_first, query_w)
    key_raw = rows_cols(hidden_first, key_w)
    value_low = rows_cols(hidden_first, value_w).astype(BF)

    saved = []
    outs = []
    for head in range(heads):
        query = rotate(head_cols(query_raw, head), cosines, sines).astype(BF)
        key = rotate(head_cols(key_raw, head), cosines, sines).astype(BF)
        value = head_cols(value_low, head)
        scores = jnp.where(seen, rows_rows(query, key) * score_scale, NEG_FILL)
        exps = jnp.exp(scores - jnp.max(scores, -1, keepdims=True))
        weights = exps / jnp.sum(exps, -1, keepdims=True)
        saved.append((query, key, value, weights))
        outs.append(rows_cols(weights.astype(BF), value).astype(BF))
    attended = jnp.concatenate(outs, 1)
    branch_part = rows_rows(attended, out_w).astype(BF)
    branch_loc = lax.psum_scatter(
        branch_part, "narrow", scatter_dimension=1, tiled=True
    ).astype(F32)
    middle = tokens.astype(F32) + branch_loc
    middle_full = lax.all_gather(middle.astype(BF), "narrow", axis=1, tiled=True).astype(F32)
    scale_second = lax.rsqrt(jnp.mean(middle_full * middle_full, -1, keepdims=True) + NORM_EPS)
    normed_second = middle_full * scale_second
    hidden_second = (normed_second * gain_second).astype(BF)
    logits = rows_cols(hidden_second, router_w)
    share_first, share_second = gate_pair(logits, hot_first, hot_second)
    weight_first = kept[:, 0] * share_first
    weight_second = kept[:, 1] * share_second

    slot_weight = jnp.sum(
        pick_first * weight_first[:, None] + pick_second * weight_second[:, None], 0
    )
    weight_high, weight_low = two_parts(slot_weight)
    pads = jnp.stack([weight_high, weight_low], 1)
    pads = jnp.pad(pads, ((0, 0), (0, 126)))
    sent_hidden = cols_cols(pick_both_low, hidden_second).astype(BF)
    sent_grad = cols_cols(pick_both_low, grad_full).astype(BF)
    sent = jnp.concatenate([sent_hidden, sent_grad, pads], 1)
    got = quad_swap(sent.reshape(EXPERTS, CAP, -1)).reshape(SLOTS, -1)
    slot_hidden = got[:, :full_width]
    slot_grad = got[:, full_width : 2 * full_width]
    slot_gate = got[:, 2 * full_width : 2 * full_width + 2].astype(F32)
    slot_gate = slot_gate[:, 0:1] + slot_gate[:, 1:2]

    gate_pre = rows_cols(slot_hidden, gate_w)
    up_pre = rows_cols(slot_hidden, up_w)
    sigmoid_gate = jax.nn.sigmoid(gate_pre)
    silu_gate = gate_pre * sigmoid_gate
    activated = (silu_gate * up_pre).astype(BF)
    expert_part = rows_rows(activated, down_w)
    act_raw = rows_cols(slot_grad, down_w)
    share_part = jnp.sum(act_raw * activated.astype(F32), 1, keepdims=True)
    grad_act = act_raw * slot_gate
    grad_gate_pre = (
        grad_act * up_pre * sigmoid_gate * (1.0 + gate_pre * (1.0 - sigmoid_gate))
    ).astype(BF)
    grad_up_pre = (grad_act * silu_gate).astype(BF)
    grad_slot = rows_rows(grad_gate_pre, gate_w) + rows_rows(grad_up_pre, up_w)
    stat_part = jnp.sum(slot_hidden.astype(F32) * grad_slot, 1, keepdims=True)
    extras = jnp.concatenate([*two_parts(share_part), *two_parts(stat_part)], 1)
    extras = jnp.pad(extras, ((0, 0), (0, 124)))
    back_parts = []
    expert_plain = expert_part.astype(BF)
    slot_plain = grad_slot.astype(BF)
    for part in range(narrow_count):
        cols = slice(part * part_width, (part + 1) * part_width)
        back_parts += [expert_plain[:, cols], slot_plain[:, cols], extras]
    back = lax.psum_scatter(
        jnp.concatenate(back_parts, 1), "narrow", scatter_dimension=1, tiled=True
    )
    back = quad_swap(back.reshape(EXPERTS, CAP, -1)).reshape(SLOTS, -1)
    picked_first = rows_cols(pick_first_low, back)
    picked_second = rows_cols(pick_second_low, back)
    output = (
        middle
        + weight_first[:, None] * picked_first[:, :part_width]
        + weight_second[:, None] * picked_second[:, :part_width]
    ).astype(BF)

    grad_weight = (slot_grad.astype(F32) * slot_gate).astype(BF)
    gate_out = share_rows(cols_cols(slot_hidden, grad_gate_pre))
    up_out = share_rows(cols_cols(slot_hidden, grad_up_pre))
    down_out = share_rows(cols_cols(grad_weight, activated))

    tail = 2 * part_width
    share_first_grad = picked_first[:, tail] + picked_first[:, tail + 1]
    share_second_grad = picked_second[:, tail] + picked_second[:, tail + 1]
    both = picked_first + picked_second
    stat_second = both[:, tail + 2] + both[:, tail + 3]
    grad_hidden_loc = both[:, part_width:tail]
    grad_local = cotangent.astype(F32)
    _, pull_gates = jax.vjp(lambda given: gate_pair(given, hot_first, hot_second), logits)
    (grad_logits,) = pull_gates((kept[:, 0] * share_first_grad, kept[:, 1] * share_second_grad))
    grad_logits_low = grad_logits.astype(BF)
    grad_router_rows = rows_rows(grad_logits_low, router_w)
    stat_total = stat_second + jnp.sum(normed_second * gain_second * grad_router_rows, 1)

    def take_cols(full_rows):
        return lax.dynamic_slice_in_dim(full_rows, narrow_at * part_width, part_width, 1)

    grad_hidden_loc = grad_hidden_loc + take_cols(grad_router_rows)
    normed_second_loc = take_cols(normed_second)
    grad_gain_second = jnp.sum(grad_hidden_loc * normed_second_loc, 0)
    grad_middle = grad_local + scale_second * (
        gain_second_loc * grad_hidden_loc - normed_second_loc * stat_total[:, None] / full_width
    )
    grad_router_w = cols_cols(hidden_second, grad_logits_low)
    grad_branch = lax.all_gather(grad_middle.astype(BF), "narrow", axis=1, tiled=True)
    grad_attended = rows_cols(grad_branch, out_w).astype(BF)
    grad_out_w = cols_cols(grad_branch, attended)
    grad_qs, grad_ks, grad_vs = [], [], []
    for head in range(heads):
        query, key, value, weights = saved[head]
        grad_out = head_cols(grad_attended, head)
        grad_weights = rows_rows(grad_out, value)
        inner = jnp.sum(weights * grad_weights, -1, keepdims=True)
        grad_scores = (weights * (grad_weights - inner)).astype(BF)
        grad_q = rows_cols(grad_scores, key) * score_scale
        grad_k = cols_cols(grad_scores, query) * score_scale
        grad_qs.append(rotate(grad_q, cosines, -sines).astype(BF))
        grad_ks.append(rotate(grad_k, cosines, -sines).astype(BF))
        grad_vs.append(cols_cols(weights.astype(BF), grad_out).astype(BF))
    grad_query_raw = jnp.concatenate(grad_qs, 1)
    grad_key_raw = jnp.concatenate(grad_ks, 1)
    grad_value_raw = jnp.concatenate(grad_vs, 1)
    grad_hidden_first = (
        rows_rows(grad_query_raw, query_w)
        + rows_rows(grad_key_raw, key_w)
        + rows_rows(grad_value_raw, value_w)
    )
    stat_first = jnp.sum(normed_first * gain_first * grad_hidden_first, 1, keepdims=True)
    extras = jnp.pad(jnp.concatenate(two_parts(stat_first), 1), ((0, 0), (0, 126)))
    grad_hidden_low = grad_hidden_first.astype(BF)
    first_parts = []
    for part in range(narrow_count):
        first_parts += [grad_hidden_low[:, part * part_width : (part + 1) * part_width], extras]
    first_back = lax.psum_scatter(
        jnp.concatenate(first_parts, 1), "narrow", scatter_dimension=1, tiled=True
    ).astype(F32)
    grad_first_loc = first_back[:, :part_width]
    stat_first = first_back[:, part_width : part_width + 1]
    stat_first = stat_first + first_back[:, part_width + 1 : part_width + 2]
    normed_first_loc = take_cols(normed_first)
    grad_gain_first = jnp.sum(grad_first_loc * normed_first_loc, 0)
    grad_tokens = grad_middle + scale_first * (
        gain_first_loc * grad_first_loc - normed_first_loc * stat_first / full_width
    )
    grad_attn_w = jnp.concatenate(
        [
            cols_cols(hidden_first, grad_query_raw).astype(BF),
            cols_cols(hidden_first, grad_key_raw).astype(BF),
            cols_cols(hidden_first, grad_value_raw).astype(BF),
            grad_out_w.astype(BF),
        ],
        1,
    )
    attn_summed = lax.psum_scatter(
        grad_attn_w, "wide", scatter_dimension=0, tiled=True
    ).astype(F32)
    router_summed = lax.psum_scatter(grad_router_w, "wide", scatter_dimension=0, tiled=True)
    gains_summed = lax.psum(jnp.stack([grad_gain_first, grad_gain_second]), "wide")
    return (
        output,
        grad_tokens,
        gains_summed[0],
        attn_summed[:, :part_width],
        attn_summed[:, part_width : 2 * part_width],
        attn_summed[:, 2 * part_width : 3 * part_width],
        attn_summed[:, 3 * part_width :],
        gains_summed[1],
        router_summed,
        gate_out,
        up_out,
        down_out,
    )


def per_device(
    tokens, gain_attn, w_query, w_key, w_value, w_out, gain_ffn, w_router,
    w_gate, w_up, w_down, segment, parents, expert_ids, slot_order, cotangent,
):
    if lax.axis_size("wide") != 8 or lax.axis_size("narrow") != 4:
        return plain_device(
            tokens, gain_attn, w_query, w_key, w_value, w_out, gain_ffn, w_router,
            w_gate, w_up, w_down, segment, parents, expert_ids, slot_order, cotangent,
        )
    (
        in_w, out_w, expert_w, slot_mid, slot_grad, slot_gate, middle, hidden_first,
        token_parts, qkv, probs, attended, stat, rope, picks, columns,
    ) = front_call(
        tokens, cotangent, gain_attn, gain_ffn, (w_query, w_key, w_value, w_out),
        w_router.T, (w_gate, w_up, w_down), segment, parents, expert_ids.T, slot_order,
    )
    back_mid, back_exp, last_exp, back_ext, grads, early_experts = mid_call(
        slot_mid, slot_grad, slot_gate, token_parts, expert_w
    )
    (
        output, grad_tokens, summed, small, router, experts,
    ) = tail_call(
        back_mid, back_exp, last_exp, back_ext, grads, picks, stat, columns, middle, cotangent, tokens,
        token_parts, qkv, probs, attended, rope, hidden_first, in_w, out_w,
    )
    (
        gate_out, up_out, down_out, output, grad_tokens, grad_q, grad_k, grad_v, grad_o,
        grad_gain_first, grad_gain_second, router,
    ) = finish_call(early_experts, experts, output, grad_tokens, summed, small, router)
    return (
        output, grad_tokens, grad_gain_first.reshape(-1), grad_q, grad_k, grad_v, grad_o,
        grad_gain_second.reshape(-1), router.T, gate_out, up_out, down_out,
    )


def solution(mesh):
    pair = P("wide", "narrow")
    part = P("narrow")
    rows = P("wide", None)
    cube = P("wide", None, "narrow")
    return jax.shard_map(
        per_device,
        mesh=mesh,
        in_specs=(
            pair, part, pair, pair, pair, pair, part, rows, cube, cube, cube,
            rows, rows, rows, rows, pair,
        ),
        out_specs=(
            pair, pair, part, pair, pair, pair, pair, part, rows, cube, cube, cube,
        ),
        check_vma=False,
    )
```

```python
import math

import jax
import jax.numpy as jnp
from jax import lax
from jax.experimental import pallas as pl
from jax.experimental.pallas import tpu as pltpu
from jax.sharding import PartitionSpec as P

HEAD_DIM = 128
EXPERTS = 4
SEGS = 13
CAP = 144
SLOTS = EXPERTS * CAP
NORM_EPS = 1e-05
NEG_FILL = -1e30
ROPE_BASE = 10000.0
BF = jnp.bfloat16
F32 = jnp.float32


def mm(left, right, dims):
    return lax.dot_general(left, right, (dims, ((), ())), preferred_element_type=F32)


def rows_cols(left, right):
    return mm(left, right, ((1,), (0,)))


def rows_rows(left, right):
    return mm(left, right, ((1,), (1,)))


def cols_cols(left, right):
    return mm(left, right, ((0,), (0,)))


def tree_layout(segment_row, parent_row):
    seg_ids = jnp.arange(SEGS, dtype=jnp.int32)
    member = segment_row[:, None] == seg_ids[None, :]
    parent_of = (parent_row[:, None] == seg_ids[None, :]) & (seg_ids[:, None] != 0)
    itself = seg_ids[:, None] == seg_ids[None, :]
    reach = itself
    for _ in range(3):
        reach = itself | jnp.any(parent_of[:, :, None] & reach[None, :, :], axis=1)
    counts = member.astype(jnp.int32)
    lengths = jnp.sum(counts, 0)
    starts = jnp.sum(jnp.where(seg_ids[None, :] < seg_ids[:, None], lengths[None, :], 0), 1)
    before = jnp.sum(jnp.where(reach, lengths[None, :], 0), 1) - lengths
    row_at = jnp.arange(segment_row.shape[0], dtype=jnp.int32)
    places = jnp.sum(counts * (before - starts)[None, :], 1) + row_at
    member_low = member.astype(BF)
    lineage = rows_cols(member_low, reach.astype(BF)).astype(BF)
    shared = rows_rows(lineage, member_low) > 0.5
    seen = shared & (row_at[None, :] <= row_at[:, None])
    return seen, places.astype(F32)


def route(expert_row, slot_rank):
    expert_range = jnp.arange(EXPERTS, dtype=jnp.int32)
    hot_first = (expert_row[:, 0:1] == expert_range[None, :]).astype(F32)
    hot_second = (expert_row[:, 1:2] == expert_range[None, :]).astype(F32)
    earlier = (slot_rank[None, :] < slot_rank[:, None]).astype(BF)
    count_first = rows_cols(earlier, hot_first.astype(BF))
    count_second = rows_cols(earlier, hot_second.astype(BF))
    ahead_first = jnp.sum(count_first * hot_first, 1)
    ahead_second = jnp.sum((count_second + jnp.sum(hot_first, 0)[None, :]) * hot_second, 1)
    slot_index = jnp.stack([ahead_first, ahead_second], 1).astype(jnp.int32)
    kept = slot_index < CAP
    flat_slot = jnp.where(kept, expert_row * CAP + slot_index, SLOTS)
    slot_range = jnp.arange(SLOTS, dtype=jnp.int32)
    pick_first = flat_slot[:, 0:1] == slot_range[None, :]
    pick_second = flat_slot[:, 1:2] == slot_range[None, :]
    return hot_first, hot_second, kept.astype(F32), pick_first, pick_second


def rotate(vectors, cosines, sines):
    half_dim = HEAD_DIM // 2
    first_half = vectors[..., :half_dim]
    second_half = vectors[..., half_dim:]
    return jnp.concatenate(
        [
            first_half * cosines - second_half * sines,
            second_half * cosines + first_half * sines,
        ],
        -1,
    )


def gate_pair(logits, hot_first, hot_second):
    chances = jax.nn.softmax(logits, axis=-1)
    first_share = jnp.sum(chances * hot_first, 1)
    second_share = jnp.sum(chances * hot_second, 1)
    pair_total = first_share + second_share
    return (first_share / pair_total, second_share / pair_total)


def two_parts(column):
    high = column.astype(BF)
    return high, (column - high.astype(F32)).astype(BF)


MESH = pl.DeviceIdType.MESH
NEAR = 3


def low_dot(left, right):
    return jnp.dot(left, right, preferred_element_type=F32)


def places_of(n):
    return [lax.rem(n + step, 4) for step in (1, 2, 3)], [lax.rem(n + 4 - step, 4) for step in (1, 2, 3)]


def plane_of(chip):
    x, y = lax.rem(chip, 2), chip // 2
    return [2 * y + 1 - x, 2 * (1 - y) + x, 2 * (1 - y) + 1 - x]


def greet(narrow_peers, plane_peers, chip, core, mate):
    barrier = pltpu.get_barrier_semaphore()
    count = 0
    for peer in narrow_peers:
        pl.semaphore_signal(barrier, inc=1, device_id={"narrow": peer}, device_id_type=MESH)
        count += 1
    for peer in plane_peers:
        pl.semaphore_signal(
            barrier, inc=1, device_id={"wide": 2 * peer + core}, device_id_type=MESH
        )
        count += 1
    if mate:
        pl.semaphore_signal(
            barrier, inc=1, device_id={"wide": 2 * chip + 1 - core}, device_id_type=MESH
        )
        count += 1
    pl.semaphore_wait(barrier, count)


class Links:
    def __init__(self, sent, landed, local):
        self.sent, self.landed, self.local = sent, landed, local
        self.used, self.local_used = 0, 0
        self.waits = []

    def slot(self):
        self.used += 1
        return self.used - 1

    def send(self, source, target, device, slot, when=None):
        copy = pltpu.make_async_remote_copy(
            src_ref=source,
            dst_ref=target,
            send_sem=self.sent.at[slot],
            recv_sem=self.landed.at[slot],
            device_id=device,
            device_id_type=MESH,
        )
        if when is None:
            copy.start()
        else:
            pl.when(when)(copy.start)
        self.waits.append((copy, when))

    def land(self, target, device, slot, when=None):
        copy = pltpu.make_async_remote_copy(
            src_ref=target,
            dst_ref=target,
            send_sem=self.sent.at[slot],
            recv_sem=self.landed.at[slot],
            device_id=device,
            device_id_type=MESH,
        )
        if when is None:
            copy.wait_recv()
        else:
            pl.when(when)(copy.wait_recv)

    def move(self, source, target):
        copy = pltpu.make_async_copy(source, target, self.local.at[self.local_used])
        self.local_used += 1
        copy.start()
        self.waits.append((copy, "local"))
        return copy

    def finish(self):
        for copy, when in self.waits:
            if when == "local":
                copy.wait()
            elif when is None:
                copy.wait_send()
            else:
                pl.when(when)(copy.wait_send)


class Chain:
    def __init__(self, links, n, block):
        self.links, self.n, self.block = links, n, block
        self.slots = [(links.slot(), links.slot()) for _ in range(3)]

    def start(self, step):
        n, links = self.n, self.links
        right, left = self.slots[step]
        block = self.block(lax.rem(n + 4 - step, 4))
        links.send(
            block, block, {"narrow": lax.rem(n + 1, 4)}, right,
            (n < 3) & (n >= step),
        )
        block = self.block(lax.rem(n + step, 4))
        links.send(
            block, block, {"narrow": lax.rem(n + 3, 4)}, left,
            (n > 0) & (n + step <= 3),
        )

    def land(self, step):
        n, links = self.n, self.links
        right, left = self.slots[step]
        links.land(
            self.block(lax.rem(n + 7 - step, 4)), {"narrow": lax.rem(n + 3, 4)}, right,
            n >= step + 1,
        )
        links.land(
            self.block(lax.rem(n + 1 + step, 4)), {"narrow": lax.rem(n + 1, 4)}, left,
            n + 1 + step <= 3,
        )


class LineSum:
    def __init__(self, links, n, outbox, inbox):
        self.links, self.n, self.outbox, self.inbox = links, n, outbox, inbox
        self.inner = (n == 1) | (n == 2)
        self.outer = (n == 0) | (n == 3)
        self.targets = [self.owner(step) for step in range(NEAR)]
        self.next = 1 + lax.rem(n, 2)
        self.slots = [links.slot() for _ in range(6)]

    def owner(self, step):
        return lax.rem((4 - step) * self.n + (3 - step), 5)

    def put(self, step, part):
        self.outbox[step] = part.astype(BF)
        self.set_out(step)

    def set_out(self, step):
        links, outbox, inbox = self.links, self.outbox, self.inbox
        goal = {"narrow": self.next if step == 0 else self.targets[step]}
        far, near = self.slots[2 * step], self.slots[2 * step + 1]
        if step == 0:
            links.send(outbox.at[0], inbox.at[3], goal, far, self.outer)
            links.send(outbox.at[0], inbox.at[0], goal, near, self.inner)
        elif step == 1:
            links.send(outbox.at[1], inbox.at[1], goal, far, self.outer)
            links.send(outbox.at[1], inbox.at[0], goal, near, self.inner)
        else:
            links.send(outbox.at[2], inbox.at[2], goal, far, self.outer)

    def join(self):
        links, outbox, inbox = self.links, self.outbox, self.inbox
        home = {"narrow": 3 * (self.n // 2)}
        links.land(inbox.at[3], home, self.slots[0], self.inner)

        @pl.when(self.inner)
        def _():
            outbox[2] = (outbox[2].astype(F32) + inbox[3].astype(F32)).astype(BF)

    def relay(self):
        self.join()
        goal = {"narrow": self.targets[2]}
        self.links.send(
            self.outbox.at[2], self.inbox.at[1], goal, self.slots[5], self.inner
        )

    def early(self, own):
        links, inbox = self.links, self.inbox
        other = {"narrow": lax.rem(self.n + 1, 4)}
        links.land(inbox.at[0], other, self.slots[1], self.inner)
        links.land(inbox.at[0], other, self.slots[3], self.outer)
        links.land(inbox.at[1], other, self.slots[2], self.inner)

        @pl.when(self.outer)
        def _():
            inbox[1] = jnp.zeros(inbox.shape[1:], BF)

        return own + inbox[0].astype(F32) + inbox[1].astype(F32)

    def total(self, own):
        links, inbox = self.links, self.inbox
        outer, inner = self.outer, self.inner
        other = {"narrow": lax.rem(self.n + 1, 4)}
        links.land(inbox.at[0], other, self.slots[1], inner)
        links.land(inbox.at[0], other, self.slots[3], outer)
        links.land(inbox.at[1], other, self.slots[2], inner)
        links.land(inbox.at[1], other, self.slots[5], outer)
        links.land(inbox.at[2], other, self.slots[4], inner)

        @pl.when(outer)
        def _():
            inbox[2] = jnp.zeros(inbox.shape[1:], BF)

        for index in range(3):
            own = own + inbox[index].astype(F32)
        return own


class PlaneGather:
    def __init__(self, links, chip, core, plane, mate, source, blocks):
        self.links, self.chip, self.core, self.plane, self.mate = links, chip, core, plane, mate
        self.blocks = blocks
        self.slots = [links.slot() for _ in range(4)]
        self.mate_slots = [links.slot() for _ in range(4)]
        own = 2 * chip + core
        for side in range(2):
            links.send(source, blocks.at[own], self.at_plane(plane[side]), self.slots[side])
        links.send(source, blocks.at[own], mate, self.mate_slots[3])

    def at_plane(self, peer):
        return {"wide": 2 * peer + self.core}

    def half(self, peer, side):
        rows = self.blocks.shape[1] // 2
        return self.blocks.at[2 * peer + self.core, pl.ds(side * rows, rows), :]

    def pass_on(self):
        links, plane = self.links, self.plane
        for side in range(2):
            block = self.blocks.at[2 * plane[side] + self.core]
            links.land(block, self.at_plane(plane[side]), self.slots[side])
            part = self.half(plane[side], side)
            links.send(part, part, self.at_plane(plane[1 - side]), self.slots[2 + side])
            links.send(block, block, self.mate, self.mate_slots[side])

    def far(self):
        links, plane = self.links, self.plane
        for side in range(2):
            links.land(
                self.half(plane[2], side), self.at_plane(plane[1 - side]), self.slots[2 + side]
            )
        block = self.blocks.at[2 * plane[2] + self.core]
        links.send(block, block, self.mate, self.mate_slots[2])

    def finish(self):
        links, plane = self.links, self.plane
        for step in range(NEAR):
            block = self.blocks.at[2 * plane[step] + 1 - self.core]
            links.land(block, self.mate, self.mate_slots[step])
        links.land(self.blocks.at[2 * self.chip + 1 - self.core], self.mate, self.mate_slots[3])


FRONT_SLOTS = 112


def front_body(
    tok_ref, cot_ref, gain_first_ref, gain_second_ref, wq_ref, wk_ref, wv_ref, wo_ref, router_ref, gate_ref, up_ref,
    down_ref, segment_ref, parents_ref, ids_ref, rank_ref,
    qkvw_out, outw_out, expert_out, x_out, dy_out, gate_out, middle_out, hidden_hbm,
    tokens_hbm, qkv_hbm, prob_hbm, att_out, stat_out, rope_out, pick_hbm, cols_out,
    hidden_out, tokens_out, qkv_out, prob_out, pick_out,
    raw_proj, seen_at, raw, moved_ref, pack, tok_pack, qkvw, outw, cot_send, y_send, br_send,
    br_recv, stat_send, stat_recv, gate_send, sent, landed, local,
):
    n = lax.axis_index("narrow")
    w = lax.axis_index("wide")
    chip, core = w // 2, lax.rem(w, 2)
    to_z, from_z = places_of(n)
    plane = plane_of(chip)
    links = Links(sent, landed, local)
    mate = {"wide": 2 * chip + 1 - core}

    def at_plane(peer):
        return {"wide": 2 * peer + core}

    token_count, part_width = tok_ref.shape
    rows_each = raw.shape[1]
    raw_loads = [
        links.move(source, raw.at[kind_at]) for kind_at, source in enumerate((gate_ref, up_ref, down_ref))
    ]
    links.waits = []
    greet(to_z, plane, chip, core, True)

    def by_expert(kind_at):
        raw_loads[kind_at].wait()

        def some_rows(index, value):
            rows = pl.ds(pl.multiple_of(index * 32, 32), 32)
            for expert in range(EXPERTS):
                moved_ref[kind_at, expert, rows, :] = raw[kind_at, rows, expert, :]
            return value

        lax.fori_loop(0, rows_each // 32, some_rows, 0)

    tok_pack[0:token_count, :] = tok_ref[...]
    for index, gain_ref in enumerate((gain_first_ref, gain_second_ref)):
        for row in range(part_width // 128):
            tok_pack[
                token_count + index : token_count + index + 1, row * 128 : (row + 1) * 128
            ] = gain_ref[row : row + 1, :]
    tokens_out[n] = tok_pack[...]
    tok_chain = Chain(links, n, lambda m: tokens_out.at[m])
    tok_chain.start(0)
    wide_shape = (token_count, token_count)
    row_at = lax.broadcasted_iota(jnp.int32, wide_shape, 0)
    col_at = lax.broadcasted_iota(jnp.int32, wide_shape, 1)
    seg_row, rank_row = segment_ref[...], rank_ref[...]
    first_row, second_row = ids_ref[0:1, :], ids_ref[1:2, :]
    stacked = [item.astype(F32) for item in (seg_row, rank_row, first_row, second_row)]
    columns = jnp.concatenate(stacked + [jnp.zeros((124, token_count), F32)], 0).T
    cols_out[...] = columns
    columns = columns.astype(jnp.int32)
    seg_col, rank_col = columns[:, 0:1], columns[:, 1:2]
    segs = parents_ref.shape[1]
    of_seg = lax.broadcasted_iota(jnp.int32, (token_count, segs), 1) == seg_col
    par_col = jnp.sum(
        jnp.where(of_seg, parents_ref[...].astype(F32), 0.0), 1, keepdims=True
    ).astype(jnp.int32)
    seen = ((seg_row == seg_col) | (seg_row == par_col) | (seg_row == 0)) & (col_at <= row_at)
    spots = jnp.sum(jnp.where(seen, 1.0, 0.0), 1, keepdims=True) - 1.0
    lane_at = lax.broadcasted_iota(jnp.int32, (token_count, HEAD_DIM), 1)
    turn = lax.rem(lane_at, HEAD_DIM // 2).astype(F32) * (-2.0 / HEAD_DIM * math.log(ROPE_BASE))
    angles = spots * jnp.exp(turn)
    cosines = jnp.cos(angles)
    sines = jnp.sin(angles) * jnp.where(lane_at < HEAD_DIM // 2, -1.0, 1.0)
    rope_out[0] = cosines
    rope_out[1] = sines
    kind = lax.broadcasted_iota(jnp.int32, (8, token_count), 0)
    hot_first = jnp.where(kind == first_row, 1.0, 0.0)
    hot_second = jnp.where(kind == second_row, 1.0, 0.0)
    earlier = jnp.where(rank_col < rank_row, 1.0, 0.0).astype(BF)
    count_first = low_dot(hot_first.astype(BF), earlier)
    count_second = low_dot(hot_second.astype(BF), earlier)
    count_second = count_second + jnp.sum(hot_first, 1, keepdims=True)
    slot_first = jnp.sum(count_first * hot_first, 0, keepdims=True)
    slot_second = jnp.sum(count_second * hot_second, 0, keepdims=True)
    kept_first = jnp.where(slot_first < CAP, 1.0, 0.0)
    kept_second = jnp.where(slot_second < CAP, 1.0, 0.0)
    flat_first = jnp.where(slot_first < CAP, first_row * CAP + slot_first.astype(jnp.int32), SLOTS)
    flat_second = jnp.where(
        slot_second < CAP, second_row * CAP + slot_second.astype(jnp.int32), SLOTS
    )
    slot_at = lax.broadcasted_iota(jnp.int32, (SLOTS, token_count), 0)
    pick_first = jnp.where(slot_at == flat_first, 1.0, 0.0)
    pick_second = jnp.where(slot_at == flat_second, 1.0, 0.0)
    pick_out[0] = pick_first.astype(BF)
    pick_out[1] = pick_second.astype(BF)
    pick_both = (pick_first + pick_second).astype(BF)

    def column_block(array):
        return lambda m: array.at[:, pl.ds(pl.multiple_of(m * part_width, part_width), part_width)]

    def slot_block(array, owner):
        return array.at[
            pl.ds(pl.multiple_of(owner * CAP, 16), CAP),
            pl.ds(pl.multiple_of(n * part_width, part_width), part_width),
        ]

    def dispatch(rows, buffer, array):
        slots = [links.slot() for _ in range(NEAR)]
        buffer[...] = low_dot(pick_both, rows).astype(BF)
        for step in range(NEAR):
            links.send(
                buffer.at[pl.ds(pl.multiple_of(plane[step] * CAP, 16), CAP), :],
                slot_block(array, chip), at_plane(plane[step]), slots[step],
            )
        own = links.move(
            buffer.at[pl.ds(pl.multiple_of(chip * CAP, 16), CAP), :], slot_block(array, chip)
        )
        return slots, own

    def arrive(array, state):
        slots, own = state
        for step in range(NEAR):
            links.land(slot_block(array, plane[step]), at_plane(plane[step]), slots[step])
        own.wait()
        links.waits = [item for item in links.waits if item[0] is not own]

    dy_state = dispatch(cot_ref[...], cot_send, dy_out)
    dy_chain = Chain(links, n, column_block(dy_out))

    pack[:, 0:512] = wq_ref[...]
    pack[:, 512:1024] = wk_ref[...]
    pack[:, 1024:1536] = wv_ref[...]
    router_rows = jnp.concatenate(
        [router_ref[...].astype(F32), jnp.zeros((128 - EXPERTS, rows_each), F32)], 0
    )
    pack[:, 1536:1664] = router_rows.T.astype(BF)
    in_gather = PlaneGather(links, chip, core, plane, mate, pack, qkvw)
    qkvw[w] = pack[...]
    outw[w] = wo_ref[...]

    tok_chain.land(0)
    tok_chain.start(1)
    by_expert(0)
    tok_chain.land(1)
    tok_chain.start(2)
    arrive(dy_out, dy_state)
    dy_chain.start(0)
    tok_chain.land(2)
    in_gather.pass_on()
    out_gather = PlaneGather(links, chip, core, plane, mate, wo_ref, outw)
    total = jnp.zeros((token_count, 1), F32)
    for m in range(4):
        part = tokens_out[m, 0:token_count, :].astype(F32)
        total = total + jnp.sum(part * part, 1, keepdims=True)
    scale_first = lax.rsqrt(total * (1.0 / (4 * part_width)) + NORM_EPS)
    for m in range(4):
        part = tokens_out[m, 0:token_count, :].astype(F32)
        gain = tokens_out[m, token_count : token_count + 1, :].astype(F32)
        hidden_out[:, m * part_width : (m + 1) * part_width] = (part * scale_first * gain).astype(BF)

    by_expert(1)

    in_gather.far()
    out_gather.pass_on()
    in_gather.finish()
    saved_in = links.move(qkvw, qkvw_out)

    pieces = ((0, 0, rows_each), (1, 0, rows_each)) + tuple(
        (2, half * rows_each // 2, rows_each // 2) for half in range(2)
    )
    expert_slots = [[links.slot() for _ in range(NEAR)] for _ in pieces]
    expert_mate = [[links.slot() for _ in range(4)] for _ in pieces]

    def piece_of(array, index):
        return array.at[pl.ds(pieces[index][1], pieces[index][2]), :]

    def landing(index, owner, side):
        return piece_of(expert_out.at[pieces[index][0], owner, side], index)

    def set_out(index):
        kind_at = pieces[index][0]
        for step in range(NEAR):
            links.send(
                piece_of(moved_ref.at[kind_at, plane[step]], index), landing(index, chip, core),
                at_plane(plane[step]), expert_slots[index][step],
            )
        own = piece_of(moved_ref.at[kind_at, chip], index)
        links.send(own, landing(index, chip, core), mate, expert_mate[index][3])
        links.move(own, landing(index, chip, core))

    set_out(0)
    set_out(1)

    def pass_on(index):
        for step in range(NEAR):
            block = landing(index, plane[step], core)
            links.land(block, at_plane(plane[step]), expert_slots[index][step])
            links.send(block, block, mate, expert_mate[index][step])

    def all_there(index):
        for step in range(NEAR):
            links.land(landing(index, plane[step], 1 - core), mate, expert_mate[index][step])
        links.land(landing(index, chip, 1 - core), mate, expert_mate[index][3])

    dy_chain.land(0)
    dy_chain.start(1)
    by_expert(2)

    score_scale = HEAD_DIM ** (-0.5)

    def one_projection(part, value):
        cols = pl.ds(pl.multiple_of(part * part_width, part_width), part_width)
        weight = qkvw[:, :, cols].reshape(4 * part_width, part_width)
        raw_proj[part] = low_dot(hidden_out[...], weight)
        return value

    lax.fori_loop(0, 3, one_projection, 0)
    seen_at[...] = jnp.where(seen, 1.0, 0.0)

    def one_head(head, value):
        cols = pl.ds(pl.multiple_of(head * HEAD_DIM, HEAD_DIM), HEAD_DIM)
        turned = []
        for part in range(2):
            proj = raw_proj[part, :, cols]
            turned.append(
                (proj * rope_out[0] + pltpu.roll(proj, HEAD_DIM // 2, 1) * rope_out[1]).astype(BF)
            )
            qkv_out[part, :, cols] = turned[part]
        values = raw_proj[2, :, cols].astype(BF)
        qkv_out[2, :, cols] = values
        scores = rows_rows(turned[0], turned[1]) * score_scale
        scores = jnp.where(seen_at[...] > 0.5, scores, NEG_FILL)
        exps = jnp.exp(scores - jnp.max(scores, 1, keepdims=True))
        weights = exps / jnp.sum(exps, 1, keepdims=True)
        prob_out[head] = weights
        att_out[:, cols] = low_dot(weights.astype(BF), values).astype(BF)
        return value

    lax.fori_loop(0, part_width // HEAD_DIM, one_head, 0)
    for source, target in (
        (hidden_out, hidden_hbm), (tokens_out, tokens_hbm), (qkv_out, qkv_hbm),
        (prob_out, prob_hbm), (pick_out, pick_hbm),
    ):
        links.move(source, target)

    dy_chain.land(1)
    dy_chain.start(2)
    out_gather.far()

    out_gather.finish()
    links.move(outw, outw_out)

    attended = att_out[...]

    def branch(m):
        weight = outw[pl.ds(2 * m, 2)].reshape(part_width, part_width)
        return rows_rows(attended, weight)

    branch_sum = LineSum(links, n, br_send, br_recv)
    for step in range(NEAR):
        branch_sum.put(step, branch(branch_sum.targets[step]))
    middle = tok_ref[...].astype(F32) + branch(n)
    branch_sum.relay()
    middle = branch_sum.total(middle)
    middle_out[...] = middle
    x_state = dispatch(middle.astype(BF), y_send, x_out)

    def cap_block(owner):
        return lambda m: x_out.at[
            pl.ds(pl.multiple_of(owner * CAP, 16), CAP),
            pl.ds(pl.multiple_of(m * part_width, part_width), part_width),
        ]

    x_chains = [Chain(links, n, cap_block(owner)) for owner in (chip, *plane)]
    x_slots, x_own = x_state
    x_own.wait()
    links.waits = [item for item in links.waits if item[0] is not x_own]
    x_chains[0].start(0)

    set_out(2)
    set_out(3)

    gain_second = tok_pack[token_count + 1 : token_count + 2, :].astype(F32)
    router = qkvw[pl.ds(2 * n, 2), :, 1536:1664].reshape(part_width, 128)
    logit_part = mm(router, (middle * gain_second).astype(BF), ((0,), (1,)))[0:8, :]
    square = middle * middle
    square_high = square.astype(BF)
    square_low = (square - square_high.astype(F32)).astype(BF)
    ones = jnp.ones((8, part_width), BF)
    square_sum = rows_rows(ones, square_high) + rows_rows(ones, square_low)
    stat = jnp.where(kind == 4, square_sum, logit_part)
    stat_send[...] = stat
    stat_slots = [links.slot() for _ in range(NEAR)]
    for step in range(NEAR):
        links.send(stat_send, stat_recv.at[step], {"narrow": to_z[step]}, stat_slots[step])

    for step in range(NEAR):
        links.land(slot_block(x_out, plane[step]), at_plane(plane[step]), x_slots[step])
        x_chains[1 + step].start(0)
    for step in range(NEAR):
        links.land(stat_recv.at[step], {"narrow": from_z[step]}, stat_slots[step])
        stat = stat + stat_recv[step]
    stat_out[...] = stat
    scale_row = lax.rsqrt(stat[4:5, :] * (1.0 / (4 * part_width)) + NORM_EPS)
    logits = jnp.where(kind < EXPERTS, stat * scale_row, NEG_FILL)
    chances = jnp.exp(logits - jnp.max(logits, 0, keepdims=True))
    chances = chances / jnp.sum(chances, 0, keepdims=True)
    share_first = jnp.sum(chances * hot_first, 0, keepdims=True)
    share_second = jnp.sum(chances * hot_second, 0, keepdims=True)
    both = share_first + share_second
    weighted = pick_first * (share_first / both) + pick_second * (share_second / both)
    slot_gate = jnp.sum(weighted, 1, keepdims=True)
    gate_send[...] = jnp.broadcast_to(slot_gate, (SLOTS, 128))

    def gate_rows(array, owner):
        return array.at[pl.ds(pl.multiple_of(owner * CAP, 16), CAP), :]

    gate_slots = [links.slot() for _ in range(NEAR)]
    for step in range(NEAR):
        links.send(
            gate_rows(gate_send, plane[step]), gate_rows(gate_out, chip),
            at_plane(plane[step]), gate_slots[step],
        )
    links.move(gate_rows(gate_send, chip), gate_rows(gate_out, chip))

    for step in range(2):
        for chain in x_chains:
            chain.land(step)
            chain.start(step + 1)
        pass_on(step)
    for chain in x_chains:
        chain.land(2)
    dy_chain.land(2)
    for step in range(NEAR):
        links.land(gate_rows(gate_out, plane[step]), at_plane(plane[step]), gate_slots[step])
    pass_on(2)
    pass_on(3)
    for index in range(len(pieces)):
        all_there(index)
    links.finish()


def front_call(tokens, cotangent, gain_attn, gain_ffn, weights, router, experts, segment, parents, ids, rank):
    token_count, part_width = tokens.shape
    full = 4 * part_width
    rows_each, _, hidden_width = experts[0].shape
    heads = part_width // HEAD_DIM
    vmem = pl.BlockSpec(memory_space=pltpu.VMEM)
    hbm = pl.BlockSpec(memory_space=pl.ANY)

    def arr(shape, dtype):
        return jax.ShapeDtypeStruct(shape, dtype)

    return pl.pallas_call(
        front_body,
        out_shape=(
            arr((8, rows_each, 1664), BF),
            arr((8, rows_each, part_width), BF),
            arr((3, 4, 2, rows_each, hidden_width), BF),
            arr((SLOTS, full), BF),
            arr((SLOTS, full), BF),
            arr((SLOTS, 128), F32),
            arr((token_count, part_width), F32),
            arr((token_count, full), BF),
            arr((4, token_count + 16, part_width), BF),
            arr((3, token_count, part_width), BF),
            arr((heads, token_count, token_count), F32),
            arr((token_count, part_width), BF),
            arr((8, token_count), F32),
            arr((2, token_count, HEAD_DIM), F32),
            arr((2, SLOTS, token_count), BF),
            arr((token_count, 128), F32),
        ),
        in_specs=[vmem] * 9 + [hbm] * 3 + [vmem] * 4,
        out_specs=(hbm,) * 5 + (vmem, vmem) + (hbm,) * 4 + (vmem,) * 3 + (hbm, vmem),
        scratch_shapes=[
            pltpu.VMEM((token_count, full), BF),
            pltpu.VMEM((4, token_count + 16, part_width), BF),
            pltpu.VMEM((3, token_count, part_width), BF),
            pltpu.VMEM((heads, token_count, token_count), F32),
            pltpu.VMEM((2, SLOTS, token_count), BF),
            pltpu.VMEM((3, token_count, part_width), F32),
            pltpu.VMEM((token_count, token_count), F32),
            pltpu.VMEM((3, rows_each, EXPERTS, hidden_width), BF),
            pltpu.VMEM((3, EXPERTS, rows_each, hidden_width), BF),
            pltpu.VMEM((rows_each, 1664), BF),
            pltpu.VMEM((token_count + 16, part_width), BF),
            pltpu.VMEM((8, rows_each, 1664), BF),
            pltpu.VMEM((8, rows_each, part_width), BF),
            pltpu.VMEM((SLOTS, part_width), BF),
            pltpu.VMEM((SLOTS, part_width), BF),
            pltpu.VMEM((NEAR, token_count, part_width), BF),
            pltpu.VMEM((NEAR + 1, token_count, part_width), BF),
            pltpu.VMEM((8, token_count), F32),
            pltpu.VMEM((NEAR, 8, token_count), F32),
            pltpu.VMEM((SLOTS, 128), F32),
            pltpu.SemaphoreType.DMA((FRONT_SLOTS,)),
            pltpu.SemaphoreType.DMA((FRONT_SLOTS,)),
            pltpu.SemaphoreType.DMA((24,)),
        ],
        compiler_params=pltpu.CompilerParams(
            collective_id=0, has_side_effects=True, vmem_limit_bytes=60 * 1024 * 1024
        ),
        cost_estimate=pl.CostEstimate(
            flops=6_000_000_000, bytes_accessed=60_000_000, transcendentals=400_000
        ),
        name="front",
    )(
        tokens, cotangent, gain_attn.reshape(-1, 128), gain_ffn.reshape(-1, 128), *weights,
        router, *experts, segment, parents, ids, rank,
    )


MID_SLOTS = 48


TILE = 512


def mid_body(
    x_ref, dy_hbm, gate_ref, tokens_ref, w_ref,
    back_mid_out, back_exp_out, last_exp_out, extra_out, grads_out, expert_out,
    dy_ref, weights, hidden, graded_send, hidden_cat, graded_cat, act_cat, gate_cat, up_cat,
    turned, down_grad, rs_send, rs_recv, ext_send, ext_recv, sent, landed, local,
):
    n = lax.axis_index("narrow")
    w = lax.axis_index("wide")
    chip, core = w // 2, lax.rem(w, 2)
    to_z, from_z = places_of(n)
    plane = plane_of(chip)
    links = Links(sent, landed, local)
    mate = {"wide": 2 * chip + 1 - core}
    slots, full = hidden.shape
    part_width = full // 4
    rows_each = full // 8
    half = full // 2
    hidden_width = weights.shape[2]

    dy_load = links.move(dy_hbm, dy_ref)
    x_load = links.move(x_ref, hidden)
    loads = [
        links.move(
            w_ref.at[kind, c, k],
            weights.at[kind, pl.ds((2 * c + k) * rows_each, rows_each), :],
        )
        for kind in range(3)
        for c in range(4)
        for k in range(2)
    ]
    links.waits = []
    greet(to_z, plane, chip, core, True)

    slot_gate = gate_ref[:, 0:1]
    dy_load.wait()
    for c in range(4):
        theirs = pl.ds(pl.multiple_of((2 * c + 1 - core) * rows_each, rows_each), rows_each)
        ours = pl.ds(pl.multiple_of((2 * c + core) * rows_each, rows_each), rows_each)
        cols = slice(c * rows_each, (c + 1) * rows_each)
        graded_cat[core, :, cols] = (dy_ref[:, ours].astype(F32) * slot_gate).astype(BF)
        graded_send[:, cols] = (dy_ref[:, theirs].astype(F32) * slot_gate).astype(BF)

    def to_mate(source, target):
        slot = links.slot()
        links.send(source, target.at[core], mate, slot)
        return lambda: links.land(target.at[1 - core], mate, slot)

    graded_there = to_mate(graded_send, graded_cat)
    x_load.wait()
    total = jnp.zeros((slots, 1), F32)
    for m in range(4):
        part = hidden[:, m * part_width : (m + 1) * part_width].astype(F32)
        total = total + jnp.sum(part * part, 1, keepdims=True)
    scale = lax.rsqrt(total * (1.0 / full) + NORM_EPS)
    gain_row = tokens_ref.shape[1] - 15
    for m in range(4):
        cols = slice(m * part_width, (m + 1) * part_width)
        gain = tokens_ref[m, gain_row : gain_row + 1, :].astype(F32)
        hidden[:, cols] = (hidden[:, cols].astype(F32) * scale * gain).astype(BF)
    hidden_slots = [links.slot() for _ in range(4)]
    for c in range(4):
        cols = pl.ds(c * rows_each, rows_each)
        theirs = pl.ds(pl.multiple_of((2 * c + 1 - core) * rows_each, rows_each), rows_each)
        ours = pl.ds(pl.multiple_of((2 * c + core) * rows_each, rows_each), rows_each)
        links.send(hidden.at[:, theirs], hidden_cat.at[core, :, cols], mate, hidden_slots[c])
        hidden_cat[core, :, c * rows_each : (c + 1) * rows_each] = hidden[:, ours]
    for load in loads:
        load.wait()

    def one_tile(cols, rows):
        gate_pre = low_dot(hidden[rows, :], weights[0, :, cols])
        up_pre = low_dot(hidden[rows, :], weights[1, :, cols])
        act_raw = low_dot(dy_ref[rows, :], weights[2, :, cols])
        sigmoid = 1.0 / (1.0 + jnp.exp(-gate_pre))
        silu = gate_pre * sigmoid
        activated = (silu * up_pre).astype(BF)
        grad_act = act_raw * gate_ref[rows, 0:1]
        act_cat[core, rows, cols] = activated
        gate_cat[core, rows, cols] = (
            grad_act * up_pre * (sigmoid * (1.0 + gate_pre * (1.0 - sigmoid)))
        ).astype(BF)
        up_cat[core, rows, cols] = (grad_act * silu).astype(BF)
        return jnp.sum(act_raw * activated.astype(F32), 1, keepdims=True)

    def over_tiles(tile, body, carry):
        whole = hidden_width // tile
        carry = lax.fori_loop(
            0, whole, lambda t, value: body(pl.ds(pl.multiple_of(t * tile, tile), tile), value), carry
        )
        if hidden_width % tile:
            carry = body(pl.ds(whole * tile, hidden_width % tile), carry)
        return carry

    share = over_tiles(
        TILE,
        lambda cols, value: tuple(
            value[index] + one_tile(cols, pl.ds(index * (slots // 2), slots // 2))
            for index in range(2)
        ),
        (jnp.zeros((slots // 2, 1), F32),) * 2,
    )
    share = jnp.concatenate(share, 0)
    acts_there = [to_mate(item.at[core], item) for item in (act_cat, gate_cat, up_cat)]

    grad_gate, grad_up = gate_cat.at[core], up_cat.at[core]
    mid_sum = LineSum(links, n, rs_send.at[0], rs_recv.at[0])

    def mid_part(owner):
        rows = pl.ds(pl.multiple_of(owner * part_width, part_width), part_width)
        block = rows_rows(grad_gate[...], weights[0, rows, :])
        block = block + rows_rows(grad_up[...], weights[1, rows, :])
        return block, jnp.sum(hidden[:, rows].astype(F32) * block, 1, keepdims=True)

    stat = jnp.zeros((slots, 1), F32)
    block, part = mid_part(mid_sum.targets[0])
    mid_sum.put(0, block)
    stat = stat + part

    expert_slots = {}

    def weight_grad(right, target):
        def body(cols, value):
            right_rows = right[:, :, cols].reshape(2 * slots, cols.size)
            target[:, cols] = low_dot(turned[...], right_rows).astype(BF)
            return value

        over_tiles(TILE, body, 0)

    def share_out(index, source):
        expert_slots[index] = [links.slot() for _ in range(NEAR)]

        def block(owner):
            first = pl.multiple_of(owner * rows_each, rows_each)
            return source.at[pl.ds(first, rows_each), :]

        for step in range(NEAR):
            links.send(
                block(plane[step]), expert_out.at[index, chip],
                {"wide": 2 * plane[step] + core}, expert_slots[index][step],
            )
        links.move(block(chip), expert_out.at[index, chip])

    graded_there()
    turned[...] = graded_cat[...].reshape(2 * slots, half).T
    acts_there[0]()
    weight_grad(act_cat, down_grad)
    share_out(0, down_grad)

    def other_part(step, stat):
        block, part = mid_part(mid_sum.owner(step))
        rs_send[0, step] = block.astype(BF)
        return stat + part

    stat = lax.fori_loop(1, 4, other_part, stat)
    mid_sum.set_out(1)
    mid_sum.set_out(2)
    lane_at = lax.broadcasted_iota(jnp.int32, (slots, 128), 1)
    columns = jnp.where(lane_at == 0, share, jnp.where(lane_at == 1, stat, 0.0))
    high = columns.astype(BF)
    rest = (columns - high.astype(F32)).astype(BF)
    pick = jnp.where(
        lax.broadcasted_iota(jnp.int32, (8, 128), 0) == lax.broadcasted_iota(jnp.int32, (8, 128), 1),
        1.0, 0.0,
    ).astype(BF)
    extra = rows_rows(pick, high) + rows_rows(pick, rest)
    ext_send[...] = extra
    ext_slots = [links.slot() for _ in range(NEAR)]
    for step in range(NEAR):
        links.send(ext_send, ext_recv.at[step], {"narrow": to_z[step]}, ext_slots[step])

    mid_sum.relay()

    activated = act_cat.at[core]
    exp_sum = LineSum(links, n, rs_send.at[1], rs_recv.at[1])

    def exp_part(owner):
        rows = pl.ds(pl.multiple_of(owner * part_width, part_width), part_width)
        return rows_rows(activated[...], weights[2, rows, :])

    def expert_part(step, value):
        rs_send[1, step] = exp_part(exp_sum.owner(step)).astype(BF)
        return value

    lax.fori_loop(0, 4, expert_part, 0)
    exp_sum.set_out(0)
    exp_sum.set_out(1)
    for slot in hidden_slots:
        index = hidden_slots.index(slot)
        links.land(
            hidden_cat.at[1 - core, :, pl.ds(index * rows_each, rows_each)], mate, slot
        )
    for there in acts_there[1:]:
        there()
    turned[...] = hidden_cat[...].reshape(2 * slots, half).T
    gate_grad = weights.at[0, pl.ds(0, half), :]
    weight_grad(gate_cat, gate_grad)
    share_out(1, gate_grad)
    up_grad = weights.at[1, pl.ds(0, half), :]
    weight_grad(up_cat, up_grad)
    links.move(up_grad, grads_out)

    for step in range(NEAR):
        links.land(ext_recv.at[step], {"narrow": from_z[step]}, ext_slots[step])
        extra = extra + ext_recv[step]
    high = extra.astype(BF)
    rest = (extra - high.astype(F32)).astype(BF)
    place = lax.broadcasted_iota(jnp.int32, (8, 128), 0) * 2
    lanes = lax.broadcasted_iota(jnp.int32, (8, 128), 1)
    spread_high = jnp.where(place == lanes, 1.0, 0.0).astype(BF)
    spread_low = jnp.where(place + 1 == lanes, 1.0, 0.0).astype(BF)
    columns = mm(high, spread_high, ((0,), (0,))) + mm(rest, spread_low, ((0,), (0,)))
    extra_out[...] = jnp.where(lane_at == 4, 1.0, columns).astype(BF)
    back_mid_out[...] = mid_sum.total(rs_send[0, 3].astype(F32)).astype(BF)
    exp_sum.join()
    last_exp_out[...] = rs_send[1, 2]
    back_exp_out[...] = exp_sum.early(rs_send[1, 3].astype(F32)).astype(BF)
    for index in range(2):
        for step in range(NEAR):
            links.land(
                expert_out.at[index, plane[step]], {"wide": 2 * plane[step] + core},
                expert_slots[index][step],
            )
    links.finish()


def mid_call(slot_mid, slot_grad, slot_gate, token_parts, expert_w):
    slots, full = slot_mid.shape
    part_width = full // 4
    rows_each, hidden_width = expert_w.shape[3:]
    vmem = pl.BlockSpec(memory_space=pltpu.VMEM)
    hbm = pl.BlockSpec(memory_space=pl.ANY)

    def arr(shape, dtype):
        return jax.ShapeDtypeStruct(shape, dtype)

    return pl.pallas_call(
        mid_body,
        out_shape=(
            arr((slots, part_width), BF),
            arr((slots, part_width), BF),
            arr((slots, part_width), BF),
            arr((slots, 128), BF),
            arr((full // 2, hidden_width), BF),
            arr((2, 4, rows_each, hidden_width), BF),
        ),
        in_specs=[hbm] * 2 + [vmem] * 2 + [hbm],
        out_specs=(vmem,) * 4 + (hbm, hbm),
        scratch_shapes=[
            pltpu.VMEM((slots, full), BF),
            pltpu.VMEM((3, full, hidden_width), BF),
            pltpu.VMEM((slots, full), BF),
            pltpu.VMEM((slots, full // 2), BF),
            pltpu.VMEM((2, slots, full // 2), BF),
            pltpu.VMEM((2, slots, full // 2), BF),
            pltpu.VMEM((2, slots, hidden_width), BF),
            pltpu.VMEM((2, slots, hidden_width), BF),
            pltpu.VMEM((2, slots, hidden_width), BF),
            pltpu.VMEM((full // 2, 2 * slots), BF),
            pltpu.VMEM((full // 2, hidden_width), BF),
            pltpu.VMEM((2, NEAR + 1, slots, part_width), BF),
            pltpu.VMEM((2, NEAR + 1, slots, part_width), BF),
            pltpu.VMEM((8, slots), F32),
            pltpu.VMEM((NEAR, 8, slots), F32),
            pltpu.SemaphoreType.DMA((MID_SLOTS,)),
            pltpu.SemaphoreType.DMA((MID_SLOTS,)),
            pltpu.SemaphoreType.DMA((32,)),
        ],
        compiler_params=pltpu.CompilerParams(
            collective_id=1, has_side_effects=True, vmem_limit_bytes=62 * 1024 * 1024
        ),
        cost_estimate=pl.CostEstimate(
            flops=30_000_000_000, bytes_accessed=40_000_000, transcendentals=800_000
        ),
        name="mid",
    )(slot_mid, slot_grad, slot_gate, token_parts, expert_w)


class PlaneSum:
    def __init__(self, links, core, chip, plane, first, send, inbox):
        self.links, self.core, self.chip = links, core, chip
        self.near, self.next, self.far = plane[first], plane[1 - first], plane[2]
        self.send, self.inbox = send, inbox
        self.slots = [links.slot() for _ in range(3)]

    def at(self, peer):
        return {"wide": 2 * peer + self.core}

    def block(self, owner):
        rows = self.inbox.shape[1]
        return self.send.at[pl.ds(pl.multiple_of(owner * rows, rows), rows), :]

    def start(self):
        links = self.links
        links.send(self.block(self.far), self.inbox.at[1], self.at(self.near), self.slots[1])
        links.send(self.block(self.near), self.inbox.at[0], self.at(self.near), self.slots[0])

    def turn(self):
        links = self.links
        links.land(self.inbox.at[1], self.at(self.near), self.slots[1])
        block = self.block(self.next)
        block[...] = (block[...].astype(F32) + self.inbox[1].astype(F32)).astype(BF)
        links.send(block, self.inbox.at[2], self.at(self.next), self.slots[2])

    def total(self):
        links = self.links
        links.land(self.inbox.at[0], self.at(self.near), self.slots[0])
        links.land(self.inbox.at[2], self.at(self.next), self.slots[2])
        own = self.block(self.chip)[...].astype(F32)
        return own + self.inbox[0].astype(F32) + self.inbox[2].astype(F32)


TAIL_SLOTS = 72


def tail_body(
    mid_ref, exp_ref, last_ref, ext_ref, moved_ref, picks_hbm, stat_ref, cols_ref, middle_ref,
    cot_ref, tok_ref, tokens_hbm, qkv_hbm, prob_hbm, att_ref, rope_ref, hidden_hbm, qkvw_ref,
    outw_ref,
    output_out, grad_tokens_out, summed_out, small_out,
    router_out, expert_out,
    picks_ref, tokens_ref, qkv_ref, prob_ref, hidden_ref, grad_att_at, exp_in, exp_sum, router_all, qkvw, outw, ret_mid, ret_exp, ret_ext, branch, hidden_cat, branch_cat, att_cat, proj_cat,
    proj_send, proj_recv, first_send, first_recv, col_send, col_recv, small_mate, small_sum,
    small_recv, last_mate, last_sum, last_recv, sent, landed, local,
):
    n = lax.axis_index("narrow")
    w = lax.axis_index("wide")
    chip, core = w // 2, lax.rem(w, 2)
    to_z, from_z = places_of(n)
    plane = plane_of(chip)
    links = Links(sent, landed, local)
    mate = {"wide": 2 * chip + 1 - core}
    token_count, part_width = tok_ref.shape
    full = 4 * part_width
    rows_each = full // 8
    heads = part_width // HEAD_DIM
    half = full // 2

    def at_plane(peer):
        return {"wide": 2 * peer + core}

    def cap_rows(array, owner):
        return array.at[pl.ds(pl.multiple_of(owner * CAP, 16), CAP), :]

    first_loads = [
        links.move(source, target)
        for source, target in (
            (hidden_hbm, hidden_ref), (picks_hbm, picks_ref), (tokens_hbm, tokens_ref),
            (qkv_hbm, qkv_ref), (prob_hbm, prob_ref),
        )
    ]
    loads = [links.move(qkvw_ref, qkvw), links.move(outw_ref, outw)]
    links.waits = []
    greet(to_z, plane, chip, core, True)

    last_slot = links.slot()
    links.send(last_ref, exp_in, {"narrow": lax.rem(2 * n + 1, 5)}, last_slot)

    back_slots = []

    def give_back(source, target):
        slots = [links.slot() for _ in range(NEAR)]
        for step in range(NEAR):
            links.send(
                cap_rows(source, plane[step]), cap_rows(target, chip), at_plane(plane[step]),
                slots[step],
            )
        own = links.move(cap_rows(source, chip), cap_rows(target, chip))
        links.waits.pop()
        back_slots.append((target, slots, own))

    give_back(mid_ref, ret_mid)
    give_back(ext_ref, ret_ext)

    def returned(which):
        target, slots, own = back_slots[which]
        for step in range(NEAR):
            links.land(cap_rows(target, plane[step]), at_plane(plane[step]), slots[step])
        own.wait()
        return target[...]

    expert_slots = [links.slot() for _ in range(NEAR)]
    for step in range(NEAR):
        block = pl.ds(pl.multiple_of(plane[step] * rows_each, rows_each), rows_each)
        links.send(
            moved_ref.at[block, :], expert_out.at[chip], at_plane(plane[step]), expert_slots[step]
        )
    block = pl.ds(pl.multiple_of(chip * rows_each, rows_each), rows_each)
    links.move(moved_ref.at[block, :], expert_out.at[chip])

    def to_mate(source, target):
        slot = links.slot()
        links.send(source, target.at[core], mate, slot)
        return lambda: links.land(target.at[1 - core], mate, slot)

    def parity_exchange(source, target):
        lands = []
        for c in range(4):
            cols = pl.ds(c * rows_each, rows_each)
            theirs = pl.ds(pl.multiple_of((2 * c + 1 - core) * rows_each, rows_each), rows_each)
            ours = pl.ds(pl.multiple_of((2 * c + core) * rows_each, rows_each), rows_each)
            slot = links.slot()
            links.send(source.at[:, theirs], target.at[core, :, cols], mate, slot)
            target[core, :, c * rows_each : (c + 1) * rows_each] = source[:, ours]
            lands.append((target.at[1 - core, :, cols], slot))
        return lambda: [links.land(block, mate, slot) for block, slot in lands]

    for load in first_loads:
        load.wait()
    hidden_there = parity_exchange(hidden_ref, hidden_cat)
    att_cat[core] = att_ref[...]
    att_there = to_mate(att_ref, att_cat)

    stat = jnp.concatenate([stat_ref[...], jnp.zeros((120, token_count), F32)], 0).T
    lane_at = lax.broadcasted_iota(jnp.int32, (token_count, 128), 1)
    scale_second = lax.rsqrt(stat[:, 4:5] * (1.0 / full) + NORM_EPS)
    logits = stat * scale_second
    hot_first = lane_at == cols_ref[:, 2:3].astype(jnp.int32)
    hot_second = lane_at == cols_ref[:, 3:4].astype(jnp.int32)
    logit_first = jnp.sum(jnp.where(hot_first, logits, 0.0), 1, keepdims=True)
    logit_second = jnp.sum(jnp.where(hot_second, logits, 0.0), 1, keepdims=True)
    apart = logit_first - logit_second
    share_first = 1.0 / (1.0 + jnp.exp(-apart))
    share_second = 1.0 / (1.0 + jnp.exp(apart))
    normed = middle_ref[...] * scale_second
    gain_second = tokens_ref[n, token_count + 1 : token_count + 2, :].astype(F32)
    hidden_second = (normed * gain_second).astype(BF)
    for load in loads:
        load.wait()
    router = qkvw[pl.ds(2 * n, 2), :, 1536:1664].reshape(part_width, 128)

    rows_mid = returned(0)
    rows_ext = returned(1)
    ext_first = cols_cols(picks_ref[0], rows_ext)
    ext_second = cols_cols(picks_ref[1], rows_ext)
    ext_both = ext_first + ext_second
    grad_share = ext_first[:, 0:1] + ext_first[:, 1:2] - ext_second[:, 0:1] - ext_second[:, 1:2]
    delta = (grad_share * share_first * share_second).astype(BF).astype(F32)
    grad_logits = jnp.where(hot_first, delta, jnp.where(hot_second, -delta, 0.0)).astype(BF)
    stat_total = ext_both[:, 2:3] + ext_both[:, 3:4] + delta * apart
    grad_hidden = cols_cols(picks_ref[0] + picks_ref[1], rows_mid) + rows_rows(grad_logits, router)
    grad_middle = cot_ref[...].astype(F32) + scale_second * (
        gain_second * grad_hidden - normed * (stat_total * (1.0 / full))
    )
    own_cols = pl.ds(pl.multiple_of(n * part_width, part_width), part_width)
    branch[:, own_cols] = grad_middle.astype(BF)
    branch_slots = [links.slot() for _ in range(NEAR)]
    for step in range(NEAR):
        links.send(
            branch.at[:, own_cols], branch.at[:, own_cols], {"narrow": to_z[step]},
            branch_slots[step],
        )

    links.land(exp_in, {"narrow": lax.rem(n + 1, 4)}, last_slot)
    exp_sum[...] = (exp_ref[...].astype(F32) + exp_in[...].astype(F32)).astype(BF)
    give_back(exp_sum, ret_exp)

    router_part = cols_cols(grad_logits, hidden_second)[0:8, :]
    gain_part = jnp.sum(grad_hidden * normed, 0, keepdims=True)
    kind_at = lax.broadcasted_iota(jnp.int32, (8, part_width), 0)
    small = jnp.where(kind_at == 4, gain_part, router_part)
    small_mate[core] = small
    small_there = to_mate(small_mate.at[core], small_mate)

    small_there()
    small = small_mate[0] + small_mate[1]
    small_sum[...] = small
    small_slots = [links.slot() for _ in range(NEAR)]
    for step in range(NEAR):
        links.send(small_sum, small_recv.at[step], at_plane(plane[step]), small_slots[step])

    for step in range(NEAR):
        cols = pl.ds(pl.multiple_of(from_z[step] * part_width, part_width), part_width)
        links.land(branch.at[:, cols], {"narrow": from_z[step]}, branch_slots[step])
    branch_there = parity_exchange(branch, branch_cat)
    grad_att = low_dot(branch[...], outw[...].reshape(full, part_width)).astype(BF)

    proj_sums = {
        part: PlaneSum(
            links, core, chip, plane, part % 2, proj_send.at[part], proj_recv.at[part]
        )
        for part in (3, 0, 1, 2)
    }

    branch_there()
    att_there()
    proj_send[3] = cols_cols(
        branch_cat[...].reshape(2 * token_count, half), att_cat[...].reshape(2 * token_count, part_width)
    ).astype(BF)
    proj_sums[3].start()
    score_scale = HEAD_DIM ** (-0.5)
    grad_att_at[...] = grad_att

    def one_head(head, stat_first):
        def lanes(start):
            return pl.ds(pl.multiple_of(start + head * HEAD_DIM, HEAD_DIM), HEAD_DIM)

        query, key, value = (qkv_ref[i, :, lanes(0)] for i in range(3))
        grad_out = grad_att_at[:, lanes(0)]
        weights = prob_ref[head]
        grad_weights = rows_rows(grad_out, value)
        inner = jnp.sum(weights * grad_weights, 1, keepdims=True)
        grad_scores = (weights * (grad_weights - inner)).astype(BF)
        grad_query = low_dot(grad_scores, key) * score_scale
        grad_key = cols_cols(grad_scores, query) * score_scale
        grad_value = cols_cols(weights.astype(BF), grad_out)
        products = (
            grad_query * query.astype(F32)
            + grad_key * key.astype(F32)
            + grad_value * value.astype(F32)
        )
        for part, grad in ((0, grad_query), (1, grad_key)):
            turned = grad * rope_ref[0] - pltpu.roll(grad, HEAD_DIM // 2, 1) * rope_ref[1]
            proj_cat[core, :, lanes(part * part_width)] = turned.astype(BF)
        proj_cat[core, :, lanes(2 * part_width)] = grad_value.astype(BF)
        return stat_first + jnp.sum(products, 1, keepdims=True)

    stat_first = lax.fori_loop(0, heads, one_head, jnp.zeros((token_count, 1), F32))
    proj_there = to_mate(proj_cat.at[core], proj_cat)
    high = stat_first.astype(BF)
    rest = (stat_first - high.astype(F32)).astype(BF)
    col_send[...] = jnp.where(
        lane_at == 0, high.astype(F32), jnp.where(lane_at == 1, rest.astype(F32), 0.0)
    ).astype(BF)
    col_slots = [links.slot() for _ in range(NEAR)]
    for step in range(NEAR):
        links.send(col_send, col_recv.at[step], {"narrow": to_z[step]}, col_slots[step])
    grads = proj_cat[core]

    def first_block(m):
        weight = qkvw[pl.ds(2 * m, 2), :, 0:1536].reshape(part_width, 1536)
        return rows_rows(grads, weight)

    def fill_first(step, value):
        first_send[step] = first_block(lax.rem(n + 1 + step, 4)).astype(BF)
        return value

    lax.fori_loop(0, NEAR, fill_first, 0)
    first_slots = [links.slot() for _ in range(NEAR)]
    for step in range(NEAR):
        links.send(
            first_send.at[step], first_recv.at[step], {"narrow": to_z[step]}, first_slots[step]
        )

    hidden_there()
    proj_there()
    hidden_rows = hidden_cat[...].reshape(2 * token_count, half)
    proj_sums[3].turn()
    for part in range(3):
        cols = slice(part * 512, (part + 1) * 512)
        proj_send[part] = cols_cols(
            hidden_rows, proj_cat[:, :, cols].reshape(2 * token_count, part_width)
        ).astype(BF)
        proj_sums[part].start()

    rows_exp = returned(2)
    output_out[...] = (
        middle_ref[...]
        + share_first * cols_cols(picks_ref[0], rows_exp)
        + share_second * cols_cols(picks_ref[1], rows_exp)
    ).astype(BF)

    grad_first = first_block(n)
    stat_first = high.astype(F32) + rest.astype(F32)
    total = jnp.zeros((token_count, 1), F32)
    for m in range(4):
        part = tokens_ref[m, 0:token_count, :].astype(F32)
        total = total + jnp.sum(part * part, 1, keepdims=True)
    scale_first = lax.rsqrt(total * (1.0 / full) + NORM_EPS)
    normed_first = tok_ref[...].astype(F32) * scale_first
    gain_first = tokens_ref[n, token_count : token_count + 1, :].astype(F32)
    for step in range(NEAR):
        links.land(col_recv.at[step], {"narrow": from_z[step]}, col_slots[step])
        stat_first = stat_first + (
            col_recv[step, :, 0:1].astype(F32) + col_recv[step, :, 1:2].astype(F32)
        )
    for step in range(NEAR):
        links.land(first_recv.at[step], {"narrow": from_z[step]}, first_slots[step])
        grad_first = grad_first + first_recv[step].astype(F32)
    grad_tokens_out[...] = grad_middle + scale_first * (
        gain_first * grad_first - normed_first * (stat_first * (1.0 / full))
    )
    gain_part = jnp.sum(grad_first * normed_first, 0, keepdims=True)
    for part in range(3):
        proj_sums[part].turn()
    last_mate[core] = jnp.broadcast_to(gain_part, (8, part_width))
    last_there = to_mate(last_mate.at[core], last_mate)

    for step in range(NEAR):
        links.land(small_recv.at[step], at_plane(plane[step]), small_slots[step])
        small = small + small_recv[step]
    last_there()
    last = last_mate[0] + last_mate[1]
    last_sum[...] = last
    last_slots = [links.slot() for _ in range(NEAR)]
    for step in range(NEAR):
        links.send(last_sum, last_recv.at[step], at_plane(plane[step]), last_slots[step])
    router_all[:, own_cols] = small
    router_slots = [links.slot() for _ in range(NEAR)]
    for step in range(NEAR):
        links.send(
            router_all.at[:, own_cols], router_all.at[:, own_cols], {"narrow": to_z[step]},
            router_slots[step],
        )
    for step in range(NEAR):
        links.land(last_recv.at[step], at_plane(plane[step]), last_slots[step])
        last = last + last_recv[step]
    small_out[...] = jnp.where(kind_at == 5, last, small)
    for step in range(NEAR):
        cols = pl.ds(pl.multiple_of(from_z[step] * part_width, part_width), part_width)
        links.land(router_all.at[:, cols], {"narrow": from_z[step]}, router_slots[step])

    router_out[...] = router_all[:, pl.ds(pl.multiple_of(w * rows_each, rows_each), rows_each)]
    for part in range(4):
        summed_out[:, part * part_width : (part + 1) * part_width] = proj_sums[part].total()
    for step in range(NEAR):
        links.land(expert_out.at[plane[step]], at_plane(plane[step]), expert_slots[step])
    links.finish()


def tail_call(*args):
    slots, part_width = args[0].shape
    half, hidden_width = args[4].shape
    token_count = args[10].shape[0]
    full, rows_each = 2 * half, half // 4
    vmem = pl.BlockSpec(memory_space=pltpu.VMEM)
    hbm = pl.BlockSpec(memory_space=pl.ANY)

    def arr(shape, dtype):
        return jax.ShapeDtypeStruct(shape, dtype)

    own = (token_count, part_width)
    return pl.pallas_call(
        tail_body,
        out_shape=(
            arr(own, BF),
            arr(own, F32),
            arr((rows_each, full), F32),
            arr((8, part_width), F32),
            arr((8, rows_each), F32),
            arr((4, rows_each, hidden_width), BF),
        ),
        in_specs=[vmem] * 4 + [hbm] * 2 + [vmem] * 5 + [hbm] * 3 + [vmem] * 2 + [hbm] * 3,
        out_specs=(vmem,) * 5 + (hbm,),
        scratch_shapes=[
            pltpu.VMEM((2, slots, token_count), BF),
            pltpu.VMEM((4, token_count + 16, part_width), BF),
            pltpu.VMEM((3,) + own, BF),
            pltpu.VMEM((part_width // HEAD_DIM, token_count, token_count), F32),
            pltpu.VMEM((token_count, full), BF),
            pltpu.VMEM(own, BF),
            pltpu.VMEM((slots, part_width), BF),
            pltpu.VMEM((slots, part_width), BF),
            pltpu.VMEM((8, full), F32),
            pltpu.VMEM((8, rows_each, 1664), BF),
            pltpu.VMEM((8, rows_each, part_width), BF),
            pltpu.VMEM((slots, part_width), BF),
            pltpu.VMEM((slots, part_width), BF),
            pltpu.VMEM((slots, 128), BF),
            pltpu.VMEM((token_count, full), BF),
            pltpu.VMEM((2, token_count, half), BF),
            pltpu.VMEM((2, token_count, half), BF),
            pltpu.VMEM((2, token_count, part_width), BF),
            pltpu.VMEM((2, token_count, 1536), BF),
            pltpu.VMEM((4, half, part_width), BF),
            pltpu.VMEM((4, NEAR, rows_each, part_width), BF),
            pltpu.VMEM((NEAR,) + own, BF),
            pltpu.VMEM((NEAR,) + own, BF),
            pltpu.VMEM((token_count, 128), BF),
            pltpu.VMEM((NEAR, token_count, 128), BF),
            pltpu.VMEM((2, 8, part_width), F32),
            pltpu.VMEM((8, part_width), F32),
            pltpu.VMEM((NEAR, 8, part_width), F32),
            pltpu.VMEM((2, 8, part_width), F32),
            pltpu.VMEM((8, part_width), F32),
            pltpu.VMEM((NEAR, 8, part_width), F32),
            pltpu.SemaphoreType.DMA((TAIL_SLOTS,)),
            pltpu.SemaphoreType.DMA((TAIL_SLOTS,)),
            pltpu.SemaphoreType.DMA((24,)),
        ],
        compiler_params=pltpu.CompilerParams(
            collective_id=2, has_side_effects=True, vmem_limit_bytes=60 * 1024 * 1024
        ),
        cost_estimate=pl.CostEstimate(
            flops=6_000_000_000, bytes_accessed=60_000_000, transcendentals=1_000
        ),
        name="tail",
    )(*args)


FINISH_ROWS = 128


def finish_body(
    early_ref, late_ref, output_ref, tokens_ref, summed_ref, small_ref, router_ref,
    gate_out, up_out, down_out, output_out, tokens_out, q_out, k_out, v_out, o_out,
    gain_first_out, gain_second_out, router_out,
    packed, spread, incoming, outgoing, passing,
):
    rows_each = packed.shape[2]
    width = tokens_ref.shape[1]
    sources = (early_ref.at[0], early_ref.at[1], late_ref)
    targets = (down_out, gate_out, up_out)
    loads = {}
    for kind in range(3):
        for part in range(rows_each // FINISH_ROWS):
            rows = pl.ds(part * FINISH_ROWS, FINISH_ROWS)
            loads[kind, part] = pltpu.make_async_copy(
                sources[kind].at[:, rows, :], packed.at[kind, :, rows, :], incoming.at[kind, part]
            )
            loads[kind, part].start()
    whole = [(output_ref, output_out), (tokens_ref, tokens_out)]
    for part, target in enumerate((q_out, k_out, v_out, o_out)):
        whole.append((summed_ref.at[:, pl.ds(part * width, width)], target))
    copies = [
        pltpu.make_async_copy(source, target, passing.at[index])
        for index, (source, target) in enumerate(whole)
    ]
    stores = []
    for (kind, part), load in loads.items():
        load.wait()

        def some_rows(index, value):
            first = pl.multiple_of(part * FINISH_ROWS + index * 16, 16)
            rows = pl.ds(first, 16)
            for expert in range(EXPERTS):
                spread[kind, rows, expert, :] = packed[kind, expert, rows, :].astype(F32)
            return value

        lax.fori_loop(0, FINISH_ROWS // 16, some_rows, 0)
        rows = pl.ds(part * FINISH_ROWS, FINISH_ROWS)
        stores.append(
            pltpu.make_async_copy(
                spread.at[kind, rows], targets[kind].at[rows], outgoing.at[kind, part]
            )
        )
        stores[-1].start()
        if kind == 0 and part == 0:
            for copy in copies:
                copy.start()
    for row, target in ((5, gain_first_out), (4, gain_second_out)):
        for index in range(width // 128):
            target[index : index + 1, :] = small_ref[
                row : row + 1, index * 128 : (index + 1) * 128
            ]
    router_out[...] = router_ref[0:EXPERTS, :]
    for copy in stores + copies:
        copy.wait()


def finish_call(early, late, output, grad_tokens, summed, small, router):
    _, rows_each, hidden_width = late.shape
    part_width = output.shape[1]
    vmem = pl.BlockSpec(memory_space=pltpu.VMEM)
    hbm = pl.BlockSpec(memory_space=pl.ANY)
    parts = rows_each // FINISH_ROWS

    def arr(shape, dtype):
        return jax.ShapeDtypeStruct(shape, dtype)

    return pl.pallas_call(
        finish_body,
        out_shape=(arr((rows_each, EXPERTS, hidden_width), F32),) * 3
        + (arr(output.shape, BF), arr(output.shape, F32))
        + (arr((rows_each, part_width), F32),) * 4
        + (arr((part_width // 128, 128), F32),) * 2
        + (arr((EXPERTS, rows_each), F32),),
        in_specs=[hbm] * 2 + [vmem] * 5,
        out_specs=(hbm,) * 9 + (vmem,) * 3,
        scratch_shapes=[
            pltpu.VMEM((3, EXPERTS, rows_each, hidden_width), BF),
            pltpu.VMEM((3, rows_each, EXPERTS, hidden_width), F32),
            pltpu.SemaphoreType.DMA((3, parts)),
            pltpu.SemaphoreType.DMA((3, parts)),
            pltpu.SemaphoreType.DMA((6,)),
        ],
        compiler_params=pltpu.CompilerParams(vmem_limit_bytes=56 * 1024 * 1024),
        name="finish",
    )(early, late, output, grad_tokens, summed, small, router)


def plain_device(
    tokens, gain_attn, w_query, w_key, w_value, w_out, gain_ffn, w_router,
    w_gate, w_up, w_down, segment, parents, expert_ids, slot_order, cotangent,
):
    narrow_count = lax.axis_size("narrow")
    wide_count = lax.axis_size("wide")
    narrow_at = lax.axis_index("narrow")
    token_count, part_width = tokens.shape
    full_width = part_width * narrow_count
    hidden_width = w_gate.shape[2]
    rows_each = w_gate.shape[0]
    blocks = wide_count // 8
    quads = [
        [8 * block + 2 * chip + core for chip in range(4)]
        for block in range(blocks)
        for core in range(2)
    ]
    mates = [
        [8 * block + 2 * chip + core for block in range(blocks) for core in range(2)]
        for chip in range(4)
    ]

    def quad_swap(array):
        return lax.all_to_all(array, "wide", 0, 0, axis_index_groups=quads, tiled=True)

    def own_rows(weight):
        moved = quad_swap(jnp.transpose(weight, (1, 0, 2)))
        joined = lax.all_gather(moved, "wide", axis=0, axis_index_groups=mates, tiled=True)
        joined = joined.reshape(blocks, 2, 4, rows_each, hidden_width).transpose(0, 2, 1, 3, 4)
        return joined.reshape(full_width, hidden_width)

    def share_rows(grad):
        parts = grad.astype(BF).reshape(blocks, 4, 2, rows_each, hidden_width)
        parts = parts.transpose(0, 2, 1, 3, 4).reshape(blocks * 2, 4, rows_each, hidden_width)
        summed = lax.psum_scatter(
            parts, "wide", scatter_dimension=0, axis_index_groups=mates, tiled=True
        )[0]
        return jnp.transpose(quad_swap(summed), (1, 0, 2)).astype(F32)

    def head_cols(array, head):
        return array[:, head * HEAD_DIM : (head + 1) * HEAD_DIM]

    heads = part_width // HEAD_DIM
    half_dim = HEAD_DIM // 2
    freqs = ROPE_BASE ** (-2.0 * jnp.arange(half_dim, dtype=F32) / HEAD_DIM)
    score_scale = HEAD_DIM ** (-0.5)
    gains = jnp.stack([gain_attn, gain_ffn])
    gain_first_loc = gain_attn.astype(F32)
    gain_second_loc = gain_ffn.astype(F32)
    hot_first, hot_second, kept, pick_first, pick_second = route(expert_ids, slot_order[0])

    gate_w, up_w, down_w = own_rows(w_gate), own_rows(w_up), own_rows(w_down)
    attn_w = lax.all_gather(
        jnp.stack([w_query, w_key, w_value, w_out], 1), "wide", axis=0, tiled=True
    )
    query_w, key_w, value_w, out_w = (attn_w[:, i] for i in range(4))
    router_w = lax.all_gather(w_router, "wide", axis=0, tiled=True)
    tokens_full = lax.all_gather(tokens, "narrow", axis=1, tiled=True)
    grad_full = lax.all_gather(cotangent, "narrow", axis=1, tiled=True)
    gains_full = lax.all_gather(gains, "narrow", axis=1, tiled=True)
    gain_first = gains_full[0].astype(F32)
    gain_second = gains_full[1].astype(F32)

    seen, places = tree_layout(segment[0], parents[0])
    pick_first_low = pick_first.astype(BF)
    pick_second_low = pick_second.astype(BF)
    pick_both_low = (pick_first | pick_second).astype(BF)

    inputs_full = tokens_full.astype(F32)
    scale_first = lax.rsqrt(jnp.mean(inputs_full * inputs_full, -1, keepdims=True) + NORM_EPS)
    normed_first = inputs_full * scale_first
    hidden_first = (normed_first * gain_first).astype(BF)
    angles = places[:, None] * freqs[None, :]
    cosines, sines = jnp.cos(angles), jnp.sin(angles)
    query_raw = rows_cols(hidden_first, query_w)
    key_raw = rows_cols(hidden_first, key_w)
    value_low = rows_cols(hidden_first, value_w).astype(BF)

    saved = []
    outs = []
    for head in range(heads):
        query = rotate(head_cols(query_raw, head), cosines, sines).astype(BF)
        key = rotate(head_cols(key_raw, head), cosines, sines).astype(BF)
        value = head_cols(value_low, head)
        scores = jnp.where(seen, rows_rows(query, key) * score_scale, NEG_FILL)
        exps = jnp.exp(scores - jnp.max(scores, -1, keepdims=True))
        weights = exps / jnp.sum(exps, -1, keepdims=True)
        saved.append((query, key, value, weights))
        outs.append(rows_cols(weights.astype(BF), value).astype(BF))
    attended = jnp.concatenate(outs, 1)
    branch_part = rows_rows(attended, out_w).astype(BF)
    branch_loc = lax.psum_scatter(
        branch_part, "narrow", scatter_dimension=1, tiled=True
    ).astype(F32)
    middle = tokens.astype(F32) + branch_loc
    middle_full = lax.all_gather(middle.astype(BF), "narrow", axis=1, tiled=True).astype(F32)
    scale_second = lax.rsqrt(jnp.mean(middle_full * middle_full, -1, keepdims=True) + NORM_EPS)
    normed_second = middle_full * scale_second
    hidden_second = (normed_second * gain_second).astype(BF)
    logits = rows_cols(hidden_second, router_w)
    share_first, share_second = gate_pair(logits, hot_first, hot_second)
    weight_first = kept[:, 0] * share_first
    weight_second = kept[:, 1] * share_second

    slot_weight = jnp.sum(
        pick_first * weight_first[:, None] + pick_second * weight_second[:, None], 0
    )
    weight_high, weight_low = two_parts(slot_weight)
    pads = jnp.stack([weight_high, weight_low], 1)
    pads = jnp.pad(pads, ((0, 0), (0, 126)))
    sent_hidden = cols_cols(pick_both_low, hidden_second).astype(BF)
    sent_grad = cols_cols(pick_both_low, grad_full).astype(BF)
    sent = jnp.concatenate([sent_hidden, sent_grad, pads], 1)
    got = quad_swap(sent.reshape(EXPERTS, CAP, -1)).reshape(SLOTS, -1)
    slot_hidden = got[:, :full_width]
    slot_grad = got[:, full_width : 2 * full_width]
    slot_gate = got[:, 2 * full_width : 2 * full_width + 2].astype(F32)
    slot_gate = slot_gate[:, 0:1] + slot_gate[:, 1:2]

    gate_pre = rows_cols(slot_hidden, gate_w)
    up_pre = rows_cols(slot_hidden, up_w)
    sigmoid_gate = jax.nn.sigmoid(gate_pre)
    silu_gate = gate_pre * sigmoid_gate
    activated = (silu_gate * up_pre).astype(BF)
    expert_part = rows_rows(activated, down_w)
    act_raw = rows_cols(slot_grad, down_w)
    share_part = jnp.sum(act_raw * activated.astype(F32), 1, keepdims=True)
    grad_act = act_raw * slot_gate
    grad_gate_pre = (
        grad_act * up_pre * sigmoid_gate * (1.0 + gate_pre * (1.0 - sigmoid_gate))
    ).astype(BF)
    grad_up_pre = (grad_act * silu_gate).astype(BF)
    grad_slot = rows_rows(grad_gate_pre, gate_w) + rows_rows(grad_up_pre, up_w)
    stat_part = jnp.sum(slot_hidden.astype(F32) * grad_slot, 1, keepdims=True)
    extras = jnp.concatenate([*two_parts(share_part), *two_parts(stat_part)], 1)
    extras = jnp.pad(extras, ((0, 0), (0, 124)))
    back_parts = []
    expert_plain = expert_part.astype(BF)
    slot_plain = grad_slot.astype(BF)
    for part in range(narrow_count):
        cols = slice(part * part_width, (part + 1) * part_width)
        back_parts += [expert_plain[:, cols], slot_plain[:, cols], extras]
    back = lax.psum_scatter(
        jnp.concatenate(back_parts, 1), "narrow", scatter_dimension=1, tiled=True
    )
    back = quad_swap(back.reshape(EXPERTS, CAP, -1)).reshape(SLOTS, -1)
    picked_first = rows_cols(pick_first_low, back)
    picked_second = rows_cols(pick_second_low, back)
    output = (
        middle
        + weight_first[:, None] * picked_first[:, :part_width]
        + weight_second[:, None] * picked_second[:, :part_width]
    ).astype(BF)

    grad_weight = (slot_grad.astype(F32) * slot_gate).astype(BF)
    gate_out = share_rows(cols_cols(slot_hidden, grad_gate_pre))
    up_out = share_rows(cols_cols(slot_hidden, grad_up_pre))
    down_out = share_rows(cols_cols(grad_weight, activated))

    tail = 2 * part_width
    share_first_grad = picked_first[:, tail] + picked_first[:, tail + 1]
    share_second_grad = picked_second[:, tail] + picked_second[:, tail + 1]
    both = picked_first + picked_second
    stat_second = both[:, tail + 2] + both[:, tail + 3]
    grad_hidden_loc = both[:, part_width:tail]
    grad_local = cotangent.astype(F32)
    _, pull_gates = jax.vjp(lambda given: gate_pair(given, hot_first, hot_second), logits)
    (grad_logits,) = pull_gates((kept[:, 0] * share_first_grad, kept[:, 1] * share_second_grad))
    grad_logits_low = grad_logits.astype(BF)
    grad_router_rows = rows_rows(grad_logits_low, router_w)
    stat_total = stat_second + jnp.sum(normed_second * gain_second * grad_router_rows, 1)

    def take_cols(full_rows):
        return lax.dynamic_slice_in_dim(full_rows, narrow_at * part_width, part_width, 1)

    grad_hidden_loc = grad_hidden_loc + take_cols(grad_router_rows)
    normed_second_loc = take_cols(normed_second)
    grad_gain_second = jnp.sum(grad_hidden_loc * normed_second_loc, 0)
    grad_middle = grad_local + scale_second * (
        gain_second_loc * grad_hidden_loc - normed_second_loc * stat_total[:, None] / full_width
    )
    grad_router_w = cols_cols(hidden_second, grad_logits_low)
    grad_branch = lax.all_gather(grad_middle.astype(BF), "narrow", axis=1, tiled=True)
    grad_attended = rows_cols(grad_branch, out_w).astype(BF)
    grad_out_w = cols_cols(grad_branch, attended)
    grad_qs, grad_ks, grad_vs = [], [], []
    for head in range(heads):
        query, key, value, weights = saved[head]
        grad_out = head_cols(grad_attended, head)
        grad_weights = rows_rows(grad_out, value)
        inner = jnp.sum(weights * grad_weights, -1, keepdims=True)
        grad_scores = (weights * (grad_weights - inner)).astype(BF)
        grad_q = rows_cols(grad_scores, key) * score_scale
        grad_k = cols_cols(grad_scores, query) * score_scale
        grad_qs.append(rotate(grad_q, cosines, -sines).astype(BF))
        grad_ks.append(rotate(grad_k, cosines, -sines).astype(BF))
        grad_vs.append(cols_cols(weights.astype(BF), grad_out).astype(BF))
    grad_query_raw = jnp.concatenate(grad_qs, 1)
    grad_key_raw = jnp.concatenate(grad_ks, 1)
    grad_value_raw = jnp.concatenate(grad_vs, 1)
    grad_hidden_first = (
        rows_rows(grad_query_raw, query_w)
        + rows_rows(grad_key_raw, key_w)
        + rows_rows(grad_value_raw, value_w)
    )
    stat_first = jnp.sum(normed_first * gain_first * grad_hidden_first, 1, keepdims=True)
    extras = jnp.pad(jnp.concatenate(two_parts(stat_first), 1), ((0, 0), (0, 126)))
    grad_hidden_low = grad_hidden_first.astype(BF)
    first_parts = []
    for part in range(narrow_count):
        first_parts += [grad_hidden_low[:, part * part_width : (part + 1) * part_width], extras]
    first_back = lax.psum_scatter(
        jnp.concatenate(first_parts, 1), "narrow", scatter_dimension=1, tiled=True
    ).astype(F32)
    grad_first_loc = first_back[:, :part_width]
    stat_first = first_back[:, part_width : part_width + 1]
    stat_first = stat_first + first_back[:, part_width + 1 : part_width + 2]
    normed_first_loc = take_cols(normed_first)
    grad_gain_first = jnp.sum(grad_first_loc * normed_first_loc, 0)
    grad_tokens = grad_middle + scale_first * (
        gain_first_loc * grad_first_loc - normed_first_loc * stat_first / full_width
    )
    grad_attn_w = jnp.concatenate(
        [
            cols_cols(hidden_first, grad_query_raw).astype(BF),
            cols_cols(hidden_first, grad_key_raw).astype(BF),
            cols_cols(hidden_first, grad_value_raw).astype(BF),
            grad_out_w.astype(BF),
        ],
        1,
    )
    attn_summed = lax.psum_scatter(
        grad_attn_w, "wide", scatter_dimension=0, tiled=True
    ).astype(F32)
    router_summed = lax.psum_scatter(grad_router_w, "wide", scatter_dimension=0, tiled=True)
    gains_summed = lax.psum(jnp.stack([grad_gain_first, grad_gain_second]), "wide")
    return (
        output,
        grad_tokens,
        gains_summed[0],
        attn_summed[:, :part_width],
        attn_summed[:, part_width : 2 * part_width],
        attn_summed[:, 2 * part_width : 3 * part_width],
        attn_summed[:, 3 * part_width :],
        gains_summed[1],
        router_summed,
        gate_out,
        up_out,
        down_out,
    )


def per_device(
    tokens, gain_attn, w_query, w_key, w_value, w_out, gain_ffn, w_router,
    w_gate, w_up, w_down, segment, parents, expert_ids, slot_order, cotangent,
):
    if lax.axis_size("wide") != 8 or lax.axis_size("narrow") != 4:
        return plain_device(
            tokens, gain_attn, w_query, w_key, w_value, w_out, gain_ffn, w_router,
            w_gate, w_up, w_down, segment, parents, expert_ids, slot_order, cotangent,
        )
    (
        in_w, out_w, expert_w, slot_mid, slot_grad, slot_gate, middle, hidden_first,
        token_parts, qkv, probs, attended, stat, rope, picks, columns,
    ) = front_call(
        tokens, cotangent, gain_attn, gain_ffn, (w_query, w_key, w_value, w_out),
        w_router.T, (w_gate, w_up, w_down), segment, parents, expert_ids.T, slot_order,
    )
    back_mid, back_exp, last_exp, back_ext, grads, early_experts = mid_call(
        slot_mid, slot_grad, slot_gate, token_parts, expert_w
    )
    (
        output, grad_tokens, summed, small, router, experts,
    ) = tail_call(
        back_mid, back_exp, last_exp, back_ext, grads, picks, stat, columns, middle, cotangent, tokens,
        token_parts, qkv, probs, attended, rope, hidden_first, in_w, out_w,
    )
    (
        gate_out, up_out, down_out, output, grad_tokens, grad_q, grad_k, grad_v, grad_o,
        grad_gain_first, grad_gain_second, router,
    ) = finish_call(early_experts, experts, output, grad_tokens, summed, small, router)
    return (
        output, grad_tokens, grad_gain_first.reshape(-1), grad_q, grad_k, grad_v, grad_o,
        grad_gain_second.reshape(-1), router.T, gate_out, up_out, down_out,
    )


def solution(mesh):
    pair = P("wide", "narrow")
    part = P("narrow")
    rows = P("wide", None)
    cube = P("wide", None, "narrow")
    return jax.shard_map(
        per_device,
        mesh=mesh,
        in_specs=(
            pair, part, pair, pair, pair, pair, part, rows, cube, cube, cube,
            rows, rows, rows, rows, pair,
        ),
        out_specs=(
            pair, pair, part, pair, pair, pair, pair, part, rows, cube, cube, cube,
        ),
        check_vma=False,
    )
```
